32 devices in a mesh: fsdp: 4 (over z), context: 4 (over y, x), tensor: 2 (over core).
Axes of the slice: x: 2, y: 2, z: 4, core: 2. Of those that a mesh axis runs over, the one named last changes fastest.
Arguments:
- tokens: bfloat16 [4, 1024, 2048], P('fsdp', 'context'), may hold values from -6 to 6
- out_grad: bfloat16 [4, 1024, 2048], P('fsdp', 'context'), may hold values from -6 to 6
- lengths: int32 [4, 4], P('fsdp'), may hold values from 1 to 512, 768 in all within a row
- attention_gain: float32 [2048], P(('fsdp', 'context')), may hold values from 0.5 to 1.5
- query_weight: float32 [2048, 2048], P(('fsdp', 'context'), 'tensor'), may hold values from -0.5 to 0.5
- key_weight: float32 [2048, 512], P(('fsdp', 'context'), 'tensor'), may hold values from -0.5 to 0.5
- value_weight: float32 [2048, 512], P(('fsdp', 'context'), 'tensor'), may hold values from -0.125 to 0.125
- output_weight: float32 [2048, 2048], P(('fsdp', 'context'), 'tensor'), may hold values from -3 to 3
- feed_gain: float32 [2048], P(('fsdp', 'context')), may hold values from 0.5 to 1.5
- gate_weight: float32 [2048, 8192], P(('fsdp', 'context'), 'tensor'), may hold values from -0.125 to 0.125
- up_weight: float32 [2048, 8192], P(('fsdp', 'context'), 'tensor'), may hold values from -0.125 to 0.125
- down_weight: float32 [2048, 8192], P(('fsdp', 'context'), 'tensor'), may hold values from -0.5 to 0.5
Outputs:
- output: bfloat16 [4, 1024, 2048], P('fsdp', 'context')
- input_grad: bfloat16 [4, 1024, 2048], P('fsdp', 'context')
- grad_attention_gain: float32 [2048], P(('fsdp', 'context'))
- grad_query: float32 [2048, 2048], P(('fsdp', 'context'), 'tensor')
- grad_key: float32 [2048, 512], P(('fsdp', 'context'), 'tensor')
- grad_value: float32 [2048, 512], P(('fsdp', 'context'), 'tensor')
- grad_output_weight: float32 [2048, 2048], P(('fsdp', 'context'), 'tensor')
- grad_feed_gain: float32 [2048], P(('fsdp', 'context'))
- grad_gate: float32 [2048, 8192], P(('fsdp', 'context'), 'tensor')
- grad_up: float32 [2048, 8192], P(('fsdp', 'context'), 'tensor')
- grad_down: float32 [2048, 8192], P(('fsdp', 'context'), 'tensor')
The draws below stay inside these ranges and needn't reach their ends.
Inputs may be any that keep to these rules, and one draw needn't show every extreme that they name: Each group's 4 lengths sum to 768 and the largest is exactly 512; sequences lie one after another from the group's first slot, the remaining slots are padding.
All inputs are finite; a program needn't handle non-finite values.
Results may differ from the reference program's by a relative error of at most 0.02.
Values may be sent and summed in bfloat16 or wider, within the bound.
A program may use at most 256 MiB of HBM per device.

```python
import math
import jax
import jax.numpy as jnp
import numpy as np
from jax import lax

D = 2048
HEADS = 32
KV_HEADS = 8
HEAD = 64
FF = 8192
NSEQ = 4
GROUPS = 4
GROUP_SLOTS = 1024
FILLED = 768
LONGEST = 512


def block_levels(key, shape, shards, smallest, largest):
    loudness = 1.0
    for dim, parts in shards:
        draws = jax.random.uniform(jax.random.fold_in(jax.random.fold_in(key, 6), dim), (parts,), jnp.float32, smallest / len(shards), largest / len(shards))
        loudness = loudness * jnp.repeat(jnp.exp(draws), shape[dim] // parts).reshape((-1,) + (1,) * (len(shape) - 1 - dim))
    return loudness


def length_profile(count, total, bound, slope):
    loads = [(1 << 20) // math.isqrt(grade ** slope) + 1 for grade in range(2, count + 1)]
    surplus, holding = total - bound - (count - 1), [1] * (count - 1)
    while surplus > 0:
        movable = [i for i in range(count - 1) if holding[i] < bound]
        pool, remaining = sum([loads[i] for i in movable]), surplus
        for i in movable:
            addition = min(bound - holding[i], max(1, remaining * loads[i] // pool), surplus)
            holding[i] = holding[i] + addition
            surplus = surplus - addition
    return np.array([bound] + holding)


def uneven(own_key, amount, total, most, skew):
    if amount == 2:
        one = jax.random.randint(own_key, (), max(1, total - most), min(most, total - 1) + 1)
        return jnp.stack([one, total - one])
    tallies = jnp.asarray(length_profile(amount, total, most, skew), jnp.int32)
    pairs = (amount - 1) // 2
    source_of, taker = tallies[1:1 + 2 * pairs:2], tallies[2:2 + 2 * pairs:2]
    slack = jnp.minimum(source_of - 1, most - taker)
    passed = jax.random.randint(jax.random.fold_in(own_key, 1), (pairs,), 0, 1 << 20) % (slack + 1)
    tallies = tallies.at[1:1 + 2 * pairs:2].set(source_of - passed).at[2:2 + 2 * pairs:2].set(taker + passed)
    return tallies[jax.random.permutation(jax.random.fold_in(own_key, 2), amount)]


def scatter_about(own_key, dims, spread, limit, split=(), kind=jnp.bfloat16):
    drawn = spread * jax.random.normal(own_key, dims, jnp.float32)
    if split:
        drawn = drawn * block_levels(own_key, dims, split, -0.22, 0.18)
    return jnp.clip(drawn, -limit, limit).astype(kind)


def setup_inputs(seed: int = 0) -> dict:
    splits = jax.random.split(jax.random.key(seed), 13)
    tokens = scatter_about(splits[0], (GROUPS, GROUP_SLOTS, D), 1.0, 6.0, ((0, 4), (1, 4)))
    out_grad = scatter_about(splits[1], (GROUPS, GROUP_SLOTS, D), 1.0, 6.0, ((0, 4), (1, 4)))
    lengths = jax.vmap(lambda own: uneven(own, NSEQ, FILLED, LONGEST, 2))(jax.random.split(splits[2], GROUPS)).reshape((GROUPS, NSEQ)).astype(jnp.int32)
    attention_gain = jnp.clip(1.0 + 0.1 * jax.random.normal(splits[3], (D,), jnp.float32), 0.5, 1.5)
    query_weight = scatter_about(splits[4], (D, HEADS * HEAD), (D // 16) ** -0.5, 0.5, ((0, 16), (1, 2)), jnp.float32)
    key_weight = scatter_about(splits[5], (D, KV_HEADS * HEAD), (D // 16) ** -0.5, 0.5, ((0, 16), (1, 2)), jnp.float32)
    value_weight = scatter_about(splits[6], (D, KV_HEADS * HEAD), D ** -0.5, 0.125, ((0, 16), (1, 2)), jnp.float32)
    output_weight = scatter_about(splits[7], (D, HEADS * HEAD), 4 ** -0.5, 3.0, ((0, 16), (1, 2)), jnp.float32)
    feed_gain = jnp.clip(1.0 + 0.1 * jax.random.normal(splits[8], (D,), jnp.float32), 0.5, 1.5)
    gate_weight = scatter_about(splits[9], (D, FF), D ** -0.5, 0.125, ((0, 16), (1, 2)), jnp.float32)
    up_weight = scatter_about(splits[10], (D, FF), D ** -0.5, 0.125, ((0, 16), (1, 2)), jnp.float32)
    down_weight = scatter_about(splits[11], (D, FF), (FF // 64) ** -0.5, 0.5, ((0, 16), (1, 2)), jnp.float32)
    return dict(tokens=tokens, out_grad=out_grad, lengths=lengths, attention_gain=attention_gain, query_weight=query_weight, key_weight=key_weight, value_weight=value_weight, output_weight=output_weight, feed_gain=feed_gain, gate_weight=gate_weight, up_weight=up_weight, down_weight=down_weight)


norm_eps = 1e-05
attention_mult = 0.015625
residual_mult = 0.22
rope_base = 10000000.0

@jax.custom_vjp
def low(v):
    return lax.optimization_barrier(v.astype(jnp.bfloat16)).astype(jnp.float32)

@jax.custom_vjp
def low_back(v):
    return v

def low_keep(v):
    return (low(v), None)

def low_pass(kept, grad):
    return (grad,)

def back_keep(v):
    return (v, None)

def back_low(kept, grad):
    return (low(grad),)
low.defvjp(low_keep, low_pass)
low_back.defvjp(back_keep, back_low)

def product(left, right):
    return jnp.dot(left, right, precision=lax.Precision.HIGHEST)

def slot_layout(seq_lengths, total_rows):
    seq_ends = jnp.cumsum(seq_lengths).astype(jnp.int32)
    starts = (seq_ends - seq_lengths).astype(jnp.int32)
    slot_ids = jnp.arange(total_rows, dtype=jnp.int32)
    before = (slot_ids[:, None] >= seq_ends[None, :]).astype(jnp.int32)
    segment = lax.optimization_barrier(jnp.sum(before, axis=1)).astype(jnp.int32)
    seq_count = seq_lengths.shape[0]
    valid_rows = segment < seq_count
    inside = (slot_ids[:, None] >= starts[None, :]) & (slot_ids[:, None] < seq_ends[None, :])
    position = lax.optimization_barrier(jnp.sum(jnp.where(inside, slot_ids[:, None] - starts[None, :], 0), axis=1)).astype(jnp.int32)
    segment = jnp.where(valid_rows, segment, seq_count + slot_ids).astype(jnp.int32)
    return (segment, position, valid_rows)

def rope_tables(position, width):
    half_width = width // 2
    frequency = rope_base ** (-jnp.arange(half_width, dtype=jnp.float32) * 2.0 / width)
    angles = position.astype(jnp.float32)[:, None] * frequency[None, :]
    angles = jnp.concatenate([angles, angles], axis=1)
    return (jnp.cos(angles), jnp.sin(angles))

def rotate(vectors, cos_table, sine_table):
    half_width = vectors.shape[-1] // 2
    turned = jnp.concatenate([-vectors[..., half_width:], vectors[..., :half_width]], axis=-1)
    return vectors * cos_table[:, None, :] + turned * sine_table[:, None, :]

def rms_norm(vectors, gain):
    inverse = lax.rsqrt(lax.optimization_barrier(jnp.mean(vectors * vectors, axis=-1, keepdims=True)) + norm_eps)
    return vectors * inverse * gain

def layer(inputs, weights, segment, position):
    attention_gain, query_weight, key_weight, value_weight, output_weight, feed_gain, gate_weight, up_weight, down_weight = weights
    total_rows = inputs.shape[0]
    per_group = HEADS // KV_HEADS
    normed = low(rms_norm(inputs, low(attention_gain)))
    queries = low_back(product(normed, low(query_weight)))
    keys_lin = low_back(product(normed, low(key_weight)))
    values = low_back(low(product(normed, low(value_weight))))
    cos_table, sine_table = rope_tables(position, HEAD)
    queries = low(rotate(queries.reshape(total_rows, HEADS, HEAD), cos_table, sine_table))
    keys_rot = low(rotate(keys_lin.reshape(total_rows, KV_HEADS, HEAD), cos_table, sine_table))
    values = values.reshape(total_rows, KV_HEADS, HEAD)
    slot_ids = jnp.arange(total_rows, dtype=jnp.int32)
    block_rows = min(512, total_rows)
    block_count = total_rows // block_rows

    def attend(pieces):
        query_block, segment_block, slot_block = pieces
        raw_scores = jnp.einsum('tkgd,skd->kgts', query_block, keys_rot, precision=lax.Precision.HIGHEST)
        scores = low_back(raw_scores) * attention_mult
        allowed = (segment_block[:, None] == segment[None, :]) & (slot_block[:, None] >= slot_ids[None, :])
        scores = jnp.where(allowed[None, None], scores, -1e+30)
        highest = lax.optimization_barrier(jnp.max(scores, axis=-1, keepdims=True))
        weight = jnp.exp(scores - highest)
        probabilities = weight / lax.optimization_barrier(jnp.sum(weight, axis=-1, keepdims=True))
        return jnp.einsum('kgts,skd->tkgd', low(probabilities), values, precision=lax.Precision.HIGHEST)
    mixed = lax.map(jax.checkpoint(attend), (queries.reshape(block_count, block_rows, KV_HEADS, per_group, HEAD), segment.reshape(block_count, block_rows), slot_ids.reshape(block_count, block_rows)))
    attended = low_back(low(mixed.reshape(total_rows, HEADS * HEAD)))
    attn_out = low_back(product(attended, low(output_weight).T))
    hidden_state = inputs + residual_mult * attn_out
    normed_two = low(rms_norm(hidden_state, low(feed_gain)))
    gate_out = low_back(product(normed_two, low(gate_weight)))
    up_out = low_back(product(normed_two, low(up_weight)))
    inner_act = low(jax.nn.silu(gate_out) * up_out)
    feed_out = low_back(product(inner_act, low(down_weight).T))
    return hidden_state + residual_mult * feed_out

def reference(tokens, out_grad, lengths, attention_gain, query_weight, key_weight, value_weight, output_weight, feed_gain, gate_weight, up_weight, down_weight):
    weights = (attention_gain, query_weight, key_weight, value_weight, output_weight, feed_gain, gate_weight, up_weight, down_weight)

    def one_group(totals, pieces):
        group_tokens, cotangent, group_lengths = pieces
        segment, position, valid_rows = slot_layout(group_lengths, group_tokens.shape[0])

        def forward(inputs, params):
            return layer(inputs, params, segment, position)
        result, pullback = jax.vjp(forward, group_tokens.astype(jnp.float32), weights)
        masked_cotangent = cotangent.astype(jnp.float32) * valid_rows[:, None].astype(jnp.float32)
        input_grad, weight_grads = pullback(masked_cotangent)
        totals = jax.tree.map(jnp.add, totals, weight_grads)
        return (totals, (result.astype(jnp.bfloat16), input_grad.astype(jnp.bfloat16)))
    empty_sums = jax.tree.map(jnp.zeros_like, weights)
    weight_grads, (output, input_grad) = lax.scan(one_group, empty_sums, (tokens, out_grad, lengths))
    return (output, input_grad, weight_grads[0], weight_grads[1], weight_grads[2], weight_grads[3], weight_grads[4], weight_grads[5], weight_grads[6], weight_grads[7], weight_grads[8])
```

```python
import jax
import jax.numpy as jnp
from jax import lax
from jax.sharding import PartitionSpec as P

HEAD = 64
FSDP, CONTEXT, TENSOR = "fsdp", "context", "tensor"


norm_eps = 1e-05
attention_mult = 0.015625
residual_mult = 0.22
rope_base = 10000000.0


def slot_layout(seq_lengths, total_rows):
    seq_ends = jnp.cumsum(seq_lengths)
    starts = seq_ends - seq_lengths
    slot_ids = jnp.arange(total_rows, dtype=jnp.int32)
    before = (slot_ids[:, None] >= seq_ends[None, :]).astype(jnp.int32)
    segment = jnp.sum(before, axis=1)
    seq_count = seq_lengths.shape[0]
    valid_rows = segment < seq_count
    inside = (slot_ids[:, None] >= starts[None, :]) & (slot_ids[:, None] < seq_ends[None, :])
    position = jnp.sum(jnp.where(inside, slot_ids[:, None] - starts[None, :], 0), axis=1)
    segment = jnp.where(valid_rows, segment, seq_count + slot_ids)
    return (segment, position, valid_rows)


def rope_tables(position, width):
    half_width = width // 2
    frequency = rope_base ** (-jnp.arange(half_width, dtype=jnp.float32) * 2.0 / width)
    angles = position.astype(jnp.float32)[:, None] * frequency[None, :]
    angles = jnp.concatenate([angles, angles], axis=1)
    return (jnp.cos(angles), jnp.sin(angles))


def turn_half(vectors):
    half_width = vectors.shape[-1] // 2
    return jnp.concatenate([-vectors[..., half_width:], vectors[..., :half_width]], axis=-1)


def rotate(vectors, cos_table, sine_table):
    return vectors * cos_table[:, None, :] + turn_half(vectors) * sine_table[:, None, :]


def rotate_back(grads, cos_table, sine_table):
    return grads * cos_table[:, None, :] - turn_half(grads * sine_table[:, None, :])


def norm_back(normed_grad, unit, gain, inverse):
    scaled = normed_grad * gain
    return inverse * (scaled - unit * jnp.mean(scaled * unit, axis=-1, keepdims=True))


def dot_first(left, right):
    return lax.dot_general(left, right, (((0,), (0,)), ((), ())), preferred_element_type=jnp.float32)


def dot_last(left, right):
    return lax.dot_general(left, right, (((1,), (1,)), ((), ())), preferred_element_type=jnp.float32)


def attention_shards(attention_gain, query_weight, key_weight, value_weight, output_weight):
    return (
        lax.all_gather(
            attention_gain.astype(jnp.bfloat16), (FSDP, CONTEXT), axis=0, tiled=True
        ),
        lax.all_gather(query_weight.astype(jnp.bfloat16), (FSDP, CONTEXT), axis=0, tiled=True),
        lax.all_gather(key_weight.astype(jnp.bfloat16), (FSDP, CONTEXT), axis=0, tiled=True),
        lax.all_gather(value_weight.astype(jnp.bfloat16), (FSDP, CONTEXT), axis=0, tiled=True),
        lax.all_gather(output_weight.astype(jnp.bfloat16), (FSDP, CONTEXT), axis=0, tiled=True),
    )


def feed_shards(feed_gain, gate_weight, up_weight, down_weight):
    return (
        lax.all_gather(feed_gain.astype(jnp.bfloat16), (FSDP, CONTEXT), axis=0, tiled=True),
        lax.all_gather(gate_weight.astype(jnp.bfloat16), (FSDP, CONTEXT), axis=0, tiled=True),
        lax.all_gather(up_weight.astype(jnp.bfloat16), (FSDP, CONTEXT), axis=0, tiled=True),
        lax.all_gather(down_weight.astype(jnp.bfloat16), (FSDP, CONTEXT), axis=0, tiled=True),
    )


def on_device(
    tokens,
    out_grad,
    lengths,
    attention_gain,
    query_weight,
    key_weight,
    value_weight,
    output_weight,
    feed_gain,
    gate_weight,
    up_weight,
    down_weight,
):
    local_rows = tokens.shape[1]
    group_rows = local_rows * lax.axis_size(CONTEXT)
    first_row = lax.axis_index(CONTEXT) * local_rows
    segment, position, valid_rows = slot_layout(lengths[0], group_rows)
    local_segment = lax.dynamic_slice_in_dim(segment, first_row, local_rows)
    local_position = lax.dynamic_slice_in_dim(position, first_row, local_rows)
    local_valid = lax.dynamic_slice_in_dim(valid_rows, first_row, local_rows)
    slot_ids = jnp.arange(group_rows, dtype=jnp.int32)
    local_slots = first_row + jnp.arange(local_rows, dtype=jnp.int32)
    allowed = (local_segment[:, None] == segment[None, :]) & (
        local_slots[:, None] >= slot_ids[None, :]
    )
    inputs = tokens[0].astype(jnp.float32)
    attn_set = attention_shards(
        attention_gain, query_weight, key_weight, value_weight, output_weight
    )
    gain_one = attn_set[0].astype(jnp.float32)
    inverse_one = lax.rsqrt(jnp.mean(inputs * inputs, axis=-1, keepdims=True) + norm_eps)
    unit_one = inputs * inverse_one
    normed_one = (unit_one * gain_one).astype(jnp.bfloat16)
    queries = jnp.dot(normed_one, attn_set[1], preferred_element_type=jnp.float32)
    keys_lin = jnp.dot(normed_one, attn_set[2], preferred_element_type=jnp.float32)
    values_low = jnp.dot(normed_one, attn_set[3], preferred_element_type=jnp.float32).astype(
        jnp.bfloat16
    )
    heads_local = queries.shape[1] // HEAD
    kv_local = keys_lin.shape[1] // HEAD
    per_group = heads_local // kv_local
    cos_table, sine_table = rope_tables(local_position, HEAD)
    queries_rot = rotate(
        queries.reshape(local_rows, heads_local, HEAD), cos_table, sine_table
    ).astype(jnp.bfloat16)
    keys_rot = rotate(keys_lin.reshape(local_rows, kv_local, HEAD), cos_table, sine_table).astype(
        jnp.bfloat16
    )
    keys_all, values_all = (
        lax.all_gather(
            keys_rot.reshape(local_rows, kv_local * HEAD), CONTEXT, axis=0, tiled=True
        ),
        lax.all_gather(values_low, CONTEXT, axis=0, tiled=True),
    )
    query_heads = queries_rot.reshape(local_rows, kv_local, per_group, HEAD).transpose(1, 0, 2, 3)
    key_heads = keys_all.reshape(group_rows, kv_local, HEAD).transpose(1, 0, 2)
    value_heads = values_all.reshape(group_rows, kv_local, HEAD).transpose(1, 0, 2)

    def head_scores(query_head, key_head):
        raw_scores = jnp.einsum(
            "tgd,sd->gts", query_head, key_head, preferred_element_type=jnp.float32
        )
        return jnp.where(allowed[None], raw_scores * attention_mult, -1e30)

    def head_forward(pieces):
        query_head, key_head, value_head = pieces
        scores = head_scores(query_head, key_head)
        highest = jnp.max(scores, axis=-1, keepdims=True)
        weight = jnp.exp(scores - highest)
        row_totals = jnp.sum(weight, axis=-1, keepdims=True)
        probabilities = (weight / row_totals).astype(jnp.bfloat16)
        mixed = jnp.einsum(
            "gts,sd->tgd", probabilities, value_head, preferred_element_type=jnp.float32
        )
        return (mixed, (highest + jnp.log(row_totals))[..., 0])

    mixed_heads, log_totals = lax.map(head_forward, (query_heads, key_heads, value_heads))
    attended = (
        mixed_heads.transpose(1, 0, 2, 3)
        .reshape(local_rows, heads_local * HEAD)
        .astype(jnp.bfloat16)
    )
    attn_part = dot_last(attended, attn_set[4])
    attn_out = lax.psum(attn_part.astype(jnp.bfloat16), TENSOR).astype(jnp.float32)
    hidden_state = inputs + residual_mult * attn_out
    feed_set = feed_shards(feed_gain, gate_weight, up_weight, down_weight)
    gain_two = feed_set[0].astype(jnp.float32)
    inverse_two = lax.rsqrt(
        jnp.mean(hidden_state * hidden_state, axis=-1, keepdims=True) + norm_eps
    )
    unit_two = hidden_state * inverse_two
    normed_two = (unit_two * gain_two).astype(jnp.bfloat16)
    gate_out = jnp.dot(normed_two, feed_set[1], preferred_element_type=jnp.float32)
    up_out = jnp.dot(normed_two, feed_set[2], preferred_element_type=jnp.float32)
    inner_act = (jax.nn.silu(gate_out) * up_out).astype(jnp.bfloat16)
    feed_part = dot_last(inner_act, feed_set[3])
    feed_out = lax.psum(feed_part.astype(jnp.bfloat16), TENSOR).astype(jnp.float32)
    output = hidden_state + residual_mult * feed_out
    cotangent = out_grad[0].astype(jnp.float32) * local_valid[:, None].astype(jnp.float32)
    feed_back = feed_shards(feed_gain, gate_weight, up_weight, down_weight)
    feed_grad = (residual_mult * cotangent).astype(jnp.bfloat16)
    down_term = dot_first(feed_grad, inner_act)
    inner_grad = jnp.dot(feed_grad, feed_back[3], preferred_element_type=jnp.float32)
    sigmoid_gate = jax.nn.sigmoid(gate_out)
    gate_grad = (
        inner_grad * up_out * sigmoid_gate * (1.0 + gate_out * (1.0 - sigmoid_gate))
    ).astype(jnp.bfloat16)
    up_grad = (inner_grad * jax.nn.silu(gate_out)).astype(jnp.bfloat16)
    gate_term = dot_first(normed_two, gate_grad)
    up_term = dot_first(normed_two, up_grad)
    normed_part_two = dot_last(gate_grad, feed_back[1])
    normed_part_two = normed_part_two + dot_last(up_grad, feed_back[2])
    normed_grad_two = lax.psum(normed_part_two.astype(jnp.bfloat16), TENSOR).astype(jnp.float32)
    feed_gain_term = jnp.sum(normed_grad_two * unit_two, axis=0)
    hidden_grad = cotangent + norm_back(normed_grad_two, unit_two, gain_two, inverse_two)
    feed_sums = (
        lax.psum_scatter(feed_gain_term, (FSDP, CONTEXT), scatter_dimension=0, tiled=True),
        lax.psum_scatter(gate_term, (FSDP, CONTEXT), scatter_dimension=0, tiled=True),
        lax.psum_scatter(up_term, (FSDP, CONTEXT), scatter_dimension=0, tiled=True),
        lax.psum_scatter(down_term, (FSDP, CONTEXT), scatter_dimension=0, tiled=True),
    )
    attn_back = attention_shards(
        attention_gain, query_weight, key_weight, value_weight, output_weight
    )
    attn_grad = (residual_mult * hidden_grad).astype(jnp.bfloat16)
    out_term = dot_first(attn_grad, attended)
    mixed_grad = jnp.dot(attn_grad, attn_back[4], preferred_element_type=jnp.float32).astype(
        jnp.bfloat16
    )
    mixed_grad_heads = mixed_grad.reshape(local_rows, kv_local, per_group, HEAD).transpose(
        1, 0, 2, 3
    )

    def head_backward(pieces):
        query_head, key_head, value_head, grad_head, log_head = pieces
        scores = head_scores(query_head, key_head)
        probabilities = jnp.exp(scores - log_head[..., None])
        prob_low = probabilities.astype(jnp.bfloat16)
        prob_grad = jnp.einsum(
            "tgd,sd->gts", grad_head, value_head, preferred_element_type=jnp.float32
        )
        row_dot = jnp.sum(probabilities * prob_grad, axis=-1, keepdims=True)
        score_grad = (attention_mult * probabilities * (prob_grad - row_dot)).astype(jnp.bfloat16)
        query_grad = jnp.einsum(
            "gts,sd->tgd", score_grad, key_head, preferred_element_type=jnp.float32
        )
        key_grad = jnp.einsum(
            "gts,tgd->sd", score_grad, query_head, preferred_element_type=jnp.float32
        )
        value_grad = jnp.einsum(
            "gts,tgd->sd", prob_low, grad_head, preferred_element_type=jnp.float32
        )
        return (query_grad, key_grad, value_grad)

    query_grads, key_grads, value_grads = lax.map(
        head_backward, (query_heads, key_heads, value_heads, mixed_grad_heads, log_totals)
    )
    key_grads = key_grads.transpose(1, 0, 2).reshape(group_rows, kv_local * HEAD)
    value_grads = value_grads.transpose(1, 0, 2).reshape(group_rows, kv_local * HEAD)
    local_key_grad, local_value_grad = (
        lax.psum_scatter(
            key_grads.astype(jnp.bfloat16), CONTEXT, scatter_dimension=0, tiled=True
        ).astype(jnp.float32),
        lax.psum_scatter(
            value_grads.astype(jnp.bfloat16), CONTEXT, scatter_dimension=0, tiled=True
        ).astype(jnp.float32),
    )
    query_grad_rot = query_grads.transpose(1, 0, 2, 3).reshape(local_rows, heads_local, HEAD)
    query_grad_low = (
        rotate_back(query_grad_rot, cos_table, sine_table)
        .reshape(local_rows, heads_local * HEAD)
        .astype(jnp.bfloat16)
    )
    key_grad_low = (
        rotate_back(local_key_grad.reshape(local_rows, kv_local, HEAD), cos_table, sine_table)
        .reshape(local_rows, kv_local * HEAD)
        .astype(jnp.bfloat16)
    )
    value_grad_low = local_value_grad.astype(jnp.bfloat16)
    query_term = dot_first(normed_one, query_grad_low)
    key_term = dot_first(normed_one, key_grad_low)
    value_term = dot_first(normed_one, value_grad_low)
    normed_part_one = dot_last(query_grad_low, attn_back[1])
    normed_part_one = normed_part_one + dot_last(key_grad_low, attn_back[2])
    normed_part_one = normed_part_one + dot_last(value_grad_low, attn_back[3])
    normed_grad_one = lax.psum(normed_part_one.astype(jnp.bfloat16), TENSOR).astype(jnp.float32)
    attn_gain_term = jnp.sum(normed_grad_one * unit_one, axis=0)
    input_grad = hidden_grad + norm_back(normed_grad_one, unit_one, gain_one, inverse_one)
    attn_sums = (
        lax.psum_scatter(attn_gain_term, (FSDP, CONTEXT), scatter_dimension=0, tiled=True),
        lax.psum_scatter(query_term, (FSDP, CONTEXT), scatter_dimension=0, tiled=True),
        lax.psum_scatter(key_term, (FSDP, CONTEXT), scatter_dimension=0, tiled=True),
        lax.psum_scatter(value_term, (FSDP, CONTEXT), scatter_dimension=0, tiled=True),
        lax.psum_scatter(out_term, (FSDP, CONTEXT), scatter_dimension=0, tiled=True),
    )
    return (
        output.astype(jnp.bfloat16)[None],
        input_grad.astype(jnp.bfloat16)[None],
        attn_sums[0],
        attn_sums[1],
        attn_sums[2],
        attn_sums[3],
        attn_sums[4],
        feed_sums[0],
        feed_sums[1],
        feed_sums[2],
        feed_sums[3],
    )


def pick_block(x, axis_name, axis):
    n = lax.axis_size(axis_name)
    size = x.shape[axis] // n
    return lax.dynamic_slice_in_dim(x, lax.axis_index(axis_name) * size, size, axis)


def gather_tokens(x, axes):
    return lax.all_gather(x, axes, axis=0, tiled=True)


def scatter_tokens(x, axes):
    return lax.psum_scatter(x, axes, scatter_dimension=0, tiled=True)


def on_device_split(
    tokens,
    out_grad,
    lengths,
    attention_gain,
    query_weight,
    key_weight,
    value_weight,
    output_weight,
    feed_gain,
    gate_weight,
    up_weight,
    down_weight,
):
    f32, bf16 = jnp.float32, jnp.bfloat16
    nz, nc, nt = (lax.axis_size(a) for a in (FSDP, CONTEXT, TENSOR))
    local_rows, width = tokens.shape[1:]
    group_rows = local_rows * nc
    filled = group_rows * 3 // 4
    part_rows = local_rows // nt
    wrows = query_weight.shape[0]
    kv_cols = key_weight.shape[1] // nc
    q_cols = query_weight.shape[1] // nc
    ff_cols = gate_weight.shape[1] // nz
    per_group = q_cols // kv_cols
    segment, position, valid_rows = slot_layout(lengths[0], group_rows)
    cos_table, sine_table = rope_tables(position, HEAD)

    attn_cols = jnp.concatenate(
        [w.astype(bf16).reshape(wrows, nc, -1) for w in (query_weight, key_weight, value_weight, output_weight)],
        axis=2,
    ).transpose(1, 0, 2)
    attn_cols = lax.all_to_all(attn_cols, CONTEXT, 0, 0, tiled=True)
    attn_all = lax.all_gather(attn_cols.reshape(nc * wrows, -1), FSDP, axis=0, tiled=True)
    w_qkv = attn_all[:, : q_cols + 2 * kv_cols]
    w_out = attn_all[:, q_cols + 2 * kv_cols :]
    gains = lax.all_gather(
        jnp.stack([attention_gain, feed_gain]).astype(bf16), (FSDP, CONTEXT), axis=1, tiled=True
    ).astype(f32)
    gain_one, gain_two = gains[0], gains[1]

    ff_part = jnp.concatenate(
        [w.astype(bf16).reshape(wrows, nz, -1) for w in (gate_weight, up_weight, down_weight)], axis=2
    ).transpose(1, 0, 2)
    ff_part = lax.all_to_all(ff_part, FSDP, 0, 0, tiled=True)
    ff_all = lax.all_gather(ff_part.reshape(nz * wrows, -1), CONTEXT, axis=0, tiled=True)
    w_gate_up = ff_all[:, : 2 * ff_cols]
    w_down = ff_all[:, 2 * ff_cols :]

    def to_ff(x):
        return x.reshape(-1, nz, nc, wrows).transpose(0, 2, 1, 3).reshape(x.shape)

    def from_ff(x):
        return x.reshape(-1, nc, nz, wrows).transpose(0, 2, 1, 3).reshape(x.shape)

    my_tokens = pick_block(tokens[0], TENSOR, 0)
    all_tokens = gather_tokens(my_tokens, (CONTEXT, TENSOR)).astype(f32)
    cotangent = pick_block(out_grad[0], TENSOR, 0)
    first_row = lax.axis_index(CONTEXT) * local_rows + lax.axis_index(TENSOR) * part_rows
    my_valid = lax.dynamic_slice_in_dim(valid_rows, first_row, part_rows)
    cotangent = cotangent.astype(f32) * my_valid[:, None].astype(f32)
    feed_grad = gather_tokens(to_ff((residual_mult * cotangent).astype(bf16)), (FSDP, TENSOR))

    inverse_all = lax.rsqrt(jnp.mean(all_tokens * all_tokens, axis=-1, keepdims=True) + norm_eps)
    normed_one = (all_tokens * inverse_all * gain_one).astype(bf16)
    qkv = jnp.dot(normed_one, w_qkv, preferred_element_type=f32)
    queries = rotate(qkv[:, :q_cols].reshape(group_rows, per_group, HEAD), cos_table, sine_table).astype(bf16)
    keys = rotate(qkv[:, q_cols : q_cols + kv_cols].reshape(group_rows, 1, HEAD), cos_table, sine_table).astype(bf16)[:, 0]
    values = qkv[:, q_cols + kv_cols :].astype(bf16)
    slot_ids = jnp.arange(filled, dtype=jnp.int32)
    allowed = (segment[:filled, None] == segment[None, :filled]) & (slot_ids[:, None] >= slot_ids[None, :])
    q_f, k_f, v_f = queries[:filled], keys[:filled], values[:filled]
    scores = jnp.einsum("tgd,sd->gts", q_f, k_f, preferred_element_type=f32)
    scores = jnp.where(allowed[None], scores * attention_mult, -1e30)
    highest = jnp.max(scores, axis=-1, keepdims=True)
    weight = jnp.exp(scores - highest)
    totals = jnp.sum(weight, axis=-1, keepdims=True)
    probabilities = weight / totals
    prob_low = probabilities.astype(bf16)
    mixed = jnp.einsum("gts,sd->tgd", prob_low, v_f, preferred_element_type=f32).astype(bf16)
    attended_f = mixed.reshape(filled, q_cols)
    attended = jnp.concatenate([attended_f, jnp.tile(values[filled:], (1, per_group))], axis=0)
    attn_part = dot_last(attended, w_out)
    attn_out = scatter_tokens(attn_part.astype(bf16), (CONTEXT, TENSOR)).astype(f32)
    my_inputs = my_tokens.astype(f32)
    hidden = my_inputs + residual_mult * attn_out
    inverse_two = lax.rsqrt(jnp.mean(hidden * hidden, axis=-1, keepdims=True) + norm_eps)
    unit_two = hidden * inverse_two
    normed_two = gather_tokens(to_ff((unit_two * gain_two).astype(bf16)), (FSDP, TENSOR))
    gate_up = jnp.dot(normed_two, w_gate_up, preferred_element_type=f32)
    gate_out, up_out = gate_up[:, :ff_cols], gate_up[:, ff_cols:]
    sig = jax.nn.sigmoid(gate_out)
    inner = (gate_out * sig * up_out).astype(bf16)
    feed_part = dot_last(inner, w_down)
    feed_out = from_ff(scatter_tokens(feed_part.astype(bf16), (FSDP, TENSOR)).astype(f32))
    output = (hidden + residual_mult * feed_out).astype(bf16)
    output = lax.all_gather(output, TENSOR, axis=0, tiled=True)

    inner_grad = jnp.dot(feed_grad, w_down, preferred_element_type=f32)
    gate_grad = (inner_grad * up_out * sig * (1.0 + gate_out * (1.0 - sig))).astype(bf16)
    up_grad = (inner_grad * gate_out * sig).astype(bf16)
    both_grad = jnp.concatenate([gate_grad, up_grad], axis=1)
    normed_part = dot_last(both_grad, w_gate_up)
    normed_grad_two = from_ff(scatter_tokens(normed_part.astype(bf16), (FSDP, TENSOR)).astype(f32))
    feed_gain_term = jnp.sum(normed_grad_two * unit_two, axis=0)
    hidden_grad = cotangent + norm_back(normed_grad_two, unit_two, gain_two, inverse_two)
    down_term = dot_first(feed_grad, inner).astype(bf16)
    gate_term = dot_first(normed_two, gate_grad).astype(bf16)
    up_term = dot_first(normed_two, up_grad).astype(bf16)
    ff_terms = jnp.concatenate(
        [
            lax.psum_scatter(t, CONTEXT, scatter_dimension=0, tiled=True).reshape(nz, wrows, -1)
            for t in (gate_term, up_term, down_term)
        ],
        axis=2,
    )
    ff_terms = lax.all_to_all(ff_terms, FSDP, 0, 0, tiled=True).astype(f32)

    def ff_out(i):
        return ff_terms[:, :, i * ff_cols : (i + 1) * ff_cols].transpose(1, 0, 2).reshape(wrows, -1)

    attn_grad = gather_tokens((residual_mult * hidden_grad).astype(bf16), (CONTEXT, TENSOR))[:filled]
    out_term = dot_first(attn_grad, attended_f)
    mixed_grad = jnp.dot(attn_grad, w_out, preferred_element_type=f32).astype(bf16).reshape(filled, per_group, HEAD)
    prob_grad = jnp.einsum("tgd,sd->gts", mixed_grad, v_f, preferred_element_type=f32)
    row_dot = jnp.sum(probabilities * prob_grad, axis=-1, keepdims=True)
    score_grad = (attention_mult * probabilities * (prob_grad - row_dot)).astype(bf16)
    query_grad = jnp.einsum("gts,sd->tgd", score_grad, k_f, preferred_element_type=f32)
    key_grad = jnp.einsum("gts,tgd->sd", score_grad, q_f, preferred_element_type=f32)
    value_grad = jnp.einsum("gts,tgd->sd", prob_low, mixed_grad, preferred_element_type=f32).astype(bf16)
    cos_f, sine_f = cos_table[:filled], sine_table[:filled]
    query_grad = rotate_back(query_grad, cos_f, sine_f).reshape(filled, q_cols).astype(bf16)
    key_grad = rotate_back(key_grad[:, None], cos_f, sine_f)[:, 0].astype(bf16)
    qkv_grad = jnp.concatenate([query_grad, key_grad, value_grad], axis=1)
    qkv_term = dot_first(normed_one[:filled], qkv_grad)
    attn_terms = jnp.concatenate([qkv_term, out_term], axis=1).astype(bf16)
    attn_terms = lax.psum_scatter(attn_terms, FSDP, scatter_dimension=0, tiled=True)
    attn_terms = lax.all_to_all(attn_terms.reshape(nc, wrows, -1), CONTEXT, 0, 0, tiled=True).astype(f32)

    def attn_out_cols(first, size):
        return attn_terms[:, :, first : first + size].transpose(1, 0, 2).reshape(wrows, -1)

    normed_part = dot_last(qkv_grad, w_qkv).astype(bf16)
    normed_part = jnp.pad(normed_part, ((0, group_rows - filled), (0, 0)))
    normed_grad_one = scatter_tokens(normed_part, (CONTEXT, TENSOR)).astype(f32)
    inverse_one = lax.rsqrt(jnp.mean(my_inputs * my_inputs, axis=-1, keepdims=True) + norm_eps)
    unit_one = my_inputs * inverse_one
    attn_gain_term = jnp.sum(normed_grad_one * unit_one, axis=0)
    input_grad = hidden_grad + norm_back(normed_grad_one, unit_one, gain_one, inverse_one)
    input_grad = lax.all_gather(input_grad.astype(bf16), TENSOR, axis=0, tiled=True)
    gain_terms = lax.psum(jnp.stack([attn_gain_term, feed_gain_term]), (FSDP, CONTEXT, TENSOR))
    gain_terms = pick_block(gain_terms, (FSDP, CONTEXT), 1)
    return (
        output[None],
        input_grad[None],
        gain_terms[0],
        attn_out_cols(0, q_cols),
        attn_out_cols(q_cols, kv_cols),
        attn_out_cols(q_cols + kv_cols, kv_cols),
        attn_out_cols(q_cols + 2 * kv_cols, q_cols),
        gain_terms[1],
        ff_out(0),
        ff_out(1),
        ff_out(2),
    )


def solution(mesh):
    kv_heads_local = 8 // mesh.shape[TENSOR]
    split = kv_heads_local == mesh.shape[CONTEXT]
    return jax.shard_map(
        on_device_split if split else on_device,
        mesh=mesh,
        in_specs=(
            P(FSDP, CONTEXT, None),
            P(FSDP, CONTEXT, None),
            P(FSDP, None),
            P((FSDP, CONTEXT)),
            P((FSDP, CONTEXT), TENSOR),
            P((FSDP, CONTEXT), TENSOR),
            P((FSDP, CONTEXT), TENSOR),
            P((FSDP, CONTEXT), TENSOR),
            P((FSDP, CONTEXT)),
            P((FSDP, CONTEXT), TENSOR),
            P((FSDP, CONTEXT), TENSOR),
            P((FSDP, CONTEXT), TENSOR),
        ),
        out_specs=(
            P(FSDP, CONTEXT, None),
            P(FSDP, CONTEXT, None),
            P((FSDP, CONTEXT)),
            P((FSDP, CONTEXT), TENSOR),
            P((FSDP, CONTEXT), TENSOR),
            P((FSDP, CONTEXT), TENSOR),
            P((FSDP, CONTEXT), TENSOR),
            P((FSDP, CONTEXT)),
            P((FSDP, CONTEXT), TENSOR),
            P((FSDP, CONTEXT), TENSOR),
            P((FSDP, CONTEXT), TENSOR),
        ),
        check_vma=False,
    )
```

```python
import jax
import jax.numpy as jnp
from jax import lax
from jax.experimental import pallas as pl
from jax.experimental.pallas import tpu as pltpu
from jax.sharding import PartitionSpec as P

HEAD = 64
FSDP, CONTEXT, TENSOR = "fsdp", "context", "tensor"


norm_eps = 1e-05
attention_mult = 0.015625
residual_mult = 0.22
rope_base = 10000000.0


def slot_layout(seq_lengths, total_rows):
    seq_ends = jnp.cumsum(seq_lengths)
    starts = seq_ends - seq_lengths
    slot_ids = jnp.arange(total_rows, dtype=jnp.int32)
    before = (slot_ids[:, None] >= seq_ends[None, :]).astype(jnp.int32)
    segment = jnp.sum(before, axis=1)
    seq_count = seq_lengths.shape[0]
    valid_rows = segment < seq_count
    inside = (slot_ids[:, None] >= starts[None, :]) & (slot_ids[:, None] < seq_ends[None, :])
    position = jnp.sum(jnp.where(inside, slot_ids[:, None] - starts[None, :], 0), axis=1)
    segment = jnp.where(valid_rows, segment, seq_count + slot_ids)
    return (segment, position, valid_rows)


def rope_tables(position, width):
    half_width = width // 2
    frequency = rope_base ** (-jnp.arange(half_width, dtype=jnp.float32) * 2.0 / width)
    angles = position.astype(jnp.float32)[:, None] * frequency[None, :]
    angles = jnp.concatenate([angles, angles], axis=1)
    return (jnp.cos(angles), jnp.sin(angles))


def turn_half(vectors):
    half_width = vectors.shape[-1] // 2
    return jnp.concatenate([-vectors[..., half_width:], vectors[..., :half_width]], axis=-1)


def rotate(vectors, cos_table, sine_table):
    return vectors * cos_table[:, None, :] + turn_half(vectors) * sine_table[:, None, :]


def rotate_back(grads, cos_table, sine_table):
    return grads * cos_table[:, None, :] - turn_half(grads * sine_table[:, None, :])


def norm_back(normed_grad, unit, gain, inverse):
    scaled = normed_grad * gain
    return inverse * (scaled - unit * jnp.mean(scaled * unit, axis=-1, keepdims=True))


def dot_first(left, right):
    return lax.dot_general(left, right, (((0,), (0,)), ((), ())), preferred_element_type=jnp.float32)


def dot_last(left, right):
    return lax.dot_general(left, right, (((1,), (1,)), ((), ())), preferred_element_type=jnp.float32)


def attention_shards(attention_gain, query_weight, key_weight, value_weight, output_weight):
    return (
        lax.all_gather(
            attention_gain.astype(jnp.bfloat16), (FSDP, CONTEXT), axis=0, tiled=True
        ),
        lax.all_gather(query_weight.astype(jnp.bfloat16), (FSDP, CONTEXT), axis=0, tiled=True),
        lax.all_gather(key_weight.astype(jnp.bfloat16), (FSDP, CONTEXT), axis=0, tiled=True),
        lax.all_gather(value_weight.astype(jnp.bfloat16), (FSDP, CONTEXT), axis=0, tiled=True),
        lax.all_gather(output_weight.astype(jnp.bfloat16), (FSDP, CONTEXT), axis=0, tiled=True),
    )


def feed_shards(feed_gain, gate_weight, up_weight, down_weight):
    return (
        lax.all_gather(feed_gain.astype(jnp.bfloat16), (FSDP, CONTEXT), axis=0, tiled=True),
        lax.all_gather(gate_weight.astype(jnp.bfloat16), (FSDP, CONTEXT), axis=0, tiled=True),
        lax.all_gather(up_weight.astype(jnp.bfloat16), (FSDP, CONTEXT), axis=0, tiled=True),
        lax.all_gather(down_weight.astype(jnp.bfloat16), (FSDP, CONTEXT), axis=0, tiled=True),
    )


def on_device(
    tokens,
    out_grad,
    lengths,
    attention_gain,
    query_weight,
    key_weight,
    value_weight,
    output_weight,
    feed_gain,
    gate_weight,
    up_weight,
    down_weight,
):
    local_rows = tokens.shape[1]
    group_rows = local_rows * lax.axis_size(CONTEXT)
    first_row = lax.axis_index(CONTEXT) * local_rows
    segment, position, valid_rows = slot_layout(lengths[0], group_rows)
    local_segment = lax.dynamic_slice_in_dim(segment, first_row, local_rows)
    local_position = lax.dynamic_slice_in_dim(position, first_row, local_rows)
    local_valid = lax.dynamic_slice_in_dim(valid_rows, first_row, local_rows)
    slot_ids = jnp.arange(group_rows, dtype=jnp.int32)
    local_slots = first_row + jnp.arange(local_rows, dtype=jnp.int32)
    allowed = (local_segment[:, None] == segment[None, :]) & (
        local_slots[:, None] >= slot_ids[None, :]
    )
    inputs = tokens[0].astype(jnp.float32)
    attn_set = attention_shards(
        attention_gain, query_weight, key_weight, value_weight, output_weight
    )
    gain_one = attn_set[0].astype(jnp.float32)
    inverse_one = lax.rsqrt(jnp.mean(inputs * inputs, axis=-1, keepdims=True) + norm_eps)
    unit_one = inputs * inverse_one
    normed_one = (unit_one * gain_one).astype(jnp.bfloat16)
    queries = jnp.dot(normed_one, attn_set[1], preferred_element_type=jnp.float32)
    keys_lin = jnp.dot(normed_one, attn_set[2], preferred_element_type=jnp.float32)
    values_low = jnp.dot(normed_one, attn_set[3], preferred_element_type=jnp.float32).astype(
        jnp.bfloat16
    )
    heads_local = queries.shape[1] // HEAD
    kv_local = keys_lin.shape[1] // HEAD
    per_group = heads_local // kv_local
    cos_table, sine_table = rope_tables(local_position, HEAD)
    queries_rot = rotate(
        queries.reshape(local_rows, heads_local, HEAD), cos_table, sine_table
    ).astype(jnp.bfloat16)
    keys_rot = rotate(keys_lin.reshape(local_rows, kv_local, HEAD), cos_table, sine_table).astype(
        jnp.bfloat16
    )
    keys_all, values_all = (
        lax.all_gather(
            keys_rot.reshape(local_rows, kv_local * HEAD), CONTEXT, axis=0, tiled=True
        ),
        lax.all_gather(values_low, CONTEXT, axis=0, tiled=True),
    )
    query_heads = queries_rot.reshape(local_rows, kv_local, per_group, HEAD).transpose(1, 0, 2, 3)
    key_heads = keys_all.reshape(group_rows, kv_local, HEAD).transpose(1, 0, 2)
    value_heads = values_all.reshape(group_rows, kv_local, HEAD).transpose(1, 0, 2)

    def head_scores(query_head, key_head):
        raw_scores = jnp.einsum(
            "tgd,sd->gts", query_head, key_head, preferred_element_type=jnp.float32
        )
        return jnp.where(allowed[None], raw_scores * attention_mult, -1e30)

    def head_forward(pieces):
        query_head, key_head, value_head = pieces
        scores = head_scores(query_head, key_head)
        highest = jnp.max(scores, axis=-1, keepdims=True)
        weight = jnp.exp(scores - highest)
        row_totals = jnp.sum(weight, axis=-1, keepdims=True)
        probabilities = (weight / row_totals).astype(jnp.bfloat16)
        mixed = jnp.einsum(
            "gts,sd->tgd", probabilities, value_head, preferred_element_type=jnp.float32
        )
        return (mixed, (highest + jnp.log(row_totals))[..., 0])

    mixed_heads, log_totals = lax.map(head_forward, (query_heads, key_heads, value_heads))
    attended = (
        mixed_heads.transpose(1, 0, 2, 3)
        .reshape(local_rows, heads_local * HEAD)
        .astype(jnp.bfloat16)
    )
    attn_part = dot_last(attended, attn_set[4])
    attn_out = lax.psum(attn_part.astype(jnp.bfloat16), TENSOR).astype(jnp.float32)
    hidden_state = inputs + residual_mult * attn_out
    feed_set = feed_shards(feed_gain, gate_weight, up_weight, down_weight)
    gain_two = feed_set[0].astype(jnp.float32)
    inverse_two = lax.rsqrt(
        jnp.mean(hidden_state * hidden_state, axis=-1, keepdims=True) + norm_eps
    )
    unit_two = hidden_state * inverse_two
    normed_two = (unit_two * gain_two).astype(jnp.bfloat16)
    gate_out = jnp.dot(normed_two, feed_set[1], preferred_element_type=jnp.float32)
    up_out = jnp.dot(normed_two, feed_set[2], preferred_element_type=jnp.float32)
    inner_act = (jax.nn.silu(gate_out) * up_out).astype(jnp.bfloat16)
    feed_part = dot_last(inner_act, feed_set[3])
    feed_out = lax.psum(feed_part.astype(jnp.bfloat16), TENSOR).astype(jnp.float32)
    output = hidden_state + residual_mult * feed_out
    cotangent = out_grad[0].astype(jnp.float32) * local_valid[:, None].astype(jnp.float32)
    feed_back = feed_shards(feed_gain, gate_weight, up_weight, down_weight)
    feed_grad = (residual_mult * cotangent).astype(jnp.bfloat16)
    down_term = dot_first(feed_grad, inner_act)
    inner_grad = jnp.dot(feed_grad, feed_back[3], preferred_element_type=jnp.float32)
    sigmoid_gate = jax.nn.sigmoid(gate_out)
    gate_grad = (
        inner_grad * up_out * sigmoid_gate * (1.0 + gate_out * (1.0 - sigmoid_gate))
    ).astype(jnp.bfloat16)
    up_grad = (inner_grad * jax.nn.silu(gate_out)).astype(jnp.bfloat16)
    gate_term = dot_first(normed_two, gate_grad)
    up_term = dot_first(normed_two, up_grad)
    normed_part_two = dot_last(gate_grad, feed_back[1])
    normed_part_two = normed_part_two + dot_last(up_grad, feed_back[2])
    normed_grad_two = lax.psum(normed_part_two.astype(jnp.bfloat16), TENSOR).astype(jnp.float32)
    feed_gain_term = jnp.sum(normed_grad_two * unit_two, axis=0)
    hidden_grad = cotangent + norm_back(normed_grad_two, unit_two, gain_two, inverse_two)
    feed_sums = (
        lax.psum_scatter(feed_gain_term, (FSDP, CONTEXT), scatter_dimension=0, tiled=True),
        lax.psum_scatter(gate_term, (FSDP, CONTEXT), scatter_dimension=0, tiled=True),
        lax.psum_scatter(up_term, (FSDP, CONTEXT), scatter_dimension=0, tiled=True),
        lax.psum_scatter(down_term, (FSDP, CONTEXT), scatter_dimension=0, tiled=True),
    )
    attn_back = attention_shards(
        attention_gain, query_weight, key_weight, value_weight, output_weight
    )
    attn_grad = (residual_mult * hidden_grad).astype(jnp.bfloat16)
    out_term = dot_first(attn_grad, attended)
    mixed_grad = jnp.dot(attn_grad, attn_back[4], preferred_element_type=jnp.float32).astype(
        jnp.bfloat16
    )
    mixed_grad_heads = mixed_grad.reshape(local_rows, kv_local, per_group, HEAD).transpose(
        1, 0, 2, 3
    )

    def head_backward(pieces):
        query_head, key_head, value_head, grad_head, log_head = pieces
        scores = head_scores(query_head, key_head)
        probabilities = jnp.exp(scores - log_head[..., None])
        prob_low = probabilities.astype(jnp.bfloat16)
        prob_grad = jnp.einsum(
            "tgd,sd->gts", grad_head, value_head, preferred_element_type=jnp.float32
        )
        row_dot = jnp.sum(probabilities * prob_grad, axis=-1, keepdims=True)
        score_grad = (attention_mult * probabilities * (prob_grad - row_dot)).astype(jnp.bfloat16)
        query_grad = jnp.einsum(
            "gts,sd->tgd", score_grad, key_head, preferred_element_type=jnp.float32
        )
        key_grad = jnp.einsum(
            "gts,tgd->sd", score_grad, query_head, preferred_element_type=jnp.float32
        )
        value_grad = jnp.einsum(
            "gts,tgd->sd", prob_low, grad_head, preferred_element_type=jnp.float32
        )
        return (query_grad, key_grad, value_grad)

    query_grads, key_grads, value_grads = lax.map(
        head_backward, (query_heads, key_heads, value_heads, mixed_grad_heads, log_totals)
    )
    key_grads = key_grads.transpose(1, 0, 2).reshape(group_rows, kv_local * HEAD)
    value_grads = value_grads.transpose(1, 0, 2).reshape(group_rows, kv_local * HEAD)
    local_key_grad, local_value_grad = (
        lax.psum_scatter(
            key_grads.astype(jnp.bfloat16), CONTEXT, scatter_dimension=0, tiled=True
        ).astype(jnp.float32),
        lax.psum_scatter(
            value_grads.astype(jnp.bfloat16), CONTEXT, scatter_dimension=0, tiled=True
        ).astype(jnp.float32),
    )
    query_grad_rot = query_grads.transpose(1, 0, 2, 3).reshape(local_rows, heads_local, HEAD)
    query_grad_low = (
        rotate_back(query_grad_rot, cos_table, sine_table)
        .reshape(local_rows, heads_local * HEAD)
        .astype(jnp.bfloat16)
    )
    key_grad_low = (
        rotate_back(local_key_grad.reshape(local_rows, kv_local, HEAD), cos_table, sine_table)
        .reshape(local_rows, kv_local * HEAD)
        .astype(jnp.bfloat16)
    )
    value_grad_low = local_value_grad.astype(jnp.bfloat16)
    query_term = dot_first(normed_one, query_grad_low)
    key_term = dot_first(normed_one, key_grad_low)
    value_term = dot_first(normed_one, value_grad_low)
    normed_part_one = dot_last(query_grad_low, attn_back[1])
    normed_part_one = normed_part_one + dot_last(key_grad_low, attn_back[2])
    normed_part_one = normed_part_one + dot_last(value_grad_low, attn_back[3])
    normed_grad_one = lax.psum(normed_part_one.astype(jnp.bfloat16), TENSOR).astype(jnp.float32)
    attn_gain_term = jnp.sum(normed_grad_one * unit_one, axis=0)
    input_grad = hidden_grad + norm_back(normed_grad_one, unit_one, gain_one, inverse_one)
    attn_sums = (
        lax.psum_scatter(attn_gain_term, (FSDP, CONTEXT), scatter_dimension=0, tiled=True),
        lax.psum_scatter(query_term, (FSDP, CONTEXT), scatter_dimension=0, tiled=True),
        lax.psum_scatter(key_term, (FSDP, CONTEXT), scatter_dimension=0, tiled=True),
        lax.psum_scatter(value_term, (FSDP, CONTEXT), scatter_dimension=0, tiled=True),
        lax.psum_scatter(out_term, (FSDP, CONTEXT), scatter_dimension=0, tiled=True),
    )
    return (
        output.astype(jnp.bfloat16)[None],
        input_grad.astype(jnp.bfloat16)[None],
        attn_sums[0],
        attn_sums[1],
        attn_sums[2],
        attn_sums[3],
        attn_sums[4],
        feed_sums[0],
        feed_sums[1],
        feed_sums[2],
        feed_sums[3],
    )


def flip(i, k):
    if k == 0:
        return i
    if k == 1:
        return i + 1 - 2 * lax.rem(i, 2)
    if k == 2:
        return lax.rem(i + 2, 4)
    return 3 - i


class Copies:
    def __init__(self, send, receive):
        self.send, self.receive = send, receive
        self.count, self.started = 0, []

    def index(self):
        self.count += 1
        return self.count - 1

    def make(self, i, source, target, device):
        return pltpu.make_async_remote_copy(
            src_ref=source,
            dst_ref=target,
            send_sem=self.send.at[i],
            recv_sem=self.receive.at[i],
            device_id=device,
            device_id_type=pl.DeviceIdType.MESH,
        )

    def start(self, source, target, device, i=None):
        i = self.index() if i is None else i
        copy = self.make(i, source, target, device)
        copy.start()
        self.started.append(copy)
        return copy


def greet(partners):
    barrier = pltpu.get_barrier_semaphore()
    for device in partners:
        pl.semaphore_signal(barrier, inc=1, device_id=device, device_id_type=pl.DeviceIdType.MESH)
    pl.semaphore_wait(barrier, len(partners))


def weights_in_kernel(wa, wf, xt, gain, wa_all, wf_all, x_all, gain_all, send, receive, local):
    z, c, t = (lax.axis_index(a) for a in (FSDP, CONTEXT, TENSOR))
    peers = [(flip(z, i), flip(c, j), t) for i in range(4) for j in range(4) if i or j]
    core = (z, c, 1 - t)
    greet(peers + [core])
    net = Copies(send, receive)
    ends = []
    own = []
    for i, (source, target) in enumerate(
        (
            (wa.at[c], wa_all.at[z, c]),
            (xt, x_all.at[c]),
            (wf.at[z], wf_all.at[z, c]),
            (gain, gain_all.at[z, c]),
        )
    ):
        own.append(pltpu.make_async_copy(source, target, local.at[i]))
        own[-1].start()

    attn_in = [net.start(wa.at[flip(c, k)], wa_all.at[z, c], (z, flip(c, k), t)) for k in (1, 2, 3)]
    tokens_in = [net.start(xt.at[t], x_all.at[c, t], (z, flip(c, k), t)) for k in (1, 2, 3)]
    for device in peers:
        ends.append(net.start(gain, gain_all.at[z, c], device))
    own[2].wait()
    forward = []
    middle = (z == 1) | (z == 2)
    for j in range(4):
        if j:
            attn_in[j - 1].wait_recv()
        else:
            own[0].wait()
        piece = wa_all.at[z, flip(c, j)]
        ends.append(net.start(piece, piece, (flip(z, 1), c, t)))
        two = net.start(piece, piece, (flip(z, 2), c, t))
        three = net.index()
        direct = net.make(three, piece, piece, (3 - z, c, t))
        pl.when(middle)(direct.start)
        passed_piece = wa_all.at[flip(z, 2), flip(c, j)]
        passed = pltpu.make_async_remote_copy(
            src_ref=passed_piece,
            dst_ref=passed_piece,
            send_sem=send.at[net.index()],
            recv_sem=receive.at[three],
            device_id=(flip(z, 1), c, t),
            device_id_type=pl.DeviceIdType.MESH,
        )
        forward.append((two, direct, passed))
    ff_in = {k: net.start(wf.at[flip(z, k)], wf_all.at[z, c], (flip(z, k), c, t)) for k in (3, 2)}
    ff_out = {0: [net.start(wf_all.at[z, c], wf_all.at[z, c], (z, flip(c, k), t)) for k in (1, 2)]}
    swaps = []
    for k, copy in zip((1, 2, 3), tokens_in):
        copy.wait_recv()
        piece = x_all.at[flip(c, k), t]
        swaps.append(net.start(piece, piece, core))
    for two, direct, passed in forward:
        two.wait_recv()
        pl.when(middle)(passed.start)
    ff_in[1] = net.start(wf.at[flip(z, 1)], wf_all.at[z, c], (flip(z, 1), c, t))
    halves = []

    def corner(k):
        zs = flip(z, k)
        one, two = ff_out[k]
        two.wait_recv()
        piece = wf_all.at[zs, flip(c, 2), pl.ds(0, 64)]
        halves.append(net.start(piece, piece, (z, flip(c, 1), t)))
        one.wait_recv()
        piece = wf_all.at[zs, flip(c, 1), pl.ds(64, 64)]
        halves.append(net.start(piece, piece, (z, flip(c, 2), t)))

    last = 0
    for k in (3, 2, 1):
        ff_in[k].wait_recv()
        piece = wf_all.at[flip(z, k), c]
        ff_out[k] = [net.start(piece, piece, (z, flip(c, j), t)) for j in (1, 2)]
        corner(last)
        last = k
    corner(last)
    for copy in halves + swaps + ends:
        copy.wait_recv()
    for _, direct, passed in forward:
        direct.wait_recv()
        pl.when(middle)(direct.wait_send)
        pl.when(middle)(passed.wait_send)
    for copy in net.started:
        copy.wait_send()
    own[1].wait()
    own[3].wait()


def weights_in(wa, wf, xt, gain):
    bf16 = jnp.bfloat16
    shapes = ((4, 4) + wa.shape[1:], (4, 4) + wf.shape[1:], (4,) + xt.shape, (4, 4) + gain.shape)
    copies = 128
    return pl.pallas_call(
        weights_in_kernel,
        out_shape=[jax.ShapeDtypeStruct(s, bf16) for s in shapes],
        in_specs=[pl.BlockSpec(memory_space=pltpu.VMEM)] * 4,
        out_specs=[pl.BlockSpec(memory_space=pl.ANY)] * 4,
        scratch_shapes=[
            pltpu.SemaphoreType.DMA((copies,)),
            pltpu.SemaphoreType.DMA((copies,)),
            pltpu.SemaphoreType.DMA((4,)),
        ],
        compiler_params=pltpu.CompilerParams(collective_id=1, has_side_effects=True, vmem_limit_bytes=48 * 2**20),
    )(wa, wf, xt, gain)


def swap(x, axis, k):
    return lax.ppermute(x, axis, [(i, i ^ k) for i in range(lax.axis_size(axis))])


def after(x, *others):
    return lax.optimization_barrier((x, *others))[0]


def put(buffer, block, *index):
    lead = len(index)
    block = block.reshape((1,) * lead + buffer.shape[lead:])
    zero = jnp.int32(0)
    start = tuple(jnp.asarray(i, jnp.int32) for i in index) + (zero,) * (buffer.ndim - lead)
    return lax.dynamic_update_slice(buffer, block, start)


def cut(x, index, size, axis):
    return lax.dynamic_slice_in_dim(x, index * size, size, axis)


def fsdp_blocks(x):
    one = swap(x, FSDP, 1)
    two = swap(x, FSDP, 2)
    three = lax.ppermute(x, FSDP, [(1, 2), (2, 1)]) + lax.ppermute(two, FSDP, [(2, 3), (1, 0)])
    return [x, one, two, three]


def context_blocks(x, axis):
    one = swap(x, CONTEXT, 1)
    two = swap(x, CONTEXT, 2)
    half = x.shape[axis] // 2
    low = swap(lax.slice_in_dim(two, 0, half, axis=axis), CONTEXT, 1)
    high = swap(lax.slice_in_dim(one, half, 2 * half, axis=axis), CONTEXT, 2)
    return one, two, low, high


def grads_out_kernel(
    ff, at, gate_out, up_out, down_out, query_out, key_out, value_out, output_out,
    terms, corner_x, corner_y, side_x, side_y, landed, at_terms, at_in, at_total, at_landed, send, receive, local,
):
    f32, bf16 = jnp.float32, jnp.bfloat16
    z, c, t = (lax.axis_index(a) for a in (FSDP, CONTEXT, TENSOR))
    greet([(flip(z, k), c, t) for k in (1, 2, 3)] + [(z, flip(c, k), t) for k in (1, 2, 3)])
    net = Copies(send, receive)
    rows = ff.shape[2]
    half = rows // 2
    order = (3, 2, 1, 0)
    loads = {}
    for k in order:
        zs = flip(z, k)
        loads[k] = pltpu.make_async_copy(ff.at[zs], terms.at[zs], local.at[k])
        loads[k].start()
    attn_load = pltpu.make_async_copy(at, at_terms, local.at[4])
    attn_load.start()
    attn_load.wait()
    attn_in = [net.start(at_terms.at[flip(z, k)], at_in.at[k - 1], (flip(z, k), c, t)) for k in (3, 2, 1)]
    first = {}
    for k in order:
        zs = flip(z, k)
        loads[k].wait()
        first[k] = (
            net.start(terms.at[zs, flip(c, 3), pl.ds(0, half)], corner_x.at[k], (z, flip(c, 1), t)),
            net.start(terms.at[zs, flip(c, 3), pl.ds(half, half)], corner_y.at[k], (z, flip(c, 2), t)),
        )
    second = {}
    for k in order:
        zs = flip(z, k)
        for copy in first[k]:
            copy.wait_recv()
        low, high = pl.ds(0, half), pl.ds(half, half)
        xb, yb = flip(c, 1), flip(c, 2)
        terms[zs, yb, low] = (terms[zs, yb, low].astype(f32) + corner_x[k].astype(f32)).astype(bf16)
        terms[zs, xb, high] = (terms[zs, xb, high].astype(f32) + corner_y[k].astype(f32)).astype(bf16)
        second[k] = (
            net.start(terms.at[zs, yb], side_y.at[k], (z, yb, t)),
            net.start(terms.at[zs, xb], side_x.at[k], (z, xb, t)),
        )
    for copy in attn_in:
        copy.wait_recv()
    for j in range(4):
        total = at_terms[z, j].astype(f32)
        for i in range(3):
            total = total + at_in[i, j].astype(f32)
        at_total[j] = total.astype(bf16)
    attn_out = [net.start(at_total.at[flip(c, k)], at_landed.at[c], (z, flip(c, k), t)) for k in (1, 2, 3)]
    at_landed[c] = at_total[c]
    third = {}
    for k in order:
        zs = flip(z, k)
        for copy in second[k]:
            copy.wait_recv()
        total = terms[zs, c].astype(f32) + side_x[k].astype(f32) + side_y[k].astype(f32)
        if k:
            terms[zs, c] = total.astype(bf16)
            third[k] = net.start(terms.at[zs, c], landed.at[k], (zs, c, t))
        else:
            landed[0] = total.astype(bf16)
    size = gate_out.shape[1] // 4
    for k in (0, 3, 2, 1):
        if k:
            third[k].wait_recv()
        zs = flip(z, k)
        columns = pl.ds(pl.multiple_of(zs * size, size), size)
        for i, out in enumerate((gate_out, up_out, down_out)):
            out[:, columns] = landed[k, :, i * size : (i + 1) * size].astype(f32)
    for copy in attn_out:
        copy.wait_recv()
    begin = 0
    for out in (query_out, key_out, value_out, output_out):
        size = out.shape[1] // 4
        for j in range(4):
            out[:, j * size : (j + 1) * size] = at_landed[j, :, begin : begin + size].astype(f32)
        begin += size
    for copy in net.started:
        copy.wait_send()


def grads_out(ff, at, sizes):
    bf16, f32 = jnp.bfloat16, jnp.float32
    rows, cols = ff.shape[2:]
    attn_cols = at.shape[3]
    copies = 32
    return pl.pallas_call(
        grads_out_kernel,
        out_shape=[jax.ShapeDtypeStruct((rows, s), f32) for s in sizes],
        in_specs=[pl.BlockSpec(memory_space=pl.ANY)] * 2,
        out_specs=[pl.BlockSpec(memory_space=pltpu.VMEM)] * len(sizes),
        scratch_shapes=[
            pltpu.VMEM((4, 4, rows, cols), bf16),
            pltpu.VMEM((4, rows // 2, cols), bf16),
            pltpu.VMEM((4, rows // 2, cols), bf16),
            pltpu.VMEM((4, rows, cols), bf16),
            pltpu.VMEM((4, rows, cols), bf16),
            pltpu.VMEM((4, rows, cols), bf16),
            pltpu.VMEM((4, 4, rows, attn_cols), bf16),
            pltpu.VMEM((3, 4, rows, attn_cols), bf16),
            pltpu.VMEM((4, rows, attn_cols), bf16),
            pltpu.VMEM((4, rows, attn_cols), bf16),
            pltpu.SemaphoreType.DMA((copies,)),
            pltpu.SemaphoreType.DMA((copies,)),
            pltpu.SemaphoreType.DMA((5,)),
        ],
        compiler_params=pltpu.CompilerParams(collective_id=2, has_side_effects=True, vmem_limit_bytes=60 * 2**20),
    )(ff, at)


def on_device_split(
    tokens,
    out_grad,
    lengths,
    attention_gain,
    query_weight,
    key_weight,
    value_weight,
    output_weight,
    feed_gain,
    gate_weight,
    up_weight,
    down_weight,
):
    f32, bf16 = jnp.float32, jnp.bfloat16
    nz, nc, nt = (lax.axis_size(a) for a in (FSDP, CONTEXT, TENSOR))
    z, c, t = (lax.axis_index(a) for a in (FSDP, CONTEXT, TENSOR))
    local_rows, width = tokens.shape[1:]
    group_rows = local_rows * nc
    filled = group_rows * 3 // 4
    part = local_rows // nt
    wrows = query_weight.shape[0]
    kv_cols = key_weight.shape[1] // nc
    q_cols = query_weight.shape[1] // nc
    qkv_cols = q_cols + 2 * kv_cols
    ff_cols = gate_weight.shape[1] // nz
    per_group = q_cols // kv_cols
    segment, position, valid_rows = slot_layout(lengths[0], group_rows)
    cos_table, sine_table = rope_tables(position, HEAD)

    wa = jnp.concatenate(
        [
            w.astype(bf16).reshape(wrows, nc, -1).transpose(1, 0, 2)
            for w in (query_weight, key_weight, value_weight, output_weight)
        ],
        axis=2,
    )
    wf = jnp.concatenate(
        [w.astype(bf16).reshape(wrows, nz, ff_cols).transpose(1, 0, 2) for w in (gate_weight, up_weight, down_weight)],
        axis=2,
    )
    gain = jnp.pad(jnp.stack([attention_gain, feed_gain]).astype(bf16), ((0, 14), (0, 0)))
    wa, wf, all_tokens, gains = weights_in(wa, wf, tokens[0].reshape(nt, part, width), gain)
    gains = gains[:, :, :2].transpose(2, 0, 1, 3).reshape(2, width).astype(f32)
    gain_one, gain_two = gains[0], gains[1]
    w_qkv = wa[..., :qkv_cols].reshape(width, qkv_cols)
    w_out = wa[..., qkv_cols:].reshape(width, q_cols)
    my_tokens = cut(tokens[0], t, part, 0)
    all_tokens = all_tokens.reshape(group_rows, width).astype(f32)
    w_gate_up = wf[..., : 2 * ff_cols].reshape(width, 2 * ff_cols)
    w_down = wf[..., 2 * ff_cols :].reshape(width, ff_cols)

    my_valid = lax.dynamic_slice_in_dim(valid_rows, c * local_rows + t * part, part)
    cotangent = cut(out_grad[0], t, part, 0).astype(f32) * my_valid[:, None].astype(f32)
    feed_grads = fsdp_blocks((residual_mult * cotangent).astype(bf16))
    feed_grads = [jnp.concatenate([b, swap(b, TENSOR, 1)], axis=0) for b in feed_grads]

    inverse_all = lax.rsqrt(jnp.mean(all_tokens * all_tokens, axis=-1, keepdims=True) + norm_eps)
    unit_all = all_tokens * inverse_all
    normed_one = (unit_all * gain_one).astype(bf16)
    qkv = jnp.dot(normed_one, w_qkv, preferred_element_type=f32)
    queries = rotate(qkv[:, :q_cols].reshape(group_rows, per_group, HEAD), cos_table, sine_table).astype(bf16)
    keys = rotate(qkv[:, q_cols : q_cols + kv_cols].reshape(group_rows, 1, HEAD), cos_table, sine_table)
    keys = keys.astype(bf16)[:, 0]
    values = qkv[:, q_cols + kv_cols :].astype(bf16)
    slot_ids = jnp.arange(filled, dtype=jnp.int32)
    allowed = (segment[:filled, None] == segment[None, :filled]) & (slot_ids[:, None] >= slot_ids[None, :])
    q_f, k_f, v_f = queries[:filled], keys[:filled], values[:filled]
    scores = jnp.einsum("tgd,sd->gts", q_f, k_f, preferred_element_type=f32)
    scores = jnp.where(allowed[None], scores * attention_mult, -1e30)
    highest = jnp.max(scores, axis=-1, keepdims=True)
    weight = jnp.exp(scores - highest)
    totals = jnp.sum(weight, axis=-1, keepdims=True)
    probabilities = weight / totals
    prob_low = probabilities.astype(bf16)
    mixed = jnp.einsum("gts,sd->tgd", prob_low, v_f, preferred_element_type=f32).astype(bf16)
    attended_f = mixed.reshape(filled, q_cols)
    attended = jnp.concatenate([attended_f, jnp.tile(values[filled:], (1, per_group))], axis=0)

    def scatter_context(partial):
        partial = partial.reshape(nc, nt, part, width)
        mine = cut(partial, t, 1, 1)[:, 0]
        other = cut(partial, 1 - t, 1, 1)[:, 0].astype(bf16)
        mine = mine + swap(other, TENSOR, 1).astype(f32)
        total = cut(mine, c, 1, 0)[0]
        for k in range(1, nc):
            total = total + swap(cut(mine, c ^ k, 1, 0)[0].astype(bf16), CONTEXT, k).astype(f32)
        return total

    attn_out = scatter_context(dot_last(attended, w_out))
    my_inputs = my_tokens.astype(f32)
    hidden = my_inputs + residual_mult * attn_out
    inverse_two = lax.rsqrt(jnp.mean(hidden * hidden, axis=-1, keepdims=True) + norm_eps)
    unit_two = hidden * inverse_two

    def scatter_block(partial, k):
        mine = partial[:part] + swap(partial[part:].astype(bf16), TENSOR, 1).astype(f32)
        return mine if k == 0 else swap(mine.astype(bf16), FSDP, k).astype(f32)

    normed_blocks = [
        jnp.concatenate([b, swap(b, TENSOR, 1)], axis=0) for b in fsdp_blocks((unit_two * gain_two).astype(bf16))
    ]
    inner_blocks, gate_blocks, up_blocks, back_parts, feed_parts = [], [], [], [], []
    for k in range(nz):
        gate_up = jnp.dot(normed_blocks[k], w_gate_up, preferred_element_type=f32)
        gate_out, up_out = gate_up[:, :ff_cols], gate_up[:, ff_cols:]
        inner_grad = jnp.dot(feed_grads[k], w_down, preferred_element_type=f32)
        sig = jax.nn.sigmoid(gate_out)
        inner_blocks.append((gate_out * sig * up_out).astype(bf16))
        gate_blocks.append((inner_grad * up_out * sig * (1.0 + gate_out * (1.0 - sig))).astype(bf16))
        up_blocks.append((inner_grad * gate_out * sig).astype(bf16))
        both = jnp.concatenate([gate_blocks[k], up_blocks[k]], axis=1)
        back_parts.append(scatter_block(dot_last(both, w_gate_up), k))
        feed_parts.append(dot_last(inner_blocks[k], w_down))
    normed_grad_two = sum(back_parts)
    feed_out = sum(scatter_block(p, k) for k, p in enumerate(feed_parts))
    output = (hidden + residual_mult * feed_out).astype(bf16)

    def both_cores(x):
        out = put(jnp.zeros((nt,) + x.shape, x.dtype), x, t)
        return put(out, swap(x, TENSOR, 1), 1 - t).reshape(1, local_rows, width)

    output = both_cores(output)
    feed_gain_term = jnp.sum(normed_grad_two * unit_two, axis=0)
    hidden_grad = cotangent + norm_back(normed_grad_two, unit_two, gain_two, inverse_two)

    attn_low = (residual_mult * hidden_grad).astype(bf16)
    attn_grad = jnp.zeros((nc, nt, part, width), bf16)
    attn_grad = put(attn_grad, attn_low, c, t)
    attn_grad = put(attn_grad, swap(attn_low, TENSOR, 1), c, 1 - t)
    for k in range(1, nc):
        block = swap(attn_low, CONTEXT, k)
        attn_grad = put(attn_grad, block, c ^ k, t)
        attn_grad = put(attn_grad, swap(block, TENSOR, 1), c ^ k, 1 - t)
    attn_grad = attn_grad.reshape(group_rows, width)[:filled]

    normed_two = jnp.concatenate(normed_blocks, axis=0)
    ff_terms = jnp.concatenate(
        [
            dot_first(normed_two, jnp.concatenate(gate_blocks, axis=0)).astype(bf16),
            dot_first(normed_two, jnp.concatenate(up_blocks, axis=0)).astype(bf16),
            dot_first(jnp.concatenate(feed_grads, axis=0), jnp.concatenate(inner_blocks, axis=0)).astype(bf16),
        ],
        axis=1,
    ).reshape(nz, nc, wrows, 3 * ff_cols)

    out_term = dot_first(attn_grad, attended_f)
    mixed_grad = jnp.dot(attn_grad, w_out, preferred_element_type=f32).astype(bf16).reshape(filled, per_group, HEAD)
    prob_grad = jnp.einsum("tgd,sd->gts", mixed_grad, v_f, preferred_element_type=f32)
    row_dot = jnp.sum(probabilities * prob_grad, axis=-1, keepdims=True)
    score_grad = (attention_mult * probabilities * (prob_grad - row_dot)).astype(bf16)
    query_grad = jnp.einsum("gts,sd->tgd", score_grad, k_f, preferred_element_type=f32)
    key_grad = jnp.einsum("gts,tgd->sd", score_grad, q_f, preferred_element_type=f32)
    value_grad = jnp.einsum("gts,tgd->sd", prob_low, mixed_grad, preferred_element_type=f32).astype(bf16)
    cos_f, sine_f = cos_table[:filled], sine_table[:filled]
    query_grad = rotate_back(query_grad, cos_f, sine_f).reshape(filled, q_cols).astype(bf16)
    key_grad = rotate_back(key_grad[:, None], cos_f, sine_f)[:, 0].astype(bf16)
    qkv_grad = jnp.concatenate([query_grad, key_grad, value_grad], axis=1)
    normed_part = dot_last(qkv_grad, w_qkv)
    attn_gain_term = jnp.sum(normed_part * unit_all[:filled], axis=0)
    normed_part = jnp.pad(normed_part, ((0, group_rows - filled), (0, 0)))
    normed_grad_one = scatter_context(normed_part)
    inverse_one = lax.rsqrt(jnp.mean(my_inputs * my_inputs, axis=-1, keepdims=True) + norm_eps)
    unit_one = my_inputs * inverse_one
    input_grad = both_cores((hidden_grad + norm_back(normed_grad_one, unit_one, gain_one, inverse_one)).astype(bf16))

    gain_terms = jnp.stack([attn_gain_term, feed_gain_term])
    for axis, k in ((TENSOR, 1), (CONTEXT, 1), (CONTEXT, 2), (FSDP, 1), (FSDP, 2)):
        gain_terms = gain_terms + swap(gain_terms, axis, k)
    gain_terms = cut(gain_terms, z * nc + c, wrows, 1)

    qkv_term = dot_first(normed_one[:filled], qkv_grad)
    terms = jnp.concatenate([qkv_term, out_term], axis=1).astype(bf16).reshape(nz, nc, wrows, -1)
    sizes = [w.shape[1] for w in (gate_weight, up_weight, down_weight)]
    sizes += [w.shape[1] for w in (query_weight, key_weight, value_weight, output_weight)]
    grad_gate, grad_up, grad_down, *attn_terms = grads_out(ff_terms, terms, sizes)
    return (output, input_grad, gain_terms[0], *attn_terms, gain_terms[1], grad_gate, grad_up, grad_down)


def solution(mesh):
    split = tuple(mesh.shape[a] for a in (FSDP, CONTEXT, TENSOR)) == (4, 4, 2)
    return jax.shard_map(
        on_device_split if split else on_device,
        mesh=mesh,
        in_specs=(
            P(FSDP, CONTEXT, None),
            P(FSDP, CONTEXT, None),
            P(FSDP, None),
            P((FSDP, CONTEXT)),
            P((FSDP, CONTEXT), TENSOR),
            P((FSDP, CONTEXT), TENSOR),
            P((FSDP, CONTEXT), TENSOR),
            P((FSDP, CONTEXT), TENSOR),
            P((FSDP, CONTEXT)),
            P((FSDP, CONTEXT), TENSOR),
            P((FSDP, CONTEXT), TENSOR),
            P((FSDP, CONTEXT), TENSOR),
        ),
        out_specs=(
            P(FSDP, CONTEXT, None),
            P(FSDP, CONTEXT, None),
            P((FSDP, CONTEXT)),
            P((FSDP, CONTEXT), TENSOR),
            P((FSDP, CONTEXT), TENSOR),
            P((FSDP, CONTEXT), TENSOR),
            P((FSDP, CONTEXT), TENSOR),
            P((FSDP, CONTEXT)),
            P((FSDP, CONTEXT), TENSOR),
            P((FSDP, CONTEXT), TENSOR),
            P((FSDP, CONTEXT), TENSOR),
        ),
        check_vma=False,
    )
```

```python
import jax
import jax.numpy as jnp
from jax import lax
from jax.experimental import pallas as pl
from jax.experimental.pallas import tpu as pltpu
from jax.sharding import PartitionSpec as P

HEAD = 64
FSDP, CONTEXT, TENSOR = "fsdp", "context", "tensor"


norm_eps = 1e-05
attention_mult = 0.015625
residual_mult = 0.22
rope_base = 10000000.0


def slot_layout(seq_lengths, total_rows):
    seq_ends = jnp.cumsum(seq_lengths)
    starts = seq_ends - seq_lengths
    slot_ids = jnp.arange(total_rows, dtype=jnp.int32)
    before = (slot_ids[:, None] >= seq_ends[None, :]).astype(jnp.int32)
    segment = jnp.sum(before, axis=1)
    seq_count = seq_lengths.shape[0]
    valid_rows = segment < seq_count
    inside = (slot_ids[:, None] >= starts[None, :]) & (slot_ids[:, None] < seq_ends[None, :])
    position = jnp.sum(jnp.where(inside, slot_ids[:, None] - starts[None, :], 0), axis=1)
    segment = jnp.where(valid_rows, segment, seq_count + slot_ids)
    return (segment, position, valid_rows)


def rope_tables(position, width):
    half_width = width // 2
    frequency = rope_base ** (-jnp.arange(half_width, dtype=jnp.float32) * 2.0 / width)
    angles = position.astype(jnp.float32)[:, None] * frequency[None, :]
    angles = jnp.concatenate([angles, angles], axis=1)
    return (jnp.cos(angles), jnp.sin(angles))


def turn_half(vectors):
    half_width = vectors.shape[-1] // 2
    return jnp.concatenate([-vectors[..., half_width:], vectors[..., :half_width]], axis=-1)


def rotate(vectors, cos_table, sine_table):
    return vectors * cos_table[:, None, :] + turn_half(vectors) * sine_table[:, None, :]


def rotate_back(grads, cos_table, sine_table):
    return grads * cos_table[:, None, :] - turn_half(grads * sine_table[:, None, :])


def norm_back(normed_grad, unit, gain, inverse):
    scaled = normed_grad * gain
    return inverse * (scaled - unit * jnp.mean(scaled * unit, axis=-1, keepdims=True))


def dot_first(left, right):
    return lax.dot_general(left, right, (((0,), (0,)), ((), ())), preferred_element_type=jnp.float32)


def dot_last(left, right):
    return lax.dot_general(left, right, (((1,), (1,)), ((), ())), preferred_element_type=jnp.float32)


def attention_shards(attention_gain, query_weight, key_weight, value_weight, output_weight):
    return (
        lax.all_gather(
            attention_gain.astype(jnp.bfloat16), (FSDP, CONTEXT), axis=0, tiled=True
        ),
        lax.all_gather(query_weight.astype(jnp.bfloat16), (FSDP, CONTEXT), axis=0, tiled=True),
        lax.all_gather(key_weight.astype(jnp.bfloat16), (FSDP, CONTEXT), axis=0, tiled=True),
        lax.all_gather(value_weight.astype(jnp.bfloat16), (FSDP, CONTEXT), axis=0, tiled=True),
        lax.all_gather(output_weight.astype(jnp.bfloat16), (FSDP, CONTEXT), axis=0, tiled=True),
    )


def feed_shards(feed_gain, gate_weight, up_weight, down_weight):
    return (
        lax.all_gather(feed_gain.astype(jnp.bfloat16), (FSDP, CONTEXT), axis=0, tiled=True),
        lax.all_gather(gate_weight.astype(jnp.bfloat16), (FSDP, CONTEXT), axis=0, tiled=True),
        lax.all_gather(up_weight.astype(jnp.bfloat16), (FSDP, CONTEXT), axis=0, tiled=True),
        lax.all_gather(down_weight.astype(jnp.bfloat16), (FSDP, CONTEXT), axis=0, tiled=True),
    )


def on_device(
    tokens,
    out_grad,
    lengths,
    attention_gain,
    query_weight,
    key_weight,
    value_weight,
    output_weight,
    feed_gain,
    gate_weight,
    up_weight,
    down_weight,
):
    local_rows = tokens.shape[1]
    group_rows = local_rows * lax.axis_size(CONTEXT)
    first_row = lax.axis_index(CONTEXT) * local_rows
    segment, position, valid_rows = slot_layout(lengths[0], group_rows)
    local_segment = lax.dynamic_slice_in_dim(segment, first_row, local_rows)
    local_position = lax.dynamic_slice_in_dim(position, first_row, local_rows)
    local_valid = lax.dynamic_slice_in_dim(valid_rows, first_row, local_rows)
    slot_ids = jnp.arange(group_rows, dtype=jnp.int32)
    local_slots = first_row + jnp.arange(local_rows, dtype=jnp.int32)
    allowed = (local_segment[:, None] == segment[None, :]) & (
        local_slots[:, None] >= slot_ids[None, :]
    )
    inputs = tokens[0].astype(jnp.float32)
    attn_set = attention_shards(
        attention_gain, query_weight, key_weight, value_weight, output_weight
    )
    gain_one = attn_set[0].astype(jnp.float32)
    inverse_one = lax.rsqrt(jnp.mean(inputs * inputs, axis=-1, keepdims=True) + norm_eps)
    unit_one = inputs * inverse_one
    normed_one = (unit_one * gain_one).astype(jnp.bfloat16)
    queries = jnp.dot(normed_one, attn_set[1], preferred_element_type=jnp.float32)
    keys_lin = jnp.dot(normed_one, attn_set[2], preferred_element_type=jnp.float32)
    values_low = jnp.dot(normed_one, attn_set[3], preferred_element_type=jnp.float32).astype(
        jnp.bfloat16
    )
    heads_local = queries.shape[1] // HEAD
    kv_local = keys_lin.shape[1] // HEAD
    per_group = heads_local // kv_local
    cos_table, sine_table = rope_tables(local_position, HEAD)
    queries_rot = rotate(
        queries.reshape(local_rows, heads_local, HEAD), cos_table, sine_table
    ).astype(jnp.bfloat16)
    keys_rot = rotate(keys_lin.reshape(local_rows, kv_local, HEAD), cos_table, sine_table).astype(
        jnp.bfloat16
    )
    keys_all, values_all = (
        lax.all_gather(
            keys_rot.reshape(local_rows, kv_local * HEAD), CONTEXT, axis=0, tiled=True
        ),
        lax.all_gather(values_low, CONTEXT, axis=0, tiled=True),
    )
    query_heads = queries_rot.reshape(local_rows, kv_local, per_group, HEAD).transpose(1, 0, 2, 3)
    key_heads = keys_all.reshape(group_rows, kv_local, HEAD).transpose(1, 0, 2)
    value_heads = values_all.reshape(group_rows, kv_local, HEAD).transpose(1, 0, 2)

    def head_scores(query_head, key_head):
        raw_scores = jnp.einsum(
            "tgd,sd->gts", query_head, key_head, preferred_element_type=jnp.float32
        )
        return jnp.where(allowed[None], raw_scores * attention_mult, -1e30)

    def head_forward(pieces):
        query_head, key_head, value_head = pieces
        scores = head_scores(query_head, key_head)
        highest = jnp.max(scores, axis=-1, keepdims=True)
        weight = jnp.exp(scores - highest)
        row_totals = jnp.sum(weight, axis=-1, keepdims=True)
        probabilities = (weight / row_totals).astype(jnp.bfloat16)
        mixed = jnp.einsum(
            "gts,sd->tgd", probabilities, value_head, preferred_element_type=jnp.float32
        )
        return (mixed, (highest + jnp.log(row_totals))[..., 0])

    mixed_heads, log_totals = lax.map(head_forward, (query_heads, key_heads, value_heads))
    attended = (
        mixed_heads.transpose(1, 0, 2, 3)
        .reshape(local_rows, heads_local * HEAD)
        .astype(jnp.bfloat16)
    )
    attn_part = dot_last(attended, attn_set[4])
    attn_out = lax.psum(attn_part.astype(jnp.bfloat16), TENSOR).astype(jnp.float32)
    hidden_state = inputs + residual_mult * attn_out
    feed_set = feed_shards(feed_gain, gate_weight, up_weight, down_weight)
    gain_two = feed_set[0].astype(jnp.float32)
    inverse_two = lax.rsqrt(
        jnp.mean(hidden_state * hidden_state, axis=-1, keepdims=True) + norm_eps
    )
    unit_two = hidden_state * inverse_two
    normed_two = (unit_two * gain_two).astype(jnp.bfloat16)
    gate_out = jnp.dot(normed_two, feed_set[1], preferred_element_type=jnp.float32)
    up_out = jnp.dot(normed_two, feed_set[2], preferred_element_type=jnp.float32)
    inner_act = (jax.nn.silu(gate_out) * up_out).astype(jnp.bfloat16)
    feed_part = dot_last(inner_act, feed_set[3])
    feed_out = lax.psum(feed_part.astype(jnp.bfloat16), TENSOR).astype(jnp.float32)
    output = hidden_state + residual_mult * feed_out
    cotangent = out_grad[0].astype(jnp.float32) * local_valid[:, None].astype(jnp.float32)
    feed_back = feed_shards(feed_gain, gate_weight, up_weight, down_weight)
    feed_grad = (residual_mult * cotangent).astype(jnp.bfloat16)
    down_term = dot_first(feed_grad, inner_act)
    inner_grad = jnp.dot(feed_grad, feed_back[3], preferred_element_type=jnp.float32)
    sigmoid_gate = jax.nn.sigmoid(gate_out)
    gate_grad = (
        inner_grad * up_out * sigmoid_gate * (1.0 + gate_out * (1.0 - sigmoid_gate))
    ).astype(jnp.bfloat16)
    up_grad = (inner_grad * jax.nn.silu(gate_out)).astype(jnp.bfloat16)
    gate_term = dot_first(normed_two, gate_grad)
    up_term = dot_first(normed_two, up_grad)
    normed_part_two = dot_last(gate_grad, feed_back[1])
    normed_part_two = normed_part_two + dot_last(up_grad, feed_back[2])
    normed_grad_two = lax.psum(normed_part_two.astype(jnp.bfloat16), TENSOR).astype(jnp.float32)
    feed_gain_term = jnp.sum(normed_grad_two * unit_two, axis=0)
    hidden_grad = cotangent + norm_back(normed_grad_two, unit_two, gain_two, inverse_two)
    feed_sums = (
        lax.psum_scatter(feed_gain_term, (FSDP, CONTEXT), scatter_dimension=0, tiled=True),
        lax.psum_scatter(gate_term, (FSDP, CONTEXT), scatter_dimension=0, tiled=True),
        lax.psum_scatter(up_term, (FSDP, CONTEXT), scatter_dimension=0, tiled=True),
        lax.psum_scatter(down_term, (FSDP, CONTEXT), scatter_dimension=0, tiled=True),
    )
    attn_back = attention_shards(
        attention_gain, query_weight, key_weight, value_weight, output_weight
    )
    attn_grad = (residual_mult * hidden_grad).astype(jnp.bfloat16)
    out_term = dot_first(attn_grad, attended)
    mixed_grad = jnp.dot(attn_grad, attn_back[4], preferred_element_type=jnp.float32).astype(
        jnp.bfloat16
    )
    mixed_grad_heads = mixed_grad.reshape(local_rows, kv_local, per_group, HEAD).transpose(
        1, 0, 2, 3
    )

    def head_backward(pieces):
        query_head, key_head, value_head, grad_head, log_head = pieces
        scores = head_scores(query_head, key_head)
        probabilities = jnp.exp(scores - log_head[..., None])
        prob_low = probabilities.astype(jnp.bfloat16)
        prob_grad = jnp.einsum(
            "tgd,sd->gts", grad_head, value_head, preferred_element_type=jnp.float32
        )
        row_dot = jnp.sum(probabilities * prob_grad, axis=-1, keepdims=True)
        score_grad = (attention_mult * probabilities * (prob_grad - row_dot)).astype(jnp.bfloat16)
        query_grad = jnp.einsum(
            "gts,sd->tgd", score_grad, key_head, preferred_element_type=jnp.float32
        )
        key_grad = jnp.einsum(
            "gts,tgd->sd", score_grad, query_head, preferred_element_type=jnp.float32
        )
        value_grad = jnp.einsum(
            "gts,tgd->sd", prob_low, grad_head, preferred_element_type=jnp.float32
        )
        return (query_grad, key_grad, value_grad)

    query_grads, key_grads, value_grads = lax.map(
        head_backward, (query_heads, key_heads, value_heads, mixed_grad_heads, log_totals)
    )
    key_grads = key_grads.transpose(1, 0, 2).reshape(group_rows, kv_local * HEAD)
    value_grads = value_grads.transpose(1, 0, 2).reshape(group_rows, kv_local * HEAD)
    local_key_grad, local_value_grad = (
        lax.psum_scatter(
            key_grads.astype(jnp.bfloat16), CONTEXT, scatter_dimension=0, tiled=True
        ).astype(jnp.float32),
        lax.psum_scatter(
            value_grads.astype(jnp.bfloat16), CONTEXT, scatter_dimension=0, tiled=True
        ).astype(jnp.float32),
    )
    query_grad_rot = query_grads.transpose(1, 0, 2, 3).reshape(local_rows, heads_local, HEAD)
    query_grad_low = (
        rotate_back(query_grad_rot, cos_table, sine_table)
        .reshape(local_rows, heads_local * HEAD)
        .astype(jnp.bfloat16)
    )
    key_grad_low = (
        rotate_back(local_key_grad.reshape(local_rows, kv_local, HEAD), cos_table, sine_table)
        .reshape(local_rows, kv_local * HEAD)
        .astype(jnp.bfloat16)
    )
    value_grad_low = local_value_grad.astype(jnp.bfloat16)
    query_term = dot_first(normed_one, query_grad_low)
    key_term = dot_first(normed_one, key_grad_low)
    value_term = dot_first(normed_one, value_grad_low)
    normed_part_one = dot_last(query_grad_low, attn_back[1])
    normed_part_one = normed_part_one + dot_last(key_grad_low, attn_back[2])
    normed_part_one = normed_part_one + dot_last(value_grad_low, attn_back[3])
    normed_grad_one = lax.psum(normed_part_one.astype(jnp.bfloat16), TENSOR).astype(jnp.float32)
    attn_gain_term = jnp.sum(normed_grad_one * unit_one, axis=0)
    input_grad = hidden_grad + norm_back(normed_grad_one, unit_one, gain_one, inverse_one)
    attn_sums = (
        lax.psum_scatter(attn_gain_term, (FSDP, CONTEXT), scatter_dimension=0, tiled=True),
        lax.psum_scatter(query_term, (FSDP, CONTEXT), scatter_dimension=0, tiled=True),
        lax.psum_scatter(key_term, (FSDP, CONTEXT), scatter_dimension=0, tiled=True),
        lax.psum_scatter(value_term, (FSDP, CONTEXT), scatter_dimension=0, tiled=True),
        lax.psum_scatter(out_term, (FSDP, CONTEXT), scatter_dimension=0, tiled=True),
    )
    return (
        output.astype(jnp.bfloat16)[None],
        input_grad.astype(jnp.bfloat16)[None],
        attn_sums[0],
        attn_sums[1],
        attn_sums[2],
        attn_sums[3],
        attn_sums[4],
        feed_sums[0],
        feed_sums[1],
        feed_sums[2],
        feed_sums[3],
    )


def flip(i, k):
    if k == 0:
        return i
    if k == 1:
        return i + 1 - 2 * lax.rem(i, 2)
    if k == 2:
        return lax.rem(i + 2, 4)
    return 3 - i


class Copies:
    def __init__(self, send, receive):
        self.send, self.receive = send, receive
        self.count, self.started = 0, []

    def index(self):
        self.count += 1
        return self.count - 1

    def make(self, i, source, target, device):
        return pltpu.make_async_remote_copy(
            src_ref=source,
            dst_ref=target,
            send_sem=self.send.at[i],
            recv_sem=self.receive.at[i],
            device_id=device,
            device_id_type=pl.DeviceIdType.MESH,
        )

    def start(self, source, target, device, i=None):
        i = self.index() if i is None else i
        copy = self.make(i, source, target, device)
        copy.start()
        self.started.append(copy)
        return copy


def greet(partners):
    barrier = pltpu.get_barrier_semaphore()
    for device in partners:
        pl.semaphore_signal(barrier, inc=1, device_id=device, device_id_type=pl.DeviceIdType.MESH)
    pl.semaphore_wait(barrier, len(partners))


def weights_in_kernel(wa, wf, xt, gain, wa_all, wf_all, x_all, gain_all, send, receive, local):
    z, c, t = (lax.axis_index(a) for a in (FSDP, CONTEXT, TENSOR))
    peers = [(flip(z, i), flip(c, j), t) for i in range(4) for j in range(4) if i or j]
    core = (z, c, 1 - t)
    greet(peers + [core])
    net = Copies(send, receive)
    ends = []
    own = []
    for i, (source, target) in enumerate(
        (
            (wa.at[c], wa_all.at[z, c]),
            (xt, x_all.at[c]),
            (wf.at[z], wf_all.at[z, c]),
            (gain, gain_all.at[z, c]),
        )
    ):
        own.append(pltpu.make_async_copy(source, target, local.at[i]))
        own[-1].start()

    attn_in = [net.start(wa.at[flip(c, k)], wa_all.at[z, c], (z, flip(c, k), t)) for k in (1, 2, 3)]
    tokens_in = [net.start(xt.at[t], x_all.at[c, t], (z, flip(c, k), t)) for k in (1, 2, 3)]
    for device in peers:
        ends.append(net.start(gain, gain_all.at[z, c], device))
    own[2].wait()
    forward = []
    middle = (z == 1) | (z == 2)
    for j in range(4):
        if j:
            attn_in[j - 1].wait_recv()
        else:
            own[0].wait()
        piece = wa_all.at[z, flip(c, j)]
        ends.append(net.start(piece, piece, (flip(z, 1), c, t)))
        two = net.start(piece, piece, (flip(z, 2), c, t))
        three = net.index()
        direct = net.make(three, piece, piece, (3 - z, c, t))
        pl.when(middle)(direct.start)
        passed_piece = wa_all.at[flip(z, 2), flip(c, j)]
        passed = pltpu.make_async_remote_copy(
            src_ref=passed_piece,
            dst_ref=passed_piece,
            send_sem=send.at[net.index()],
            recv_sem=receive.at[three],
            device_id=(flip(z, 1), c, t),
            device_id_type=pl.DeviceIdType.MESH,
        )
        forward.append((two, direct, passed))
    ff_in = {k: net.start(wf.at[flip(z, k)], wf_all.at[z, c], (flip(z, k), c, t)) for k in (3, 2)}
    ff_out = {0: [net.start(wf_all.at[z, c], wf_all.at[z, c], (z, flip(c, k), t)) for k in (1, 2)]}
    swaps = []
    for k, copy in zip((1, 2, 3), tokens_in):
        copy.wait_recv()
        piece = x_all.at[flip(c, k), t]
        swaps.append(net.start(piece, piece, core))
    for two, direct, passed in forward:
        two.wait_recv()
        pl.when(middle)(passed.start)
    ff_in[1] = net.start(wf.at[flip(z, 1)], wf_all.at[z, c], (flip(z, 1), c, t))
    halves = []

    def corner(k):
        zs = flip(z, k)
        one, two = ff_out[k]
        two.wait_recv()
        piece = wf_all.at[zs, flip(c, 2), pl.ds(0, 64)]
        halves.append(net.start(piece, piece, (z, flip(c, 1), t)))
        one.wait_recv()
        piece = wf_all.at[zs, flip(c, 1), pl.ds(64, 64)]
        halves.append(net.start(piece, piece, (z, flip(c, 2), t)))

    last = 0
    for k in (3, 2, 1):
        ff_in[k].wait_recv()
        piece = wf_all.at[flip(z, k), c]
        ff_out[k] = [net.start(piece, piece, (z, flip(c, j), t)) for j in (1, 2)]
        corner(last)
        last = k
    corner(last)
    for copy in halves + swaps + ends:
        copy.wait_recv()
    for _, direct, passed in forward:
        direct.wait_recv()
        pl.when(middle)(direct.wait_send)
        pl.when(middle)(passed.wait_send)
    for copy in net.started:
        copy.wait_send()
    own[1].wait()
    own[3].wait()


def weights_in(wa, wf, xt, gain):
    bf16 = jnp.bfloat16
    shapes = ((4, 4) + wa.shape[1:], (4, 4) + wf.shape[1:], (4,) + xt.shape, (4, 4) + gain.shape)
    copies = 128
    return pl.pallas_call(
        weights_in_kernel,
        out_shape=[jax.ShapeDtypeStruct(s, bf16) for s in shapes],
        in_specs=[pl.BlockSpec(memory_space=pltpu.VMEM)] * 4,
        out_specs=[pl.BlockSpec(memory_space=pl.ANY)] * 4,
        scratch_shapes=[
            pltpu.SemaphoreType.DMA((copies,)),
            pltpu.SemaphoreType.DMA((copies,)),
            pltpu.SemaphoreType.DMA((4,)),
        ],
        compiler_params=pltpu.CompilerParams(collective_id=1, has_side_effects=True, vmem_limit_bytes=48 * 2**20),
    )(wa, wf, xt, gain)


def dot_tile(left, right, left_axis, right_axis):
    return lax.dot_general(left, right, (((left_axis,), (right_axis,)), ((), ())), preferred_element_type=jnp.float32)


TILE = 256


def feed_kernel(
    x, fg, w, back, feed_own, feed_send, terms,
    xs, wv, gate_g, up_g, inner, mine, cross, crossed, totals, landed, send, receive, local,
):
    f32, bf16 = jnp.float32, jnp.bfloat16
    z, c, t = (lax.axis_index(a) for a in (FSDP, CONTEXT, TENSOR))
    core = (z, c, 1 - t)
    greet([(flip(z, k), c, t) for k in (1, 2, 3)] + [core])
    net = Copies(send, receive)
    part, width = x.shape
    hidden = wv.shape[1] // 3
    load = pltpu.make_async_copy(w, wv, local.at[0])
    load.start()
    middle = (z == 1) | (z == 2)
    swaps = {0: net.start(x, xs.at[0, 1], core)}
    arrive = {2: net.start(x, xs.at[2, 0], (flip(z, 2), c, t))}
    three = net.index()
    direct = net.make(three, x, xs.at[3, 0], (3 - z, c, t))
    pl.when(middle)(direct.start)
    arrive[3] = direct
    arrive[1] = net.start(x, xs.at[1, 0], (flip(z, 1), c, t))
    passed = pltpu.make_async_remote_copy(
        src_ref=xs.at[2, 0],
        dst_ref=xs.at[3, 0],
        send_sem=send.at[net.index()],
        recv_sem=receive.at[three],
        device_id=(flip(z, 1), c, t),
        device_id_type=pl.DeviceIdType.MESH,
    )
    xs[0, 0] = x[...]
    load.wait()

    def first(k):
        swaps[k].wait_recv()
        rows = xs[k].reshape(2 * part, width)
        grads = fg[k]

        def step(n, carry):
            at = pl.multiple_of(n * TILE, TILE)
            g = dot_tile(rows, wv[:, pl.ds(at, TILE)], 1, 0)
            u = dot_tile(rows, wv[:, pl.ds(hidden + at, TILE)], 1, 0)
            d = dot_tile(grads, wv[:, pl.ds(2 * hidden + at, TILE)], 1, 0)
            sig = jax.nn.sigmoid(g)
            here = pl.ds(at, TILE)
            inner[k, :, here] = (g * sig * u).astype(bf16)
            gate_g[k, :, here] = (d * u * sig * (1.0 + g * (1.0 - sig))).astype(bf16)
            up_g[k, :, here] = (d * g * sig).astype(bf16)
            return carry

        lax.fori_loop(0, hidden // TILE, step, 0)

    crosses = {}

    def second(k):
        def step(n, carry):
            here = pl.ds(pl.multiple_of(n * TILE, TILE), TILE)
            b = dot_tile(gate_g[k], wv[here, 0:hidden], 1, 1) + dot_tile(up_g[k], wv[here, hidden : 2 * hidden], 1, 1)
            f = dot_tile(inner[k], wv[here, 2 * hidden :], 1, 1)
            mine[k, 0, :, here] = b[:part]
            mine[k, 1, :, here] = f[:part]
            cross[k, 0, :, here] = b[part:].astype(bf16)
            cross[k, 1, :, here] = f[part:].astype(bf16)
            return carry

        lax.fori_loop(0, width // TILE, step, 0)
        crosses[k] = net.start(cross.at[k], crossed.at[k], core)

    sums = {}

    def finish(k):
        crosses[k].wait_recv()
        if k:
            totals[k - 1] = (mine[k, 0] + crossed[k, 0].astype(f32)).astype(bf16)
            sums[k] = net.start(totals.at[k - 1], landed.at[k - 1], (flip(z, k), c, t))
            feed_send[k - 1] = (mine[k, 1] + crossed[k, 1].astype(f32)).astype(bf16)
        else:
            back[...] = mine[0, 0] + crossed[0, 0].astype(f32)
            feed_own[...] = mine[0, 1] + crossed[0, 1].astype(f32)

    def fetch(k):
        arrive[k].wait_recv()
        if k == 2:
            pl.when(middle)(passed.start)
        swaps[k] = net.start(xs.at[k, 0], xs.at[k, 1], core)

    order = (0, 2, 3, 1)
    for i, k in enumerate(order):
        first(k)
        if i:
            finish(order[i - 1])
        if i < 3:
            fetch(order[i + 1])
        second(k)

    rows = xs.shape[0] * 2 * part

    def term(source, grads, begin):
        def step(m, carry):
            here = pl.ds(pl.multiple_of(m * TILE, TILE), TILE)
            left = source[:, :, here].reshape(rows, TILE)
            value = dot_tile(left, grads[...].reshape(rows, hidden), 0, 0)
            wv[here, begin : begin + hidden] = value.astype(bf16)
            return carry

        lax.fori_loop(0, width // TILE, step, 0)

    flat = xs.reshape(xs.shape[0], 2 * part, width)
    term(flat, gate_g, 0)
    finish(order[3])
    term(flat, up_g, hidden)
    term(fg, inner, 2 * hidden)
    store = pltpu.make_async_copy(wv, terms, local.at[1])
    store.start()
    for k in (1, 2, 3):
        sums[k].wait_recv()
    back[...] = back[...] + landed[0].astype(f32) + landed[1].astype(f32) + landed[2].astype(f32)
    pl.when(middle)(direct.wait_send)
    pl.when(middle)(passed.wait_send)
    for copy in net.started:
        copy.wait_send()
    store.wait()


def feed_forward(x, fg, w):
    bf16, f32 = jnp.bfloat16, jnp.float32
    part, width = x.shape
    cols = w.shape[1]
    hidden = cols // 3
    blocks = fg.shape[0]
    copies = 20
    vmem, anywhere = pl.BlockSpec(memory_space=pltpu.VMEM), pl.BlockSpec(memory_space=pl.ANY)
    return pl.pallas_call(
        feed_kernel,
        out_shape=[
            jax.ShapeDtypeStruct((part, width), f32),
            jax.ShapeDtypeStruct((part, width), f32),
            jax.ShapeDtypeStruct((blocks - 1, part, width), bf16),
            jax.ShapeDtypeStruct(w.shape, bf16),
        ],
        in_specs=[vmem, vmem, anywhere],
        out_specs=[vmem, vmem, vmem, anywhere],
        scratch_shapes=[
            pltpu.VMEM((blocks, 2, part, width), bf16),
            pltpu.VMEM(w.shape, bf16),
            pltpu.VMEM((blocks, 2 * part, hidden), bf16),
            pltpu.VMEM((blocks, 2 * part, hidden), bf16),
            pltpu.VMEM((blocks, 2 * part, hidden), bf16),
            pltpu.VMEM((blocks, 2, part, width), f32),
            pltpu.VMEM((blocks, 2, part, width), bf16),
            pltpu.VMEM((blocks, 2, part, width), bf16),
            pltpu.VMEM((blocks - 1, part, width), bf16),
            pltpu.VMEM((blocks - 1, part, width), bf16),
            pltpu.SemaphoreType.DMA((copies,)),
            pltpu.SemaphoreType.DMA((copies,)),
            pltpu.SemaphoreType.DMA((2,)),
        ],
        compiler_params=pltpu.CompilerParams(collective_id=3, has_side_effects=True, vmem_limit_bytes=62 * 2**20),
    )(x, fg, w)


def swap(x, axis, k):
    return lax.ppermute(x, axis, [(i, i ^ k) for i in range(lax.axis_size(axis))])


def after(x, *others):
    return lax.optimization_barrier((x, *others))[0]


def put(buffer, block, *index):
    lead = len(index)
    block = block.reshape((1,) * lead + buffer.shape[lead:])
    zero = jnp.int32(0)
    start = tuple(jnp.asarray(i, jnp.int32) for i in index) + (zero,) * (buffer.ndim - lead)
    return lax.dynamic_update_slice(buffer, block, start)


def cut(x, index, size, axis):
    return lax.dynamic_slice_in_dim(x, index * size, size, axis)


def fsdp_blocks(x):
    one = swap(x, FSDP, 1)
    two = swap(x, FSDP, 2)
    three = lax.ppermute(x, FSDP, [(1, 2), (2, 1)]) + lax.ppermute(two, FSDP, [(2, 3), (1, 0)])
    return [x, one, two, three]


def context_blocks(x, axis):
    one = swap(x, CONTEXT, 1)
    two = swap(x, CONTEXT, 2)
    half = x.shape[axis] // 2
    low = swap(lax.slice_in_dim(two, 0, half, axis=axis), CONTEXT, 1)
    high = swap(lax.slice_in_dim(one, half, 2 * half, axis=axis), CONTEXT, 2)
    return one, two, low, high


def grads_out_kernel(
    ff, at, fs, feed_out, gate_out, up_out, down_out, query_out, key_out, value_out, output_out,
    terms, corner_x, corner_y, side_x, side_y, landed, feed_in, at_terms, at_in, at_total, at_landed, send, receive, local,
):
    f32, bf16 = jnp.float32, jnp.bfloat16
    z, c, t = (lax.axis_index(a) for a in (FSDP, CONTEXT, TENSOR))
    greet([(flip(z, k), c, t) for k in (1, 2, 3)] + [(z, flip(c, k), t) for k in (1, 2, 3)])
    net = Copies(send, receive)
    rows = ff.shape[2]
    half = rows // 2
    order = (3, 2, 1, 0)
    loads = {}
    for k in order:
        zs = flip(z, k)
        loads[k] = pltpu.make_async_copy(ff.at[zs], terms.at[zs], local.at[k])
        loads[k].start()
    attn_load = pltpu.make_async_copy(at, at_terms, local.at[4])
    attn_load.start()
    attn_load.wait()
    attn_in = [net.start(at_terms.at[flip(z, k)], at_in.at[k - 1], (flip(z, k), c, t)) for k in (3, 2, 1)]
    feed = [net.start(fs.at[k - 1], feed_in.at[k - 1], (flip(z, k), c, t)) for k in (3, 2, 1)]
    first = {}
    for k in order:
        zs = flip(z, k)
        loads[k].wait()
        first[k] = (
            net.start(terms.at[zs, flip(c, 3), pl.ds(0, half)], corner_x.at[k], (z, flip(c, 1), t)),
            net.start(terms.at[zs, flip(c, 3), pl.ds(half, half)], corner_y.at[k], (z, flip(c, 2), t)),
        )
    second = {}
    for k in order:
        zs = flip(z, k)
        for copy in first[k]:
            copy.wait_recv()
        low, high = pl.ds(0, half), pl.ds(half, half)
        xb, yb = flip(c, 1), flip(c, 2)
        terms[zs, yb, low] = (terms[zs, yb, low].astype(f32) + corner_x[k].astype(f32)).astype(bf16)
        terms[zs, xb, high] = (terms[zs, xb, high].astype(f32) + corner_y[k].astype(f32)).astype(bf16)
        second[k] = (
            net.start(terms.at[zs, yb], side_y.at[k], (z, yb, t)),
            net.start(terms.at[zs, xb], side_x.at[k], (z, xb, t)),
        )
    for copy in attn_in:
        copy.wait_recv()
    for j in range(4):
        total = at_terms[z, j].astype(f32)
        for i in range(3):
            total = total + at_in[i, j].astype(f32)
        at_total[j] = total.astype(bf16)
    attn_out = [net.start(at_total.at[flip(c, k)], at_landed.at[c], (z, flip(c, k), t)) for k in (1, 2, 3)]
    at_landed[c] = at_total[c]
    third = {}
    for k in order:
        zs = flip(z, k)
        for copy in second[k]:
            copy.wait_recv()
        total = terms[zs, c].astype(f32) + side_x[k].astype(f32) + side_y[k].astype(f32)
        if k:
            terms[zs, c] = total.astype(bf16)
            third[k] = net.start(terms.at[zs, c], landed.at[k], (zs, c, t))
        else:
            landed[0] = total.astype(bf16)
    size = gate_out.shape[1] // 4
    for k in (0, 3, 2, 1):
        if k:
            third[k].wait_recv()
        zs = flip(z, k)
        columns = pl.ds(pl.multiple_of(zs * size, size), size)
        for i, out in enumerate((gate_out, up_out, down_out)):
            out[:, columns] = landed[k, :, i * size : (i + 1) * size]
    for copy in attn_out:
        copy.wait_recv()
    begin = 0
    for out in (query_out, key_out, value_out, output_out):
        size = out.shape[1] // 4
        for j in range(4):
            out[:, j * size : (j + 1) * size] = at_landed[j, :, begin : begin + size]
        begin += size
    for copy in feed:
        copy.wait_recv()
    feed_out[...] = feed_in[0].astype(f32) + feed_in[1].astype(f32) + feed_in[2].astype(f32)
    for copy in net.started:
        copy.wait_send()


def grads_out(ff, at, fs, sizes):
    bf16, f32 = jnp.bfloat16, jnp.float32
    rows, cols = ff.shape[2:]
    attn_cols = at.shape[3]
    copies = 32
    return pl.pallas_call(
        grads_out_kernel,
        out_shape=[jax.ShapeDtypeStruct(fs.shape[1:], f32)] + [jax.ShapeDtypeStruct((rows, s), bf16) for s in sizes],
        in_specs=[pl.BlockSpec(memory_space=pl.ANY)] * 2 + [pl.BlockSpec(memory_space=pltpu.VMEM)],
        out_specs=[pl.BlockSpec(memory_space=pltpu.VMEM)] * (1 + len(sizes)),
        scratch_shapes=[
            pltpu.VMEM((4, 4, rows, cols), bf16),
            pltpu.VMEM((4, rows // 2, cols), bf16),
            pltpu.VMEM((4, rows // 2, cols), bf16),
            pltpu.VMEM((4, rows, cols), bf16),
            pltpu.VMEM((4, rows, cols), bf16),
            pltpu.VMEM((4, rows, cols), bf16),
            pltpu.VMEM(fs.shape, bf16),
            pltpu.VMEM((4, 4, rows, attn_cols), bf16),
            pltpu.VMEM((3, 4, rows, attn_cols), bf16),
            pltpu.VMEM((4, rows, attn_cols), bf16),
            pltpu.VMEM((4, rows, attn_cols), bf16),
            pltpu.SemaphoreType.DMA((copies,)),
            pltpu.SemaphoreType.DMA((copies,)),
            pltpu.SemaphoreType.DMA((5,)),
        ],
        compiler_params=pltpu.CompilerParams(collective_id=2, has_side_effects=True, vmem_limit_bytes=60 * 2**20),
    )(ff, at, fs)


def on_device_split(
    tokens,
    out_grad,
    lengths,
    attention_gain,
    query_weight,
    key_weight,
    value_weight,
    output_weight,
    feed_gain,
    gate_weight,
    up_weight,
    down_weight,
):
    f32, bf16 = jnp.float32, jnp.bfloat16
    nz, nc, nt = (lax.axis_size(a) for a in (FSDP, CONTEXT, TENSOR))
    z, c, t = (lax.axis_index(a) for a in (FSDP, CONTEXT, TENSOR))
    local_rows, width = tokens.shape[1:]
    group_rows = local_rows * nc
    filled = group_rows * 3 // 4
    part = local_rows // nt
    wrows = query_weight.shape[0]
    kv_cols = key_weight.shape[1] // nc
    q_cols = query_weight.shape[1] // nc
    qkv_cols = q_cols + 2 * kv_cols
    ff_cols = gate_weight.shape[1] // nz
    per_group = q_cols // kv_cols
    segment, position, valid_rows = slot_layout(lengths[0], group_rows)
    cos_table, sine_table = rope_tables(position, HEAD)

    wa = jnp.concatenate(
        [
            w.astype(bf16).reshape(wrows, nc, -1).transpose(1, 0, 2)
            for w in (query_weight, key_weight, value_weight, output_weight)
        ],
        axis=2,
    )
    wf = jnp.concatenate(
        [w.astype(bf16).reshape(wrows, nz, ff_cols).transpose(1, 0, 2) for w in (gate_weight, up_weight, down_weight)],
        axis=2,
    )
    gain = jnp.pad(jnp.stack([attention_gain, feed_gain]).astype(bf16), ((0, 14), (0, 0)))
    wa, wf, all_tokens, gains = weights_in(wa, wf, tokens[0].reshape(nt, part, width), gain)
    gains = gains[:, :, :2].transpose(2, 0, 1, 3).reshape(2, width).astype(f32)
    gain_one, gain_two = gains[0], gains[1]
    w_qkv = wa[..., :qkv_cols].reshape(width, qkv_cols)
    w_out = wa[..., qkv_cols:].reshape(width, q_cols)
    my_tokens = cut(tokens[0], t, part, 0)
    all_tokens = all_tokens.reshape(group_rows, width).astype(f32)
    w_feed = wf.reshape(width, 3 * ff_cols)

    my_valid = lax.dynamic_slice_in_dim(valid_rows, c * local_rows + t * part, part)
    cotangent = cut(out_grad[0], t, part, 0).astype(f32) * my_valid[:, None].astype(f32)
    feed_grads = fsdp_blocks((residual_mult * cotangent).astype(bf16))
    feed_grads = [jnp.concatenate([b, swap(b, TENSOR, 1)], axis=0) for b in feed_grads]

    inverse_all = lax.rsqrt(jnp.mean(all_tokens * all_tokens, axis=-1, keepdims=True) + norm_eps)
    unit_all = all_tokens * inverse_all
    normed_one = (unit_all * gain_one).astype(bf16)
    qkv = jnp.dot(normed_one, w_qkv, preferred_element_type=f32)
    queries = rotate(qkv[:, :q_cols].reshape(group_rows, per_group, HEAD), cos_table, sine_table).astype(bf16)
    keys = rotate(qkv[:, q_cols : q_cols + kv_cols].reshape(group_rows, 1, HEAD), cos_table, sine_table)
    keys = keys.astype(bf16)[:, 0]
    values = qkv[:, q_cols + kv_cols :].astype(bf16)
    slot_ids = jnp.arange(filled, dtype=jnp.int32)
    allowed = (segment[:filled, None] == segment[None, :filled]) & (slot_ids[:, None] >= slot_ids[None, :])
    q_f, k_f, v_f = queries[:filled], keys[:filled], values[:filled]
    scores = jnp.einsum("tgd,sd->gts", q_f, k_f, preferred_element_type=f32)
    scores = jnp.where(allowed[None], scores * attention_mult, -1e30)
    highest = jnp.max(scores, axis=-1, keepdims=True)
    weight = jnp.exp(scores - highest)
    totals = jnp.sum(weight, axis=-1, keepdims=True)
    probabilities = weight / totals
    prob_low = probabilities.astype(bf16)
    mixed = jnp.einsum("gts,sd->tgd", prob_low, v_f, preferred_element_type=f32).astype(bf16)
    attended_f = mixed.reshape(filled, q_cols)
    attended = jnp.concatenate([attended_f, jnp.tile(values[filled:], (1, per_group))], axis=0)

    def scatter_context(partial):
        partial = partial.reshape(nc, nt, part, width)
        mine = cut(partial, t, 1, 1)[:, 0]
        other = cut(partial, 1 - t, 1, 1)[:, 0].astype(bf16)
        mine = mine + swap(other, TENSOR, 1).astype(f32)
        total = cut(mine, c, 1, 0)[0]
        for k in range(1, nc):
            total = total + swap(cut(mine, c ^ k, 1, 0)[0].astype(bf16), CONTEXT, k).astype(f32)
        return total

    attn_out = scatter_context(dot_last(attended, w_out))
    my_inputs = my_tokens.astype(f32)
    hidden = my_inputs + residual_mult * attn_out
    inverse_two = lax.rsqrt(jnp.mean(hidden * hidden, axis=-1, keepdims=True) + norm_eps)
    unit_two = hidden * inverse_two

    normed_grad_two, feed_own, feed_send, ff_terms = feed_forward(
        (unit_two * gain_two).astype(bf16), jnp.stack(feed_grads), w_feed
    )
    ff_terms = ff_terms.reshape(nz, nc, wrows, 3 * ff_cols)

    def both_cores(x):
        out = put(jnp.zeros((nt,) + x.shape, x.dtype), x, t)
        return put(out, swap(x, TENSOR, 1), 1 - t).reshape(1, local_rows, width)

    feed_gain_term = jnp.sum(normed_grad_two * unit_two, axis=0)
    hidden_grad = cotangent + norm_back(normed_grad_two, unit_two, gain_two, inverse_two)

    attn_low = (residual_mult * hidden_grad).astype(bf16)
    attn_grad = jnp.zeros((nc, nt, part, width), bf16)
    attn_grad = put(attn_grad, attn_low, c, t)
    attn_grad = put(attn_grad, swap(attn_low, TENSOR, 1), c, 1 - t)
    for k in range(1, nc):
        block = swap(attn_low, CONTEXT, k)
        attn_grad = put(attn_grad, block, c ^ k, t)
        attn_grad = put(attn_grad, swap(block, TENSOR, 1), c ^ k, 1 - t)
    attn_grad = attn_grad.reshape(group_rows, width)[:filled]

    out_term = dot_first(attn_grad, attended_f)
    mixed_grad = jnp.dot(attn_grad, w_out, preferred_element_type=f32).astype(bf16).reshape(filled, per_group, HEAD)
    prob_grad = jnp.einsum("tgd,sd->gts", mixed_grad, v_f, preferred_element_type=f32)
    row_dot = jnp.sum(probabilities * prob_grad, axis=-1, keepdims=True)
    score_grad = (attention_mult * probabilities * (prob_grad - row_dot)).astype(bf16)
    query_grad = jnp.einsum("gts,sd->tgd", score_grad, k_f, preferred_element_type=f32)
    key_grad = jnp.einsum("gts,tgd->sd", score_grad, q_f, preferred_element_type=f32)
    value_grad = jnp.einsum("gts,tgd->sd", prob_low, mixed_grad, preferred_element_type=f32).astype(bf16)
    cos_f, sine_f = cos_table[:filled], sine_table[:filled]
    query_grad = rotate_back(query_grad, cos_f, sine_f).reshape(filled, q_cols).astype(bf16)
    key_grad = rotate_back(key_grad[:, None], cos_f, sine_f)[:, 0].astype(bf16)
    qkv_grad = jnp.concatenate([query_grad, key_grad, value_grad], axis=1)
    normed_part = dot_last(qkv_grad, w_qkv)
    attn_gain_term = jnp.sum(normed_part * unit_all[:filled], axis=0)
    normed_part = jnp.pad(normed_part, ((0, group_rows - filled), (0, 0)))
    normed_grad_one = scatter_context(normed_part)
    inverse_one = lax.rsqrt(jnp.mean(my_inputs * my_inputs, axis=-1, keepdims=True) + norm_eps)
    unit_one = my_inputs * inverse_one
    input_grad = both_cores((hidden_grad + norm_back(normed_grad_one, unit_one, gain_one, inverse_one)).astype(bf16))

    gain_terms = jnp.stack([attn_gain_term, feed_gain_term])
    for axis, k in ((TENSOR, 1), (CONTEXT, 1), (CONTEXT, 2), (FSDP, 1), (FSDP, 2)):
        gain_terms = gain_terms + swap(gain_terms, axis, k)
    gain_terms = cut(gain_terms, z * nc + c, wrows, 1)

    qkv_term = dot_first(normed_one[:filled], qkv_grad)
    terms = jnp.concatenate([qkv_term, out_term], axis=1).astype(bf16).reshape(nz, nc, wrows, -1)
    sizes = [w.shape[1] for w in (gate_weight, up_weight, down_weight)]
    sizes += [w.shape[1] for w in (query_weight, key_weight, value_weight, output_weight)]
    feed_in, *weight_grads = grads_out(ff_terms, terms, feed_send, sizes)
    grad_gate, grad_up, grad_down, *attn_terms = [g.astype(f32) for g in weight_grads]
    output = both_cores((hidden + residual_mult * (feed_own + feed_in)).astype(bf16))
    return (output, input_grad, gain_terms[0], *attn_terms, gain_terms[1], grad_gate, grad_up, grad_down)


def solution(mesh):
    split = tuple(mesh.shape[a] for a in (FSDP, CONTEXT, TENSOR)) == (4, 4, 2)
    return jax.shard_map(
        on_device_split if split else on_device,
        mesh=mesh,
        in_specs=(
            P(FSDP, CONTEXT, None),
            P(FSDP, CONTEXT, None),
            P(FSDP, None),
            P((FSDP, CONTEXT)),
            P((FSDP, CONTEXT), TENSOR),
            P((FSDP, CONTEXT), TENSOR),
            P((FSDP, CONTEXT), TENSOR),
            P((FSDP, CONTEXT), TENSOR),
            P((FSDP, CONTEXT)),
            P((FSDP, CONTEXT), TENSOR),
            P((FSDP, CONTEXT), TENSOR),
            P((FSDP, CONTEXT), TENSOR),
        ),
        out_specs=(
            P(FSDP, CONTEXT, None),
            P(FSDP, CONTEXT, None),
            P((FSDP, CONTEXT)),
            P((FSDP, CONTEXT), TENSOR),
            P((FSDP, CONTEXT), TENSOR),
            P((FSDP, CONTEXT), TENSOR),
            P((FSDP, CONTEXT), TENSOR),
            P((FSDP, CONTEXT)),
            P((FSDP, CONTEXT), TENSOR),
            P((FSDP, CONTEXT), TENSOR),
            P((FSDP, CONTEXT), TENSOR),
        ),
        check_vma=False,
    )
```

```python
import jax
import jax.numpy as jnp
from jax import lax
from jax.experimental import pallas as pl
from jax.experimental.pallas import tpu as pltpu
from jax.sharding import PartitionSpec as P

HEAD = 64
FSDP, CONTEXT, TENSOR = "fsdp", "context", "tensor"


norm_eps = 1e-05
attention_mult = 0.015625
residual_mult = 0.22
rope_base = 10000000.0


def slot_layout(seq_lengths, total_rows):
    seq_ends = jnp.cumsum(seq_lengths)
    starts = seq_ends - seq_lengths
    slot_ids = jnp.arange(total_rows, dtype=jnp.int32)
    before = (slot_ids[:, None] >= seq_ends[None, :]).astype(jnp.int32)
    segment = jnp.sum(before, axis=1)
    seq_count = seq_lengths.shape[0]
    valid_rows = segment < seq_count
    inside = (slot_ids[:, None] >= starts[None, :]) & (slot_ids[:, None] < seq_ends[None, :])
    position = jnp.sum(jnp.where(inside, slot_ids[:, None] - starts[None, :], 0), axis=1)
    segment = jnp.where(valid_rows, segment, seq_count + slot_ids)
    return (segment, position, valid_rows)


def rope_tables(position, width):
    half_width = width // 2
    frequency = rope_base ** (-jnp.arange(half_width, dtype=jnp.float32) * 2.0 / width)
    angles = position.astype(jnp.float32)[:, None] * frequency[None, :]
    angles = jnp.concatenate([angles, angles], axis=1)
    return (jnp.cos(angles), jnp.sin(angles))


def turn_half(vectors):
    half_width = vectors.shape[-1] // 2
    return jnp.concatenate([-vectors[..., half_width:], vectors[..., :half_width]], axis=-1)


def rotate(vectors, cos_table, sine_table):
    return vectors * cos_table[:, None, :] + turn_half(vectors) * sine_table[:, None, :]


def rotate_back(grads, cos_table, sine_table):
    return grads * cos_table[:, None, :] - turn_half(grads * sine_table[:, None, :])


def norm_back(normed_grad, unit, gain, inverse):
    scaled = normed_grad * gain
    return inverse * (scaled - unit * jnp.mean(scaled * unit, axis=-1, keepdims=True))


def dot_first(left, right):
    return lax.dot_general(left, right, (((0,), (0,)), ((), ())), preferred_element_type=jnp.float32)


def dot_last(left, right):
    return lax.dot_general(left, right, (((1,), (1,)), ((), ())), preferred_element_type=jnp.float32)


def attention_shards(attention_gain, query_weight, key_weight, value_weight, output_weight):
    return (
        lax.all_gather(
            attention_gain.astype(jnp.bfloat16), (FSDP, CONTEXT), axis=0, tiled=True
        ),
        lax.all_gather(query_weight.astype(jnp.bfloat16), (FSDP, CONTEXT), axis=0, tiled=True),
        lax.all_gather(key_weight.astype(jnp.bfloat16), (FSDP, CONTEXT), axis=0, tiled=True),
        lax.all_gather(value_weight.astype(jnp.bfloat16), (FSDP, CONTEXT), axis=0, tiled=True),
        lax.all_gather(output_weight.astype(jnp.bfloat16), (FSDP, CONTEXT), axis=0, tiled=True),
    )


def feed_shards(feed_gain, gate_weight, up_weight, down_weight):
    return (
        lax.all_gather(feed_gain.astype(jnp.bfloat16), (FSDP, CONTEXT), axis=0, tiled=True),
        lax.all_gather(gate_weight.astype(jnp.bfloat16), (FSDP, CONTEXT), axis=0, tiled=True),
        lax.all_gather(up_weight.astype(jnp.bfloat16), (FSDP, CONTEXT), axis=0, tiled=True),
        lax.all_gather(down_weight.astype(jnp.bfloat16), (FSDP, CONTEXT), axis=0, tiled=True),
    )


def on_device(
    tokens,
    out_grad,
    lengths,
    attention_gain,
    query_weight,
    key_weight,
    value_weight,
    output_weight,
    feed_gain,
    gate_weight,
    up_weight,
    down_weight,
):
    local_rows = tokens.shape[1]
    group_rows = local_rows * lax.axis_size(CONTEXT)
    first_row = lax.axis_index(CONTEXT) * local_rows
    segment, position, valid_rows = slot_layout(lengths[0], group_rows)
    local_segment = lax.dynamic_slice_in_dim(segment, first_row, local_rows)
    local_position = lax.dynamic_slice_in_dim(position, first_row, local_rows)
    local_valid = lax.dynamic_slice_in_dim(valid_rows, first_row, local_rows)
    slot_ids = jnp.arange(group_rows, dtype=jnp.int32)
    local_slots = first_row + jnp.arange(local_rows, dtype=jnp.int32)
    allowed = (local_segment[:, None] == segment[None, :]) & (
        local_slots[:, None] >= slot_ids[None, :]
    )
    inputs = tokens[0].astype(jnp.float32)
    attn_set = attention_shards(
        attention_gain, query_weight, key_weight, value_weight, output_weight
    )
    gain_one = attn_set[0].astype(jnp.float32)
    inverse_one = lax.rsqrt(jnp.mean(inputs * inputs, axis=-1, keepdims=True) + norm_eps)
    unit_one = inputs * inverse_one
    normed_one = (unit_one * gain_one).astype(jnp.bfloat16)
    queries = jnp.dot(normed_one, attn_set[1], preferred_element_type=jnp.float32)
    keys_lin = jnp.dot(normed_one, attn_set[2], preferred_element_type=jnp.float32)
    values_low = jnp.dot(normed_one, attn_set[3], preferred_element_type=jnp.float32).astype(
        jnp.bfloat16
    )
    heads_local = queries.shape[1] // HEAD
    kv_local = keys_lin.shape[1] // HEAD
    per_group = heads_local // kv_local
    cos_table, sine_table = rope_tables(local_position, HEAD)
    queries_rot = rotate(
        queries.reshape(local_rows, heads_local, HEAD), cos_table, sine_table
    ).astype(jnp.bfloat16)
    keys_rot = rotate(keys_lin.reshape(local_rows, kv_local, HEAD), cos_table, sine_table).astype(
        jnp.bfloat16
    )
    keys_all, values_all = (
        lax.all_gather(
            keys_rot.reshape(local_rows, kv_local * HEAD), CONTEXT, axis=0, tiled=True
        ),
        lax.all_gather(values_low, CONTEXT, axis=0, tiled=True),
    )
    query_heads = queries_rot.reshape(local_rows, kv_local, per_group, HEAD).transpose(1, 0, 2, 3)
    key_heads = keys_all.reshape(group_rows, kv_local, HEAD).transpose(1, 0, 2)
    value_heads = values_all.reshape(group_rows, kv_local, HEAD).transpose(1, 0, 2)

    def head_scores(query_head, key_head):
        raw_scores = jnp.einsum(
            "tgd,sd->gts", query_head, key_head, preferred_element_type=jnp.float32
        )
        return jnp.where(allowed[None], raw_scores * attention_mult, -1e30)

    def head_forward(pieces):
        query_head, key_head, value_head = pieces
        scores = head_scores(query_head, key_head)
        highest = jnp.max(scores, axis=-1, keepdims=True)
        weight = jnp.exp(scores - highest)
        row_totals = jnp.sum(weight, axis=-1, keepdims=True)
        probabilities = (weight / row_totals).astype(jnp.bfloat16)
        mixed = jnp.einsum(
            "gts,sd->tgd", probabilities, value_head, preferred_element_type=jnp.float32
        )
        return (mixed, (highest + jnp.log(row_totals))[..., 0])

    mixed_heads, log_totals = lax.map(head_forward, (query_heads, key_heads, value_heads))
    attended = (
        mixed_heads.transpose(1, 0, 2, 3)
        .reshape(local_rows, heads_local * HEAD)
        .astype(jnp.bfloat16)
    )
    attn_part = dot_last(attended, attn_set[4])
    attn_out = lax.psum(attn_part.astype(jnp.bfloat16), TENSOR).astype(jnp.float32)
    hidden_state = inputs + residual_mult * attn_out
    feed_set = feed_shards(feed_gain, gate_weight, up_weight, down_weight)
    gain_two = feed_set[0].astype(jnp.float32)
    inverse_two = lax.rsqrt(
        jnp.mean(hidden_state * hidden_state, axis=-1, keepdims=True) + norm_eps
    )
    unit_two = hidden_state * inverse_two
    normed_two = (unit_two * gain_two).astype(jnp.bfloat16)
    gate_out = jnp.dot(normed_two, feed_set[1], preferred_element_type=jnp.float32)
    up_out = jnp.dot(normed_two, feed_set[2], preferred_element_type=jnp.float32)
    inner_act = (jax.nn.silu(gate_out) * up_out).astype(jnp.bfloat16)
    feed_part = dot_last(inner_act, feed_set[3])
    feed_out = lax.psum(feed_part.astype(jnp.bfloat16), TENSOR).astype(jnp.float32)
    output = hidden_state + residual_mult * feed_out
    cotangent = out_grad[0].astype(jnp.float32) * local_valid[:, None].astype(jnp.float32)
    feed_back = feed_shards(feed_gain, gate_weight, up_weight, down_weight)
    feed_grad = (residual_mult * cotangent).astype(jnp.bfloat16)
    down_term = dot_first(feed_grad, inner_act)
    inner_grad = jnp.dot(feed_grad, feed_back[3], preferred_element_type=jnp.float32)
    sigmoid_gate = jax.nn.sigmoid(gate_out)
    gate_grad = (
        inner_grad * up_out * sigmoid_gate * (1.0 + gate_out * (1.0 - sigmoid_gate))
    ).astype(jnp.bfloat16)
    up_grad = (inner_grad * jax.nn.silu(gate_out)).astype(jnp.bfloat16)
    gate_term = dot_first(normed_two, gate_grad)
    up_term = dot_first(normed_two, up_grad)
    normed_part_two = dot_last(gate_grad, feed_back[1])
    normed_part_two = normed_part_two + dot_last(up_grad, feed_back[2])
    normed_grad_two = lax.psum(normed_part_two.astype(jnp.bfloat16), TENSOR).astype(jnp.float32)
    feed_gain_term = jnp.sum(normed_grad_two * unit_two, axis=0)
    hidden_grad = cotangent + norm_back(normed_grad_two, unit_two, gain_two, inverse_two)
    feed_sums = (
        lax.psum_scatter(feed_gain_term, (FSDP, CONTEXT), scatter_dimension=0, tiled=True),
        lax.psum_scatter(gate_term, (FSDP, CONTEXT), scatter_dimension=0, tiled=True),
        lax.psum_scatter(up_term, (FSDP, CONTEXT), scatter_dimension=0, tiled=True),
        lax.psum_scatter(down_term, (FSDP, CONTEXT), scatter_dimension=0, tiled=True),
    )
    attn_back = attention_shards(
        attention_gain, query_weight, key_weight, value_weight, output_weight
    )
    attn_grad = (residual_mult * hidden_grad).astype(jnp.bfloat16)
    out_term = dot_first(attn_grad, attended)
    mixed_grad = jnp.dot(attn_grad, attn_back[4], preferred_element_type=jnp.float32).astype(
        jnp.bfloat16
    )
    mixed_grad_heads = mixed_grad.reshape(local_rows, kv_local, per_group, HEAD).transpose(
        1, 0, 2, 3
    )

    def head_backward(pieces):
        query_head, key_head, value_head, grad_head, log_head = pieces
        scores = head_scores(query_head, key_head)
        probabilities = jnp.exp(scores - log_head[..., None])
        prob_low = probabilities.astype(jnp.bfloat16)
        prob_grad = jnp.einsum(
            "tgd,sd->gts", grad_head, value_head, preferred_element_type=jnp.float32
        )
        row_dot = jnp.sum(probabilities * prob_grad, axis=-1, keepdims=True)
        score_grad = (attention_mult * probabilities * (prob_grad - row_dot)).astype(jnp.bfloat16)
        query_grad = jnp.einsum(
            "gts,sd->tgd", score_grad, key_head, preferred_element_type=jnp.float32
        )
        key_grad = jnp.einsum(
            "gts,tgd->sd", score_grad, query_head, preferred_element_type=jnp.float32
        )
        value_grad = jnp.einsum(
            "gts,tgd->sd", prob_low, grad_head, preferred_element_type=jnp.float32
        )
        return (query_grad, key_grad, value_grad)

    query_grads, key_grads, value_grads = lax.map(
        head_backward, (query_heads, key_heads, value_heads, mixed_grad_heads, log_totals)
    )
    key_grads = key_grads.transpose(1, 0, 2).reshape(group_rows, kv_local * HEAD)
    value_grads = value_grads.transpose(1, 0, 2).reshape(group_rows, kv_local * HEAD)
    local_key_grad, local_value_grad = (
        lax.psum_scatter(
            key_grads.astype(jnp.bfloat16), CONTEXT, scatter_dimension=0, tiled=True
        ).astype(jnp.float32),
        lax.psum_scatter(
            value_grads.astype(jnp.bfloat16), CONTEXT, scatter_dimension=0, tiled=True
        ).astype(jnp.float32),
    )
    query_grad_rot = query_grads.transpose(1, 0, 2, 3).reshape(local_rows, heads_local, HEAD)
    query_grad_low = (
        rotate_back(query_grad_rot, cos_table, sine_table)
        .reshape(local_rows, heads_local * HEAD)
        .astype(jnp.bfloat16)
    )
    key_grad_low = (
        rotate_back(local_key_grad.reshape(local_rows, kv_local, HEAD), cos_table, sine_table)
        .reshape(local_rows, kv_local * HEAD)
        .astype(jnp.bfloat16)
    )
    value_grad_low = local_value_grad.astype(jnp.bfloat16)
    query_term = dot_first(normed_one, query_grad_low)
    key_term = dot_first(normed_one, key_grad_low)
    value_term = dot_first(normed_one, value_grad_low)
    normed_part_one = dot_last(query_grad_low, attn_back[1])
    normed_part_one = normed_part_one + dot_last(key_grad_low, attn_back[2])
    normed_part_one = normed_part_one + dot_last(value_grad_low, attn_back[3])
    normed_grad_one = lax.psum(normed_part_one.astype(jnp.bfloat16), TENSOR).astype(jnp.float32)
    attn_gain_term = jnp.sum(normed_grad_one * unit_one, axis=0)
    input_grad = hidden_grad + norm_back(normed_grad_one, unit_one, gain_one, inverse_one)
    attn_sums = (
        lax.psum_scatter(attn_gain_term, (FSDP, CONTEXT), scatter_dimension=0, tiled=True),
        lax.psum_scatter(query_term, (FSDP, CONTEXT), scatter_dimension=0, tiled=True),
        lax.psum_scatter(key_term, (FSDP, CONTEXT), scatter_dimension=0, tiled=True),
        lax.psum_scatter(value_term, (FSDP, CONTEXT), scatter_dimension=0, tiled=True),
        lax.psum_scatter(out_term, (FSDP, CONTEXT), scatter_dimension=0, tiled=True),
    )
    return (
        output.astype(jnp.bfloat16)[None],
        input_grad.astype(jnp.bfloat16)[None],
        attn_sums[0],
        attn_sums[1],
        attn_sums[2],
        attn_sums[3],
        attn_sums[4],
        feed_sums[0],
        feed_sums[1],
        feed_sums[2],
        feed_sums[3],
    )


def flip(i, k):
    if k == 0:
        return i
    if k == 1:
        return i + 1 - 2 * lax.rem(i, 2)
    if k == 2:
        return lax.rem(i + 2, 4)
    return 3 - i


class Copies:
    def __init__(self, send, receive):
        self.send, self.receive = send, receive
        self.count, self.started = 0, []

    def index(self):
        self.count += 1
        return self.count - 1

    def make(self, i, source, target, device):
        return pltpu.make_async_remote_copy(
            src_ref=source,
            dst_ref=target,
            send_sem=self.send.at[i],
            recv_sem=self.receive.at[i],
            device_id=device,
            device_id_type=pl.DeviceIdType.MESH,
        )

    def start(self, source, target, device, i=None):
        i = self.index() if i is None else i
        copy = self.make(i, source, target, device)
        copy.start()
        self.started.append(copy)
        return copy


def greet(partners):
    barrier = pltpu.get_barrier_semaphore()
    for device in partners:
        pl.semaphore_signal(barrier, inc=1, device_id=device, device_id_type=pl.DeviceIdType.MESH)
    pl.semaphore_wait(barrier, len(partners))


def dot_tile(left, right, left_axis, right_axis):
    return lax.dot_general(left, right, (((left_axis,), (right_axis,)), ((), ())), preferred_element_type=jnp.float32)


TILE = 256


def turn_lanes(x, low):
    return jnp.where(low, pltpu.roll(x, x.shape[1] - HEAD // 2, 1), pltpu.roll(x, HEAD // 2, 1))


def low_lanes(shape, width):
    return lax.rem(lax.broadcasted_iota(jnp.int32, shape, 1), 2 * width) < width


def split_pair(x):
    low = low_lanes(x.shape, HEAD)
    a, b = jnp.where(low, x, 0.0), jnp.where(low, 0.0, x)
    return a, pltpu.roll(a, HEAD, 1), pltpu.roll(b, HEAD, 1), b


def attention_kernel(
    wa, wf, xt, gain, fgx, cos, sin, seg_col, seg_row,
    wa_out, wf_all, normed_out, q, kv, logs, attended, hidden_out, normed_two, fg_all, gains,
    wa_all, x_all, gain_all, normed, pairs, sums, mine, cross, crossed, totals, landed, send, receive, local,
):
    f32, bf16 = jnp.float32, jnp.bfloat16
    z, c, t = (lax.axis_index(a) for a in (FSDP, CONTEXT, TENSOR))
    peers = [(flip(z, i), flip(c, j), t) for i in range(4) for j in range(4) if i or j]
    core = (z, c, 1 - t)
    greet(peers + [core])
    net = Copies(send, receive)
    middle = (z == 1) | (z == 2)
    nt, part, width = xt.shape
    rows = nt * part
    q_cols = q.shape[1]
    qkv_cols = q_cols + 2 * HEAD
    ends = []
    own = []
    for i, (source, target) in enumerate(
        (
            (wa.at[c], wa_all.at[z, c]),
            (xt, x_all.at[c]),
            (wf.at[z], wf_all.at[z, c]),
            (gain, gain_all.at[z, c]),
            (fgx, fg_all.at[0, 0]),
        )
    ):
        own.append(pltpu.make_async_copy(source, target, local.at[i]))
        own[-1].start()

    def spread(source, slot, forward):
        one = net.start(source, slot(1), (flip(z, 1), c, t))
        two = net.start(source, slot(2), (flip(z, 2), c, t))
        three = net.index()
        direct = net.make(three, source, slot(3), (3 - z, c, t))
        pl.when(middle)(direct.start)
        passed = pltpu.make_async_remote_copy(
            src_ref=forward[0],
            dst_ref=forward[1],
            send_sem=send.at[net.index()],
            recv_sem=receive.at[three],
            device_id=(flip(z, 1), c, t),
            device_id_type=pl.DeviceIdType.MESH,
        )
        return one, two, direct, passed

    attn_in = [net.start(wa.at[flip(c, k)], wa_all.at[z, c], (z, flip(c, k), t)) for k in (1, 2, 3)]
    tokens_in = [net.start(xt.at[t], x_all.at[c, t], (z, flip(c, k), t)) for k in (1, 2, 3)]
    ff_in = {1: net.start(wf.at[flip(z, 1)], wf_all.at[z, c], (flip(z, 1), c, t))}
    for device in peers:
        ends.append(net.start(gain, gain_all.at[z, c], device))
    own[2].wait()
    ff_out = {0: [net.start(wf_all.at[z, c], wf_all.at[z, c], (z, flip(c, k), t)) for k in (1, 2)]}
    weights = []
    for j in range(4):
        if j:
            attn_in[j - 1].wait_recv()
        else:
            own[0].wait()
        piece = wa_all.at[z, flip(c, j)]
        passed_piece = wa_all.at[flip(z, 2), flip(c, j)]
        weights.append(spread(piece, lambda k, piece=piece: piece, (passed_piece, passed_piece)))
    for k in (3, 2):
        ff_in[k] = net.start(wf.at[flip(z, k)], wf_all.at[z, c], (flip(z, k), c, t))
    feed = spread(fgx, lambda k: fg_all.at[k, 0], (fg_all.at[2, 0], fg_all.at[3, 0]))
    swaps = [net.start(fgx, fg_all.at[0, 1], core)]
    token_swaps = []
    for k, copy in zip((1, 2, 3), tokens_in):
        copy.wait_recv()
        piece = x_all.at[flip(c, k), t]
        token_swaps.append(net.start(piece, piece, core))
    halves = []

    def corner(k):
        zs = flip(z, k)
        one, two = ff_out[k]
        two.wait_recv()
        piece = wf_all.at[zs, flip(c, 2), pl.ds(0, 64)]
        halves.append(net.start(piece, piece, (z, flip(c, 1), t)))
        one.wait_recv()
        piece = wf_all.at[zs, flip(c, 1), pl.ds(64, 64)]
        halves.append(net.start(piece, piece, (z, flip(c, 2), t)))

    def onward(k):
        ff_in[k].wait_recv()
        piece = wf_all.at[flip(z, k), c]
        ff_out[k] = [net.start(piece, piece, (z, flip(c, j), t)) for j in (1, 2)]

    own[1].wait()
    own[3].wait()
    for copy in token_swaps + ends:
        copy.wait_recv()
    for i in range(2):
        gains[i : i + 1, :] = jnp.concatenate(
            [gain_all[a, b, i : i + 1, :].astype(f32) for a in range(4) for b in range(4)], axis=1
        )

    def norm_rows(i, carry):
        x = x_all[i].reshape(rows, width).astype(f32)
        inverse = lax.rsqrt(jnp.mean(x * x, axis=-1, keepdims=True) + norm_eps)
        normed[i] = (x * inverse * gains[0:1, :]).astype(bf16)
        return carry

    lax.fori_loop(0, 4, norm_rows, 0)
    save = [pltpu.make_async_copy(normed, normed_out, local.at[5])]
    save[0].start()
    onward(1)
    corner(0)
    for one, two, direct, passed in weights:
        two.wait_recv()
        pl.when(middle)(passed.start)
    for one, two, direct, passed in weights:
        one.wait_recv()
        direct.wait_recv()
    save.append(pltpu.make_async_copy(wa_all, wa_out, local.at[6]))
    save[1].start()

    def project(i, carry):
        here = pl.ds(pl.multiple_of(i * rows, rows), rows)
        w = wa_all[...].reshape(width, wa_all.shape[3])
        qkv = dot_tile(normed[i], w[:, :qkv_cols], 1, 0)
        cos_b, sin_b = cos[here, :], sin[here, :]
        quarter = low_lanes(cos_b.shape, HEAD // 2)
        half = low_lanes(cos_b.shape, HEAD)
        for p in range(q_cols // 128):
            block = qkv[:, p * 128 : (p + 1) * 128]
            q[here, p * 128 : (p + 1) * 128] = (block * cos_b + turn_lanes(block, quarter) * sin_b).astype(bf16)
        block = qkv[:, q_cols:]
        block = jnp.where(half, block * cos_b + turn_lanes(block, quarter) * sin_b, block)
        kv[here, :] = block.astype(bf16)
        for j, piece in enumerate(split_pair(block)):
            pairs[j, here, :] = piece.astype(bf16)
        return carry

    lax.fori_loop(0, 4, project, 0)
    corner(1)

    def attend(i):
        count = (i + 1) * rows
        here = pl.ds(i * rows, rows)
        keep = (seg_col[here, :] == seg_row[:, :count]) & (
            lax.broadcasted_iota(jnp.int32, (rows, count), 0) + i * rows
            >= lax.broadcasted_iota(jnp.int32, (rows, count), 1)
        )
        lane = lax.broadcasted_iota(jnp.int32, (rows, 128), 1)
        log_sums = jnp.zeros((rows, 128), f32)
        for p in range(q_cols // 128):
            out = jnp.zeros((rows, 128), f32)
            for e in range(2):
                scores = dot_tile(q[here, p * 128 : (p + 1) * 128], pairs[e, :count, :], 1, 1)
                scores = jnp.where(keep, scores * attention_mult, -1e30)
                highest = jnp.max(scores, axis=-1, keepdims=True)
                weight = jnp.exp(scores - highest)
                total = jnp.sum(weight, axis=-1, keepdims=True)
                out = out + dot_tile((weight / total).astype(bf16), pairs[2 + e, :count, :], 1, 0)
                log_sums = jnp.where(lane == 2 * p + e, highest + jnp.log(total), log_sums)
            attended[here, p * 128 : (p + 1) * 128] = out.astype(bf16)
        logs[here, :] = log_sums

    attend(0)
    attend(1)
    onward(3)
    attend(2)
    last = pl.ds(3 * rows, rows)
    both = (pairs[2, last, :] + pairs[3, last, :]).astype(bf16)
    for p in range(q_cols // 128):
        attended[last, p * 128 : (p + 1) * 128] = both
    corner(3)

    crosses, outs = {}, {}
    for k in (3, 1, 2, 0):
        mine_rows = pl.ds(pl.multiple_of(flip(c, k) * rows, rows), rows)

        def out_tile(n, carry, mine_rows=mine_rows):
            here = pl.ds(pl.multiple_of(n * 128, 128), 128)
            w = wa_all[lax.div(n, 4), lax.rem(n, 4), :, qkv_cols:]
            sums[:, here] = dot_tile(attended[mine_rows, :], w, 1, 1)
            return carry

        lax.fori_loop(0, width // 128, out_tile, 0)
        mine[k] = sums[pl.ds(pl.multiple_of(t * part, part), part), :]
        cross[k] = sums[pl.ds(pl.multiple_of((1 - t) * part, part), part), :].astype(bf16)
        crosses[k] = net.start(cross.at[k], crossed.at[k], core)
    for k in (3, 1, 2):
        crosses[k].wait_recv()
        totals[k - 1] = (mine[k] + crossed[k].astype(f32)).astype(bf16)
        outs[k] = net.start(totals.at[k - 1], landed.at[k - 1], (z, flip(c, k), t))
    onward(2)
    one, two, direct, passed = feed
    two.wait_recv()
    pl.when(middle)(passed.start)
    swaps.append(net.start(fg_all.at[2, 0], fg_all.at[2, 1], core))
    one.wait_recv()
    swaps.append(net.start(fg_all.at[1, 0], fg_all.at[1, 1], core))
    crosses[0].wait_recv()
    total = mine[0] + crossed[0].astype(f32)
    for k in (1, 2, 3):
        outs[k].wait_recv()
        total = total + landed[k - 1].astype(f32)
    hidden = xt[t].astype(f32) + residual_mult * total
    hidden_out[...] = hidden
    inverse = lax.rsqrt(jnp.mean(hidden * hidden, axis=-1, keepdims=True) + norm_eps)
    normed_two[...] = (hidden * inverse * gains[1:2, :]).astype(bf16)
    direct.wait_recv()
    swaps.append(net.start(fg_all.at[3, 0], fg_all.at[3, 1], core))
    corner(2)
    for copy in halves + swaps:
        copy.wait_recv()
    for _, _, direct, passed in weights + [feed]:
        pl.when(middle)(direct.wait_send)
        pl.when(middle)(passed.wait_send)
    for copy in net.started:
        copy.wait_send()
    own[4].wait()
    for copy in save:
        copy.wait()


def attention_forward(wa, wf, xt, gain, fgx, cos, sin, seg_col, seg_row):
    bf16, f32 = jnp.bfloat16, jnp.float32
    nt, part, width = xt.shape
    rows = nt * part
    total = 4 * rows
    wa_cols = wa.shape[2]
    q_cols = (wa_cols - 2 * HEAD) // 2
    filled = seg_col.shape[0]
    copies = 96
    vmem, anywhere = pl.BlockSpec(memory_space=pltpu.VMEM), pl.BlockSpec(memory_space=pl.ANY)
    outs = (
        ((4, 4) + wa.shape[1:], bf16, anywhere),
        ((4, 4) + wf.shape[1:], bf16, anywhere),
        ((4, rows, width), bf16, anywhere),
        ((total, q_cols), bf16, vmem),
        ((total, 2 * HEAD), bf16, vmem),
        ((filled, 128), f32, vmem),
        ((total, q_cols), bf16, vmem),
        ((part, width), f32, vmem),
        ((part, width), bf16, vmem),
        ((4, nt, part, width), bf16, anywhere),
        ((2, width), f32, vmem),
    )
    return pl.pallas_call(
        attention_kernel,
        out_shape=[jax.ShapeDtypeStruct(shape, dtype) for shape, dtype, _ in outs],
        in_specs=[vmem] * 9,
        out_specs=[spec for _, _, spec in outs],
        scratch_shapes=[
            pltpu.VMEM((4, 4) + wa.shape[1:], bf16),
            pltpu.VMEM((4, nt, part, width), bf16),
            pltpu.VMEM((4, 4) + gain.shape, bf16),
            pltpu.VMEM((4, rows, width), bf16),
            pltpu.VMEM((4, total, 2 * HEAD), bf16),
            pltpu.VMEM((rows, width), f32),
            pltpu.VMEM((4, part, width), f32),
            pltpu.VMEM((4, part, width), bf16),
            pltpu.VMEM((4, part, width), bf16),
            pltpu.VMEM((3, part, width), bf16),
            pltpu.VMEM((3, part, width), bf16),
            pltpu.SemaphoreType.DMA((copies,)),
            pltpu.SemaphoreType.DMA((copies,)),
            pltpu.SemaphoreType.DMA((7,)),
        ],
        compiler_params=pltpu.CompilerParams(collective_id=1, has_side_effects=True, vmem_limit_bytes=60 * 2**20),
    )(wa, wf, xt, gain, fgx, cos, sin, seg_col, seg_row)


def feed_kernel(
    x, fg, w, back, feed_own, feed_send, terms,
    xs, wv, gate_g, up_g, inner, mine, cross, crossed, totals, landed, send, receive, local,
):
    f32, bf16 = jnp.float32, jnp.bfloat16
    z, c, t = (lax.axis_index(a) for a in (FSDP, CONTEXT, TENSOR))
    core = (z, c, 1 - t)
    greet([(flip(z, k), c, t) for k in (1, 2, 3)] + [core])
    net = Copies(send, receive)
    part, width = x.shape
    hidden = wv.shape[1] // 3
    load = pltpu.make_async_copy(w, wv, local.at[0])
    load.start()
    middle = (z == 1) | (z == 2)
    swaps = {0: net.start(x, xs.at[0, 1], core)}
    arrive = {2: net.start(x, xs.at[2, 0], (flip(z, 2), c, t))}
    three = net.index()
    direct = net.make(three, x, xs.at[3, 0], (3 - z, c, t))
    pl.when(middle)(direct.start)
    arrive[3] = direct
    arrive[1] = net.start(x, xs.at[1, 0], (flip(z, 1), c, t))
    passed = pltpu.make_async_remote_copy(
        src_ref=xs.at[2, 0],
        dst_ref=xs.at[3, 0],
        send_sem=send.at[net.index()],
        recv_sem=receive.at[three],
        device_id=(flip(z, 1), c, t),
        device_id_type=pl.DeviceIdType.MESH,
    )
    xs[0, 0] = x[...]
    load.wait()

    def first(k):
        swaps[k].wait_recv()
        rows = xs[k].reshape(2 * part, width)
        grads = fg[k]

        def step(n, carry):
            at = pl.multiple_of(n * TILE, TILE)
            g = dot_tile(rows, wv[:, pl.ds(at, TILE)], 1, 0)
            u = dot_tile(rows, wv[:, pl.ds(hidden + at, TILE)], 1, 0)
            d = dot_tile(grads, wv[:, pl.ds(2 * hidden + at, TILE)], 1, 0)
            sig = jax.nn.sigmoid(g)
            here = pl.ds(at, TILE)
            inner[k, :, here] = (g * sig * u).astype(bf16)
            gate_g[k, :, here] = (d * u * sig * (1.0 + g * (1.0 - sig))).astype(bf16)
            up_g[k, :, here] = (d * g * sig).astype(bf16)
            return carry

        lax.fori_loop(0, hidden // TILE, step, 0)

    crosses = {}

    def second(k):
        def step(n, carry):
            here = pl.ds(pl.multiple_of(n * TILE, TILE), TILE)
            b = dot_tile(gate_g[k], wv[here, 0:hidden], 1, 1) + dot_tile(up_g[k], wv[here, hidden : 2 * hidden], 1, 1)
            f = dot_tile(inner[k], wv[here, 2 * hidden :], 1, 1)
            mine[k, 0, :, here] = b[:part]
            mine[k, 1, :, here] = f[:part]
            cross[k, 0, :, here] = b[part:].astype(bf16)
            cross[k, 1, :, here] = f[part:].astype(bf16)
            return carry

        lax.fori_loop(0, width // TILE, step, 0)
        crosses[k] = net.start(cross.at[k], crossed.at[k], core)

    sums = {}

    def finish(k):
        crosses[k].wait_recv()
        if k:
            totals[k - 1] = (mine[k, 0] + crossed[k, 0].astype(f32)).astype(bf16)
            sums[k] = net.start(totals.at[k - 1], landed.at[k - 1], (flip(z, k), c, t))
            feed_send[k - 1] = (mine[k, 1] + crossed[k, 1].astype(f32)).astype(bf16)
        else:
            back[...] = mine[0, 0] + crossed[0, 0].astype(f32)
            feed_own[...] = mine[0, 1] + crossed[0, 1].astype(f32)

    def fetch(k):
        arrive[k].wait_recv()
        if k == 2:
            pl.when(middle)(passed.start)
        swaps[k] = net.start(xs.at[k, 0], xs.at[k, 1], core)

    order = (0, 2, 3, 1)
    for i, k in enumerate(order):
        first(k)
        if i:
            finish(order[i - 1])
        if i < 3:
            fetch(order[i + 1])
        second(k)

    rows = xs.shape[0] * 2 * part

    def term(source, grads, begin):
        def step(m, carry):
            here = pl.ds(pl.multiple_of(m * TILE, TILE), TILE)
            left = source[:, :, here].reshape(rows, TILE)
            value = dot_tile(left, grads[...].reshape(rows, hidden), 0, 0)
            wv[here, begin : begin + hidden] = value.astype(bf16)
            return carry

        lax.fori_loop(0, width // TILE, step, 0)

    flat = xs.reshape(xs.shape[0], 2 * part, width)
    term(flat, gate_g, 0)
    finish(order[3])
    term(flat, up_g, hidden)
    term(fg, inner, 2 * hidden)
    store = pltpu.make_async_copy(wv, terms, local.at[1])
    store.start()
    for k in (1, 2, 3):
        sums[k].wait_recv()
    back[...] = back[...] + landed[0].astype(f32) + landed[1].astype(f32) + landed[2].astype(f32)
    pl.when(middle)(direct.wait_send)
    pl.when(middle)(passed.wait_send)
    for copy in net.started:
        copy.wait_send()
    store.wait()


def feed_forward(x, fg, w):
    bf16, f32 = jnp.bfloat16, jnp.float32
    part, width = x.shape
    cols = w.shape[1]
    hidden = cols // 3
    blocks = fg.shape[0]
    copies = 20
    vmem, anywhere = pl.BlockSpec(memory_space=pltpu.VMEM), pl.BlockSpec(memory_space=pl.ANY)
    return pl.pallas_call(
        feed_kernel,
        out_shape=[
            jax.ShapeDtypeStruct((part, width), f32),
            jax.ShapeDtypeStruct((part, width), f32),
            jax.ShapeDtypeStruct((blocks - 1, part, width), bf16),
            jax.ShapeDtypeStruct(w.shape, bf16),
        ],
        in_specs=[vmem, vmem, anywhere],
        out_specs=[vmem, vmem, vmem, anywhere],
        scratch_shapes=[
            pltpu.VMEM((blocks, 2, part, width), bf16),
            pltpu.VMEM(w.shape, bf16),
            pltpu.VMEM((blocks, 2 * part, hidden), bf16),
            pltpu.VMEM((blocks, 2 * part, hidden), bf16),
            pltpu.VMEM((blocks, 2 * part, hidden), bf16),
            pltpu.VMEM((blocks, 2, part, width), f32),
            pltpu.VMEM((blocks, 2, part, width), bf16),
            pltpu.VMEM((blocks, 2, part, width), bf16),
            pltpu.VMEM((blocks - 1, part, width), bf16),
            pltpu.VMEM((blocks - 1, part, width), bf16),
            pltpu.SemaphoreType.DMA((copies,)),
            pltpu.SemaphoreType.DMA((copies,)),
            pltpu.SemaphoreType.DMA((2,)),
        ],
        compiler_params=pltpu.CompilerParams(collective_id=3, has_side_effects=True, vmem_limit_bytes=62 * 2**20),
    )(x, fg, w)


def swap(x, axis, k):
    return lax.ppermute(x, axis, [(i, i ^ k) for i in range(lax.axis_size(axis))])


def put(buffer, block, *index):
    lead = len(index)
    block = block.reshape((1,) * lead + buffer.shape[lead:])
    zero = jnp.int32(0)
    start = tuple(jnp.asarray(i, jnp.int32) for i in index) + (zero,) * (buffer.ndim - lead)
    return lax.dynamic_update_slice(buffer, block, start)


def cut(x, index, size, axis):
    return lax.dynamic_slice_in_dim(x, index * size, size, axis)


def grads_out_kernel(
    ff, at, fs, feed_out, gate_out, up_out, down_out, query_out, key_out, value_out, output_out,
    terms, corner_x, corner_y, side_x, side_y, landed, feed_in, at_terms, at_in, at_total, at_landed, send, receive, local,
):
    f32, bf16 = jnp.float32, jnp.bfloat16
    z, c, t = (lax.axis_index(a) for a in (FSDP, CONTEXT, TENSOR))
    greet([(flip(z, k), c, t) for k in (1, 2, 3)] + [(z, flip(c, k), t) for k in (1, 2, 3)])
    net = Copies(send, receive)
    rows = ff.shape[2]
    half = rows // 2
    order = (3, 2, 1, 0)
    loads = {}
    for k in order:
        zs = flip(z, k)
        loads[k] = pltpu.make_async_copy(ff.at[zs], terms.at[zs], local.at[k])
        loads[k].start()
    attn_load = pltpu.make_async_copy(at, at_terms, local.at[4])
    attn_load.start()
    attn_load.wait()
    attn_in = [net.start(at_terms.at[flip(z, k)], at_in.at[k - 1], (flip(z, k), c, t)) for k in (3, 2, 1)]
    feed = [net.start(fs.at[k - 1], feed_in.at[k - 1], (flip(z, k), c, t)) for k in (3, 2, 1)]
    first = {}
    for k in order:
        zs = flip(z, k)
        loads[k].wait()
        first[k] = (
            net.start(terms.at[zs, flip(c, 3), pl.ds(0, half)], corner_x.at[k], (z, flip(c, 1), t)),
            net.start(terms.at[zs, flip(c, 3), pl.ds(half, half)], corner_y.at[k], (z, flip(c, 2), t)),
        )
    second = {}
    for k in order:
        zs = flip(z, k)
        for copy in first[k]:
            copy.wait_recv()
        low, high = pl.ds(0, half), pl.ds(half, half)
        xb, yb = flip(c, 1), flip(c, 2)
        terms[zs, yb, low] = (terms[zs, yb, low].astype(f32) + corner_x[k].astype(f32)).astype(bf16)
        terms[zs, xb, high] = (terms[zs, xb, high].astype(f32) + corner_y[k].astype(f32)).astype(bf16)
        second[k] = (
            net.start(terms.at[zs, yb], side_y.at[k], (z, yb, t)),
            net.start(terms.at[zs, xb], side_x.at[k], (z, xb, t)),
        )
    for copy in attn_in:
        copy.wait_recv()
    for j in range(4):
        total = at_terms[z, j].astype(f32)
        for i in range(3):
            total = total + at_in[i, j].astype(f32)
        at_total[j] = total.astype(bf16)
    attn_out = [net.start(at_total.at[flip(c, k)], at_landed.at[c], (z, flip(c, k), t)) for k in (1, 2, 3)]
    at_landed[c] = at_total[c]
    third = {}
    for k in order:
        zs = flip(z, k)
        for copy in second[k]:
            copy.wait_recv()
        total = terms[zs, c].astype(f32) + side_x[k].astype(f32) + side_y[k].astype(f32)
        if k:
            terms[zs, c] = total.astype(bf16)
            third[k] = net.start(terms.at[zs, c], landed.at[k], (zs, c, t))
        else:
            landed[0] = total.astype(bf16)
    size = gate_out.shape[1] // 4
    for k in (0, 3, 2, 1):
        if k:
            third[k].wait_recv()
        zs = flip(z, k)
        columns = pl.ds(pl.multiple_of(zs * size, size), size)
        for i, out in enumerate((gate_out, up_out, down_out)):
            out[:, columns] = landed[k, :, i * size : (i + 1) * size]
    for copy in attn_out:
        copy.wait_recv()
    begin = 0
    for out in (query_out, key_out, value_out, output_out):
        size = out.shape[1] // 4
        for j in range(4):
            out[:, j * size : (j + 1) * size] = at_landed[j, :, begin : begin + size]
        begin += size
    for copy in feed:
        copy.wait_recv()
    feed_out[...] = feed_in[0].astype(f32) + feed_in[1].astype(f32) + feed_in[2].astype(f32)
    for copy in net.started:
        copy.wait_send()


def grads_out(ff, at, fs, sizes):
    bf16, f32 = jnp.bfloat16, jnp.float32
    rows, cols = ff.shape[2:]
    attn_cols = at.shape[3]
    copies = 32
    return pl.pallas_call(
        grads_out_kernel,
        out_shape=[jax.ShapeDtypeStruct(fs.shape[1:], f32)] + [jax.ShapeDtypeStruct((rows, s), bf16) for s in sizes],
        in_specs=[pl.BlockSpec(memory_space=pl.ANY)] * 2 + [pl.BlockSpec(memory_space=pltpu.VMEM)],
        out_specs=[pl.BlockSpec(memory_space=pltpu.VMEM)] * (1 + len(sizes)),
        scratch_shapes=[
            pltpu.VMEM((4, 4, rows, cols), bf16),
            pltpu.VMEM((4, rows // 2, cols), bf16),
            pltpu.VMEM((4, rows // 2, cols), bf16),
            pltpu.VMEM((4, rows, cols), bf16),
            pltpu.VMEM((4, rows, cols), bf16),
            pltpu.VMEM((4, rows, cols), bf16),
            pltpu.VMEM(fs.shape, bf16),
            pltpu.VMEM((4, 4, rows, attn_cols), bf16),
            pltpu.VMEM((3, 4, rows, attn_cols), bf16),
            pltpu.VMEM((4, rows, attn_cols), bf16),
            pltpu.VMEM((4, rows, attn_cols), bf16),
            pltpu.SemaphoreType.DMA((copies,)),
            pltpu.SemaphoreType.DMA((copies,)),
            pltpu.SemaphoreType.DMA((5,)),
        ],
        compiler_params=pltpu.CompilerParams(collective_id=2, has_side_effects=True, vmem_limit_bytes=60 * 2**20),
    )(ff, at, fs)


def on_device_split(
    tokens,
    out_grad,
    lengths,
    attention_gain,
    query_weight,
    key_weight,
    value_weight,
    output_weight,
    feed_gain,
    gate_weight,
    up_weight,
    down_weight,
):
    f32, bf16 = jnp.float32, jnp.bfloat16
    nz, nc, nt = (lax.axis_size(a) for a in (FSDP, CONTEXT, TENSOR))
    z, c, t = (lax.axis_index(a) for a in (FSDP, CONTEXT, TENSOR))
    local_rows, width = tokens.shape[1:]
    group_rows = local_rows * nc
    filled = group_rows * 3 // 4
    part = local_rows // nt
    wrows = query_weight.shape[0]
    kv_cols = key_weight.shape[1] // nc
    q_cols = query_weight.shape[1] // nc
    qkv_cols = q_cols + 2 * kv_cols
    ff_cols = gate_weight.shape[1] // nz
    per_group = q_cols // kv_cols
    segment, position, valid_rows = slot_layout(lengths[0], group_rows)
    cos_table, sine_table = rope_tables(position, HEAD)

    wa = jnp.concatenate(
        [
            w.astype(bf16).reshape(wrows, nc, -1).transpose(1, 0, 2)
            for w in (query_weight, key_weight, value_weight, output_weight)
        ],
        axis=2,
    )
    wf = jnp.concatenate(
        [w.astype(bf16).reshape(wrows, nz, ff_cols).transpose(1, 0, 2) for w in (gate_weight, up_weight, down_weight)],
        axis=2,
    )
    gain = jnp.pad(jnp.stack([attention_gain, feed_gain]).astype(bf16), ((0, 14), (0, 0)))
    my_valid = lax.dynamic_slice_in_dim(valid_rows, c * local_rows + t * part, part)
    cotangent = cut(out_grad[0], t, part, 0).astype(f32) * my_valid[:, None].astype(f32)
    feed_grad = (residual_mult * cotangent).astype(bf16)
    sign = jnp.where(jnp.arange(HEAD) < HEAD // 2, -1.0, 1.0).astype(f32)
    wide_cos = jnp.concatenate([cos_table, cos_table], axis=1)
    wide_sin = jnp.concatenate([sine_table * sign, sine_table * sign], axis=1)
    wa, wf, normed_one, queries, pair, logs, attended, hidden, normed_two, feed_grads, gains = attention_forward(
        wa, wf, tokens[0].reshape(nt, part, width), gain, feed_grad, wide_cos, wide_sin,
        segment[:filled, None], segment[None, :filled],
    )
    gain_one, gain_two = gains[0], gains[1]
    w_qkv = wa[..., :qkv_cols].reshape(width, qkv_cols)
    w_out = wa[..., qkv_cols:].reshape(width, q_cols)
    w_feed = wf.reshape(width, 3 * ff_cols)
    normed_one = normed_one.reshape(group_rows, width)
    q_f = queries[:filled].reshape(filled, per_group, HEAD)
    k_f, v_f = pair[:filled, :HEAD], pair[:filled, HEAD:]
    attended_f = attended[:filled]
    slot_ids = jnp.arange(filled, dtype=jnp.int32)
    allowed = (segment[:filled, None] == segment[None, :filled]) & (slot_ids[:, None] >= slot_ids[None, :])

    def scatter_context(partial):
        partial = partial.reshape(nc, nt, part, width)
        mine = cut(partial, t, 1, 1)[:, 0]
        other = cut(partial, 1 - t, 1, 1)[:, 0].astype(bf16)
        mine = mine + swap(other, TENSOR, 1).astype(f32)
        total = cut(mine, c, 1, 0)[0]
        for k in range(1, nc):
            total = total + swap(cut(mine, c ^ k, 1, 0)[0].astype(bf16), CONTEXT, k).astype(f32)
        return total

    my_inputs = cut(tokens[0], t, part, 0).astype(f32)
    inverse_two = lax.rsqrt(jnp.mean(hidden * hidden, axis=-1, keepdims=True) + norm_eps)
    unit_two = hidden * inverse_two

    normed_grad_two, feed_own, feed_send, ff_terms = feed_forward(
        normed_two, feed_grads.reshape(nz, local_rows, width), w_feed
    )
    ff_terms = ff_terms.reshape(nz, nc, wrows, 3 * ff_cols)

    def both_cores(x):
        out = put(jnp.zeros((nt,) + x.shape, x.dtype), x, t)
        return put(out, swap(x, TENSOR, 1), 1 - t).reshape(1, local_rows, width)

    feed_gain_term = jnp.sum(normed_grad_two * unit_two, axis=0)
    hidden_grad = cotangent + norm_back(normed_grad_two, unit_two, gain_two, inverse_two)

    attn_low = (residual_mult * hidden_grad).astype(bf16)
    attn_grad = jnp.zeros((nc, nt, part, width), bf16)
    attn_grad = put(attn_grad, attn_low, c, t)
    attn_grad = put(attn_grad, swap(attn_low, TENSOR, 1), c, 1 - t)
    for k in range(1, nc):
        block = swap(attn_low, CONTEXT, k)
        attn_grad = put(attn_grad, block, c ^ k, t)
        attn_grad = put(attn_grad, swap(block, TENSOR, 1), c ^ k, 1 - t)
    attn_grad = attn_grad.reshape(group_rows, width)[:filled]

    out_term = dot_first(attn_grad, attended_f)
    mixed_grad = jnp.dot(attn_grad, w_out, preferred_element_type=f32).astype(bf16).reshape(filled, per_group, HEAD)
    scores = jnp.einsum("tgd,sd->gts", q_f, k_f, preferred_element_type=f32)
    scores = jnp.where(allowed[None], scores * attention_mult, -1e30)
    probabilities = jnp.exp(scores - logs[:, :per_group].T[:, :, None])
    prob_low = probabilities.astype(bf16)
    prob_grad = jnp.einsum("tgd,sd->gts", mixed_grad, v_f, preferred_element_type=f32)
    row_dot = jnp.sum(probabilities * prob_grad, axis=-1, keepdims=True)
    score_grad = (attention_mult * probabilities * (prob_grad - row_dot)).astype(bf16)
    query_grad = jnp.einsum("gts,sd->tgd", score_grad, k_f, preferred_element_type=f32)
    key_grad = jnp.einsum("gts,tgd->sd", score_grad, q_f, preferred_element_type=f32)
    value_grad = jnp.einsum("gts,tgd->sd", prob_low, mixed_grad, preferred_element_type=f32).astype(bf16)
    cos_f, sine_f = cos_table[:filled], sine_table[:filled]
    query_grad = rotate_back(query_grad, cos_f, sine_f).reshape(filled, q_cols).astype(bf16)
    key_grad = rotate_back(key_grad[:, None], cos_f, sine_f)[:, 0].astype(bf16)
    qkv_grad = jnp.concatenate([query_grad, key_grad, value_grad], axis=1)
    normed_part = dot_last(qkv_grad, w_qkv)
    normed_part = jnp.pad(normed_part, ((0, group_rows - filled), (0, 0)))
    normed_grad_one = scatter_context(normed_part)
    inverse_one = lax.rsqrt(jnp.mean(my_inputs * my_inputs, axis=-1, keepdims=True) + norm_eps)
    unit_one = my_inputs * inverse_one
    attn_gain_term = jnp.sum(normed_grad_one * unit_one, axis=0)
    input_grad = both_cores((hidden_grad + norm_back(normed_grad_one, unit_one, gain_one, inverse_one)).astype(bf16))

    gain_terms = jnp.stack([attn_gain_term, feed_gain_term])
    for axis, k in ((TENSOR, 1), (CONTEXT, 1), (CONTEXT, 2), (FSDP, 1), (FSDP, 2)):
        gain_terms = gain_terms + swap(gain_terms, axis, k)
    gain_terms = cut(gain_terms, z * nc + c, wrows, 1)

    qkv_term = dot_first(normed_one[:filled], qkv_grad)
    terms = jnp.concatenate([qkv_term, out_term], axis=1).astype(bf16).reshape(nz, nc, wrows, -1)
    sizes = [w.shape[1] for w in (gate_weight, up_weight, down_weight)]
    sizes += [w.shape[1] for w in (query_weight, key_weight, value_weight, output_weight)]
    feed_in, *weight_grads = grads_out(ff_terms, terms, feed_send, sizes)
    grad_gate, grad_up, grad_down, *attn_terms = [g.astype(f32) for g in weight_grads]
    output = both_cores((hidden + residual_mult * (feed_own + feed_in)).astype(bf16))
    return (output, input_grad, gain_terms[0], *attn_terms, gain_terms[1], grad_gate, grad_up, grad_down)


def solution(mesh):
    split = tuple(mesh.shape[a] for a in (FSDP, CONTEXT, TENSOR)) == (4, 4, 2)
    return jax.shard_map(
        on_device_split if split else on_device,
        mesh=mesh,
        in_specs=(
            P(FSDP, CONTEXT, None),
            P(FSDP, CONTEXT, None),
            P(FSDP, None),
            P((FSDP, CONTEXT)),
            P((FSDP, CONTEXT), TENSOR),
            P((FSDP, CONTEXT), TENSOR),
            P((FSDP, CONTEXT), TENSOR),
            P((FSDP, CONTEXT), TENSOR),
            P((FSDP, CONTEXT)),
            P((FSDP, CONTEXT), TENSOR),
            P((FSDP, CONTEXT), TENSOR),
            P((FSDP, CONTEXT), TENSOR),
        ),
        out_specs=(
            P(FSDP, CONTEXT, None),
            P(FSDP, CONTEXT, None),
            P((FSDP, CONTEXT)),
            P((FSDP, CONTEXT), TENSOR),
            P((FSDP, CONTEXT), TENSOR),
            P((FSDP, CONTEXT), TENSOR),
            P((FSDP, CONTEXT), TENSOR),
            P((FSDP, CONTEXT)),
            P((FSDP, CONTEXT), TENSOR),
            P((FSDP, CONTEXT), TENSOR),
            P((FSDP, CONTEXT), TENSOR),
        ),
        check_vma=False,
    )
```

```python
import jax
import jax.numpy as jnp
from jax import lax
from jax.experimental import pallas as pl
from jax.experimental.pallas import tpu as pltpu
from jax.sharding import PartitionSpec as P

HEAD = 64
FSDP, CONTEXT, TENSOR = "fsdp", "context", "tensor"


norm_eps = 1e-05
attention_mult = 0.015625
residual_mult = 0.22
rope_base = 10000000.0


def slot_layout(seq_lengths, total_rows):
    seq_ends = jnp.cumsum(seq_lengths)
    starts = seq_ends - seq_lengths
    slot_ids = jnp.arange(total_rows, dtype=jnp.int32)
    before = (slot_ids[:, None] >= seq_ends[None, :]).astype(jnp.int32)
    segment = jnp.sum(before, axis=1)
    seq_count = seq_lengths.shape[0]
    valid_rows = segment < seq_count
    inside = (slot_ids[:, None] >= starts[None, :]) & (slot_ids[:, None] < seq_ends[None, :])
    position = jnp.sum(jnp.where(inside, slot_ids[:, None] - starts[None, :], 0), axis=1)
    segment = jnp.where(valid_rows, segment, seq_count + slot_ids)
    return (segment, position, valid_rows)


def rope_tables(position, width):
    half_width = width // 2
    frequency = rope_base ** (-jnp.arange(half_width, dtype=jnp.float32) * 2.0 / width)
    angles = position.astype(jnp.float32)[:, None] * frequency[None, :]
    angles = jnp.concatenate([angles, angles], axis=1)
    return (jnp.cos(angles), jnp.sin(angles))


def turn_half(vectors):
    half_width = vectors.shape[-1] // 2
    return jnp.concatenate([-vectors[..., half_width:], vectors[..., :half_width]], axis=-1)


def rotate(vectors, cos_table, sine_table):
    return vectors * cos_table[:, None, :] + turn_half(vectors) * sine_table[:, None, :]


def rotate_back(grads, cos_table, sine_table):
    return grads * cos_table[:, None, :] - turn_half(grads * sine_table[:, None, :])


def norm_back(normed_grad, unit, gain, inverse):
    scaled = normed_grad * gain
    return inverse * (scaled - unit * jnp.mean(scaled * unit, axis=-1, keepdims=True))


def dot_first(left, right):
    return lax.dot_general(left, right, (((0,), (0,)), ((), ())), preferred_element_type=jnp.float32)


def dot_last(left, right):
    return lax.dot_general(left, right, (((1,), (1,)), ((), ())), preferred_element_type=jnp.float32)


def attention_shards(attention_gain, query_weight, key_weight, value_weight, output_weight):
    return (
        lax.all_gather(
            attention_gain.astype(jnp.bfloat16), (FSDP, CONTEXT), axis=0, tiled=True
        ),
        lax.all_gather(query_weight.astype(jnp.bfloat16), (FSDP, CONTEXT), axis=0, tiled=True),
        lax.all_gather(key_weight.astype(jnp.bfloat16), (FSDP, CONTEXT), axis=0, tiled=True),
        lax.all_gather(value_weight.astype(jnp.bfloat16), (FSDP, CONTEXT), axis=0, tiled=True),
        lax.all_gather(output_weight.astype(jnp.bfloat16), (FSDP, CONTEXT), axis=0, tiled=True),
    )


def feed_shards(feed_gain, gate_weight, up_weight, down_weight):
    return (
        lax.all_gather(feed_gain.astype(jnp.bfloat16), (FSDP, CONTEXT), axis=0, tiled=True),
        lax.all_gather(gate_weight.astype(jnp.bfloat16), (FSDP, CONTEXT), axis=0, tiled=True),
        lax.all_gather(up_weight.astype(jnp.bfloat16), (FSDP, CONTEXT), axis=0, tiled=True),
        lax.all_gather(down_weight.astype(jnp.bfloat16), (FSDP, CONTEXT), axis=0, tiled=True),
    )


def on_device(
    tokens,
    out_grad,
    lengths,
    attention_gain,
    query_weight,
    key_weight,
    value_weight,
    output_weight,
    feed_gain,
    gate_weight,
    up_weight,
    down_weight,
):
    local_rows = tokens.shape[1]
    group_rows = local_rows * lax.axis_size(CONTEXT)
    first_row = lax.axis_index(CONTEXT) * local_rows
    segment, position, valid_rows = slot_layout(lengths[0], group_rows)
    local_segment = lax.dynamic_slice_in_dim(segment, first_row, local_rows)
    local_position = lax.dynamic_slice_in_dim(position, first_row, local_rows)
    local_valid = lax.dynamic_slice_in_dim(valid_rows, first_row, local_rows)
    slot_ids = jnp.arange(group_rows, dtype=jnp.int32)
    local_slots = first_row + jnp.arange(local_rows, dtype=jnp.int32)
    allowed = (local_segment[:, None] == segment[None, :]) & (
        local_slots[:, None] >= slot_ids[None, :]
    )
    inputs = tokens[0].astype(jnp.float32)
    attn_set = attention_shards(
        attention_gain, query_weight, key_weight, value_weight, output_weight
    )
    gain_one = attn_set[0].astype(jnp.float32)
    inverse_one = lax.rsqrt(jnp.mean(inputs * inputs, axis=-1, keepdims=True) + norm_eps)
    unit_one = inputs * inverse_one
    normed_one = (unit_one * gain_one).astype(jnp.bfloat16)
    queries = jnp.dot(normed_one, attn_set[1], preferred_element_type=jnp.float32)
    keys_lin = jnp.dot(normed_one, attn_set[2], preferred_element_type=jnp.float32)
    values_low = jnp.dot(normed_one, attn_set[3], preferred_element_type=jnp.float32).astype(
        jnp.bfloat16
    )
    heads_local = queries.shape[1] // HEAD
    kv_local = keys_lin.shape[1] // HEAD
    per_group = heads_local // kv_local
    cos_table, sine_table = rope_tables(local_position, HEAD)
    queries_rot = rotate(
        queries.reshape(local_rows, heads_local, HEAD), cos_table, sine_table
    ).astype(jnp.bfloat16)
    keys_rot = rotate(keys_lin.reshape(local_rows, kv_local, HEAD), cos_table, sine_table).astype(
        jnp.bfloat16
    )
    keys_all, values_all = (
        lax.all_gather(
            keys_rot.reshape(local_rows, kv_local * HEAD), CONTEXT, axis=0, tiled=True
        ),
        lax.all_gather(values_low, CONTEXT, axis=0, tiled=True),
    )
    query_heads = queries_rot.reshape(local_rows, kv_local, per_group, HEAD).transpose(1, 0, 2, 3)
    key_heads = keys_all.reshape(group_rows, kv_local, HEAD).transpose(1, 0, 2)
    value_heads = values_all.reshape(group_rows, kv_local, HEAD).transpose(1, 0, 2)

    def head_scores(query_head, key_head):
        raw_scores = jnp.einsum(
            "tgd,sd->gts", query_head, key_head, preferred_element_type=jnp.float32
        )
        return jnp.where(allowed[None], raw_scores * attention_mult, -1e30)

    def head_forward(pieces):
        query_head, key_head, value_head = pieces
        scores = head_scores(query_head, key_head)
        highest = jnp.max(scores, axis=-1, keepdims=True)
        weight = jnp.exp(scores - highest)
        row_totals = jnp.sum(weight, axis=-1, keepdims=True)
        probabilities = (weight / row_totals).astype(jnp.bfloat16)
        mixed = jnp.einsum(
            "gts,sd->tgd", probabilities, value_head, preferred_element_type=jnp.float32
        )
        return (mixed, (highest + jnp.log(row_totals))[..., 0])

    mixed_heads, log_totals = lax.map(head_forward, (query_heads, key_heads, value_heads))
    attended = (
        mixed_heads.transpose(1, 0, 2, 3)
        .reshape(local_rows, heads_local * HEAD)
        .astype(jnp.bfloat16)
    )
    attn_part = dot_last(attended, attn_set[4])
    attn_out = lax.psum(attn_part.astype(jnp.bfloat16), TENSOR).astype(jnp.float32)
    hidden_state = inputs + residual_mult * attn_out
    feed_set = feed_shards(feed_gain, gate_weight, up_weight, down_weight)
    gain_two = feed_set[0].astype(jnp.float32)
    inverse_two = lax.rsqrt(
        jnp.mean(hidden_state * hidden_state, axis=-1, keepdims=True) + norm_eps
    )
    unit_two = hidden_state * inverse_two
    normed_two = (unit_two * gain_two).astype(jnp.bfloat16)
    gate_out = jnp.dot(normed_two, feed_set[1], preferred_element_type=jnp.float32)
    up_out = jnp.dot(normed_two, feed_set[2], preferred_element_type=jnp.float32)
    inner_act = (jax.nn.silu(gate_out) * up_out).astype(jnp.bfloat16)
    feed_part = dot_last(inner_act, feed_set[3])
    feed_out = lax.psum(feed_part.astype(jnp.bfloat16), TENSOR).astype(jnp.float32)
    output = hidden_state + residual_mult * feed_out
    cotangent = out_grad[0].astype(jnp.float32) * local_valid[:, None].astype(jnp.float32)
    feed_back = feed_shards(feed_gain, gate_weight, up_weight, down_weight)
    feed_grad = (residual_mult * cotangent).astype(jnp.bfloat16)
    down_term = dot_first(feed_grad, inner_act)
    inner_grad = jnp.dot(feed_grad, feed_back[3], preferred_element_type=jnp.float32)
    sigmoid_gate = jax.nn.sigmoid(gate_out)
    gate_grad = (
        inner_grad * up_out * sigmoid_gate * (1.0 + gate_out * (1.0 - sigmoid_gate))
    ).astype(jnp.bfloat16)
    up_grad = (inner_grad * jax.nn.silu(gate_out)).astype(jnp.bfloat16)
    gate_term = dot_first(normed_two, gate_grad)
    up_term = dot_first(normed_two, up_grad)
    normed_part_two = dot_last(gate_grad, feed_back[1])
    normed_part_two = normed_part_two + dot_last(up_grad, feed_back[2])
    normed_grad_two = lax.psum(normed_part_two.astype(jnp.bfloat16), TENSOR).astype(jnp.float32)
    feed_gain_term = jnp.sum(normed_grad_two * unit_two, axis=0)
    hidden_grad = cotangent + norm_back(normed_grad_two, unit_two, gain_two, inverse_two)
    feed_sums = (
        lax.psum_scatter(feed_gain_term, (FSDP, CONTEXT), scatter_dimension=0, tiled=True),
        lax.psum_scatter(gate_term, (FSDP, CONTEXT), scatter_dimension=0, tiled=True),
        lax.psum_scatter(up_term, (FSDP, CONTEXT), scatter_dimension=0, tiled=True),
        lax.psum_scatter(down_term, (FSDP, CONTEXT), scatter_dimension=0, tiled=True),
    )
    attn_back = attention_shards(
        attention_gain, query_weight, key_weight, value_weight, output_weight
    )
    attn_grad = (residual_mult * hidden_grad).astype(jnp.bfloat16)
    out_term = dot_first(attn_grad, attended)
    mixed_grad = jnp.dot(attn_grad, attn_back[4], preferred_element_type=jnp.float32).astype(
        jnp.bfloat16
    )
    mixed_grad_heads = mixed_grad.reshape(local_rows, kv_local, per_group, HEAD).transpose(
        1, 0, 2, 3
    )

    def head_backward(pieces):
        query_head, key_head, value_head, grad_head, log_head = pieces
        scores = head_scores(query_head, key_head)
        probabilities = jnp.exp(scores - log_head[..., None])
        prob_low = probabilities.astype(jnp.bfloat16)
        prob_grad = jnp.einsum(
            "tgd,sd->gts", grad_head, value_head, preferred_element_type=jnp.float32
        )
        row_dot = jnp.sum(probabilities * prob_grad, axis=-1, keepdims=True)
        score_grad = (attention_mult * probabilities * (prob_grad - row_dot)).astype(jnp.bfloat16)
        query_grad = jnp.einsum(
            "gts,sd->tgd", score_grad, key_head, preferred_element_type=jnp.float32
        )
        key_grad = jnp.einsum(
            "gts,tgd->sd", score_grad, query_head, preferred_element_type=jnp.float32
        )
        value_grad = jnp.einsum(
            "gts,tgd->sd", prob_low, grad_head, preferred_element_type=jnp.float32
        )
        return (query_grad, key_grad, value_grad)

    query_grads, key_grads, value_grads = lax.map(
        head_backward, (query_heads, key_heads, value_heads, mixed_grad_heads, log_totals)
    )
    key_grads = key_grads.transpose(1, 0, 2).reshape(group_rows, kv_local * HEAD)
    value_grads = value_grads.transpose(1, 0, 2).reshape(group_rows, kv_local * HEAD)
    local_key_grad, local_value_grad = (
        lax.psum_scatter(
            key_grads.astype(jnp.bfloat16), CONTEXT, scatter_dimension=0, tiled=True
        ).astype(jnp.float32),
        lax.psum_scatter(
            value_grads.astype(jnp.bfloat16), CONTEXT, scatter_dimension=0, tiled=True
        ).astype(jnp.float32),
    )
    query_grad_rot = query_grads.transpose(1, 0, 2, 3).reshape(local_rows, heads_local, HEAD)
    query_grad_low = (
        rotate_back(query_grad_rot, cos_table, sine_table)
        .reshape(local_rows, heads_local * HEAD)
        .astype(jnp.bfloat16)
    )
    key_grad_low = (
        rotate_back(local_key_grad.reshape(local_rows, kv_local, HEAD), cos_table, sine_table)
        .reshape(local_rows, kv_local * HEAD)
        .astype(jnp.bfloat16)
    )
    value_grad_low = local_value_grad.astype(jnp.bfloat16)
    query_term = dot_first(normed_one, query_grad_low)
    key_term = dot_first(normed_one, key_grad_low)
    value_term = dot_first(normed_one, value_grad_low)
    normed_part_one = dot_last(query_grad_low, attn_back[1])
    normed_part_one = normed_part_one + dot_last(key_grad_low, attn_back[2])
    normed_part_one = normed_part_one + dot_last(value_grad_low, attn_back[3])
    normed_grad_one = lax.psum(normed_part_one.astype(jnp.bfloat16), TENSOR).astype(jnp.float32)
    attn_gain_term = jnp.sum(normed_grad_one * unit_one, axis=0)
    input_grad = hidden_grad + norm_back(normed_grad_one, unit_one, gain_one, inverse_one)
    attn_sums = (
        lax.psum_scatter(attn_gain_term, (FSDP, CONTEXT), scatter_dimension=0, tiled=True),
        lax.psum_scatter(query_term, (FSDP, CONTEXT), scatter_dimension=0, tiled=True),
        lax.psum_scatter(key_term, (FSDP, CONTEXT), scatter_dimension=0, tiled=True),
        lax.psum_scatter(value_term, (FSDP, CONTEXT), scatter_dimension=0, tiled=True),
        lax.psum_scatter(out_term, (FSDP, CONTEXT), scatter_dimension=0, tiled=True),
    )
    return (
        output.astype(jnp.bfloat16)[None],
        input_grad.astype(jnp.bfloat16)[None],
        attn_sums[0],
        attn_sums[1],
        attn_sums[2],
        attn_sums[3],
        attn_sums[4],
        feed_sums[0],
        feed_sums[1],
        feed_sums[2],
        feed_sums[3],
    )


def flip(i, k):
    if k == 0:
        return i
    if k == 1:
        return i + 1 - 2 * lax.rem(i, 2)
    if k == 2:
        return lax.rem(i + 2, 4)
    return 3 - i


class Copies:
    def __init__(self, send, receive):
        self.send, self.receive = send, receive
        self.count, self.started = 0, []

    def index(self):
        self.count += 1
        return self.count - 1

    def make(self, i, source, target, device):
        return pltpu.make_async_remote_copy(
            src_ref=source,
            dst_ref=target,
            send_sem=self.send.at[i],
            recv_sem=self.receive.at[i],
            device_id=device,
            device_id_type=pl.DeviceIdType.MESH,
        )

    def start(self, source, target, device, i=None):
        i = self.index() if i is None else i
        copy = self.make(i, source, target, device)
        copy.start()
        self.started.append(copy)
        return copy


def greet(partners):
    barrier = pltpu.get_barrier_semaphore()
    for device in partners:
        pl.semaphore_signal(barrier, inc=1, device_id=device, device_id_type=pl.DeviceIdType.MESH)
    pl.semaphore_wait(barrier, len(partners))


def dot_tile(left, right, left_axis, right_axis):
    return lax.dot_general(left, right, (((left_axis,), (right_axis,)), ((), ())), preferred_element_type=jnp.float32)


TILE = 256


def turn_lanes(x, low):
    return jnp.where(low, pltpu.roll(x, x.shape[1] - HEAD // 2, 1), pltpu.roll(x, HEAD // 2, 1))


def low_lanes(shape, width):
    return lax.rem(lax.broadcasted_iota(jnp.int32, shape, 1), 2 * width) < width


def split_pair(x):
    low = low_lanes(x.shape, HEAD)
    a, b = jnp.where(low, x, 0.0), jnp.where(low, 0.0, x)
    return a, pltpu.roll(a, HEAD, 1), pltpu.roll(b, HEAD, 1), b


def attention_kernel(
    wa, wf, xt, gain, fgx, cos, sin, seg_col, seg_row,
    wa_out, wf_all, normed_out, q, kv, logs, attended, hidden_out, normed_two, fg_all, gains,
    wa_all, x_all, gain_all, normed, pairs, sums, mine, cross, crossed, totals, landed, send, receive, local,
):
    f32, bf16 = jnp.float32, jnp.bfloat16
    z, c, t = (lax.axis_index(a) for a in (FSDP, CONTEXT, TENSOR))
    peers = [(flip(z, i), flip(c, j), t) for i in range(4) for j in range(4) if i or j]
    core = (z, c, 1 - t)
    greet(peers + [core])
    net = Copies(send, receive)
    middle = (z == 1) | (z == 2)
    nt, part, width = xt.shape
    rows = nt * part
    q_cols = q.shape[1]
    qkv_cols = q_cols + 2 * HEAD
    ends = []
    own = []
    for i, (source, target) in enumerate(
        (
            (wa.at[c], wa_all.at[z, c]),
            (xt, x_all.at[c]),
            (wf.at[z], wf_all.at[z, c]),
            (gain, gain_all.at[z, c]),
            (fgx, fg_all.at[0, 0]),
        )
    ):
        own.append(pltpu.make_async_copy(source, target, local.at[i]))
        own[-1].start()

    def spread(source, slot, forward):
        one = net.start(source, slot(1), (flip(z, 1), c, t))
        two = net.start(source, slot(2), (flip(z, 2), c, t))
        three = net.index()
        direct = net.make(three, source, slot(3), (3 - z, c, t))
        pl.when(middle)(direct.start)
        passed = pltpu.make_async_remote_copy(
            src_ref=forward[0],
            dst_ref=forward[1],
            send_sem=send.at[net.index()],
            recv_sem=receive.at[three],
            device_id=(flip(z, 1), c, t),
            device_id_type=pl.DeviceIdType.MESH,
        )
        return one, two, direct, passed

    attn_in = [net.start(wa.at[flip(c, k)], wa_all.at[z, c], (z, flip(c, k), t)) for k in (1, 2, 3)]
    tokens_in = [net.start(xt.at[t], x_all.at[c, t], (z, flip(c, k), t)) for k in (1, 2, 3)]
    ff_in = {1: net.start(wf.at[flip(z, 1)], wf_all.at[z, c], (flip(z, 1), c, t))}
    for device in peers:
        ends.append(net.start(gain, gain_all.at[z, c], device))
    own[2].wait()
    ff_out = {0: [net.start(wf_all.at[z, c], wf_all.at[z, c], (z, flip(c, k), t)) for k in (1, 2)]}
    weights = []
    for j in range(4):
        if j:
            attn_in[j - 1].wait_recv()
        else:
            own[0].wait()
        piece = wa_all.at[z, flip(c, j)]
        passed_piece = wa_all.at[flip(z, 2), flip(c, j)]
        weights.append(spread(piece, lambda k, piece=piece: piece, (passed_piece, passed_piece)))
    for k in (3, 2):
        ff_in[k] = net.start(wf.at[flip(z, k)], wf_all.at[z, c], (flip(z, k), c, t))
    feed = spread(fgx, lambda k: fg_all.at[k, 0], (fg_all.at[2, 0], fg_all.at[3, 0]))
    swaps = [net.start(fgx, fg_all.at[0, 1], core)]
    token_swaps = []
    for k, copy in zip((1, 2, 3), tokens_in):
        copy.wait_recv()
        piece = x_all.at[flip(c, k), t]
        token_swaps.append(net.start(piece, piece, core))
    halves = []

    def corner(k):
        zs = flip(z, k)
        one, two = ff_out[k]
        two.wait_recv()
        piece = wf_all.at[zs, flip(c, 2), pl.ds(0, 64)]
        halves.append(net.start(piece, piece, (z, flip(c, 1), t)))
        one.wait_recv()
        piece = wf_all.at[zs, flip(c, 1), pl.ds(64, 64)]
        halves.append(net.start(piece, piece, (z, flip(c, 2), t)))

    def onward(k):
        ff_in[k].wait_recv()
        piece = wf_all.at[flip(z, k), c]
        ff_out[k] = [net.start(piece, piece, (z, flip(c, j), t)) for j in (1, 2)]

    own[1].wait()
    own[3].wait()
    for copy in token_swaps + ends:
        copy.wait_recv()
    for i in range(2):
        gains[i : i + 1, :] = jnp.concatenate(
            [gain_all[a, b, i : i + 1, :].astype(f32) for a in range(4) for b in range(4)], axis=1
        )

    def norm_rows(i, carry):
        x = x_all[i].reshape(rows, width).astype(f32)
        inverse = lax.rsqrt(jnp.mean(x * x, axis=-1, keepdims=True) + norm_eps)
        normed[i] = (x * inverse * gains[0:1, :]).astype(bf16)
        return carry

    lax.fori_loop(0, 4, norm_rows, 0)
    save = [pltpu.make_async_copy(normed, normed_out, local.at[5])]
    save[0].start()
    onward(1)
    corner(0)
    for one, two, direct, passed in weights:
        two.wait_recv()
        pl.when(middle)(passed.start)
    for one, two, direct, passed in weights:
        one.wait_recv()
        direct.wait_recv()
    save.append(pltpu.make_async_copy(wa_all, wa_out, local.at[6]))
    save[1].start()

    def project(i, carry):
        here = pl.ds(pl.multiple_of(i * rows, rows), rows)
        w = wa_all[...].reshape(width, wa_all.shape[3])
        qkv = dot_tile(normed[i], w[:, :qkv_cols], 1, 0)
        cos_b, sin_b = cos[here, :], sin[here, :]
        quarter = low_lanes(cos_b.shape, HEAD // 2)
        half = low_lanes(cos_b.shape, HEAD)
        for p in range(q_cols // 128):
            block = qkv[:, p * 128 : (p + 1) * 128]
            q[here, p * 128 : (p + 1) * 128] = (block * cos_b + turn_lanes(block, quarter) * sin_b).astype(bf16)
        block = qkv[:, q_cols:]
        block = jnp.where(half, block * cos_b + turn_lanes(block, quarter) * sin_b, block)
        kv[here, :] = block.astype(bf16)
        for j, piece in enumerate(split_pair(block)):
            pairs[j, here, :] = piece.astype(bf16)
        return carry

    lax.fori_loop(0, 4, project, 0)
    corner(1)

    def attend(i):
        count = (i + 1) * rows
        here = pl.ds(i * rows, rows)
        keep = (seg_col[here, :] == seg_row[:, :count]) & (
            lax.broadcasted_iota(jnp.int32, (rows, count), 0) + i * rows
            >= lax.broadcasted_iota(jnp.int32, (rows, count), 1)
        )
        lane = lax.broadcasted_iota(jnp.int32, (rows, 128), 1)
        log_sums = jnp.zeros((rows, 128), f32)
        for p in range(q_cols // 128):
            out = jnp.zeros((rows, 128), f32)
            for e in range(2):
                scores = dot_tile(q[here, p * 128 : (p + 1) * 128], pairs[e, :count, :], 1, 1)
                scores = jnp.where(keep, scores * attention_mult, -1e30)
                highest = jnp.max(scores, axis=-1, keepdims=True)
                weight = jnp.exp(scores - highest)
                total = jnp.sum(weight, axis=-1, keepdims=True)
                out = out + dot_tile((weight / total).astype(bf16), pairs[2 + e, :count, :], 1, 0)
                log_sums = jnp.where(lane == 2 * p + e, highest + jnp.log(total), log_sums)
            attended[here, p * 128 : (p + 1) * 128] = out.astype(bf16)
        logs[here, :] = log_sums

    attend(0)
    attend(1)
    onward(3)
    attend(2)
    last = pl.ds(3 * rows, rows)
    both = (pairs[2, last, :] + pairs[3, last, :]).astype(bf16)
    for p in range(q_cols // 128):
        attended[last, p * 128 : (p + 1) * 128] = both
    corner(3)

    crosses, outs = {}, {}
    for k in (3, 1, 2, 0):
        mine_rows = pl.ds(pl.multiple_of(flip(c, k) * rows, rows), rows)

        def out_tile(n, carry, mine_rows=mine_rows):
            here = pl.ds(pl.multiple_of(n * 128, 128), 128)
            w = wa_all[lax.div(n, 4), lax.rem(n, 4), :, qkv_cols:]
            sums[:, here] = dot_tile(attended[mine_rows, :], w, 1, 1)
            return carry

        lax.fori_loop(0, width // 128, out_tile, 0)
        mine[k] = sums[pl.ds(pl.multiple_of(t * part, part), part), :]
        cross[k] = sums[pl.ds(pl.multiple_of((1 - t) * part, part), part), :].astype(bf16)
        crosses[k] = net.start(cross.at[k], crossed.at[k], core)
    for k in (3, 1, 2):
        crosses[k].wait_recv()
        totals[k - 1] = (mine[k] + crossed[k].astype(f32)).astype(bf16)
        outs[k] = net.start(totals.at[k - 1], landed.at[k - 1], (z, flip(c, k), t))
    onward(2)
    one, two, direct, passed = feed
    two.wait_recv()
    pl.when(middle)(passed.start)
    swaps.append(net.start(fg_all.at[2, 0], fg_all.at[2, 1], core))
    one.wait_recv()
    swaps.append(net.start(fg_all.at[1, 0], fg_all.at[1, 1], core))
    crosses[0].wait_recv()
    total = mine[0] + crossed[0].astype(f32)
    for k in (1, 2, 3):
        outs[k].wait_recv()
        total = total + landed[k - 1].astype(f32)
    hidden = xt[t].astype(f32) + residual_mult * total
    hidden_out[...] = hidden
    inverse = lax.rsqrt(jnp.mean(hidden * hidden, axis=-1, keepdims=True) + norm_eps)
    normed_two[...] = (hidden * inverse * gains[1:2, :]).astype(bf16)
    direct.wait_recv()
    swaps.append(net.start(fg_all.at[3, 0], fg_all.at[3, 1], core))
    corner(2)
    for copy in halves + swaps:
        copy.wait_recv()
    for _, _, direct, passed in weights + [feed]:
        pl.when(middle)(direct.wait_send)
        pl.when(middle)(passed.wait_send)
    for copy in net.started:
        copy.wait_send()
    own[4].wait()
    for copy in save:
        copy.wait()


def attention_forward(wa, wf, xt, gain, fgx, cos, sin, seg_col, seg_row):
    bf16, f32 = jnp.bfloat16, jnp.float32
    nt, part, width = xt.shape
    rows = nt * part
    total = 4 * rows
    wa_cols = wa.shape[2]
    q_cols = (wa_cols - 2 * HEAD) // 2
    filled = seg_col.shape[0]
    copies = 96
    vmem, anywhere = pl.BlockSpec(memory_space=pltpu.VMEM), pl.BlockSpec(memory_space=pl.ANY)
    outs = (
        ((4, 4) + wa.shape[1:], bf16, anywhere),
        ((4, 4) + wf.shape[1:], bf16, anywhere),
        ((4, rows, width), bf16, anywhere),
        ((total, q_cols), bf16, vmem),
        ((total, 2 * HEAD), bf16, vmem),
        ((filled, 128), f32, vmem),
        ((total, q_cols), bf16, vmem),
        ((part, width), f32, vmem),
        ((part, width), bf16, vmem),
        ((4, nt, part, width), bf16, anywhere),
        ((2, width), f32, vmem),
    )
    return pl.pallas_call(
        attention_kernel,
        out_shape=[jax.ShapeDtypeStruct(shape, dtype) for shape, dtype, _ in outs],
        in_specs=[vmem] * 9,
        out_specs=[spec for _, _, spec in outs],
        scratch_shapes=[
            pltpu.VMEM((4, 4) + wa.shape[1:], bf16),
            pltpu.VMEM((4, nt, part, width), bf16),
            pltpu.VMEM((4, 4) + gain.shape, bf16),
            pltpu.VMEM((4, rows, width), bf16),
            pltpu.VMEM((4, total, 2 * HEAD), bf16),
            pltpu.VMEM((rows, width), f32),
            pltpu.VMEM((4, part, width), f32),
            pltpu.VMEM((4, part, width), bf16),
            pltpu.VMEM((4, part, width), bf16),
            pltpu.VMEM((3, part, width), bf16),
            pltpu.VMEM((3, part, width), bf16),
            pltpu.SemaphoreType.DMA((copies,)),
            pltpu.SemaphoreType.DMA((copies,)),
            pltpu.SemaphoreType.DMA((7,)),
        ],
        compiler_params=pltpu.CompilerParams(collective_id=1, has_side_effects=True, vmem_limit_bytes=60 * 2**20),
    )(wa, wf, xt, gain, fgx, cos, sin, seg_col, seg_row)


def feed_kernel(
    x, fg, w, back, feed_own, feed_send, terms,
    xs, wv, gate_g, up_g, inner, mine, cross, crossed, totals, landed, send, receive, local,
):
    f32, bf16 = jnp.float32, jnp.bfloat16
    z, c, t = (lax.axis_index(a) for a in (FSDP, CONTEXT, TENSOR))
    core = (z, c, 1 - t)
    greet([(flip(z, k), c, t) for k in (1, 2, 3)] + [core])
    net = Copies(send, receive)
    part, width = x.shape
    hidden = wv.shape[1] // 3
    load = pltpu.make_async_copy(w, wv, local.at[0])
    load.start()
    middle = (z == 1) | (z == 2)
    swaps = {0: net.start(x, xs.at[0, 1], core)}
    arrive = {2: net.start(x, xs.at[2, 0], (flip(z, 2), c, t))}
    three = net.index()
    direct = net.make(three, x, xs.at[3, 0], (3 - z, c, t))
    pl.when(middle)(direct.start)
    arrive[3] = direct
    arrive[1] = net.start(x, xs.at[1, 0], (flip(z, 1), c, t))
    passed = pltpu.make_async_remote_copy(
        src_ref=xs.at[2, 0],
        dst_ref=xs.at[3, 0],
        send_sem=send.at[net.index()],
        recv_sem=receive.at[three],
        device_id=(flip(z, 1), c, t),
        device_id_type=pl.DeviceIdType.MESH,
    )
    xs[0, 0] = x[...]
    load.wait()

    def first(k):
        swaps[k].wait_recv()
        rows = xs[k].reshape(2 * part, width)
        grads = fg[k]

        def step(n, carry):
            at = pl.multiple_of(n * TILE, TILE)
            g = dot_tile(rows, wv[:, pl.ds(at, TILE)], 1, 0)
            u = dot_tile(rows, wv[:, pl.ds(hidden + at, TILE)], 1, 0)
            d = dot_tile(grads, wv[:, pl.ds(2 * hidden + at, TILE)], 1, 0)
            sig = jax.nn.sigmoid(g)
            here = pl.ds(at, TILE)
            inner[k, :, here] = (g * sig * u).astype(bf16)
            gate_g[k, :, here] = (d * u * sig * (1.0 + g * (1.0 - sig))).astype(bf16)
            up_g[k, :, here] = (d * g * sig).astype(bf16)
            return carry

        lax.fori_loop(0, hidden // TILE, step, 0)

    crosses = {}

    def second(k):
        def step(n, carry):
            here = pl.ds(pl.multiple_of(n * TILE, TILE), TILE)
            b = dot_tile(gate_g[k], wv[here, 0:hidden], 1, 1) + dot_tile(up_g[k], wv[here, hidden : 2 * hidden], 1, 1)
            f = dot_tile(inner[k], wv[here, 2 * hidden :], 1, 1)
            mine[k, 0, :, here] = b[:part]
            mine[k, 1, :, here] = f[:part]
            cross[k, 0, :, here] = b[part:].astype(bf16)
            cross[k, 1, :, here] = f[part:].astype(bf16)
            return carry

        lax.fori_loop(0, width // TILE, step, 0)
        crosses[k] = net.start(cross.at[k], crossed.at[k], core)

    sums = {}

    def finish(k):
        crosses[k].wait_recv()
        if k:
            totals[k - 1] = (mine[k, 0] + crossed[k, 0].astype(f32)).astype(bf16)
            sums[k] = net.start(totals.at[k - 1], landed.at[k - 1], (flip(z, k), c, t))
            feed_send[k - 1] = (mine[k, 1] + crossed[k, 1].astype(f32)).astype(bf16)
        else:
            back[...] = mine[0, 0] + crossed[0, 0].astype(f32)
            feed_own[...] = mine[0, 1] + crossed[0, 1].astype(f32)

    def fetch(k):
        arrive[k].wait_recv()
        if k == 2:
            pl.when(middle)(passed.start)
        swaps[k] = net.start(xs.at[k, 0], xs.at[k, 1], core)

    order = (0, 2, 3, 1)
    for i, k in enumerate(order):
        first(k)
        if i:
            finish(order[i - 1])
        if i < 3:
            fetch(order[i + 1])
        second(k)

    rows = xs.shape[0] * 2 * part

    def term(source, grads, begin):
        def step(m, carry):
            here = pl.ds(pl.multiple_of(m * TILE, TILE), TILE)
            left = source[:, :, here].reshape(rows, TILE)
            value = dot_tile(left, grads[...].reshape(rows, hidden), 0, 0)
            wv[here, begin : begin + hidden] = value.astype(bf16)
            return carry

        lax.fori_loop(0, width // TILE, step, 0)

    flat = xs.reshape(xs.shape[0], 2 * part, width)
    term(flat, gate_g, 0)
    finish(order[3])
    term(flat, up_g, hidden)
    term(fg, inner, 2 * hidden)
    store = pltpu.make_async_copy(wv, terms, local.at[1])
    store.start()
    for k in (1, 2, 3):
        sums[k].wait_recv()
    back[...] = back[...] + landed[0].astype(f32) + landed[1].astype(f32) + landed[2].astype(f32)
    pl.when(middle)(direct.wait_send)
    pl.when(middle)(passed.wait_send)
    for copy in net.started:
        copy.wait_send()
    store.wait()


def feed_forward(x, fg, w):
    bf16, f32 = jnp.bfloat16, jnp.float32
    part, width = x.shape
    cols = w.shape[1]
    hidden = cols // 3
    blocks = fg.shape[0]
    copies = 20
    vmem, anywhere = pl.BlockSpec(memory_space=pltpu.VMEM), pl.BlockSpec(memory_space=pl.ANY)
    return pl.pallas_call(
        feed_kernel,
        out_shape=[
            jax.ShapeDtypeStruct((part, width), f32),
            jax.ShapeDtypeStruct((part, width), f32),
            jax.ShapeDtypeStruct((blocks - 1, part, width), bf16),
            jax.ShapeDtypeStruct(w.shape, bf16),
        ],
        in_specs=[vmem, vmem, anywhere],
        out_specs=[vmem, vmem, vmem, anywhere],
        scratch_shapes=[
            pltpu.VMEM((blocks, 2, part, width), bf16),
            pltpu.VMEM(w.shape, bf16),
            pltpu.VMEM((blocks, 2 * part, hidden), bf16),
            pltpu.VMEM((blocks, 2 * part, hidden), bf16),
            pltpu.VMEM((blocks, 2 * part, hidden), bf16),
            pltpu.VMEM((blocks, 2, part, width), f32),
            pltpu.VMEM((blocks, 2, part, width), bf16),
            pltpu.VMEM((blocks, 2, part, width), bf16),
            pltpu.VMEM((blocks - 1, part, width), bf16),
            pltpu.VMEM((blocks - 1, part, width), bf16),
            pltpu.SemaphoreType.DMA((copies,)),
            pltpu.SemaphoreType.DMA((copies,)),
            pltpu.SemaphoreType.DMA((2,)),
        ],
        compiler_params=pltpu.CompilerParams(collective_id=3, has_side_effects=True, vmem_limit_bytes=62 * 2**20),
    )(x, fg, w)


def swap(x, axis, k):
    return lax.ppermute(x, axis, [(i, i ^ k) for i in range(lax.axis_size(axis))])


def put(buffer, block, *index):
    lead = len(index)
    block = block.reshape((1,) * lead + buffer.shape[lead:])
    zero = jnp.int32(0)
    start = tuple(jnp.asarray(i, jnp.int32) for i in index) + (zero,) * (buffer.ndim - lead)
    return lax.dynamic_update_slice(buffer, block, start)


def cut(x, index, size, axis):
    return lax.dynamic_slice_in_dim(x, index * size, size, axis)


def backward_kernel(
    ff, fs, al, wa_in, normed_in, q, kv, logs, attended, cos, sin, seg_col, seg_row,
    feed_in, back_own, back_in, ff_out, at_out,
    terms, corner_x, corner_y, side_x, side_y, at_terms, at_in, at_total, wa, normed, ag, pairs, mixed, acc, dqkv,
    sums, mine, cross, crossed, totals, send, receive, local,
):
    f32, bf16 = jnp.float32, jnp.bfloat16
    z, c, t = (lax.axis_index(a) for a in (FSDP, CONTEXT, TENSOR))
    core = (z, c, 1 - t)
    greet([(flip(z, k), c, t) for k in (1, 2, 3)] + [(z, flip(c, k), t) for k in (1, 2, 3)] + [core])
    net = Copies(send, receive)
    wrows = ff.shape[2]
    half = wrows // 2
    part, width = al.shape
    rows = 2 * part
    q_cols = q.shape[1]
    qkv_cols = q_cols + 2 * HEAD
    blocks = normed.shape[0]
    order = (3, 2, 1, 0)
    loads = {}
    for k in order:
        zs = flip(z, k)
        loads[k] = pltpu.make_async_copy(ff.at[zs], terms.at[zs], local.at[k])
        loads[k].start()
    wa_load = pltpu.make_async_copy(wa_in, wa, local.at[4])
    wa_load.start()
    normed_load = pltpu.make_async_copy(normed_in.at[pl.ds(0, blocks)], normed, local.at[5])
    normed_load.start()
    ag_in = [net.start(al, ag.at[c, t], (z, flip(c, k), t)) for k in (3, 1, 2)]
    swaps = [net.start(al, ag.at[c, t], core)]
    feed = [net.start(fs.at[k - 1], feed_in.at[k - 1], (flip(z, k), c, t)) for k in (3, 2, 1)]
    first = {}
    for k in order:
        zs = flip(z, k)
        loads[k].wait()
        first[k] = (
            net.start(terms.at[zs, flip(c, 3), pl.ds(0, half)], corner_x.at[k], (z, flip(c, 1), t)),
            net.start(terms.at[zs, flip(c, 3), pl.ds(half, half)], corner_y.at[k], (z, flip(c, 2), t)),
        )
    ag[c, t] = al[...]
    for j, piece in enumerate(split_pair(kv[...].astype(f32))):
        pairs[j] = piece.astype(bf16)
    acc[...] = jnp.zeros_like(acc)
    dqkv[pl.ds(blocks * rows, rows), :] = jnp.zeros((rows, qkv_cols), bf16)
    for k, copy in zip((3, 1, 2), ag_in):
        copy.wait_recv()
        piece = ag.at[flip(c, k), t]
        swaps.append(net.start(piece, piece, core))
    second, third = {}, {}

    def sides(k):
        zs = flip(z, k)
        for copy in first[k]:
            copy.wait_recv()
        low, high = pl.ds(0, half), pl.ds(half, half)
        xb, yb = flip(c, 1), flip(c, 2)
        terms[zs, yb, low] = (terms[zs, yb, low].astype(f32) + corner_x[k].astype(f32)).astype(bf16)
        terms[zs, xb, high] = (terms[zs, xb, high].astype(f32) + corner_y[k].astype(f32)).astype(bf16)
        second[k] = (
            net.start(terms.at[zs, yb], side_y.at[k], (z, yb, t)),
            net.start(terms.at[zs, xb], side_x.at[k], (z, xb, t)),
        )

    def owners(k):
        zs = flip(z, k)
        for copy in second[k]:
            copy.wait_recv()
        total = terms[zs, c].astype(f32) + side_x[k].astype(f32) + side_y[k].astype(f32)
        terms[zs, c] = total.astype(bf16)
        if k:
            third[k] = net.start(terms.at[zs, c], ff_out.at[z], (zs, c, t))
        else:
            third[0] = pltpu.make_async_copy(terms.at[z, c], ff_out.at[z], local.at[6])
            third[0].start()

    for copy in swaps:
        copy.wait_recv()
    wa_load.wait()
    normed_load.wait()

    def mix(i, carry):
        w = wa[...].reshape(width, wa.shape[3])[:, qkv_cols:]
        here = pl.ds(pl.multiple_of(i * rows, rows), rows)
        mixed[here, :] = dot_tile(ag[i].reshape(rows, width), w, 1, 0).astype(bf16)
        return carry

    lax.fori_loop(0, blocks, mix, 0)
    sides(3)

    def out_term(m, carry):
        here = pl.ds(pl.multiple_of(m * wrows, wrows), wrows)
        left = ag[0:blocks, :, :, here].reshape(blocks * rows, wrows)
        value = dot_tile(left, attended[0 : blocks * rows, :], 0, 0)
        at_terms[lax.div(m, 4), lax.rem(m, 4), :, qkv_cols:] = value.astype(bf16)
        return carry

    lax.fori_loop(0, width // wrows, out_term, 0)
    sides(2)

    def attend(i):
        count = (i + 1) * rows
        here = pl.ds(i * rows, rows)
        keep = (seg_col[here, :] == seg_row[:, :count]) & (
            lax.broadcasted_iota(jnp.int32, (rows, count), 0) + i * rows
            >= lax.broadcasted_iota(jnp.int32, (rows, count), 1)
        )
        log_sums = logs[here, :]
        lane = lax.broadcasted_iota(jnp.int32, (rows, 128), 1)
        cos_b, sin_b = cos[here, :], sin[here, :]
        quarter = low_lanes(cos_b.shape, HEAD // 2)
        for p in range(q_cols // 128):
            block = slice(p * 128, (p + 1) * 128)
            grad = jnp.zeros((rows, 128), f32)
            for e in range(2):
                scores = dot_tile(q[here, block], pairs[e, :count, :], 1, 1)
                scores = jnp.where(keep, scores * attention_mult, -1e30)
                log = jnp.sum(jnp.where(lane == 2 * p + e, log_sums, 0.0), axis=-1, keepdims=True)
                prob = jnp.exp(scores - log)
                prob_grad = dot_tile(mixed[here, block], pairs[2 + e, :count, :], 1, 1)
                row_dot = jnp.sum(prob * prob_grad, axis=-1, keepdims=True)
                score_grad = (attention_mult * prob * (prob_grad - row_dot)).astype(bf16)
                grad = grad + dot_tile(score_grad, pairs[e, :count, :], 1, 0)
                acc[e, :count, :] += dot_tile(score_grad, q[here, block], 0, 0)
                acc[2 + e, :count, :] += dot_tile(prob.astype(bf16), mixed[here, block], 0, 0)
            dqkv[here, block] = (grad * cos_b + turn_lanes(grad * sin_b, quarter)).astype(bf16)

    attend(0)
    sides(1)
    attend(1)
    sides(0)
    attend(2)
    owners(3)
    filled = blocks * rows
    low = low_lanes((filled, 128), HEAD)
    key_grad = jnp.where(low, acc[0], 0.0) + pltpu.roll(jnp.where(low, 0.0, acc[1]), HEAD, 1)
    value_grad = jnp.where(low, 0.0, acc[3]) + pltpu.roll(jnp.where(low, acc[2], 0.0), HEAD, 1)
    turned = turn_lanes(key_grad * sin[0:filled, :], low_lanes((filled, 128), HEAD // 2))
    key_grad = key_grad * cos[0:filled, :] + turned
    dqkv[0:filled, q_cols:] = jnp.where(low, key_grad, value_grad).astype(bf16)

    crosses, outs = {}, {}
    for k in (3, 1, 2, 0):
        mine_rows = pl.ds(pl.multiple_of(flip(c, k) * rows, rows), rows)

        def back_tile(n, carry, mine_rows=mine_rows):
            here = pl.ds(pl.multiple_of(n * 128, 128), 128)
            w = wa[lax.div(n, 4), lax.rem(n, 4), :, :qkv_cols]
            sums[:, here] = dot_tile(dqkv[mine_rows, :], w, 1, 1)
            return carry

        lax.fori_loop(0, width // 128, back_tile, 0)
        mine[k] = sums[pl.ds(pl.multiple_of(t * part, part), part), :]
        cross[k] = sums[pl.ds(pl.multiple_of((1 - t) * part, part), part), :].astype(bf16)
        crosses[k] = net.start(cross.at[k], crossed.at[k], core)
    owners(2)
    for k in (3, 1, 2):
        crosses[k].wait_recv()
        totals[k - 1] = (mine[k] + crossed[k].astype(f32)).astype(bf16)
        outs[k] = net.start(totals.at[k - 1], back_in.at[k - 1], (z, flip(c, k), t))
    crosses[0].wait_recv()
    back_own[...] = mine[0] + crossed[0].astype(f32)

    def qkv_term(m, carry):
        here = pl.ds(pl.multiple_of(m * wrows, wrows), wrows)
        left = normed[:, :, here].reshape(filled, wrows)
        value = dot_tile(left, dqkv[0:filled, :], 0, 0)
        at_terms[lax.div(m, 4), lax.rem(m, 4), :, :qkv_cols] = value.astype(bf16)
        return carry

    lax.fori_loop(0, width // wrows, qkv_term, 0)
    attn_in = [net.start(at_terms.at[flip(z, k)], at_in.at[k - 1], (flip(z, k), c, t)) for k in (3, 2, 1)]
    owners(1)
    owners(0)
    for copy in attn_in:
        copy.wait_recv()
    for j in range(4):
        total = at_terms[z, j].astype(f32)
        for i in range(3):
            total = total + at_in[i, j].astype(f32)
        at_total[j] = total.astype(bf16)
    attn_out = [net.start(at_total.at[flip(c, k)], at_out.at[c], (z, flip(c, k), t)) for k in (1, 2, 3)]
    keep_own = pltpu.make_async_copy(at_total.at[c], at_out.at[c], local.at[7])
    keep_own.start()
    for copy in feed + attn_out + [outs[k] for k in (1, 2, 3)] + [third[k] for k in (1, 2, 3)]:
        copy.wait_recv()
    for copy in net.started:
        copy.wait_send()
    third[0].wait()
    keep_own.wait()


def backward(ff, fs, al, wa, normed, q, kv, logs, attended, cos, sin, seg_col, seg_row):
    bf16, f32 = jnp.bfloat16, jnp.float32
    wrows, cols = ff.shape[2:]
    attn_cols = wa.shape[3]
    part, width = al.shape
    total = q.shape[0]
    filled = seg_col.shape[0]
    rows = 2 * part
    blocks = filled // rows
    copies = 48
    vmem, anywhere = pl.BlockSpec(memory_space=pltpu.VMEM), pl.BlockSpec(memory_space=pl.ANY)
    return pl.pallas_call(
        backward_kernel,
        out_shape=[
            jax.ShapeDtypeStruct(fs.shape, bf16),
            jax.ShapeDtypeStruct(al.shape, f32),
            jax.ShapeDtypeStruct(fs.shape, bf16),
            jax.ShapeDtypeStruct((4, wrows, cols), bf16),
            jax.ShapeDtypeStruct((4, wrows, attn_cols), bf16),
        ],
        in_specs=[anywhere, vmem, vmem, anywhere, anywhere] + [vmem] * 8,
        out_specs=[anywhere, vmem, anywhere, anywhere, anywhere],
        scratch_shapes=[
            pltpu.VMEM((4, 4, wrows, cols), bf16),
            pltpu.VMEM((4, wrows // 2, cols), bf16),
            pltpu.VMEM((4, wrows // 2, cols), bf16),
            pltpu.VMEM((4, wrows, cols), bf16),
            pltpu.VMEM((4, wrows, cols), bf16),
            pltpu.VMEM((4, 4, wrows, attn_cols), bf16),
            pltpu.VMEM((3, 4, wrows, attn_cols), bf16),
            pltpu.VMEM((4, wrows, attn_cols), bf16),
            pltpu.VMEM(wa.shape, bf16),
            pltpu.VMEM((blocks, rows, width), bf16),
            pltpu.VMEM((4, 2, part, width), bf16),
            pltpu.VMEM((4, total, 2 * HEAD), bf16),
            pltpu.VMEM((filled, q.shape[1]), bf16),
            pltpu.VMEM((4, filled, 2 * HEAD), f32),
            pltpu.VMEM((total, q.shape[1] + 2 * HEAD), bf16),
            pltpu.VMEM((rows, width), f32),
            pltpu.VMEM((4, part, width), f32),
            pltpu.VMEM((4, part, width), bf16),
            pltpu.VMEM((4, part, width), bf16),
            pltpu.VMEM((3, part, width), bf16),
            pltpu.SemaphoreType.DMA((copies,)),
            pltpu.SemaphoreType.DMA((copies,)),
            pltpu.SemaphoreType.DMA((8,)),
        ],
        compiler_params=pltpu.CompilerParams(collective_id=2, has_side_effects=True, vmem_limit_bytes=63 * 2**20),
    )(ff, fs, al, wa, normed, q, kv, logs, attended, cos, sin, seg_col, seg_row)


def on_device_split(
    tokens,
    out_grad,
    lengths,
    attention_gain,
    query_weight,
    key_weight,
    value_weight,
    output_weight,
    feed_gain,
    gate_weight,
    up_weight,
    down_weight,
):
    f32, bf16 = jnp.float32, jnp.bfloat16
    nz, nc, nt = (lax.axis_size(a) for a in (FSDP, CONTEXT, TENSOR))
    z, c, t = (lax.axis_index(a) for a in (FSDP, CONTEXT, TENSOR))
    local_rows, width = tokens.shape[1:]
    group_rows = local_rows * nc
    filled = group_rows * 3 // 4
    part = local_rows // nt
    wrows = query_weight.shape[0]
    kv_cols = key_weight.shape[1] // nc
    q_cols = query_weight.shape[1] // nc
    qkv_cols = q_cols + 2 * kv_cols
    ff_cols = gate_weight.shape[1] // nz
    per_group = q_cols // kv_cols
    segment, position, valid_rows = slot_layout(lengths[0], group_rows)
    cos_table, sine_table = rope_tables(position, HEAD)

    wa = jnp.concatenate(
        [
            w.astype(bf16).reshape(wrows, nc, -1).transpose(1, 0, 2)
            for w in (query_weight, key_weight, value_weight, output_weight)
        ],
        axis=2,
    )
    wf = jnp.concatenate(
        [w.astype(bf16).reshape(wrows, nz, ff_cols).transpose(1, 0, 2) for w in (gate_weight, up_weight, down_weight)],
        axis=2,
    )
    gain = jnp.pad(jnp.stack([attention_gain, feed_gain]).astype(bf16), ((0, 14), (0, 0)))
    my_valid = lax.dynamic_slice_in_dim(valid_rows, c * local_rows + t * part, part)
    cotangent = cut(out_grad[0], t, part, 0).astype(f32) * my_valid[:, None].astype(f32)
    feed_grad = (residual_mult * cotangent).astype(bf16)
    sign = jnp.where(jnp.arange(HEAD) < HEAD // 2, -1.0, 1.0).astype(f32)
    wide_cos = jnp.concatenate([cos_table, cos_table], axis=1)
    wide_sin = jnp.concatenate([sine_table * sign, sine_table * sign], axis=1)
    wa, wf, normed_one, queries, pair, logs, attended, hidden, normed_two, feed_grads, gains = attention_forward(
        wa, wf, tokens[0].reshape(nt, part, width), gain, feed_grad, wide_cos, wide_sin,
        segment[:filled, None], segment[None, :filled],
    )
    gain_one, gain_two = gains[0], gains[1]
    w_feed = wf.reshape(width, 3 * ff_cols)
    my_inputs = cut(tokens[0], t, part, 0).astype(f32)
    inverse_two = lax.rsqrt(jnp.mean(hidden * hidden, axis=-1, keepdims=True) + norm_eps)
    unit_two = hidden * inverse_two

    normed_grad_two, feed_own, feed_send, ff_terms = feed_forward(
        normed_two, feed_grads.reshape(nz, local_rows, width), w_feed
    )
    ff_terms = ff_terms.reshape(nz, nc, wrows, 3 * ff_cols)

    def both_cores(x):
        out = put(jnp.zeros((nt,) + x.shape, x.dtype), x, t)
        return put(out, swap(x, TENSOR, 1), 1 - t).reshape(1, local_rows, width)

    feed_gain_term = jnp.sum(normed_grad_two * unit_two, axis=0)
    hidden_grad = cotangent + norm_back(normed_grad_two, unit_two, gain_two, inverse_two)

    attn_low = (residual_mult * hidden_grad).astype(bf16)
    feed_in, back_own, back_in, ff_grads, attn_grads = backward(
        ff_terms, feed_send, attn_low, wa, normed_one, queries, pair, logs, attended, wide_cos, wide_sin,
        segment[:filled, None], segment[None, :filled],
    )
    output = both_cores((hidden + residual_mult * (feed_own + jnp.sum(feed_in.astype(f32), axis=0))).astype(bf16))
    normed_grad_one = back_own + jnp.sum(back_in.astype(f32), axis=0)
    inverse_one = lax.rsqrt(jnp.mean(my_inputs * my_inputs, axis=-1, keepdims=True) + norm_eps)
    unit_one = my_inputs * inverse_one
    attn_gain_term = jnp.sum(normed_grad_one * unit_one, axis=0)
    input_grad = both_cores((hidden_grad + norm_back(normed_grad_one, unit_one, gain_one, inverse_one)).astype(bf16))

    gain_terms = jnp.stack([attn_gain_term, feed_gain_term])
    for axis, k in ((TENSOR, 1), (CONTEXT, 1), (CONTEXT, 2), (FSDP, 1), (FSDP, 2)):
        gain_terms = gain_terms + swap(gain_terms, axis, k)
    gain_terms = cut(gain_terms, z * nc + c, wrows, 1)

    def columns(x, begin, size):
        return x[:, :, begin : begin + size].transpose(1, 0, 2).reshape(wrows, -1).astype(f32)

    grad_gate, grad_up, grad_down = (columns(ff_grads, i * ff_cols, ff_cols) for i in range(3))
    begins = (0, q_cols, q_cols + kv_cols, qkv_cols)
    attn_terms = [columns(attn_grads, i, n) for i, n in zip(begins, (q_cols, kv_cols, kv_cols, q_cols))]
    return (output, input_grad, gain_terms[0], *attn_terms, gain_terms[1], grad_gate, grad_up, grad_down)


def solution(mesh):
    split = tuple(mesh.shape[a] for a in (FSDP, CONTEXT, TENSOR)) == (4, 4, 2)
    return jax.shard_map(
        on_device_split if split else on_device,
        mesh=mesh,
        in_specs=(
            P(FSDP, CONTEXT, None),
            P(FSDP, CONTEXT, None),
            P(FSDP, None),
            P((FSDP, CONTEXT)),
            P((FSDP, CONTEXT), TENSOR),
            P((FSDP, CONTEXT), TENSOR),
            P((FSDP, CONTEXT), TENSOR),
            P((FSDP, CONTEXT), TENSOR),
            P((FSDP, CONTEXT)),
            P((FSDP, CONTEXT), TENSOR),
            P((FSDP, CONTEXT), TENSOR),
            P((FSDP, CONTEXT), TENSOR),
        ),
        out_specs=(
            P(FSDP, CONTEXT, None),
            P(FSDP, CONTEXT, None),
            P((FSDP, CONTEXT)),
            P((FSDP, CONTEXT), TENSOR),
            P((FSDP, CONTEXT), TENSOR),
            P((FSDP, CONTEXT), TENSOR),
            P((FSDP, CONTEXT), TENSOR),
            P((FSDP, CONTEXT)),
            P((FSDP, CONTEXT), TENSOR),
            P((FSDP, CONTEXT), TENSOR),
            P((FSDP, CONTEXT), TENSOR),
        ),
        check_vma=False,
    )
```

```python
import jax
import jax.numpy as jnp
from jax import lax
from jax.experimental import pallas as pl
from jax.experimental.pallas import tpu as pltpu
from jax.sharding import PartitionSpec as P

HEAD = 64
FSDP, CONTEXT, TENSOR = "fsdp", "context", "tensor"


norm_eps = 1e-05
attention_mult = 0.015625
residual_mult = 0.22
rope_base = 10000000.0


def slot_layout(seq_lengths, total_rows):
    seq_ends = jnp.cumsum(seq_lengths)
    starts = seq_ends - seq_lengths
    slot_ids = jnp.arange(total_rows, dtype=jnp.int32)
    before = (slot_ids[:, None] >= seq_ends[None, :]).astype(jnp.int32)
    segment = jnp.sum(before, axis=1)
    seq_count = seq_lengths.shape[0]
    valid_rows = segment < seq_count
    inside = (slot_ids[:, None] >= starts[None, :]) & (slot_ids[:, None] < seq_ends[None, :])
    position = jnp.sum(jnp.where(inside, slot_ids[:, None] - starts[None, :], 0), axis=1)
    segment = jnp.where(valid_rows, segment, seq_count + slot_ids)
    return (segment, position, valid_rows)


def rope_tables(position, width):
    half_width = width // 2
    frequency = rope_base ** (-jnp.arange(half_width, dtype=jnp.float32) * 2.0 / width)
    angles = position.astype(jnp.float32)[:, None] * frequency[None, :]
    angles = jnp.concatenate([angles, angles], axis=1)
    return (jnp.cos(angles), jnp.sin(angles))


def turn_half(vectors):
    half_width = vectors.shape[-1] // 2
    return jnp.concatenate([-vectors[..., half_width:], vectors[..., :half_width]], axis=-1)


def rotate(vectors, cos_table, sine_table):
    return vectors * cos_table[:, None, :] + turn_half(vectors) * sine_table[:, None, :]


def rotate_back(grads, cos_table, sine_table):
    return grads * cos_table[:, None, :] - turn_half(grads * sine_table[:, None, :])


def norm_back(normed_grad, unit, gain, inverse):
    scaled = normed_grad * gain
    return inverse * (scaled - unit * jnp.mean(scaled * unit, axis=-1, keepdims=True))


def dot_first(left, right):
    return lax.dot_general(left, right, (((0,), (0,)), ((), ())), preferred_element_type=jnp.float32)


def dot_last(left, right):
    return lax.dot_general(left, right, (((1,), (1,)), ((), ())), preferred_element_type=jnp.float32)


def attention_shards(attention_gain, query_weight, key_weight, value_weight, output_weight):
    return (
        lax.all_gather(
            attention_gain.astype(jnp.bfloat16), (FSDP, CONTEXT), axis=0, tiled=True
        ),
        lax.all_gather(query_weight.astype(jnp.bfloat16), (FSDP, CONTEXT), axis=0, tiled=True),
        lax.all_gather(key_weight.astype(jnp.bfloat16), (FSDP, CONTEXT), axis=0, tiled=True),
        lax.all_gather(value_weight.astype(jnp.bfloat16), (FSDP, CONTEXT), axis=0, tiled=True),
        lax.all_gather(output_weight.astype(jnp.bfloat16), (FSDP, CONTEXT), axis=0, tiled=True),
    )


def feed_shards(feed_gain, gate_weight, up_weight, down_weight):
    return (
        lax.all_gather(feed_gain.astype(jnp.bfloat16), (FSDP, CONTEXT), axis=0, tiled=True),
        lax.all_gather(gate_weight.astype(jnp.bfloat16), (FSDP, CONTEXT), axis=0, tiled=True),
        lax.all_gather(up_weight.astype(jnp.bfloat16), (FSDP, CONTEXT), axis=0, tiled=True),
        lax.all_gather(down_weight.astype(jnp.bfloat16), (FSDP, CONTEXT), axis=0, tiled=True),
    )


def on_device(
    tokens,
    out_grad,
    lengths,
    attention_gain,
    query_weight,
    key_weight,
    value_weight,
    output_weight,
    feed_gain,
    gate_weight,
    up_weight,
    down_weight,
):
    local_rows = tokens.shape[1]
    group_rows = local_rows * lax.axis_size(CONTEXT)
    first_row = lax.axis_index(CONTEXT) * local_rows
    segment, position, valid_rows = slot_layout(lengths[0], group_rows)
    local_segment = lax.dynamic_slice_in_dim(segment, first_row, local_rows)
    local_position = lax.dynamic_slice_in_dim(position, first_row, local_rows)
    local_valid = lax.dynamic_slice_in_dim(valid_rows, first_row, local_rows)
    slot_ids = jnp.arange(group_rows, dtype=jnp.int32)
    local_slots = first_row + jnp.arange(local_rows, dtype=jnp.int32)
    allowed = (local_segment[:, None] == segment[None, :]) & (
        local_slots[:, None] >= slot_ids[None, :]
    )
    inputs = tokens[0].astype(jnp.float32)
    attn_set = attention_shards(
        attention_gain, query_weight, key_weight, value_weight, output_weight
    )
    gain_one = attn_set[0].astype(jnp.float32)
    inverse_one = lax.rsqrt(jnp.mean(inputs * inputs, axis=-1, keepdims=True) + norm_eps)
    unit_one = inputs * inverse_one
    normed_one = (unit_one * gain_one).astype(jnp.bfloat16)
    queries = jnp.dot(normed_one, attn_set[1], preferred_element_type=jnp.float32)
    keys_lin = jnp.dot(normed_one, attn_set[2], preferred_element_type=jnp.float32)
    values_low = jnp.dot(normed_one, attn_set[3], preferred_element_type=jnp.float32).astype(
        jnp.bfloat16
    )
    heads_local = queries.shape[1] // HEAD
    kv_local = keys_lin.shape[1] // HEAD
    per_group = heads_local // kv_local
    cos_table, sine_table = rope_tables(local_position, HEAD)
    queries_rot = rotate(
        queries.reshape(local_rows, heads_local, HEAD), cos_table, sine_table
    ).astype(jnp.bfloat16)
    keys_rot = rotate(keys_lin.reshape(local_rows, kv_local, HEAD), cos_table, sine_table).astype(
        jnp.bfloat16
    )
    keys_all, values_all = (
        lax.all_gather(
            keys_rot.reshape(local_rows, kv_local * HEAD), CONTEXT, axis=0, tiled=True
        ),
        lax.all_gather(values_low, CONTEXT, axis=0, tiled=True),
    )
    query_heads = queries_rot.reshape(local_rows, kv_local, per_group, HEAD).transpose(1, 0, 2, 3)
    key_heads = keys_all.reshape(group_rows, kv_local, HEAD).transpose(1, 0, 2)
    value_heads = values_all.reshape(group_rows, kv_local, HEAD).transpose(1, 0, 2)

    def head_scores(query_head, key_head):
        raw_scores = jnp.einsum(
            "tgd,sd->gts", query_head, key_head, preferred_element_type=jnp.float32
        )
        return jnp.where(allowed[None], raw_scores * attention_mult, -1e30)

    def head_forward(pieces):
        query_head, key_head, value_head = pieces
        scores = head_scores(query_head, key_head)
        highest = jnp.max(scores, axis=-1, keepdims=True)
        weight = jnp.exp(scores - highest)
        row_totals = jnp.sum(weight, axis=-1, keepdims=True)
        probabilities = (weight / row_totals).astype(jnp.bfloat16)
        mixed = jnp.einsum(
            "gts,sd->tgd", probabilities, value_head, preferred_element_type=jnp.float32
        )
        return (mixed, (highest + jnp.log(row_totals))[..., 0])

    mixed_heads, log_totals = lax.map(head_forward, (query_heads, key_heads, value_heads))
    attended = (
        mixed_heads.transpose(1, 0, 2, 3)
        .reshape(local_rows, heads_local * HEAD)
        .astype(jnp.bfloat16)
    )
    attn_part = dot_last(attended, attn_set[4])
    attn_out = lax.psum(attn_part.astype(jnp.bfloat16), TENSOR).astype(jnp.float32)
    hidden_state = inputs + residual_mult * attn_out
    feed_set = feed_shards(feed_gain, gate_weight, up_weight, down_weight)
    gain_two = feed_set[0].astype(jnp.float32)
    inverse_two = lax.rsqrt(
        jnp.mean(hidden_state * hidden_state, axis=-1, keepdims=True) + norm_eps
    )
    unit_two = hidden_state * inverse_two
    normed_two = (unit_two * gain_two).astype(jnp.bfloat16)
    gate_out = jnp.dot(normed_two, feed_set[1], preferred_element_type=jnp.float32)
    up_out = jnp.dot(normed_two, feed_set[2], preferred_element_type=jnp.float32)
    inner_act = (jax.nn.silu(gate_out) * up_out).astype(jnp.bfloat16)
    feed_part = dot_last(inner_act, feed_set[3])
    feed_out = lax.psum(feed_part.astype(jnp.bfloat16), TENSOR).astype(jnp.float32)
    output = hidden_state + residual_mult * feed_out
    cotangent = out_grad[0].astype(jnp.float32) * local_valid[:, None].astype(jnp.float32)
    feed_back = feed_shards(feed_gain, gate_weight, up_weight, down_weight)
    feed_grad = (residual_mult * cotangent).astype(jnp.bfloat16)
    down_term = dot_first(feed_grad, inner_act)
    inner_grad = jnp.dot(feed_grad, feed_back[3], preferred_element_type=jnp.float32)
    sigmoid_gate = jax.nn.sigmoid(gate_out)
    gate_grad = (
        inner_grad * up_out * sigmoid_gate * (1.0 + gate_out * (1.0 - sigmoid_gate))
    ).astype(jnp.bfloat16)
    up_grad = (inner_grad * jax.nn.silu(gate_out)).astype(jnp.bfloat16)
    gate_term = dot_first(normed_two, gate_grad)
    up_term = dot_first(normed_two, up_grad)
    normed_part_two = dot_last(gate_grad, feed_back[1])
    normed_part_two = normed_part_two + dot_last(up_grad, feed_back[2])
    normed_grad_two = lax.psum(normed_part_two.astype(jnp.bfloat16), TENSOR).astype(jnp.float32)
    feed_gain_term = jnp.sum(normed_grad_two * unit_two, axis=0)
    hidden_grad = cotangent + norm_back(normed_grad_two, unit_two, gain_two, inverse_two)
    feed_sums = (
        lax.psum_scatter(feed_gain_term, (FSDP, CONTEXT), scatter_dimension=0, tiled=True),
        lax.psum_scatter(gate_term, (FSDP, CONTEXT), scatter_dimension=0, tiled=True),
        lax.psum_scatter(up_term, (FSDP, CONTEXT), scatter_dimension=0, tiled=True),
        lax.psum_scatter(down_term, (FSDP, CONTEXT), scatter_dimension=0, tiled=True),
    )
    attn_back = attention_shards(
        attention_gain, query_weight, key_weight, value_weight, output_weight
    )
    attn_grad = (residual_mult * hidden_grad).astype(jnp.bfloat16)
    out_term = dot_first(attn_grad, attended)
    mixed_grad = jnp.dot(attn_grad, attn_back[4], preferred_element_type=jnp.float32).astype(
        jnp.bfloat16
    )
    mixed_grad_heads = mixed_grad.reshape(local_rows, kv_local, per_group, HEAD).transpose(
        1, 0, 2, 3
    )

    def head_backward(pieces):
        query_head, key_head, value_head, grad_head, log_head = pieces
        scores = head_scores(query_head, key_head)
        probabilities = jnp.exp(scores - log_head[..., None])
        prob_low = probabilities.astype(jnp.bfloat16)
        prob_grad = jnp.einsum(
            "tgd,sd->gts", grad_head, value_head, preferred_element_type=jnp.float32
        )
        row_dot = jnp.sum(probabilities * prob_grad, axis=-1, keepdims=True)
        score_grad = (attention_mult * probabilities * (prob_grad - row_dot)).astype(jnp.bfloat16)
        query_grad = jnp.einsum(
            "gts,sd->tgd", score_grad, key_head, preferred_element_type=jnp.float32
        )
        key_grad = jnp.einsum(
            "gts,tgd->sd", score_grad, query_head, preferred_element_type=jnp.float32
        )
        value_grad = jnp.einsum(
            "gts,tgd->sd", prob_low, grad_head, preferred_element_type=jnp.float32
        )
        return (query_grad, key_grad, value_grad)

    query_grads, key_grads, value_grads = lax.map(
        head_backward, (query_heads, key_heads, value_heads, mixed_grad_heads, log_totals)
    )
    key_grads = key_grads.transpose(1, 0, 2).reshape(group_rows, kv_local * HEAD)
    value_grads = value_grads.transpose(1, 0, 2).reshape(group_rows, kv_local * HEAD)
    local_key_grad, local_value_grad = (
        lax.psum_scatter(
            key_grads.astype(jnp.bfloat16), CONTEXT, scatter_dimension=0, tiled=True
        ).astype(jnp.float32),
        lax.psum_scatter(
            value_grads.astype(jnp.bfloat16), CONTEXT, scatter_dimension=0, tiled=True
        ).astype(jnp.float32),
    )
    query_grad_rot = query_grads.transpose(1, 0, 2, 3).reshape(local_rows, heads_local, HEAD)
    query_grad_low = (
        rotate_back(query_grad_rot, cos_table, sine_table)
        .reshape(local_rows, heads_local * HEAD)
        .astype(jnp.bfloat16)
    )
    key_grad_low = (
        rotate_back(local_key_grad.reshape(local_rows, kv_local, HEAD), cos_table, sine_table)
        .reshape(local_rows, kv_local * HEAD)
        .astype(jnp.bfloat16)
    )
    value_grad_low = local_value_grad.astype(jnp.bfloat16)
    query_term = dot_first(normed_one, query_grad_low)
    key_term = dot_first(normed_one, key_grad_low)
    value_term = dot_first(normed_one, value_grad_low)
    normed_part_one = dot_last(query_grad_low, attn_back[1])
    normed_part_one = normed_part_one + dot_last(key_grad_low, attn_back[2])
    normed_part_one = normed_part_one + dot_last(value_grad_low, attn_back[3])
    normed_grad_one = lax.psum(normed_part_one.astype(jnp.bfloat16), TENSOR).astype(jnp.float32)
    attn_gain_term = jnp.sum(normed_grad_one * unit_one, axis=0)
    input_grad = hidden_grad + norm_back(normed_grad_one, unit_one, gain_one, inverse_one)
    attn_sums = (
        lax.psum_scatter(attn_gain_term, (FSDP, CONTEXT), scatter_dimension=0, tiled=True),
        lax.psum_scatter(query_term, (FSDP, CONTEXT), scatter_dimension=0, tiled=True),
        lax.psum_scatter(key_term, (FSDP, CONTEXT), scatter_dimension=0, tiled=True),
        lax.psum_scatter(value_term, (FSDP, CONTEXT), scatter_dimension=0, tiled=True),
        lax.psum_scatter(out_term, (FSDP, CONTEXT), scatter_dimension=0, tiled=True),
    )
    return (
        output.astype(jnp.bfloat16)[None],
        input_grad.astype(jnp.bfloat16)[None],
        attn_sums[0],
        attn_sums[1],
        attn_sums[2],
        attn_sums[3],
        attn_sums[4],
        feed_sums[0],
        feed_sums[1],
        feed_sums[2],
        feed_sums[3],
    )


def flip(i, k):
    if k == 0:
        return i
    if k == 1:
        return i + 1 - 2 * lax.rem(i, 2)
    if k == 2:
        return lax.rem(i + 2, 4)
    return 3 - i


class Copies:
    def __init__(self, send, receive):
        self.send, self.receive = send, receive
        self.count, self.started = 0, []

    def index(self):
        self.count += 1
        return self.count - 1

    def make(self, i, source, target, device):
        return pltpu.make_async_remote_copy(
            src_ref=source,
            dst_ref=target,
            send_sem=self.send.at[i],
            recv_sem=self.receive.at[i],
            device_id=device,
            device_id_type=pl.DeviceIdType.MESH,
        )

    def start(self, source, target, device, i=None):
        i = self.index() if i is None else i
        copy = self.make(i, source, target, device)
        copy.start()
        self.started.append(copy)
        return copy


def greet(partners):
    barrier = pltpu.get_barrier_semaphore()
    for device in partners:
        pl.semaphore_signal(barrier, inc=1, device_id=device, device_id_type=pl.DeviceIdType.MESH)
    pl.semaphore_wait(barrier, len(partners))


def dot_tile(left, right, left_axis, right_axis):
    return lax.dot_general(left, right, (((left_axis,), (right_axis,)), ((), ())), preferred_element_type=jnp.float32)


TILE = 256


def turn_lanes(x, low):
    return jnp.where(low, pltpu.roll(x, x.shape[1] - HEAD // 2, 1), pltpu.roll(x, HEAD // 2, 1))


def low_lanes(shape, width):
    return lax.rem(lax.broadcasted_iota(jnp.int32, shape, 1), 2 * width) < width


def split_pair(x):
    low = low_lanes(x.shape, HEAD)
    a, b = jnp.where(low, x, 0.0), jnp.where(low, 0.0, x)
    return a, pltpu.roll(a, HEAD, 1), pltpu.roll(b, HEAD, 1), b


def attention_kernel(
    wa, wf, xt, gain, fgx, cos, sin, seg_col, seg_row,
    wa_out, wf_all, normed_out, q, kv, logs, attended, hidden_out, normed_two, fg_all, gains,
    wa_all, x_all, gain_all, normed, pairs, sums, mine, cross, crossed, totals, landed, send, receive, local,
):
    f32, bf16 = jnp.float32, jnp.bfloat16
    z, c, t = (lax.axis_index(a) for a in (FSDP, CONTEXT, TENSOR))
    peers = [(flip(z, i), flip(c, j), t) for i in range(4) for j in range(4) if i or j]
    core = (z, c, 1 - t)
    greet(peers + [core])
    net = Copies(send, receive)
    middle = (z == 1) | (z == 2)
    nt, part, width = xt.shape
    rows = nt * part
    q_cols = q.shape[1]
    hidden = wf_all.shape[4]

    def columns(owner):
        return pl.ds(pl.multiple_of(owner * hidden, hidden), hidden)

    qkv_cols = q_cols + 2 * HEAD
    ends = []
    own = []
    for i, (source, target) in enumerate(
        (
            (wa.at[c], wa_all.at[z, c]),
            (xt, x_all.at[c]),
            (wf.at[:, :, columns(z)], wf_all.at[:, z, c]),
            (gain, gain_all.at[z, c]),
            (fgx, fg_all.at[0, 0]),
        )
    ):
        own.append(pltpu.make_async_copy(source, target, local.at[i]))
        own[-1].start()

    def spread(source, slot, forward):
        one = net.start(source, slot(1), (flip(z, 1), c, t))
        two = net.start(source, slot(2), (flip(z, 2), c, t))
        three = net.index()
        direct = net.make(three, source, slot(3), (3 - z, c, t))
        pl.when(middle)(direct.start)
        passed = pltpu.make_async_remote_copy(
            src_ref=forward[0],
            dst_ref=forward[1],
            send_sem=send.at[net.index()],
            recv_sem=receive.at[three],
            device_id=(flip(z, 1), c, t),
            device_id_type=pl.DeviceIdType.MESH,
        )
        return one, two, direct, passed

    attn_in = [net.start(wa.at[flip(c, k)], wa_all.at[z, c], (z, flip(c, k), t)) for k in (1, 2, 3)]
    tokens_in = [net.start(xt.at[t], x_all.at[c, t], (z, flip(c, k), t)) for k in (1, 2, 3)]
    parts = {k: (0, 1, 2) if k == 2 else (slice(None),) for k in range(4)}

    def weights_to(k):
        there = columns(flip(z, k))
        return [net.start(wf.at[m, :, there], wf_all.at[m, z, c], (flip(z, k), c, t)) for m in parts[k]]

    ff_in = {1: weights_to(1)}
    for device in peers:
        ends.append(net.start(gain, gain_all.at[z, c], device))
    own[2].wait()
    ff_out = {}

    def pass_on(k, m):
        piece = wf_all.at[m, flip(z, k), c]
        ff_out.setdefault(k, []).append([net.start(piece, piece, (z, flip(c, j), t)) for j in (1, 2)])

    pass_on(0, slice(None))
    weights = []
    for j in range(4):
        if j:
            attn_in[j - 1].wait_recv()
        else:
            own[0].wait()
        piece = wa_all.at[z, flip(c, j)]
        passed_piece = wa_all.at[flip(z, 2), flip(c, j)]
        weights.append(spread(piece, lambda k, piece=piece: piece, (passed_piece, passed_piece)))
    for k in (3, 2):
        ff_in[k] = weights_to(k)
    feed = spread(fgx, lambda k: fg_all.at[k, 0], (fg_all.at[2, 0], fg_all.at[3, 0]))
    swaps = [net.start(fgx, fg_all.at[0, 1], core)]
    token_swaps = []
    for k, copy in zip((1, 2, 3), tokens_in):
        copy.wait_recv()
        piece = x_all.at[flip(c, k), t]
        token_swaps.append(net.start(piece, piece, core))
    halves = []

    def corner(k):
        zs = flip(z, k)
        for m, (one, two) in zip(parts[k], ff_out[k]):
            two.wait_recv()
            piece = wf_all.at[m, zs, flip(c, 2), pl.ds(0, 64)]
            halves.append(net.start(piece, piece, (z, flip(c, 1), t)))
            one.wait_recv()
            piece = wf_all.at[m, zs, flip(c, 1), pl.ds(64, 64)]
            halves.append(net.start(piece, piece, (z, flip(c, 2), t)))

    def onward(k):
        for m, copy in zip(parts[k], ff_in[k]):
            copy.wait_recv()
            pass_on(k, m)

    own[1].wait()
    own[3].wait()
    for copy in token_swaps + ends:
        copy.wait_recv()
    for i in range(2):
        gains[i : i + 1, :] = jnp.concatenate(
            [gain_all[a, b, i : i + 1, :].astype(f32) for a in range(4) for b in range(4)], axis=1
        )

    def norm_rows(i, carry):
        x = x_all[i].reshape(rows, width).astype(f32)
        inverse = lax.rsqrt(jnp.mean(x * x, axis=-1, keepdims=True) + norm_eps)
        normed[i] = (x * inverse * gains[0:1, :]).astype(bf16)
        return carry

    lax.fori_loop(0, 4, norm_rows, 0)
    save = [pltpu.make_async_copy(normed, normed_out, local.at[5])]
    save[0].start()
    onward(1)
    corner(0)
    for one, two, direct, passed in weights:
        two.wait_recv()
        pl.when(middle)(passed.start)
    for one, two, direct, passed in weights:
        one.wait_recv()
        direct.wait_recv()
    save.append(pltpu.make_async_copy(wa_all, wa_out, local.at[6]))
    save[1].start()

    def project(i, carry):
        here = pl.ds(pl.multiple_of(i * rows, rows), rows)
        w = wa_all[...].reshape(width, wa_all.shape[3])
        qkv = dot_tile(normed[i], w[:, :qkv_cols], 1, 0)
        cos_b, sin_b = cos[here, :], sin[here, :]
        quarter = low_lanes(cos_b.shape, HEAD // 2)
        half = low_lanes(cos_b.shape, HEAD)
        for p in range(q_cols // 128):
            block = qkv[:, p * 128 : (p + 1) * 128]
            q[here, p * 128 : (p + 1) * 128] = (block * cos_b + turn_lanes(block, quarter) * sin_b).astype(bf16)
        block = qkv[:, q_cols:]
        block = jnp.where(half, block * cos_b + turn_lanes(block, quarter) * sin_b, block)
        kv[here, :] = block.astype(bf16)
        for j, piece in enumerate(split_pair(block)):
            pairs[j, here, :] = piece.astype(bf16)
        return carry

    lax.fori_loop(0, 4, project, 0)
    corner(1)

    def attend(i):
        count = (i + 1) * rows
        here = pl.ds(i * rows, rows)
        keep = (seg_col[here, :] == seg_row[:, :count]) & (
            lax.broadcasted_iota(jnp.int32, (rows, count), 0) + i * rows
            >= lax.broadcasted_iota(jnp.int32, (rows, count), 1)
        )
        lane = lax.broadcasted_iota(jnp.int32, (rows, 128), 1)
        log_sums = jnp.zeros((rows, 128), f32)
        for p in range(q_cols // 128):
            out = jnp.zeros((rows, 128), f32)
            for e in range(2):
                scores = dot_tile(q[here, p * 128 : (p + 1) * 128], pairs[e, :count, :], 1, 1)
                scores = jnp.where(keep, scores * attention_mult, -1e30)
                highest = jnp.max(scores, axis=-1, keepdims=True)
                weight = jnp.exp(scores - highest)
                total = jnp.sum(weight, axis=-1, keepdims=True)
                out = out + dot_tile((weight / total).astype(bf16), pairs[2 + e, :count, :], 1, 0)
                log_sums = jnp.where(lane == 2 * p + e, highest + jnp.log(total), log_sums)
            attended[here, p * 128 : (p + 1) * 128] = out.astype(bf16)
        logs[here, :] = log_sums

    attend(0)
    attend(1)
    onward(3)
    attend(2)
    last = pl.ds(3 * rows, rows)
    both = (pairs[2, last, :] + pairs[3, last, :]).astype(bf16)
    for p in range(q_cols // 128):
        attended[last, p * 128 : (p + 1) * 128] = both
    corner(3)

    crosses, outs = {}, {}
    for k in (3, 1, 2, 0):
        mine_rows = pl.ds(pl.multiple_of(flip(c, k) * rows, rows), rows)

        def out_tile(n, carry, mine_rows=mine_rows):
            here = pl.ds(pl.multiple_of(n * 128, 128), 128)
            w = wa_all[lax.div(n, 4), lax.rem(n, 4), :, qkv_cols:]
            sums[:, here] = dot_tile(attended[mine_rows, :], w, 1, 1)
            return carry

        lax.fori_loop(0, width // 128, out_tile, 0)
        mine[k] = sums[pl.ds(pl.multiple_of(t * part, part), part), :]
        cross[k] = sums[pl.ds(pl.multiple_of((1 - t) * part, part), part), :].astype(bf16)
        crosses[k] = net.start(cross.at[k], crossed.at[k], core)
    for k in (3, 1, 2):
        crosses[k].wait_recv()
        totals[k - 1] = (mine[k] + crossed[k].astype(f32)).astype(bf16)
        outs[k] = net.start(totals.at[k - 1], landed.at[k - 1], (z, flip(c, k), t))
    onward(2)
    one, two, direct, passed = feed
    two.wait_recv()
    pl.when(middle)(passed.start)
    swaps.append(net.start(fg_all.at[2, 0], fg_all.at[2, 1], core))
    one.wait_recv()
    swaps.append(net.start(fg_all.at[1, 0], fg_all.at[1, 1], core))
    crosses[0].wait_recv()
    total = mine[0] + crossed[0].astype(f32)
    for k in (1, 2, 3):
        outs[k].wait_recv()
        total = total + landed[k - 1].astype(f32)
    hidden = xt[t].astype(f32) + residual_mult * total
    hidden_out[...] = hidden
    inverse = lax.rsqrt(jnp.mean(hidden * hidden, axis=-1, keepdims=True) + norm_eps)
    normed_two[...] = (hidden * inverse * gains[1:2, :]).astype(bf16)
    direct.wait_recv()
    swaps.append(net.start(fg_all.at[3, 0], fg_all.at[3, 1], core))
    corner(2)
    for copy in halves + swaps:
        copy.wait_recv()
    for _, _, direct, passed in weights + [feed]:
        pl.when(middle)(direct.wait_send)
        pl.when(middle)(passed.wait_send)
    for copy in net.started:
        copy.wait_send()
    own[4].wait()
    for copy in save:
        copy.wait()


def attention_forward(wa, wf, xt, gain, fgx, cos, sin, seg_col, seg_row):
    bf16, f32 = jnp.bfloat16, jnp.float32
    nt, part, width = xt.shape
    rows = nt * part
    total = 4 * rows
    wa_cols = wa.shape[2]
    q_cols = (wa_cols - 2 * HEAD) // 2
    filled = seg_col.shape[0]
    copies = 112
    vmem, anywhere = pl.BlockSpec(memory_space=pltpu.VMEM), pl.BlockSpec(memory_space=pl.ANY)
    outs = (
        ((4, 4) + wa.shape[1:], bf16, anywhere),
        ((3, 4, 4, wf.shape[1], wf.shape[2] // 4), bf16, anywhere),
        ((4, rows, width), bf16, anywhere),
        ((total, q_cols), bf16, vmem),
        ((total, 2 * HEAD), bf16, vmem),
        ((filled, 128), f32, vmem),
        ((total, q_cols), bf16, vmem),
        ((part, width), f32, vmem),
        ((part, width), bf16, vmem),
        ((4, nt, part, width), bf16, anywhere),
        ((2, width), f32, vmem),
    )
    return pl.pallas_call(
        attention_kernel,
        out_shape=[jax.ShapeDtypeStruct(shape, dtype) for shape, dtype, _ in outs],
        in_specs=[vmem] * 9,
        out_specs=[spec for _, _, spec in outs],
        scratch_shapes=[
            pltpu.VMEM((4, 4) + wa.shape[1:], bf16),
            pltpu.VMEM((4, nt, part, width), bf16),
            pltpu.VMEM((4, 4) + gain.shape, bf16),
            pltpu.VMEM((4, rows, width), bf16),
            pltpu.VMEM((4, total, 2 * HEAD), bf16),
            pltpu.VMEM((rows, width), f32),
            pltpu.VMEM((4, part, width), f32),
            pltpu.VMEM((4, part, width), bf16),
            pltpu.VMEM((4, part, width), bf16),
            pltpu.VMEM((3, part, width), bf16),
            pltpu.VMEM((3, part, width), bf16),
            pltpu.SemaphoreType.DMA((copies,)),
            pltpu.SemaphoreType.DMA((copies,)),
            pltpu.SemaphoreType.DMA((7,)),
        ],
        compiler_params=pltpu.CompilerParams(collective_id=1, has_side_effects=True, vmem_limit_bytes=60 * 2**20),
    )(wa, wf, xt, gain, fgx, cos, sin, seg_col, seg_row)


def feed_kernel(
    x, fg, w, back, feed_own, feed_send, terms,
    xs, wv, gate_g, up_g, inner, mine, cross, crossed, totals, landed, send, receive, local,
):
    f32, bf16 = jnp.float32, jnp.bfloat16
    z, c, t = (lax.axis_index(a) for a in (FSDP, CONTEXT, TENSOR))
    core = (z, c, 1 - t)
    greet([(flip(z, k), c, t) for k in (1, 2, 3)] + [core])
    net = Copies(send, receive)
    part, width = x.shape
    hidden = wv.shape[2]
    load = pltpu.make_async_copy(w, wv, local.at[0])
    load.start()
    middle = (z == 1) | (z == 2)
    swaps = {0: net.start(x, xs.at[0, 1], core)}
    arrive = {2: net.start(x, xs.at[2, 0], (flip(z, 2), c, t))}
    three = net.index()
    direct = net.make(three, x, xs.at[3, 0], (3 - z, c, t))
    pl.when(middle)(direct.start)
    arrive[3] = direct
    arrive[1] = net.start(x, xs.at[1, 0], (flip(z, 1), c, t))
    passed = pltpu.make_async_remote_copy(
        src_ref=xs.at[2, 0],
        dst_ref=xs.at[3, 0],
        send_sem=send.at[net.index()],
        recv_sem=receive.at[three],
        device_id=(flip(z, 1), c, t),
        device_id_type=pl.DeviceIdType.MESH,
    )
    xs[0, 0] = x[...]
    load.wait()

    def first(k):
        swaps[k].wait_recv()
        rows = xs[k].reshape(2 * part, width)
        grads = fg[k]

        def step(n, carry):
            at = pl.multiple_of(n * TILE, TILE)
            g = dot_tile(rows, wv[0, :, pl.ds(at, TILE)], 1, 0)
            u = dot_tile(rows, wv[1, :, pl.ds(at, TILE)], 1, 0)
            d = dot_tile(grads, wv[2, :, pl.ds(at, TILE)], 1, 0)
            sig = jax.nn.sigmoid(g)
            here = pl.ds(at, TILE)
            inner[k, :, here] = (g * sig * u).astype(bf16)
            gate_g[k, :, here] = (d * u * sig * (1.0 + g * (1.0 - sig))).astype(bf16)
            up_g[k, :, here] = (d * g * sig).astype(bf16)
            return carry

        lax.fori_loop(0, hidden // TILE, step, 0)

    crosses = {}

    def second(k):
        def step(n, carry):
            here = pl.ds(pl.multiple_of(n * TILE, TILE), TILE)
            b = dot_tile(gate_g[k], wv[0, here, :], 1, 1) + dot_tile(up_g[k], wv[1, here, :], 1, 1)
            f = dot_tile(inner[k], wv[2, here, :], 1, 1)
            mine[k, 0, :, here] = b[:part]
            mine[k, 1, :, here] = f[:part]
            cross[k, 0, :, here] = b[part:].astype(bf16)
            cross[k, 1, :, here] = f[part:].astype(bf16)
            return carry

        lax.fori_loop(0, width // TILE, step, 0)
        crosses[k] = net.start(cross.at[k], crossed.at[k], core)

    sums = {}

    def finish(k):
        crosses[k].wait_recv()
        if k:
            totals[k - 1] = (mine[k, 0] + crossed[k, 0].astype(f32)).astype(bf16)
            sums[k] = net.start(totals.at[k - 1], landed.at[k - 1], (flip(z, k), c, t))
            feed_send[k - 1] = (mine[k, 1] + crossed[k, 1].astype(f32)).astype(bf16)
        else:
            back[...] = mine[0, 0] + crossed[0, 0].astype(f32)
            feed_own[...] = mine[0, 1] + crossed[0, 1].astype(f32)

    def fetch(k):
        arrive[k].wait_recv()
        if k == 2:
            pl.when(middle)(passed.start)
        swaps[k] = net.start(xs.at[k, 0], xs.at[k, 1], core)

    order = (0, 2, 3, 1)
    for i, k in enumerate(order):
        first(k)
        if i:
            finish(order[i - 1])
        if i < 3:
            fetch(order[i + 1])
        second(k)

    rows = xs.shape[0] * 2 * part

    def term(source, grads, i):
        def step(m, carry):
            here = pl.ds(pl.multiple_of(m * TILE, TILE), TILE)
            left = source[:, :, here].reshape(rows, TILE)
            value = dot_tile(left, grads[...].reshape(rows, hidden), 0, 0)
            wv[i, here, :] = value.astype(bf16)
            return carry

        lax.fori_loop(0, width // TILE, step, 0)

    flat = xs.reshape(xs.shape[0], 2 * part, width)
    term(flat, gate_g, 0)
    finish(order[3])
    term(flat, up_g, 1)
    term(fg, inner, 2)
    store = pltpu.make_async_copy(wv, terms, local.at[1])
    store.start()
    for k in (1, 2, 3):
        sums[k].wait_recv()
    back[...] = back[...] + landed[0].astype(f32) + landed[1].astype(f32) + landed[2].astype(f32)
    pl.when(middle)(direct.wait_send)
    pl.when(middle)(passed.wait_send)
    for copy in net.started:
        copy.wait_send()
    store.wait()


def feed_forward(x, fg, w):
    bf16, f32 = jnp.bfloat16, jnp.float32
    part, width = x.shape
    hidden = w.shape[2]
    blocks = fg.shape[0]
    copies = 20
    vmem, anywhere = pl.BlockSpec(memory_space=pltpu.VMEM), pl.BlockSpec(memory_space=pl.ANY)
    return pl.pallas_call(
        feed_kernel,
        out_shape=[
            jax.ShapeDtypeStruct((part, width), f32),
            jax.ShapeDtypeStruct((part, width), f32),
            jax.ShapeDtypeStruct((blocks - 1, part, width), bf16),
            jax.ShapeDtypeStruct(w.shape, bf16),
        ],
        in_specs=[vmem, vmem, anywhere],
        out_specs=[vmem, vmem, vmem, anywhere],
        scratch_shapes=[
            pltpu.VMEM((blocks, 2, part, width), bf16),
            pltpu.VMEM(w.shape, bf16),
            pltpu.VMEM((blocks, 2 * part, hidden), bf16),
            pltpu.VMEM((blocks, 2 * part, hidden), bf16),
            pltpu.VMEM((blocks, 2 * part, hidden), bf16),
            pltpu.VMEM((blocks, 2, part, width), f32),
            pltpu.VMEM((blocks, 2, part, width), bf16),
            pltpu.VMEM((blocks, 2, part, width), bf16),
            pltpu.VMEM((blocks - 1, part, width), bf16),
            pltpu.VMEM((blocks - 1, part, width), bf16),
            pltpu.SemaphoreType.DMA((copies,)),
            pltpu.SemaphoreType.DMA((copies,)),
            pltpu.SemaphoreType.DMA((2,)),
        ],
        compiler_params=pltpu.CompilerParams(collective_id=3, has_side_effects=True, vmem_limit_bytes=62 * 2**20),
    )(x, fg, w)


def swap(x, axis, k):
    return lax.ppermute(x, axis, [(i, i ^ k) for i in range(lax.axis_size(axis))])


def cut(x, index, size, axis):
    return lax.dynamic_slice_in_dim(x, index * size, size, axis)


def backward_kernel(
    ff, fs, al, wa_in, normed_in, q, kv, logs, attended, cos, sin, seg_col, seg_row,
    feed_in, back_own, back_in, ff_out, query_out, kv_out, output_out,
    terms, corner_x, corner_y, side_x, side_y, at_terms, at_in, at_total, wa, normed, ag, pairs, mixed, acc, dqkv,
    sums, mine, cross, crossed, totals, send, receive, local,
):
    f32, bf16 = jnp.float32, jnp.bfloat16
    z, c, t = (lax.axis_index(a) for a in (FSDP, CONTEXT, TENSOR))
    core = (z, c, 1 - t)
    greet([(flip(z, k), c, t) for k in (1, 2, 3)] + [(z, flip(c, k), t) for k in (1, 2, 3)] + [core])
    net = Copies(send, receive)
    wrows, hidden = ff.shape[3:]
    half = wrows // 2
    part, width = al.shape
    rows = 2 * part
    q_cols = q.shape[1]
    qkv_cols = q_cols + 2 * HEAD
    blocks = normed.shape[0]
    order = (3, 2, 1, 0)
    loads = {}
    for k in order:
        zs = flip(z, k)
        loads[k] = pltpu.make_async_copy(ff.at[:, zs], terms.at[:, zs], local.at[k])
        loads[k].start()
    wa_load = pltpu.make_async_copy(wa_in, wa, local.at[4])
    wa_load.start()
    normed_load = pltpu.make_async_copy(normed_in.at[pl.ds(0, blocks)], normed, local.at[5])
    normed_load.start()
    first = {}

    def corners(k):
        zs = flip(z, k)
        loads[k].wait()
        first[k] = (
            net.start(terms.at[:, zs, flip(c, 3), pl.ds(0, half)], corner_x.at[k], (z, flip(c, 1), t)),
            net.start(terms.at[:, zs, flip(c, 3), pl.ds(half, half)], corner_y.at[k], (z, flip(c, 2), t)),
        )

    corners(3)
    ag_in = [net.start(al, ag.at[c, t], (z, flip(c, k), t)) for k in (3, 1, 2)]
    swaps = [net.start(al, ag.at[c, t], core)]
    feed = [net.start(fs.at[k - 1], feed_in.at[k - 1], (flip(z, k), c, t)) for k in (3, 2, 1)]
    corners(2)
    ag[c, t] = al[...]
    for j, piece in enumerate(split_pair(kv[...].astype(f32))):
        pairs[j] = piece.astype(bf16)
    acc[...] = jnp.zeros_like(acc)
    dqkv[pl.ds(blocks * rows, rows), :] = jnp.zeros((rows, qkv_cols), bf16)
    for k, copy in zip((3, 1, 2), ag_in):
        copy.wait_recv()
        piece = ag.at[flip(c, k), t]
        swaps.append(net.start(piece, piece, core))
    second, third = {}, {}

    def sides(k):
        zs = flip(z, k)
        for copy in first[k]:
            copy.wait_recv()
        low, high = pl.ds(0, half), pl.ds(half, half)
        xb, yb = flip(c, 1), flip(c, 2)
        for m in range(3):
            terms[m, zs, yb, low] = (terms[m, zs, yb, low].astype(f32) + corner_x[k, m].astype(f32)).astype(bf16)
            terms[m, zs, xb, high] = (terms[m, zs, xb, high].astype(f32) + corner_y[k, m].astype(f32)).astype(bf16)
        second[k] = (
            net.start(terms.at[:, zs, yb], side_y.at[k], (z, yb, t)),
            net.start(terms.at[:, zs, xb], side_x.at[k], (z, xb, t)),
        )

    def owners(k):
        zs = flip(z, k)
        for copy in second[k]:
            copy.wait_recv()
        for m in range(3):
            total = terms[m, zs, c].astype(f32) + side_x[k, m].astype(f32) + side_y[k, m].astype(f32)
            terms[m, zs, c] = total.astype(bf16)
        columns = ff_out.at[:, :, pl.ds(pl.multiple_of(z * hidden, hidden), hidden)]
        if k:
            third[k] = net.start(terms.at[:, zs, c], columns, (zs, c, t))
        else:
            third[0] = pltpu.make_async_copy(terms.at[:, z, c], columns, local.at[6])
            third[0].start()

    for copy in swaps:
        copy.wait_recv()
    wa_load.wait()
    normed_load.wait()

    def mix(i, carry):
        w = wa[...].reshape(width, wa.shape[3])[:, qkv_cols:]
        here = pl.ds(pl.multiple_of(i * rows, rows), rows)
        mixed[here, :] = dot_tile(ag[i].reshape(rows, width), w, 1, 0).astype(bf16)
        return carry

    lax.fori_loop(0, blocks, mix, 0)
    sides(3)
    corners(1)

    def out_term(m, carry):
        here = pl.ds(pl.multiple_of(m * wrows, wrows), wrows)
        left = ag[0:blocks, :, :, here].reshape(blocks * rows, wrows)
        value = dot_tile(left, attended[0 : blocks * rows, :], 0, 0)
        at_terms[lax.div(m, 4), lax.rem(m, 4), :, qkv_cols:] = value.astype(bf16)
        return carry

    lax.fori_loop(0, width // wrows, out_term, 0)

    def terms_to(columns):
        return [
            net.start(
                at_terms.at[flip(z, k), :, :, columns], at_in.at[k - 1, :, :, columns], (flip(z, k), c, t)
            )
            for k in (3, 2, 1)
        ]

    attn_in = terms_to(pl.ds(qkv_cols, q_cols))
    sides(2)
    corners(0)

    def attend(i):
        count = (i + 1) * rows
        here = pl.ds(i * rows, rows)
        keep = (seg_col[here, :] == seg_row[:, :count]) & (
            lax.broadcasted_iota(jnp.int32, (rows, count), 0) + i * rows
            >= lax.broadcasted_iota(jnp.int32, (rows, count), 1)
        )
        log_sums = logs[here, :]
        lane = lax.broadcasted_iota(jnp.int32, (rows, 128), 1)
        cos_b, sin_b = cos[here, :], sin[here, :]
        quarter = low_lanes(cos_b.shape, HEAD // 2)
        for p in range(q_cols // 128):
            block = slice(p * 128, (p + 1) * 128)
            grad = jnp.zeros((rows, 128), f32)
            for e in range(2):
                scores = dot_tile(q[here, block], pairs[e, :count, :], 1, 1)
                scores = jnp.where(keep, scores * attention_mult, -1e30)
                log = jnp.sum(jnp.where(lane == 2 * p + e, log_sums, 0.0), axis=-1, keepdims=True)
                prob = jnp.exp(scores - log)
                prob_grad = dot_tile(mixed[here, block], pairs[2 + e, :count, :], 1, 1)
                row_dot = jnp.sum(prob * prob_grad, axis=-1, keepdims=True)
                score_grad = (attention_mult * prob * (prob_grad - row_dot)).astype(bf16)
                grad = grad + dot_tile(score_grad, pairs[e, :count, :], 1, 0)
                acc[e, :count, :] += dot_tile(score_grad, q[here, block], 0, 0)
                acc[2 + e, :count, :] += dot_tile(prob.astype(bf16), mixed[here, block], 0, 0)
            dqkv[here, block] = (grad * cos_b + turn_lanes(grad * sin_b, quarter)).astype(bf16)

    attend(0)
    attend(1)
    owners(3)
    sides(1)
    attend(2)
    sides(0)
    owners(2)
    filled = blocks * rows
    low = low_lanes((filled, 128), HEAD)
    key_grad = jnp.where(low, acc[0], 0.0) + pltpu.roll(jnp.where(low, 0.0, acc[1]), HEAD, 1)
    value_grad = jnp.where(low, 0.0, acc[3]) + pltpu.roll(jnp.where(low, acc[2], 0.0), HEAD, 1)
    turned = turn_lanes(key_grad * sin[0:filled, :], low_lanes((filled, 128), HEAD // 2))
    key_grad = key_grad * cos[0:filled, :] + turned
    dqkv[0:filled, q_cols:] = jnp.where(low, key_grad, value_grad).astype(bf16)

    crosses, outs = {}, {}
    for k in (3, 1, 2, 0):
        mine_rows = pl.ds(pl.multiple_of(flip(c, k) * rows, rows), rows)

        def back_tile(n, carry, mine_rows=mine_rows):
            here = pl.ds(pl.multiple_of(n * 128, 128), 128)
            w = wa[lax.div(n, 4), lax.rem(n, 4), :, :qkv_cols]
            sums[:, here] = dot_tile(dqkv[mine_rows, :], w, 1, 1)
            return carry

        lax.fori_loop(0, width // 128, back_tile, 0)
        mine[k] = sums[pl.ds(pl.multiple_of(t * part, part), part), :]
        cross[k] = sums[pl.ds(pl.multiple_of((1 - t) * part, part), part), :].astype(bf16)
        crosses[k] = net.start(cross.at[k], crossed.at[k], core)
    for k in (3, 1, 2):
        crosses[k].wait_recv()
        totals[k - 1] = (mine[k] + crossed[k].astype(f32)).astype(bf16)
        outs[k] = net.start(totals.at[k - 1], back_in.at[k - 1], (z, flip(c, k), t))
    crosses[0].wait_recv()
    back_own[...] = mine[0] + crossed[0].astype(f32)

    def qkv_term(m, carry):
        here = pl.ds(pl.multiple_of(m * wrows, wrows), wrows)
        left = normed[:, :, here].reshape(filled, wrows)
        value = dot_tile(left, dqkv[0:filled, :], 0, 0)
        at_terms[lax.div(m, 4), lax.rem(m, 4), :, :qkv_cols] = value.astype(bf16)
        return carry

    lax.fori_loop(0, width // wrows, qkv_term, 0)
    attn_in += terms_to(pl.ds(0, qkv_cols))
    owners(1)
    owners(0)
    for copy in attn_in:
        copy.wait_recv()
    for j in range(4):
        total = at_terms[z, j].astype(f32)
        for i in range(3):
            total = total + at_in[i, j].astype(f32)
        at_total[j] = total.astype(bf16)
    here = pl.ds(pl.multiple_of(c * q_cols, q_cols), q_cols)
    attn_out, keep_own = [], []
    for i, (columns, target) in enumerate(
        (
            (pl.ds(0, q_cols), query_out.at[:, here]),
            (pl.ds(q_cols, 2 * HEAD), kv_out.at[c]),
            (pl.ds(qkv_cols, q_cols), output_out.at[:, here]),
        )
    ):
        attn_out += [net.start(at_total.at[flip(c, k), :, columns], target, (z, flip(c, k), t)) for k in (1, 2, 3)]
        keep_own.append(pltpu.make_async_copy(at_total.at[c, :, columns], target, local.at[7 + i]))
        keep_own[-1].start()
    for copy in feed + attn_out + [outs[k] for k in (1, 2, 3)] + [third[k] for k in (1, 2, 3)]:
        copy.wait_recv()
    for copy in net.started:
        copy.wait_send()
    third[0].wait()
    for copy in keep_own:
        copy.wait()


def backward(ff, fs, al, wa, normed, q, kv, logs, attended, cos, sin, seg_col, seg_row):
    bf16, f32 = jnp.bfloat16, jnp.float32
    wrows, hidden = ff.shape[3:]
    attn_cols = wa.shape[3]
    part, width = al.shape
    total = q.shape[0]
    filled = seg_col.shape[0]
    rows = 2 * part
    blocks = filled // rows
    copies = 64
    vmem, anywhere = pl.BlockSpec(memory_space=pltpu.VMEM), pl.BlockSpec(memory_space=pl.ANY)
    return pl.pallas_call(
        backward_kernel,
        out_shape=[
            jax.ShapeDtypeStruct(fs.shape, bf16),
            jax.ShapeDtypeStruct(al.shape, f32),
            jax.ShapeDtypeStruct(fs.shape, bf16),
            jax.ShapeDtypeStruct((3, wrows, 4 * hidden), bf16),
            jax.ShapeDtypeStruct((wrows, 4 * q.shape[1]), bf16),
            jax.ShapeDtypeStruct((4, wrows, 2 * HEAD), bf16),
            jax.ShapeDtypeStruct((wrows, 4 * q.shape[1]), bf16),
        ],
        in_specs=[anywhere, vmem, vmem, anywhere, anywhere] + [vmem] * 8,
        out_specs=[anywhere, vmem] + [anywhere] * 5,
        scratch_shapes=[
            pltpu.VMEM(ff.shape, bf16),
            pltpu.VMEM((4, 3, wrows // 2, hidden), bf16),
            pltpu.VMEM((4, 3, wrows // 2, hidden), bf16),
            pltpu.VMEM((4, 3, wrows, hidden), bf16),
            pltpu.VMEM((4, 3, wrows, hidden), bf16),
            pltpu.VMEM((4, 4, wrows, attn_cols), bf16),
            pltpu.VMEM((3, 4, wrows, attn_cols), bf16),
            pltpu.VMEM((4, wrows, attn_cols), bf16),
            pltpu.VMEM(wa.shape, bf16),
            pltpu.VMEM((blocks, rows, width), bf16),
            pltpu.VMEM((4, 2, part, width), bf16),
            pltpu.VMEM((4, total, 2 * HEAD), bf16),
            pltpu.VMEM((filled, q.shape[1]), bf16),
            pltpu.VMEM((4, filled, 2 * HEAD), f32),
            pltpu.VMEM((total, q.shape[1] + 2 * HEAD), bf16),
            pltpu.VMEM((rows, width), f32),
            pltpu.VMEM((4, part, width), f32),
            pltpu.VMEM((4, part, width), bf16),
            pltpu.VMEM((4, part, width), bf16),
            pltpu.VMEM((3, part, width), bf16),
            pltpu.SemaphoreType.DMA((copies,)),
            pltpu.SemaphoreType.DMA((copies,)),
            pltpu.SemaphoreType.DMA((10,)),
        ],
        compiler_params=pltpu.CompilerParams(collective_id=2, has_side_effects=True, vmem_limit_bytes=63 * 2**20),
    )(ff, fs, al, wa, normed, q, kv, logs, attended, cos, sin, seg_col, seg_row)


def on_device_split(
    tokens,
    out_grad,
    lengths,
    attention_gain,
    query_weight,
    key_weight,
    value_weight,
    output_weight,
    feed_gain,
    gate_weight,
    up_weight,
    down_weight,
):
    f32, bf16 = jnp.float32, jnp.bfloat16
    nz, nc, nt = (lax.axis_size(a) for a in (FSDP, CONTEXT, TENSOR))
    z, c, t = (lax.axis_index(a) for a in (FSDP, CONTEXT, TENSOR))
    local_rows, width = tokens.shape[1:]
    group_rows = local_rows * nc
    filled = group_rows * 3 // 4
    part = local_rows // nt
    wrows = query_weight.shape[0]
    kv_cols = key_weight.shape[1] // nc
    q_cols = query_weight.shape[1] // nc
    qkv_cols = q_cols + 2 * kv_cols
    ff_cols = gate_weight.shape[1] // nz
    per_group = q_cols // kv_cols
    segment, position, valid_rows = slot_layout(lengths[0], group_rows)
    cos_table, sine_table = rope_tables(position, HEAD)

    wa = jnp.concatenate(
        [
            w.astype(bf16).reshape(wrows, nc, -1).transpose(1, 0, 2)
            for w in (query_weight, key_weight, value_weight, output_weight)
        ],
        axis=2,
    )
    wf = jnp.stack([w.astype(bf16) for w in (gate_weight, up_weight, down_weight)])
    gain = jnp.pad(jnp.stack([attention_gain, feed_gain]).astype(bf16), ((0, 14), (0, 0)))
    my_valid = lax.dynamic_slice_in_dim(valid_rows, c * local_rows + t * part, part)
    cotangent = cut(out_grad[0], t, part, 0).astype(f32) * my_valid[:, None].astype(f32)
    feed_grad = (residual_mult * cotangent).astype(bf16)
    sign = jnp.where(jnp.arange(HEAD) < HEAD // 2, -1.0, 1.0).astype(f32)
    wide_cos = jnp.concatenate([cos_table, cos_table], axis=1)
    wide_sin = jnp.concatenate([sine_table * sign, sine_table * sign], axis=1)
    wa, wf, normed_one, queries, pair, logs, attended, hidden, normed_two, feed_grads, gains = attention_forward(
        wa, wf, tokens[0].reshape(nt, part, width), gain, feed_grad, wide_cos, wide_sin,
        segment[:filled, None], segment[None, :filled],
    )
    gain_one, gain_two = gains[0], gains[1]
    w_feed = wf.reshape(3, width, ff_cols)
    my_inputs = cut(tokens[0], t, part, 0).astype(f32)
    inverse_two = lax.rsqrt(jnp.mean(hidden * hidden, axis=-1, keepdims=True) + norm_eps)
    unit_two = hidden * inverse_two

    normed_grad_two, feed_own, feed_send, ff_terms = feed_forward(
        normed_two, feed_grads.reshape(nz, local_rows, width), w_feed
    )
    ff_terms = ff_terms.reshape(3, nz, nc, wrows, ff_cols)

    def both_cores(x):
        other = swap(x, TENSOR, 1)
        first, last = jnp.where(t == 0, x, other), jnp.where(t == 0, other, x)
        return jnp.concatenate([first, last], axis=0)[None]

    feed_gain_term = jnp.sum(normed_grad_two * unit_two, axis=0)
    hidden_grad = cotangent + norm_back(normed_grad_two, unit_two, gain_two, inverse_two)

    attn_low = (residual_mult * hidden_grad).astype(bf16)
    feed_in, back_own, back_in, ff_grads, grad_query, kv_grads, grad_output = backward(
        ff_terms, feed_send, attn_low, wa, normed_one, queries, pair, logs, attended, wide_cos, wide_sin,
        segment[:filled, None], segment[None, :filled],
    )
    output = both_cores((hidden + residual_mult * (feed_own + jnp.sum(feed_in.astype(f32), axis=0))).astype(bf16))
    normed_grad_one = back_own + jnp.sum(back_in.astype(f32), axis=0)
    inverse_one = lax.rsqrt(jnp.mean(my_inputs * my_inputs, axis=-1, keepdims=True) + norm_eps)
    unit_one = my_inputs * inverse_one
    attn_gain_term = jnp.sum(normed_grad_one * unit_one, axis=0)
    input_grad = both_cores((hidden_grad + norm_back(normed_grad_one, unit_one, gain_one, inverse_one)).astype(bf16))

    gain_terms = jnp.stack([attn_gain_term, feed_gain_term])
    for axis in (TENSOR, CONTEXT, FSDP):
        gain_terms = gain_terms + sum(swap(gain_terms, axis, k) for k in range(1, lax.axis_size(axis)))
    gain_terms = cut(gain_terms, z * nc + c, wrows, 1)

    grad_gate, grad_up, grad_down = (ff_grads[i].astype(f32) for i in range(3))
    grad_key, grad_value = (
        kv_grads[:, :, i : i + HEAD].transpose(1, 0, 2).reshape(wrows, -1).astype(f32) for i in (0, HEAD)
    )
    attn_terms = (grad_query.astype(f32), grad_key, grad_value, grad_output.astype(f32))
    return (output, input_grad, gain_terms[0], *attn_terms, gain_terms[1], grad_gate, grad_up, grad_down)


def solution(mesh):
    split = tuple(mesh.shape[a] for a in (FSDP, CONTEXT, TENSOR)) == (4, 4, 2)
    return jax.shard_map(
        on_device_split if split else on_device,
        mesh=mesh,
        in_specs=(
            P(FSDP, CONTEXT, None),
            P(FSDP, CONTEXT, None),
            P(FSDP, None),
            P((FSDP, CONTEXT)),
            P((FSDP, CONTEXT), TENSOR),
            P((FSDP, CONTEXT), TENSOR),
            P((FSDP, CONTEXT), TENSOR),
            P((FSDP, CONTEXT), TENSOR),
            P((FSDP, CONTEXT)),
            P((FSDP, CONTEXT), TENSOR),
            P((FSDP, CONTEXT), TENSOR),
            P((FSDP, CONTEXT), TENSOR),
        ),
        out_specs=(
            P(FSDP, CONTEXT, None),
            P(FSDP, CONTEXT, None),
            P((FSDP, CONTEXT)),
            P((FSDP, CONTEXT), TENSOR),
            P((FSDP, CONTEXT), TENSOR),
            P((FSDP, CONTEXT), TENSOR),
            P((FSDP, CONTEXT), TENSOR),
            P((FSDP, CONTEXT)),
            P((FSDP, CONTEXT), TENSOR),
            P((FSDP, CONTEXT), TENSOR),
            P((FSDP, CONTEXT), TENSOR),
        ),
        check_vma=False,
    )
```

```python
import jax
import jax.numpy as jnp
from jax import lax
from jax.experimental import pallas as pl
from jax.experimental.pallas import tpu as pltpu
from jax.sharding import PartitionSpec as P

HEAD = 64
FSDP, CONTEXT, TENSOR = "fsdp", "context", "tensor"


norm_eps = 1e-05
attention_mult = 0.015625
residual_mult = 0.22
rope_base = 10000000.0


def slot_layout(seq_lengths, total_rows):
    seq_ends = jnp.cumsum(seq_lengths)
    starts = seq_ends - seq_lengths
    slot_ids = jnp.arange(total_rows, dtype=jnp.int32)
    before = (slot_ids[:, None] >= seq_ends[None, :]).astype(jnp.int32)
    segment = jnp.sum(before, axis=1)
    seq_count = seq_lengths.shape[0]
    valid_rows = segment < seq_count
    inside = (slot_ids[:, None] >= starts[None, :]) & (slot_ids[:, None] < seq_ends[None, :])
    position = jnp.sum(jnp.where(inside, slot_ids[:, None] - starts[None, :], 0), axis=1)
    segment = jnp.where(valid_rows, segment, seq_count + slot_ids)
    return (segment, position, valid_rows)


def rope_tables(position, width):
    half_width = width // 2
    frequency = rope_base ** (-jnp.arange(half_width, dtype=jnp.float32) * 2.0 / width)
    angles = position.astype(jnp.float32)[:, None] * frequency[None, :]
    angles = jnp.concatenate([angles, angles], axis=1)
    return (jnp.cos(angles), jnp.sin(angles))


def turn_half(vectors):
    half_width = vectors.shape[-1] // 2
    return jnp.concatenate([-vectors[..., half_width:], vectors[..., :half_width]], axis=-1)


def rotate(vectors, cos_table, sine_table):
    return vectors * cos_table[:, None, :] + turn_half(vectors) * sine_table[:, None, :]


def rotate_back(grads, cos_table, sine_table):
    return grads * cos_table[:, None, :] - turn_half(grads * sine_table[:, None, :])


def norm_back(normed_grad, unit, gain, inverse):
    scaled = normed_grad * gain
    return inverse * (scaled - unit * jnp.mean(scaled * unit, axis=-1, keepdims=True))


def dot_first(left, right):
    return lax.dot_general(left, right, (((0,), (0,)), ((), ())), preferred_element_type=jnp.float32)


def dot_last(left, right):
    return lax.dot_general(left, right, (((1,), (1,)), ((), ())), preferred_element_type=jnp.float32)


def attention_shards(attention_gain, query_weight, key_weight, value_weight, output_weight):
    return (
        lax.all_gather(
            attention_gain.astype(jnp.bfloat16), (FSDP, CONTEXT), axis=0, tiled=True
        ),
        lax.all_gather(query_weight.astype(jnp.bfloat16), (FSDP, CONTEXT), axis=0, tiled=True),
        lax.all_gather(key_weight.astype(jnp.bfloat16), (FSDP, CONTEXT), axis=0, tiled=True),
        lax.all_gather(value_weight.astype(jnp.bfloat16), (FSDP, CONTEXT), axis=0, tiled=True),
        lax.all_gather(output_weight.astype(jnp.bfloat16), (FSDP, CONTEXT), axis=0, tiled=True),
    )


def feed_shards(feed_gain, gate_weight, up_weight, down_weight):
    return (
        lax.all_gather(feed_gain.astype(jnp.bfloat16), (FSDP, CONTEXT), axis=0, tiled=True),
        lax.all_gather(gate_weight.astype(jnp.bfloat16), (FSDP, CONTEXT), axis=0, tiled=True),
        lax.all_gather(up_weight.astype(jnp.bfloat16), (FSDP, CONTEXT), axis=0, tiled=True),
        lax.all_gather(down_weight.astype(jnp.bfloat16), (FSDP, CONTEXT), axis=0, tiled=True),
    )


def on_device(
    tokens,
    out_grad,
    lengths,
    attention_gain,
    query_weight,
    key_weight,
    value_weight,
    output_weight,
    feed_gain,
    gate_weight,
    up_weight,
    down_weight,
):
    local_rows = tokens.shape[1]
    group_rows = local_rows * lax.axis_size(CONTEXT)
    first_row = lax.axis_index(CONTEXT) * local_rows
    segment, position, valid_rows = slot_layout(lengths[0], group_rows)
    local_segment = lax.dynamic_slice_in_dim(segment, first_row, local_rows)
    local_position = lax.dynamic_slice_in_dim(position, first_row, local_rows)
    local_valid = lax.dynamic_slice_in_dim(valid_rows, first_row, local_rows)
    slot_ids = jnp.arange(group_rows, dtype=jnp.int32)
    local_slots = first_row + jnp.arange(local_rows, dtype=jnp.int32)
    allowed = (local_segment[:, None] == segment[None, :]) & (
        local_slots[:, None] >= slot_ids[None, :]
    )
    inputs = tokens[0].astype(jnp.float32)
    attn_set = attention_shards(
        attention_gain, query_weight, key_weight, value_weight, output_weight
    )
    gain_one = attn_set[0].astype(jnp.float32)
    inverse_one = lax.rsqrt(jnp.mean(inputs * inputs, axis=-1, keepdims=True) + norm_eps)
    unit_one = inputs * inverse_one
    normed_one = (unit_one * gain_one).astype(jnp.bfloat16)
    queries = jnp.dot(normed_one, attn_set[1], preferred_element_type=jnp.float32)
    keys_lin = jnp.dot(normed_one, attn_set[2], preferred_element_type=jnp.float32)
    values_low = jnp.dot(normed_one, attn_set[3], preferred_element_type=jnp.float32).astype(
        jnp.bfloat16
    )
    heads_local = queries.shape[1] // HEAD
    kv_local = keys_lin.shape[1] // HEAD
    per_group = heads_local // kv_local
    cos_table, sine_table = rope_tables(local_position, HEAD)
    queries_rot = rotate(
        queries.reshape(local_rows, heads_local, HEAD), cos_table, sine_table
    ).astype(jnp.bfloat16)
    keys_rot = rotate(keys_lin.reshape(local_rows, kv_local, HEAD), cos_table, sine_table).astype(
        jnp.bfloat16
    )
    keys_all, values_all = (
        lax.all_gather(
            keys_rot.reshape(local_rows, kv_local * HEAD), CONTEXT, axis=0, tiled=True
        ),
        lax.all_gather(values_low, CONTEXT, axis=0, tiled=True),
    )
    query_heads = queries_rot.reshape(local_rows, kv_local, per_group, HEAD).transpose(1, 0, 2, 3)
    key_heads = keys_all.reshape(group_rows, kv_local, HEAD).transpose(1, 0, 2)
    value_heads = values_all.reshape(group_rows, kv_local, HEAD).transpose(1, 0, 2)

    def head_scores(query_head, key_head):
        raw_scores = jnp.einsum(
            "tgd,sd->gts", query_head, key_head, preferred_element_type=jnp.float32
        )
        return jnp.where(allowed[None], raw_scores * attention_mult, -1e30)

    def head_forward(pieces):
        query_head, key_head, value_head = pieces
        scores = head_scores(query_head, key_head)
        highest = jnp.max(scores, axis=-1, keepdims=True)
        weight = jnp.exp(scores - highest)
        row_totals = jnp.sum(weight, axis=-1, keepdims=True)
        probabilities = (weight / row_totals).astype(jnp.bfloat16)
        mixed = jnp.einsum(
            "gts,sd->tgd", probabilities, value_head, preferred_element_type=jnp.float32
        )
        return (mixed, (highest + jnp.log(row_totals))[..., 0])

    mixed_heads, log_totals = lax.map(head_forward, (query_heads, key_heads, value_heads))
    attended = (
        mixed_heads.transpose(1, 0, 2, 3)
        .reshape(local_rows, heads_local * HEAD)
        .astype(jnp.bfloat16)
    )
    attn_part = dot_last(attended, attn_set[4])
    attn_out = lax.psum(attn_part.astype(jnp.bfloat16), TENSOR).astype(jnp.float32)
    hidden_state = inputs + residual_mult * attn_out
    feed_set = feed_shards(feed_gain, gate_weight, up_weight, down_weight)
    gain_two = feed_set[0].astype(jnp.float32)
    inverse_two = lax.rsqrt(
        jnp.mean(hidden_state * hidden_state, axis=-1, keepdims=True) + norm_eps
    )
    unit_two = hidden_state * inverse_two
    normed_two = (unit_two * gain_two).astype(jnp.bfloat16)
    gate_out = jnp.dot(normed_two, feed_set[1], preferred_element_type=jnp.float32)
    up_out = jnp.dot(normed_two, feed_set[2], preferred_element_type=jnp.float32)
    inner_act = (jax.nn.silu(gate_out) * up_out).astype(jnp.bfloat16)
    feed_part = dot_last(inner_act, feed_set[3])
    feed_out = lax.psum(feed_part.astype(jnp.bfloat16), TENSOR).astype(jnp.float32)
    output = hidden_state + residual_mult * feed_out
    cotangent = out_grad[0].astype(jnp.float32) * local_valid[:, None].astype(jnp.float32)
    feed_back = feed_shards(feed_gain, gate_weight, up_weight, down_weight)
    feed_grad = (residual_mult * cotangent).astype(jnp.bfloat16)
    down_term = dot_first(feed_grad, inner_act)
    inner_grad = jnp.dot(feed_grad, feed_back[3], preferred_element_type=jnp.float32)
    sigmoid_gate = jax.nn.sigmoid(gate_out)
    gate_grad = (
        inner_grad * up_out * sigmoid_gate * (1.0 + gate_out * (1.0 - sigmoid_gate))
    ).astype(jnp.bfloat16)
    up_grad = (inner_grad * jax.nn.silu(gate_out)).astype(jnp.bfloat16)
    gate_term = dot_first(normed_two, gate_grad)
    up_term = dot_first(normed_two, up_grad)
    normed_part_two = dot_last(gate_grad, feed_back[1])
    normed_part_two = normed_part_two + dot_last(up_grad, feed_back[2])
    normed_grad_two = lax.psum(normed_part_two.astype(jnp.bfloat16), TENSOR).astype(jnp.float32)
    feed_gain_term = jnp.sum(normed_grad_two * unit_two, axis=0)
    hidden_grad = cotangent + norm_back(normed_grad_two, unit_two, gain_two, inverse_two)
    feed_sums = (
        lax.psum_scatter(feed_gain_term, (FSDP, CONTEXT), scatter_dimension=0, tiled=True),
        lax.psum_scatter(gate_term, (FSDP, CONTEXT), scatter_dimension=0, tiled=True),
        lax.psum_scatter(up_term, (FSDP, CONTEXT), scatter_dimension=0, tiled=True),
        lax.psum_scatter(down_term, (FSDP, CONTEXT), scatter_dimension=0, tiled=True),
    )
    attn_back = attention_shards(
        attention_gain, query_weight, key_weight, value_weight, output_weight
    )
    attn_grad = (residual_mult * hidden_grad).astype(jnp.bfloat16)
    out_term = dot_first(attn_grad, attended)
    mixed_grad = jnp.dot(attn_grad, attn_back[4], preferred_element_type=jnp.float32).astype(
        jnp.bfloat16
    )
    mixed_grad_heads = mixed_grad.reshape(local_rows, kv_local, per_group, HEAD).transpose(
        1, 0, 2, 3
    )

    def head_backward(pieces):
        query_head, key_head, value_head, grad_head, log_head = pieces
        scores = head_scores(query_head, key_head)
        probabilities = jnp.exp(scores - log_head[..., None])
        prob_low = probabilities.astype(jnp.bfloat16)
        prob_grad = jnp.einsum(
            "tgd,sd->gts", grad_head, value_head, preferred_element_type=jnp.float32
        )
        row_dot = jnp.sum(probabilities * prob_grad, axis=-1, keepdims=True)
        score_grad = (attention_mult * probabilities * (prob_grad - row_dot)).astype(jnp.bfloat16)
        query_grad = jnp.einsum(
            "gts,sd->tgd", score_grad, key_head, preferred_element_type=jnp.float32
        )
        key_grad = jnp.einsum(
            "gts,tgd->sd", score_grad, query_head, preferred_element_type=jnp.float32
        )
        value_grad = jnp.einsum(
            "gts,tgd->sd", prob_low, grad_head, preferred_element_type=jnp.float32
        )
        return (query_grad, key_grad, value_grad)

    query_grads, key_grads, value_grads = lax.map(
        head_backward, (query_heads, key_heads, value_heads, mixed_grad_heads, log_totals)
    )
    key_grads = key_grads.transpose(1, 0, 2).reshape(group_rows, kv_local * HEAD)
    value_grads = value_grads.transpose(1, 0, 2).reshape(group_rows, kv_local * HEAD)
    local_key_grad, local_value_grad = (
        lax.psum_scatter(
            key_grads.astype(jnp.bfloat16), CONTEXT, scatter_dimension=0, tiled=True
        ).astype(jnp.float32),
        lax.psum_scatter(
            value_grads.astype(jnp.bfloat16), CONTEXT, scatter_dimension=0, tiled=True
        ).astype(jnp.float32),
    )
    query_grad_rot = query_grads.transpose(1, 0, 2, 3).reshape(local_rows, heads_local, HEAD)
    query_grad_low = (
        rotate_back(query_grad_rot, cos_table, sine_table)
        .reshape(local_rows, heads_local * HEAD)
        .astype(jnp.bfloat16)
    )
    key_grad_low = (
        rotate_back(local_key_grad.reshape(local_rows, kv_local, HEAD), cos_table, sine_table)
        .reshape(local_rows, kv_local * HEAD)
        .astype(jnp.bfloat16)
    )
    value_grad_low = local_value_grad.astype(jnp.bfloat16)
    query_term = dot_first(normed_one, query_grad_low)
    key_term = dot_first(normed_one, key_grad_low)
    value_term = dot_first(normed_one, value_grad_low)
    normed_part_one = dot_last(query_grad_low, attn_back[1])
    normed_part_one = normed_part_one + dot_last(key_grad_low, attn_back[2])
    normed_part_one = normed_part_one + dot_last(value_grad_low, attn_back[3])
    normed_grad_one = lax.psum(normed_part_one.astype(jnp.bfloat16), TENSOR).astype(jnp.float32)
    attn_gain_term = jnp.sum(normed_grad_one * unit_one, axis=0)
    input_grad = hidden_grad + norm_back(normed_grad_one, unit_one, gain_one, inverse_one)
    attn_sums = (
        lax.psum_scatter(attn_gain_term, (FSDP, CONTEXT), scatter_dimension=0, tiled=True),
        lax.psum_scatter(query_term, (FSDP, CONTEXT), scatter_dimension=0, tiled=True),
        lax.psum_scatter(key_term, (FSDP, CONTEXT), scatter_dimension=0, tiled=True),
        lax.psum_scatter(value_term, (FSDP, CONTEXT), scatter_dimension=0, tiled=True),
        lax.psum_scatter(out_term, (FSDP, CONTEXT), scatter_dimension=0, tiled=True),
    )
    return (
        output.astype(jnp.bfloat16)[None],
        input_grad.astype(jnp.bfloat16)[None],
        attn_sums[0],
        attn_sums[1],
        attn_sums[2],
        attn_sums[3],
        attn_sums[4],
        feed_sums[0],
        feed_sums[1],
        feed_sums[2],
        feed_sums[3],
    )


def flip(i, k):
    if k == 0:
        return i
    if k == 1:
        return i + 1 - 2 * lax.rem(i, 2)
    if k == 2:
        return lax.rem(i + 2, 4)
    return 3 - i


class Copies:
    def __init__(self, send, receive):
        self.send, self.receive = send, receive
        self.count, self.started = 0, []

    def index(self):
        self.count += 1
        return self.count - 1

    def make(self, i, source, target, device):
        return pltpu.make_async_remote_copy(
            src_ref=source,
            dst_ref=target,
            send_sem=self.send.at[i],
            recv_sem=self.receive.at[i],
            device_id=device,
            device_id_type=pl.DeviceIdType.MESH,
        )

    def start(self, source, target, device, i=None):
        i = self.index() if i is None else i
        copy = self.make(i, source, target, device)
        copy.start()
        self.started.append(copy)
        return copy


def greet(partners):
    barrier = pltpu.get_barrier_semaphore()
    for device in partners:
        pl.semaphore_signal(barrier, inc=1, device_id=device, device_id_type=pl.DeviceIdType.MESH)
    pl.semaphore_wait(barrier, len(partners))


def dot_tile(left, right, left_axis, right_axis):
    return lax.dot_general(left, right, (((left_axis,), (right_axis,)), ((), ())), preferred_element_type=jnp.float32)


TILE = 256


def turn_lanes(x, low):
    return jnp.where(low, pltpu.roll(x, x.shape[1] - HEAD // 2, 1), pltpu.roll(x, HEAD // 2, 1))


def low_lanes(shape, width):
    return lax.rem(lax.broadcasted_iota(jnp.int32, shape, 1), 2 * width) < width


def split_pair(x):
    low = low_lanes(x.shape, HEAD)
    a, b = jnp.where(low, x, 0.0), jnp.where(low, 0.0, x)
    return a, pltpu.roll(a, HEAD, 1), pltpu.roll(b, HEAD, 1), b


def attention_kernel(
    wa, wf, xt, gain, fgx, cos, sin, seg_col, seg_row,
    wa_out, wf_all, normed_out, q, kv, logs, attended, hidden_out, normed_two, fg_all, gains,
    wa_all, x_all, gain_all, normed, pairs, sums, mine, cross, crossed, totals, landed, send, receive, local,
):
    f32, bf16 = jnp.float32, jnp.bfloat16
    z, c, t = (lax.axis_index(a) for a in (FSDP, CONTEXT, TENSOR))
    peers = [(flip(z, i), flip(c, j), t) for i in range(4) for j in range(4) if i or j]
    core = (z, c, 1 - t)
    greet(peers + [core])
    net = Copies(send, receive)
    middle = (z == 1) | (z == 2)
    nt, part, width = xt.shape
    rows = nt * part
    q_cols = q.shape[1]
    hidden = wf_all.shape[4]

    def columns(owner):
        return pl.ds(pl.multiple_of(owner * hidden, hidden), hidden)

    qkv_cols = q_cols + 2 * HEAD
    ends = []
    own = []
    for i, (source, target) in enumerate(
        (
            (wa.at[c], wa_all.at[z, c]),
            (xt, x_all.at[c]),
            (wf.at[:, :, columns(z)], wf_all.at[:, z, c]),
            (gain, gain_all.at[z, c]),
            (fgx, fg_all.at[0, 0]),
        )
    ):
        own.append(pltpu.make_async_copy(source, target, local.at[i]))
        own[-1].start()

    def spread(source, slot, forward):
        one = net.start(source, slot(1), (flip(z, 1), c, t))
        two = net.start(source, slot(2), (flip(z, 2), c, t))
        three = net.index()
        direct = net.make(three, source, slot(3), (3 - z, c, t))
        pl.when(middle)(direct.start)
        passed = pltpu.make_async_remote_copy(
            src_ref=forward[0],
            dst_ref=forward[1],
            send_sem=send.at[net.index()],
            recv_sem=receive.at[three],
            device_id=(flip(z, 1), c, t),
            device_id_type=pl.DeviceIdType.MESH,
        )
        return one, two, direct, passed

    class Chain:
        def __init__(self, source, block):
            self.one = net.start(source, block(0, 1), (flip(z, 1), c, t))
            two, three = net.index(), net.index()
            self.direct = net.make(three, source, block(0, 3), (3 - z, c, t))
            self.near = net.make(two, block(1, 1), block(1, 2), (3 - z, c, t))
            self.over = self.hop(two, block(3, 3), block(3, 2))
            self.far = self.hop(three, block(2, 2), block(2, 3))
            pl.when(middle)(self.direct.start)

        def hop(self, receives, source, target):
            return pltpu.make_async_remote_copy(
                src_ref=source,
                dst_ref=target,
                send_sem=send.at[net.index()],
                recv_sem=receive.at[receives],
                device_id=(flip(z, 1), c, t),
                device_id_type=pl.DeviceIdType.MESH,
            )

        def pass_near(self):
            self.one.wait_recv()
            pl.when(middle)(self.near.start)

        def pass_far(self):
            self.direct.wait_recv()
            pl.when(middle)(self.over.start)
            self.near.wait_recv()
            pl.when(middle)(self.far.start)

        def end(self):
            for copy in (self.direct, self.near, self.over, self.far):
                pl.when(middle)(copy.wait_send)

    attn_in = [net.start(wa.at[flip(c, k)], wa_all.at[z, c], (z, flip(c, k), t)) for k in (1, 2, 3)]
    tokens_in = [net.start(xt.at[t], x_all.at[c, t], (z, flip(c, k), t)) for k in (1, 2, 3)]
    parts = {k: (0, 1, 2) if k == 2 else (slice(None),) for k in range(4)}

    def weights_to(k):
        there = columns(flip(z, k))
        return [net.start(wf.at[m, :, there], wf_all.at[m, z, c], (flip(z, k), c, t)) for m in parts[k]]

    ff_in = {1: weights_to(1)}
    for device in peers:
        ends.append(net.start(gain, gain_all.at[z, c], device))
    own[2].wait()
    ff_out = {}

    def pass_on(k, m):
        piece = wf_all.at[m, flip(z, k), c]
        ff_out.setdefault(k, []).append([net.start(piece, piece, (z, flip(c, j), t)) for j in (1, 2)])

    pass_on(0, slice(None))
    weights = []
    for j in range(4):
        if j:
            attn_in[j - 1].wait_recv()
        else:
            own[0].wait()
        piece = wa_all.at[z, flip(c, j)]
        passed_piece = wa_all.at[flip(z, 2), flip(c, j)]
        weights.append(spread(piece, lambda k, piece=piece: piece, (passed_piece, passed_piece)))
    for k in (3, 2):
        ff_in[k] = weights_to(k)
    feed = Chain(fgx, lambda _, j: fg_all.at[j, 0])
    swaps = [net.start(fgx, fg_all.at[0, 1], core)]
    token_swaps = []
    for k, copy in zip((1, 2, 3), tokens_in):
        copy.wait_recv()
        piece = x_all.at[flip(c, k), t]
        token_swaps.append(net.start(piece, piece, core))
    halves = []

    def corner(k):
        zs = flip(z, k)
        for m, (one, two) in zip(parts[k], ff_out[k]):
            two.wait_recv()
            piece = wf_all.at[m, zs, flip(c, 2), pl.ds(0, 64)]
            halves.append(net.start(piece, piece, (z, flip(c, 1), t)))
            one.wait_recv()
            piece = wf_all.at[m, zs, flip(c, 1), pl.ds(64, 64)]
            halves.append(net.start(piece, piece, (z, flip(c, 2), t)))

    def onward(k):
        for m, copy in zip(parts[k], ff_in[k]):
            copy.wait_recv()
            pass_on(k, m)

    own[1].wait()
    own[3].wait()
    for copy in token_swaps + ends:
        copy.wait_recv()
    for i in range(2):
        gains[i : i + 1, :] = jnp.concatenate(
            [gain_all[a, b, i : i + 1, :].astype(f32) for a in range(4) for b in range(4)], axis=1
        )

    def norm_rows(i, carry):
        x = x_all[i].reshape(rows, width).astype(f32)
        inverse = lax.rsqrt(jnp.mean(x * x, axis=-1, keepdims=True) + norm_eps)
        normed[i] = (x * inverse * gains[0:1, :]).astype(bf16)
        return carry

    lax.fori_loop(0, 4, norm_rows, 0)
    save = [pltpu.make_async_copy(normed, normed_out, local.at[5])]
    save[0].start()
    onward(1)
    corner(0)
    for one, two, direct, passed in weights:
        two.wait_recv()
        pl.when(middle)(passed.start)
    for one, two, direct, passed in weights:
        one.wait_recv()
        direct.wait_recv()
    save.append(pltpu.make_async_copy(wa_all, wa_out, local.at[6]))
    save[1].start()

    def project(i, carry):
        here = pl.ds(pl.multiple_of(i * rows, rows), rows)
        w = wa_all[...].reshape(width, wa_all.shape[3])
        qkv = dot_tile(normed[i], w[:, :qkv_cols], 1, 0)
        cos_b, sin_b = cos[here, :], sin[here, :]
        quarter = low_lanes(cos_b.shape, HEAD // 2)
        half = low_lanes(cos_b.shape, HEAD)
        for p in range(q_cols // 128):
            block = qkv[:, p * 128 : (p + 1) * 128]
            q[here, p * 128 : (p + 1) * 128] = (block * cos_b + turn_lanes(block, quarter) * sin_b).astype(bf16)
        block = qkv[:, q_cols:]
        block = jnp.where(half, block * cos_b + turn_lanes(block, quarter) * sin_b, block)
        kv[here, :] = block.astype(bf16)
        for j, piece in enumerate(split_pair(block)):
            pairs[j, here, :] = piece.astype(bf16)
        return carry

    lax.fori_loop(0, 4, project, 0)
    corner(1)
    feed.pass_near()

    def attend(i):
        count = (i + 1) * rows
        here = pl.ds(i * rows, rows)
        keep = (seg_col[here, :] == seg_row[:, :count]) & (
            lax.broadcasted_iota(jnp.int32, (rows, count), 0) + i * rows
            >= lax.broadcasted_iota(jnp.int32, (rows, count), 1)
        )
        lane = lax.broadcasted_iota(jnp.int32, (rows, 128), 1)
        log_sums = jnp.zeros((rows, 128), f32)
        for p in range(q_cols // 128):
            out = jnp.zeros((rows, 128), f32)
            for e in range(2):
                scores = dot_tile(q[here, p * 128 : (p + 1) * 128], pairs[e, :count, :], 1, 1)
                scores = jnp.where(keep, scores * attention_mult, -1e30)
                highest = jnp.max(scores, axis=-1, keepdims=True)
                weight = jnp.exp(scores - highest)
                total = jnp.sum(weight, axis=-1, keepdims=True)
                out = out + dot_tile((weight / total).astype(bf16), pairs[2 + e, :count, :], 1, 0)
                log_sums = jnp.where(lane == 2 * p + e, highest + jnp.log(total), log_sums)
            attended[here, p * 128 : (p + 1) * 128] = out.astype(bf16)
        logs[here, :] = log_sums

    attend(0)
    attend(1)
    onward(3)
    attend(2)
    last = pl.ds(3 * rows, rows)
    both = (pairs[2, last, :] + pairs[3, last, :]).astype(bf16)
    for p in range(q_cols // 128):
        attended[last, p * 128 : (p + 1) * 128] = both
    corner(3)

    crosses, outs = {}, {}
    for k in (3, 1, 2, 0):
        mine_rows = pl.ds(pl.multiple_of(flip(c, k) * rows, rows), rows)

        def out_tile(n, carry, mine_rows=mine_rows):
            here = pl.ds(pl.multiple_of(n * 128, 128), 128)
            w = wa_all[lax.div(n, 4), lax.rem(n, 4), :, qkv_cols:]
            sums[:, here] = dot_tile(attended[mine_rows, :], w, 1, 1)
            return carry

        lax.fori_loop(0, width // 128, out_tile, 0)
        mine[k] = sums[pl.ds(pl.multiple_of(t * part, part), part), :]
        cross[k] = sums[pl.ds(pl.multiple_of((1 - t) * part, part), part), :].astype(bf16)
        crosses[k] = net.start(cross.at[k], crossed.at[k], core)
    for k in (3, 1, 2):
        crosses[k].wait_recv()
        totals[k - 1] = (mine[k] + crossed[k].astype(f32)).astype(bf16)
        outs[k] = net.start(totals.at[k - 1], landed.at[k - 1], (z, flip(c, k), t))
    onward(2)
    swaps.append(net.start(fg_all.at[1, 0], fg_all.at[1, 1], core))
    crosses[0].wait_recv()
    total = mine[0] + crossed[0].astype(f32)
    for k in (1, 2, 3):
        outs[k].wait_recv()
        total = total + landed[k - 1].astype(f32)
    hidden = xt[t].astype(f32) + residual_mult * total
    hidden_out[...] = hidden
    inverse = lax.rsqrt(jnp.mean(hidden * hidden, axis=-1, keepdims=True) + norm_eps)
    normed_two[...] = (hidden * inverse * gains[1:2, :]).astype(bf16)
    feed.pass_far()
    for k in (2, 3):
        swaps.append(net.start(fg_all.at[k, 0], fg_all.at[k, 1], core))
    corner(2)
    for copy in halves + swaps:
        copy.wait_recv()
    feed.end()
    for _, _, direct, passed in weights:
        pl.when(middle)(direct.wait_send)
        pl.when(middle)(passed.wait_send)
    for copy in net.started:
        copy.wait_send()
    own[4].wait()
    for copy in save:
        copy.wait()


def attention_forward(wa, wf, xt, gain, fgx, cos, sin, seg_col, seg_row):
    bf16, f32 = jnp.bfloat16, jnp.float32
    nt, part, width = xt.shape
    rows = nt * part
    total = 4 * rows
    wa_cols = wa.shape[2]
    q_cols = (wa_cols - 2 * HEAD) // 2
    filled = seg_col.shape[0]
    copies = 112
    vmem, anywhere = pl.BlockSpec(memory_space=pltpu.VMEM), pl.BlockSpec(memory_space=pl.ANY)
    outs = (
        ((4, 4) + wa.shape[1:], bf16, anywhere),
        ((3, 4, 4, wf.shape[1], wf.shape[2] // 4), bf16, anywhere),
        ((4, rows, width), bf16, anywhere),
        ((total, q_cols), bf16, vmem),
        ((total, 2 * HEAD), bf16, vmem),
        ((filled, 128), f32, vmem),
        ((total, q_cols), bf16, vmem),
        ((part, width), f32, vmem),
        ((part, width), bf16, vmem),
        ((4, nt, part, width), bf16, anywhere),
        ((2, width), f32, vmem),
    )
    return pl.pallas_call(
        attention_kernel,
        out_shape=[jax.ShapeDtypeStruct(shape, dtype) for shape, dtype, _ in outs],
        in_specs=[vmem] * 9,
        out_specs=[spec for _, _, spec in outs],
        scratch_shapes=[
            pltpu.VMEM((4, 4) + wa.shape[1:], bf16),
            pltpu.VMEM((4, nt, part, width), bf16),
            pltpu.VMEM((4, 4) + gain.shape, bf16),
            pltpu.VMEM((4, rows, width), bf16),
            pltpu.VMEM((4, total, 2 * HEAD), bf16),
            pltpu.VMEM((rows, width), f32),
            pltpu.VMEM((4, part, width), f32),
            pltpu.VMEM((4, part, width), bf16),
            pltpu.VMEM((4, part, width), bf16),
            pltpu.VMEM((3, part, width), bf16),
            pltpu.VMEM((3, part, width), bf16),
            pltpu.SemaphoreType.DMA((copies,)),
            pltpu.SemaphoreType.DMA((copies,)),
            pltpu.SemaphoreType.DMA((7,)),
        ],
        compiler_params=pltpu.CompilerParams(collective_id=1, has_side_effects=True, vmem_limit_bytes=60 * 2**20),
    )(wa, wf, xt, gain, fgx, cos, sin, seg_col, seg_row)


def feed_kernel(
    x, fg, w, back, feed_own, feed_send, terms,
    xs, wv, gate_g, up_g, inner, mine, cross, crossed, totals, landed, send, receive, local,
):
    f32, bf16 = jnp.float32, jnp.bfloat16
    z, c, t = (lax.axis_index(a) for a in (FSDP, CONTEXT, TENSOR))
    core = (z, c, 1 - t)
    greet([(flip(z, k), c, t) for k in (1, 2, 3)] + [core])
    net = Copies(send, receive)
    part, width = x.shape
    hidden = wv.shape[2]
    load = pltpu.make_async_copy(w, wv, local.at[0])
    load.start()
    middle = (z == 1) | (z == 2)
    swaps = {0: net.start(x, xs.at[0, 1], core)}
    arrive = {2: net.start(x, xs.at[2, 0], (flip(z, 2), c, t))}
    three = net.index()
    direct = net.make(three, x, xs.at[3, 0], (3 - z, c, t))
    pl.when(middle)(direct.start)
    arrive[3] = direct
    arrive[1] = net.start(x, xs.at[1, 0], (flip(z, 1), c, t))
    passed = pltpu.make_async_remote_copy(
        src_ref=xs.at[2, 0],
        dst_ref=xs.at[3, 0],
        send_sem=send.at[net.index()],
        recv_sem=receive.at[three],
        device_id=(flip(z, 1), c, t),
        device_id_type=pl.DeviceIdType.MESH,
    )
    xs[0, 0] = x[...]
    load.wait()

    def first(k):
        swaps[k].wait_recv()
        rows = xs[k].reshape(2 * part, width)
        grads = fg[k]

        def step(n, carry):
            at = pl.multiple_of(n * TILE, TILE)
            g = dot_tile(rows, wv[0, :, pl.ds(at, TILE)], 1, 0)
            u = dot_tile(rows, wv[1, :, pl.ds(at, TILE)], 1, 0)
            d = dot_tile(grads, wv[2, :, pl.ds(at, TILE)], 1, 0)
            sig = jax.nn.sigmoid(g)
            here = pl.ds(at, TILE)
            inner[k, :, here] = (g * sig * u).astype(bf16)
            gate_g[k, :, here] = (d * u * sig * (1.0 + g * (1.0 - sig))).astype(bf16)
            up_g[k, :, here] = (d * g * sig).astype(bf16)
            return carry

        lax.fori_loop(0, hidden // TILE, step, 0)

    crosses = {}

    def second(k):
        def step(n, carry):
            here = pl.ds(pl.multiple_of(n * TILE, TILE), TILE)
            b = dot_tile(gate_g[k], wv[0, here, :], 1, 1) + dot_tile(up_g[k], wv[1, here, :], 1, 1)
            f = dot_tile(inner[k], wv[2, here, :], 1, 1)
            mine[k, 0, :, here] = b[:part]
            mine[k, 1, :, here] = f[:part]
            cross[k, 0, :, here] = b[part:].astype(bf16)
            cross[k, 1, :, here] = f[part:].astype(bf16)
            return carry

        lax.fori_loop(0, width // TILE, step, 0)
        crosses[k] = net.start(cross.at[k], crossed.at[k], core)

    sums = {}

    def finish(k):
        crosses[k].wait_recv()
        if k:
            totals[k - 1] = (mine[k, 0] + crossed[k, 0].astype(f32)).astype(bf16)
            sums[k] = net.start(totals.at[k - 1], landed.at[k - 1], (flip(z, k), c, t))
            feed_send[k - 1] = (mine[k, 1] + crossed[k, 1].astype(f32)).astype(bf16)
        else:
            back[...] = mine[0, 0] + crossed[0, 0].astype(f32)
            feed_own[...] = mine[0, 1] + crossed[0, 1].astype(f32)

    def fetch(k):
        arrive[k].wait_recv()
        if k == 2:
            pl.when(middle)(passed.start)
        swaps[k] = net.start(xs.at[k, 0], xs.at[k, 1], core)

    order = (0, 2, 3, 1)
    for i, k in enumerate(order):
        first(k)
        if i:
            finish(order[i - 1])
        if i < 3:
            fetch(order[i + 1])
        second(k)

    rows = xs.shape[0] * 2 * part

    def term(source, grads, i):
        def step(m, carry):
            here = pl.ds(pl.multiple_of(m * TILE, TILE), TILE)
            left = source[:, :, here].reshape(rows, TILE)
            value = dot_tile(left, grads[...].reshape(rows, hidden), 0, 0)
            wv[i, here, :] = value.astype(bf16)
            return carry

        lax.fori_loop(0, width // TILE, step, 0)

    flat = xs.reshape(xs.shape[0], 2 * part, width)
    term(flat, gate_g, 0)
    finish(order[3])
    term(flat, up_g, 1)
    term(fg, inner, 2)
    store = pltpu.make_async_copy(wv, terms, local.at[1])
    store.start()
    for k in (1, 2, 3):
        sums[k].wait_recv()
    back[...] = back[...] + landed[0].astype(f32) + landed[1].astype(f32) + landed[2].astype(f32)
    pl.when(middle)(direct.wait_send)
    pl.when(middle)(passed.wait_send)
    for copy in net.started:
        copy.wait_send()
    store.wait()


def feed_forward(x, fg, w):
    bf16, f32 = jnp.bfloat16, jnp.float32
    part, width = x.shape
    hidden = w.shape[2]
    blocks = fg.shape[0]
    copies = 20
    vmem, anywhere = pl.BlockSpec(memory_space=pltpu.VMEM), pl.BlockSpec(memory_space=pl.ANY)
    return pl.pallas_call(
        feed_kernel,
        out_shape=[
            jax.ShapeDtypeStruct((part, width), f32),
            jax.ShapeDtypeStruct((part, width), f32),
            jax.ShapeDtypeStruct((blocks - 1, part, width), bf16),
            jax.ShapeDtypeStruct(w.shape, bf16),
        ],
        in_specs=[vmem, vmem, anywhere],
        out_specs=[vmem, vmem, vmem, anywhere],
        scratch_shapes=[
            pltpu.VMEM((blocks, 2, part, width), bf16),
            pltpu.VMEM(w.shape, bf16),
            pltpu.VMEM((blocks, 2 * part, hidden), bf16),
            pltpu.VMEM((blocks, 2 * part, hidden), bf16),
            pltpu.VMEM((blocks, 2 * part, hidden), bf16),
            pltpu.VMEM((blocks, 2, part, width), f32),
            pltpu.VMEM((blocks, 2, part, width), bf16),
            pltpu.VMEM((blocks, 2, part, width), bf16),
            pltpu.VMEM((blocks - 1, part, width), bf16),
            pltpu.VMEM((blocks - 1, part, width), bf16),
            pltpu.SemaphoreType.DMA((copies,)),
            pltpu.SemaphoreType.DMA((copies,)),
            pltpu.SemaphoreType.DMA((2,)),
        ],
        compiler_params=pltpu.CompilerParams(collective_id=3, has_side_effects=True, vmem_limit_bytes=62 * 2**20),
    )(x, fg, w)


def swap(x, axis, k):
    return lax.ppermute(x, axis, [(i, i ^ k) for i in range(lax.axis_size(axis))])


def cut(x, index, size, axis):
    return lax.dynamic_slice_in_dim(x, index * size, size, axis)


def backward_kernel(
    ff, fs, al, wa_in, normed_in, q, kv, logs, attended, cos, sin, seg_col, seg_row,
    feed_in, back_own, back_in, ff_out, query_out, kv_out, output_out,
    terms, corner_x, corner_y, side_x, side_y, at_terms, at_in, at_total, wa, normed, ag, pairs, mixed, acc, dqkv,
    sums, mine, cross, crossed, totals, held_feed, held_terms, send, receive, local,
):
    f32, bf16 = jnp.float32, jnp.bfloat16
    z, c, t = (lax.axis_index(a) for a in (FSDP, CONTEXT, TENSOR))
    core = (z, c, 1 - t)
    greet([(flip(z, k), c, t) for k in (1, 2, 3)] + [(z, flip(c, k), t) for k in (1, 2, 3)] + [core])
    net = Copies(send, receive)
    wrows, hidden = ff.shape[3:]
    half = wrows // 2
    part, width = al.shape
    rows = 2 * part
    q_cols = q.shape[1]
    qkv_cols = q_cols + 2 * HEAD
    blocks = normed.shape[0]
    order = (3, 2, 1, 0)
    loads = {}
    for k in order:
        zs = flip(z, k)
        loads[k] = pltpu.make_async_copy(ff.at[:, zs], terms.at[:, zs], local.at[k])
        loads[k].start()
    wa_load = pltpu.make_async_copy(wa_in, wa, local.at[4])
    wa_load.start()
    normed_load = pltpu.make_async_copy(normed_in.at[pl.ds(0, blocks)], normed, local.at[5])
    normed_load.start()
    first = {}

    def corners(k):
        zs = flip(z, k)
        loads[k].wait()
        first[k] = (
            net.start(terms.at[:, zs, flip(c, 3), pl.ds(0, half)], corner_x.at[k], (z, flip(c, 1), t)),
            net.start(terms.at[:, zs, flip(c, 3), pl.ds(half, half)], corner_y.at[k], (z, flip(c, 2), t)),
        )

    corners(3)
    ag_in = [net.start(al, ag.at[c, t], (z, flip(c, k), t)) for k in (3, 1, 2)]
    swaps = [net.start(al, ag.at[c, t], core)]
    middle = (z == 1) | (z == 2)
    chains = []

    class Sums:
        def __init__(self, mine, held, landed):
            self.mine, self.held, self.landed = mine, held, landed
            neighbour = (flip(z, 1), c, t)
            self.ends = [net.make(net.index(), mine(k), held(k), neighbour) for k in (3, 2)]
            for copy in self.ends:
                pl.when(jnp.logical_not(middle))(copy.start)
            self.one = net.start(mine(1), landed(0), neighbour)
            two, spare = net.index(), net.index()
            self.out = [net.make(two, held(2), landed(1), (3 - z, c, t))]
            self.out.append(
                pltpu.make_async_remote_copy(
                    src_ref=held(3),
                    dst_ref=landed(1),
                    send_sem=send.at[spare],
                    recv_sem=receive.at[two],
                    device_id=(flip(z, 2), c, t),
                    device_id_type=pl.DeviceIdType.MESH,
                )
            )
            chains.append(self)

        def add(self, k, own):
            held, mine = self.held(k), self.mine(own)
            for i in range(held.shape[0]) if len(held.shape) == 3 else (slice(None),):
                held[i] = (held[i].astype(f32) + mine[i].astype(f32)).astype(bf16)

        def hand_on(self):
            @pl.when(middle)
            def _():
                for copy in self.ends:
                    copy.wait_recv()
                self.add(3, 2)
                self.out[1].start()
                self.add(2, 3)
                self.out[0].start()

        def wait_in(self):
            self.one.wait_recv()
            self.out[0].wait_recv()

        def wait_out(self):
            for copy in self.ends:
                pl.when(jnp.logical_not(middle))(copy.wait_send)
            for copy in self.out:
                pl.when(middle)(copy.wait_send)

    feed = Sums(lambda k: fs.at[k - 1], lambda k: held_feed.at[k - 2], lambda i: feed_in.at[i])
    corners(2)
    ag[c, t] = al[...]
    for j, piece in enumerate(split_pair(kv[...].astype(f32))):
        pairs[j] = piece.astype(bf16)
    acc[...] = jnp.zeros_like(acc)
    dqkv[pl.ds(blocks * rows, rows), :] = jnp.zeros((rows, qkv_cols), bf16)
    for k, copy in zip((3, 1, 2), ag_in):
        copy.wait_recv()
        piece = ag.at[flip(c, k), t]
        swaps.append(net.start(piece, piece, core))
    second, third = {}, {}

    def sides(k):
        zs = flip(z, k)
        for copy in first[k]:
            copy.wait_recv()
        low, high = pl.ds(0, half), pl.ds(half, half)
        xb, yb = flip(c, 1), flip(c, 2)
        for m in range(3):
            terms[m, zs, yb, low] = (terms[m, zs, yb, low].astype(f32) + corner_x[k, m].astype(f32)).astype(bf16)
            terms[m, zs, xb, high] = (terms[m, zs, xb, high].astype(f32) + corner_y[k, m].astype(f32)).astype(bf16)
        second[k] = (
            net.start(terms.at[:, zs, yb], side_y.at[k], (z, yb, t)),
            net.start(terms.at[:, zs, xb], side_x.at[k], (z, xb, t)),
        )

    def owners(k):
        zs = flip(z, k)
        for copy in second[k]:
            copy.wait_recv()
        for m in range(3):
            total = terms[m, zs, c].astype(f32) + side_x[k, m].astype(f32) + side_y[k, m].astype(f32)
            terms[m, zs, c] = total.astype(bf16)
        columns = ff_out.at[:, :, pl.ds(pl.multiple_of(z * hidden, hidden), hidden)]
        if k:
            third[k] = net.start(terms.at[:, zs, c], columns, (zs, c, t))
        else:
            third[0] = pltpu.make_async_copy(terms.at[:, z, c], columns, local.at[6])
            third[0].start()

    for copy in swaps:
        copy.wait_recv()
    wa_load.wait()
    normed_load.wait()

    def mix(i, carry):
        w = wa[...].reshape(width, wa.shape[3])[:, qkv_cols:]
        here = pl.ds(pl.multiple_of(i * rows, rows), rows)
        mixed[here, :] = dot_tile(ag[i].reshape(rows, width), w, 1, 0).astype(bf16)
        return carry

    lax.fori_loop(0, blocks, mix, 0)
    sides(3)
    corners(1)

    def out_term(m, carry):
        here = pl.ds(pl.multiple_of(m * wrows, wrows), wrows)
        left = ag[0:blocks, :, :, here].reshape(blocks * rows, wrows)
        value = dot_tile(left, attended[0 : blocks * rows, :], 0, 0)
        at_terms[lax.div(m, 4), lax.rem(m, 4), :, qkv_cols:] = value.astype(bf16)
        return carry

    lax.fori_loop(0, width // wrows, out_term, 0)

    def terms_to(columns):
        return Sums(
            lambda k: at_terms.at[flip(z, k), :, :, columns],
            lambda k: held_terms.at[k - 2, :, :, columns],
            lambda i: at_in.at[i, :, :, columns],
        )

    output_sums = terms_to(pl.ds(qkv_cols, q_cols))
    feed.hand_on()
    sides(2)
    corners(0)

    def attend(i):
        count = (i + 1) * rows
        here = pl.ds(i * rows, rows)
        keep = (seg_col[here, :] == seg_row[:, :count]) & (
            lax.broadcasted_iota(jnp.int32, (rows, count), 0) + i * rows
            >= lax.broadcasted_iota(jnp.int32, (rows, count), 1)
        )
        log_sums = logs[here, :]
        lane = lax.broadcasted_iota(jnp.int32, (rows, 128), 1)
        cos_b, sin_b = cos[here, :], sin[here, :]
        quarter = low_lanes(cos_b.shape, HEAD // 2)
        for p in range(q_cols // 128):
            block = slice(p * 128, (p + 1) * 128)
            grad = jnp.zeros((rows, 128), f32)
            for e in range(2):
                scores = dot_tile(q[here, block], pairs[e, :count, :], 1, 1)
                scores = jnp.where(keep, scores * attention_mult, -1e30)
                log = jnp.sum(jnp.where(lane == 2 * p + e, log_sums, 0.0), axis=-1, keepdims=True)
                prob = jnp.exp(scores - log)
                prob_grad = dot_tile(mixed[here, block], pairs[2 + e, :count, :], 1, 1)
                row_dot = jnp.sum(prob * prob_grad, axis=-1, keepdims=True)
                score_grad = (attention_mult * prob * (prob_grad - row_dot)).astype(bf16)
                grad = grad + dot_tile(score_grad, pairs[e, :count, :], 1, 0)
                acc[e, :count, :] += dot_tile(score_grad, q[here, block], 0, 0)
                acc[2 + e, :count, :] += dot_tile(prob.astype(bf16), mixed[here, block], 0, 0)
            dqkv[here, block] = (grad * cos_b + turn_lanes(grad * sin_b, quarter)).astype(bf16)

    attend(0)
    output_sums.hand_on()
    attend(1)
    owners(3)
    sides(1)
    attend(2)
    sides(0)
    owners(2)
    filled = blocks * rows
    low = low_lanes((filled, 128), HEAD)
    key_grad = jnp.where(low, acc[0], 0.0) + pltpu.roll(jnp.where(low, 0.0, acc[1]), HEAD, 1)
    value_grad = jnp.where(low, 0.0, acc[3]) + pltpu.roll(jnp.where(low, acc[2], 0.0), HEAD, 1)
    turned = turn_lanes(key_grad * sin[0:filled, :], low_lanes((filled, 128), HEAD // 2))
    key_grad = key_grad * cos[0:filled, :] + turned
    dqkv[0:filled, q_cols:] = jnp.where(low, key_grad, value_grad).astype(bf16)

    crosses, outs = {}, {}
    for k in (3, 1, 2, 0):
        mine_rows = pl.ds(pl.multiple_of(flip(c, k) * rows, rows), rows)

        def back_tile(n, carry, mine_rows=mine_rows):
            here = pl.ds(pl.multiple_of(n * 128, 128), 128)
            w = wa[lax.div(n, 4), lax.rem(n, 4), :, :qkv_cols]
            sums[:, here] = dot_tile(dqkv[mine_rows, :], w, 1, 1)
            return carry

        lax.fori_loop(0, width // 128, back_tile, 0)
        mine[k] = sums[pl.ds(pl.multiple_of(t * part, part), part), :]
        cross[k] = sums[pl.ds(pl.multiple_of((1 - t) * part, part), part), :].astype(bf16)
        crosses[k] = net.start(cross.at[k], crossed.at[k], core)
    for k in (3, 1, 2):
        crosses[k].wait_recv()
        totals[k - 1] = (mine[k] + crossed[k].astype(f32)).astype(bf16)
        outs[k] = net.start(totals.at[k - 1], back_in.at[k - 1], (z, flip(c, k), t))
    crosses[0].wait_recv()
    back_own[...] = mine[0] + crossed[0].astype(f32)

    def qkv_term(m, carry):
        here = pl.ds(pl.multiple_of(m * wrows, wrows), wrows)
        left = normed[:, :, here].reshape(filled, wrows)
        value = dot_tile(left, dqkv[0:filled, :], 0, 0)
        at_terms[lax.div(m, 4), lax.rem(m, 4), :, :qkv_cols] = value.astype(bf16)
        return carry

    lax.fori_loop(0, width // wrows, qkv_term, 0)
    qkv_sums = terms_to(pl.ds(0, qkv_cols))
    owners(1)
    owners(0)
    qkv_sums.hand_on()
    output_sums.wait_in()
    qkv_sums.wait_in()
    for j in range(4):
        total = at_terms[z, j].astype(f32)
        for i in range(2):
            total = total + at_in[i, j].astype(f32)
        at_total[j] = total.astype(bf16)
    here = pl.ds(pl.multiple_of(c * q_cols, q_cols), q_cols)
    attn_out, keep_own = [], []
    for i, (columns, target) in enumerate(
        (
            (pl.ds(0, q_cols), query_out.at[:, here]),
            (pl.ds(q_cols, 2 * HEAD), kv_out.at[c]),
            (pl.ds(qkv_cols, q_cols), output_out.at[:, here]),
        )
    ):
        attn_out += [net.start(at_total.at[flip(c, k), :, columns], target, (z, flip(c, k), t)) for k in (1, 2, 3)]
        keep_own.append(pltpu.make_async_copy(at_total.at[c, :, columns], target, local.at[7 + i]))
        keep_own[-1].start()
    feed.wait_in()
    for chain in chains:
        chain.wait_out()
    for copy in attn_out + [outs[k] for k in (1, 2, 3)] + [third[k] for k in (1, 2, 3)]:
        copy.wait_recv()
    for copy in net.started:
        copy.wait_send()
    third[0].wait()
    for copy in keep_own:
        copy.wait()


def backward(ff, fs, al, wa, normed, q, kv, logs, attended, cos, sin, seg_col, seg_row):
    bf16, f32 = jnp.bfloat16, jnp.float32
    wrows, hidden = ff.shape[3:]
    attn_cols = wa.shape[3]
    part, width = al.shape
    total = q.shape[0]
    filled = seg_col.shape[0]
    rows = 2 * part
    blocks = filled // rows
    copies = 64
    vmem, anywhere = pl.BlockSpec(memory_space=pltpu.VMEM), pl.BlockSpec(memory_space=pl.ANY)
    return pl.pallas_call(
        backward_kernel,
        out_shape=[
            jax.ShapeDtypeStruct((2,) + al.shape, bf16),
            jax.ShapeDtypeStruct(al.shape, f32),
            jax.ShapeDtypeStruct(fs.shape, bf16),
            jax.ShapeDtypeStruct((3, wrows, 4 * hidden), bf16),
            jax.ShapeDtypeStruct((wrows, 4 * q.shape[1]), bf16),
            jax.ShapeDtypeStruct((4, wrows, 2 * HEAD), bf16),
            jax.ShapeDtypeStruct((wrows, 4 * q.shape[1]), bf16),
        ],
        in_specs=[anywhere, vmem, vmem, anywhere, anywhere] + [vmem] * 8,
        out_specs=[anywhere, vmem] + [anywhere] * 5,
        scratch_shapes=[
            pltpu.VMEM(ff.shape, bf16),
            pltpu.VMEM((4, 3, wrows // 2, hidden), bf16),
            pltpu.VMEM((4, 3, wrows // 2, hidden), bf16),
            pltpu.VMEM((4, 3, wrows, hidden), bf16),
            pltpu.VMEM((4, 3, wrows, hidden), bf16),
            pltpu.VMEM((4, 4, wrows, attn_cols), bf16),
            pltpu.VMEM((2, 4, wrows, attn_cols), bf16),
            pltpu.VMEM((4, wrows, attn_cols), bf16),
            pltpu.VMEM(wa.shape, bf16),
            pltpu.VMEM((blocks, rows, width), bf16),
            pltpu.VMEM((4, 2, part, width), bf16),
            pltpu.VMEM((4, total, 2 * HEAD), bf16),
            pltpu.VMEM((filled, q.shape[1]), bf16),
            pltpu.VMEM((4, filled, 2 * HEAD), f32),
            pltpu.VMEM((total, q.shape[1] + 2 * HEAD), bf16),
            pltpu.VMEM((rows, width), f32),
            pltpu.VMEM((4, part, width), f32),
            pltpu.VMEM((4, part, width), bf16),
            pltpu.VMEM((4, part, width), bf16),
            pltpu.VMEM((3, part, width), bf16),
            pltpu.VMEM((2, part, width), bf16),
            pltpu.VMEM((2, 4, wrows, attn_cols), bf16),
            pltpu.SemaphoreType.DMA((copies,)),
            pltpu.SemaphoreType.DMA((copies,)),
            pltpu.SemaphoreType.DMA((10,)),
        ],
        compiler_params=pltpu.CompilerParams(collective_id=2, has_side_effects=True, vmem_limit_bytes=63 * 2**20),
    )(ff, fs, al, wa, normed, q, kv, logs, attended, cos, sin, seg_col, seg_row)


def on_device_split(
    tokens,
    out_grad,
    lengths,
    attention_gain,
    query_weight,
    key_weight,
    value_weight,
    output_weight,
    feed_gain,
    gate_weight,
    up_weight,
    down_weight,
):
    f32, bf16 = jnp.float32, jnp.bfloat16
    nz, nc, nt = (lax.axis_size(a) for a in (FSDP, CONTEXT, TENSOR))
    z, c, t = (lax.axis_index(a) for a in (FSDP, CONTEXT, TENSOR))
    local_rows, width = tokens.shape[1:]
    group_rows = local_rows * nc
    filled = group_rows * 3 // 4
    part = local_rows // nt
    wrows = query_weight.shape[0]
    kv_cols = key_weight.shape[1] // nc
    q_cols = query_weight.shape[1] // nc
    qkv_cols = q_cols + 2 * kv_cols
    ff_cols = gate_weight.shape[1] // nz
    per_group = q_cols // kv_cols
    segment, position, valid_rows = slot_layout(lengths[0], group_rows)
    cos_table, sine_table = rope_tables(position, HEAD)

    wa = jnp.concatenate(
        [
            w.astype(bf16).reshape(wrows, nc, -1).transpose(1, 0, 2)
            for w in (query_weight, key_weight, value_weight, output_weight)
        ],
        axis=2,
    )
    wf = jnp.stack([w.astype(bf16) for w in (gate_weight, up_weight, down_weight)])
    gain = jnp.pad(jnp.stack([attention_gain, feed_gain]).astype(bf16), ((0, 14), (0, 0)))
    my_valid = lax.dynamic_slice_in_dim(valid_rows, c * local_rows + t * part, part)
    cotangent = cut(out_grad[0], t, part, 0).astype(f32) * my_valid[:, None].astype(f32)
    feed_grad = (residual_mult * cotangent).astype(bf16)
    sign = jnp.where(jnp.arange(HEAD) < HEAD // 2, -1.0, 1.0).astype(f32)
    wide_cos = jnp.concatenate([cos_table, cos_table], axis=1)
    wide_sin = jnp.concatenate([sine_table * sign, sine_table * sign], axis=1)
    wa, wf, normed_one, queries, pair, logs, attended, hidden, normed_two, feed_grads, gains = attention_forward(
        wa, wf, tokens[0].reshape(nt, part, width), gain, feed_grad, wide_cos, wide_sin,
        segment[:filled, None], segment[None, :filled],
    )
    gain_one, gain_two = gains[0], gains[1]
    w_feed = wf.reshape(3, width, ff_cols)
    my_inputs = cut(tokens[0], t, part, 0).astype(f32)
    inverse_two = lax.rsqrt(jnp.mean(hidden * hidden, axis=-1, keepdims=True) + norm_eps)
    unit_two = hidden * inverse_two

    normed_grad_two, feed_own, feed_send, ff_terms = feed_forward(
        normed_two, feed_grads.reshape(nz, local_rows, width), w_feed
    )
    ff_terms = ff_terms.reshape(3, nz, nc, wrows, ff_cols)

    def both_cores(x):
        other = swap(x, TENSOR, 1)
        first, last = jnp.where(t == 0, x, other), jnp.where(t == 0, other, x)
        return jnp.concatenate([first, last], axis=0)[None]

    feed_gain_term = jnp.sum(normed_grad_two * unit_two, axis=0)
    hidden_grad = cotangent + norm_back(normed_grad_two, unit_two, gain_two, inverse_two)

    attn_low = (residual_mult * hidden_grad).astype(bf16)
    feed_in, back_own, back_in, ff_grads, grad_query, kv_grads, grad_output = backward(
        ff_terms, feed_send, attn_low, wa, normed_one, queries, pair, logs, attended, wide_cos, wide_sin,
        segment[:filled, None], segment[None, :filled],
    )
    output = both_cores((hidden + residual_mult * (feed_own + jnp.sum(feed_in.astype(f32), axis=0))).astype(bf16))
    normed_grad_one = back_own + jnp.sum(back_in.astype(f32), axis=0)
    inverse_one = lax.rsqrt(jnp.mean(my_inputs * my_inputs, axis=-1, keepdims=True) + norm_eps)
    unit_one = my_inputs * inverse_one
    attn_gain_term = jnp.sum(normed_grad_one * unit_one, axis=0)
    input_grad = both_cores((hidden_grad + norm_back(normed_grad_one, unit_one, gain_one, inverse_one)).astype(bf16))

    gain_terms = jnp.stack([attn_gain_term, feed_gain_term])
    for axis in (TENSOR, CONTEXT, FSDP):
        gain_terms = gain_terms + sum(swap(gain_terms, axis, k) for k in range(1, lax.axis_size(axis)))
    gain_terms = cut(gain_terms, z * nc + c, wrows, 1)

    grad_gate, grad_up, grad_down = (ff_grads[i].astype(f32) for i in range(3))
    grad_key, grad_value = (
        kv_grads[:, :, i : i + HEAD].transpose(1, 0, 2).reshape(wrows, -1).astype(f32) for i in (0, HEAD)
    )
    attn_terms = (grad_query.astype(f32), grad_key, grad_value, grad_output.astype(f32))
    return (output, input_grad, gain_terms[0], *attn_terms, gain_terms[1], grad_gate, grad_up, grad_down)


def solution(mesh):
    split = tuple(mesh.shape[a] for a in (FSDP, CONTEXT, TENSOR)) == (4, 4, 2)
    return jax.shard_map(
        on_device_split if split else on_device,
        mesh=mesh,
        in_specs=(
            P(FSDP, CONTEXT, None),
            P(FSDP, CONTEXT, None),
            P(FSDP, None),
            P((FSDP, CONTEXT)),
            P((FSDP, CONTEXT), TENSOR),
            P((FSDP, CONTEXT), TENSOR),
            P((FSDP, CONTEXT), TENSOR),
            P((FSDP, CONTEXT), TENSOR),
            P((FSDP, CONTEXT)),
            P((FSDP, CONTEXT), TENSOR),
            P((FSDP, CONTEXT), TENSOR),
            P((FSDP, CONTEXT), TENSOR),
        ),
        out_specs=(
            P(FSDP, CONTEXT, None),
            P(FSDP, CONTEXT, None),
            P((FSDP, CONTEXT)),
            P((FSDP, CONTEXT), TENSOR),
            P((FSDP, CONTEXT), TENSOR),
            P((FSDP, CONTEXT), TENSOR),
            P((FSDP, CONTEXT), TENSOR),
            P((FSDP, CONTEXT)),
            P((FSDP, CONTEXT), TENSOR),
            P((FSDP, CONTEXT), TENSOR),
            P((FSDP, CONTEXT), TENSOR),
        ),
        check_vma=False,
    )
```

```python
import jax
import jax.numpy as jnp
from jax import lax
from jax.experimental import pallas as pl
from jax.experimental.pallas import tpu as pltpu
from jax.sharding import PartitionSpec as P

HEAD = 64
FSDP, CONTEXT, TENSOR = "fsdp", "context", "tensor"


norm_eps = 1e-05
attention_mult = 0.015625
residual_mult = 0.22
rope_base = 10000000.0


def slot_layout(seq_lengths, total_rows):
    seq_ends = jnp.cumsum(seq_lengths)
    starts = seq_ends - seq_lengths
    slot_ids = jnp.arange(total_rows, dtype=jnp.int32)
    before = (slot_ids[:, None] >= seq_ends[None, :]).astype(jnp.int32)
    segment = jnp.sum(before, axis=1)
    seq_count = seq_lengths.shape[0]
    valid_rows = segment < seq_count
    inside = (slot_ids[:, None] >= starts[None, :]) & (slot_ids[:, None] < seq_ends[None, :])
    position = jnp.sum(jnp.where(inside, slot_ids[:, None] - starts[None, :], 0), axis=1)
    segment = jnp.where(valid_rows, segment, seq_count + slot_ids)
    return (segment, position, valid_rows)


def rope_tables(position, width):
    half_width = width // 2
    frequency = rope_base ** (-jnp.arange(half_width, dtype=jnp.float32) * 2.0 / width)
    angles = position.astype(jnp.float32)[:, None] * frequency[None, :]
    angles = jnp.concatenate([angles, angles], axis=1)
    return (jnp.cos(angles), jnp.sin(angles))


def turn_half(vectors):
    half_width = vectors.shape[-1] // 2
    return jnp.concatenate([-vectors[..., half_width:], vectors[..., :half_width]], axis=-1)


def rotate(vectors, cos_table, sine_table):
    return vectors * cos_table[:, None, :] + turn_half(vectors) * sine_table[:, None, :]


def rotate_back(grads, cos_table, sine_table):
    return grads * cos_table[:, None, :] - turn_half(grads * sine_table[:, None, :])


def norm_back(normed_grad, unit, gain, inverse):
    scaled = normed_grad * gain
    return inverse * (scaled - unit * jnp.mean(scaled * unit, axis=-1, keepdims=True))


def dot_first(left, right):
    return lax.dot_general(left, right, (((0,), (0,)), ((), ())), preferred_element_type=jnp.float32)


def dot_last(left, right):
    return lax.dot_general(left, right, (((1,), (1,)), ((), ())), preferred_element_type=jnp.float32)


def attention_shards(attention_gain, query_weight, key_weight, value_weight, output_weight):
    return (
        lax.all_gather(
            attention_gain.astype(jnp.bfloat16), (FSDP, CONTEXT), axis=0, tiled=True
        ),
        lax.all_gather(query_weight.astype(jnp.bfloat16), (FSDP, CONTEXT), axis=0, tiled=True),
        lax.all_gather(key_weight.astype(jnp.bfloat16), (FSDP, CONTEXT), axis=0, tiled=True),
        lax.all_gather(value_weight.astype(jnp.bfloat16), (FSDP, CONTEXT), axis=0, tiled=True),
        lax.all_gather(output_weight.astype(jnp.bfloat16), (FSDP, CONTEXT), axis=0, tiled=True),
    )


def feed_shards(feed_gain, gate_weight, up_weight, down_weight):
    return (
        lax.all_gather(feed_gain.astype(jnp.bfloat16), (FSDP, CONTEXT), axis=0, tiled=True),
        lax.all_gather(gate_weight.astype(jnp.bfloat16), (FSDP, CONTEXT), axis=0, tiled=True),
        lax.all_gather(up_weight.astype(jnp.bfloat16), (FSDP, CONTEXT), axis=0, tiled=True),
        lax.all_gather(down_weight.astype(jnp.bfloat16), (FSDP, CONTEXT), axis=0, tiled=True),
    )


def on_device(
    tokens,
    out_grad,
    lengths,
    attention_gain,
    query_weight,
    key_weight,
    value_weight,
    output_weight,
    feed_gain,
    gate_weight,
    up_weight,
    down_weight,
):
    local_rows = tokens.shape[1]
    group_rows = local_rows * lax.axis_size(CONTEXT)
    first_row = lax.axis_index(CONTEXT) * local_rows
    segment, position, valid_rows = slot_layout(lengths[0], group_rows)
    local_segment = lax.dynamic_slice_in_dim(segment, first_row, local_rows)
    local_position = lax.dynamic_slice_in_dim(position, first_row, local_rows)
    local_valid = lax.dynamic_slice_in_dim(valid_rows, first_row, local_rows)
    slot_ids = jnp.arange(group_rows, dtype=jnp.int32)
    local_slots = first_row + jnp.arange(local_rows, dtype=jnp.int32)
    allowed = (local_segment[:, None] == segment[None, :]) & (
        local_slots[:, None] >= slot_ids[None, :]
    )
    inputs = tokens[0].astype(jnp.float32)
    attn_set = attention_shards(
        attention_gain, query_weight, key_weight, value_weight, output_weight
    )
    gain_one = attn_set[0].astype(jnp.float32)
    inverse_one = lax.rsqrt(jnp.mean(inputs * inputs, axis=-1, keepdims=True) + norm_eps)
    unit_one = inputs * inverse_one
    normed_one = (unit_one * gain_one).astype(jnp.bfloat16)
    queries = jnp.dot(normed_one, attn_set[1], preferred_element_type=jnp.float32)
    keys_lin = jnp.dot(normed_one, attn_set[2], preferred_element_type=jnp.float32)
    values_low = jnp.dot(normed_one, attn_set[3], preferred_element_type=jnp.float32).astype(
        jnp.bfloat16
    )
    heads_local = queries.shape[1] // HEAD
    kv_local = keys_lin.shape[1] // HEAD
    per_group = heads_local // kv_local
    cos_table, sine_table = rope_tables(local_position, HEAD)
    queries_rot = rotate(
        queries.reshape(local_rows, heads_local, HEAD), cos_table, sine_table
    ).astype(jnp.bfloat16)
    keys_rot = rotate(keys_lin.reshape(local_rows, kv_local, HEAD), cos_table, sine_table).astype(
        jnp.bfloat16
    )
    keys_all, values_all = (
        lax.all_gather(
            keys_rot.reshape(local_rows, kv_local * HEAD), CONTEXT, axis=0, tiled=True
        ),
        lax.all_gather(values_low, CONTEXT, axis=0, tiled=True),
    )
    query_heads = queries_rot.reshape(local_rows, kv_local, per_group, HEAD).transpose(1, 0, 2, 3)
    key_heads = keys_all.reshape(group_rows, kv_local, HEAD).transpose(1, 0, 2)
    value_heads = values_all.reshape(group_rows, kv_local, HEAD).transpose(1, 0, 2)

    def head_scores(query_head, key_head):
        raw_scores = jnp.einsum(
            "tgd,sd->gts", query_head, key_head, preferred_element_type=jnp.float32
        )
        return jnp.where(allowed[None], raw_scores * attention_mult, -1e30)

    def head_forward(pieces):
        query_head, key_head, value_head = pieces
        scores = head_scores(query_head, key_head)
        highest = jnp.max(scores, axis=-1, keepdims=True)
        weight = jnp.exp(scores - highest)
        row_totals = jnp.sum(weight, axis=-1, keepdims=True)
        probabilities = (weight / row_totals).astype(jnp.bfloat16)
        mixed = jnp.einsum(
            "gts,sd->tgd", probabilities, value_head, preferred_element_type=jnp.float32
        )
        return (mixed, (highest + jnp.log(row_totals))[..., 0])

    mixed_heads, log_totals = lax.map(head_forward, (query_heads, key_heads, value_heads))
    attended = (
        mixed_heads.transpose(1, 0, 2, 3)
        .reshape(local_rows, heads_local * HEAD)
        .astype(jnp.bfloat16)
    )
    attn_part = dot_last(attended, attn_set[4])
    attn_out = lax.psum(attn_part.astype(jnp.bfloat16), TENSOR).astype(jnp.float32)
    hidden_state = inputs + residual_mult * attn_out
    feed_set = feed_shards(feed_gain, gate_weight, up_weight, down_weight)
    gain_two = feed_set[0].astype(jnp.float32)
    inverse_two = lax.rsqrt(
        jnp.mean(hidden_state * hidden_state, axis=-1, keepdims=True) + norm_eps
    )
    unit_two = hidden_state * inverse_two
    normed_two = (unit_two * gain_two).astype(jnp.bfloat16)
    gate_out = jnp.dot(normed_two, feed_set[1], preferred_element_type=jnp.float32)
    up_out = jnp.dot(normed_two, feed_set[2], preferred_element_type=jnp.float32)
    inner_act = (jax.nn.silu(gate_out) * up_out).astype(jnp.bfloat16)
    feed_part = dot_last(inner_act, feed_set[3])
    feed_out = lax.psum(feed_part.astype(jnp.bfloat16), TENSOR).astype(jnp.float32)
    output = hidden_state + residual_mult * feed_out
    cotangent = out_grad[0].astype(jnp.float32) * local_valid[:, None].astype(jnp.float32)
    feed_back = feed_shards(feed_gain, gate_weight, up_weight, down_weight)
    feed_grad = (residual_mult * cotangent).astype(jnp.bfloat16)
    down_term = dot_first(feed_grad, inner_act)
    inner_grad = jnp.dot(feed_grad, feed_back[3], preferred_element_type=jnp.float32)
    sigmoid_gate = jax.nn.sigmoid(gate_out)
    gate_grad = (
        inner_grad * up_out * sigmoid_gate * (1.0 + gate_out * (1.0 - sigmoid_gate))
    ).astype(jnp.bfloat16)
    up_grad = (inner_grad * jax.nn.silu(gate_out)).astype(jnp.bfloat16)
    gate_term = dot_first(normed_two, gate_grad)
    up_term = dot_first(normed_two, up_grad)
    normed_part_two = dot_last(gate_grad, feed_back[1])
    normed_part_two = normed_part_two + dot_last(up_grad, feed_back[2])
    normed_grad_two = lax.psum(normed_part_two.astype(jnp.bfloat16), TENSOR).astype(jnp.float32)
    feed_gain_term = jnp.sum(normed_grad_two * unit_two, axis=0)
    hidden_grad = cotangent + norm_back(normed_grad_two, unit_two, gain_two, inverse_two)
    feed_sums = (
        lax.psum_scatter(feed_gain_term, (FSDP, CONTEXT), scatter_dimension=0, tiled=True),
        lax.psum_scatter(gate_term, (FSDP, CONTEXT), scatter_dimension=0, tiled=True),
        lax.psum_scatter(up_term, (FSDP, CONTEXT), scatter_dimension=0, tiled=True),
        lax.psum_scatter(down_term, (FSDP, CONTEXT), scatter_dimension=0, tiled=True),
    )
    attn_back = attention_shards(
        attention_gain, query_weight, key_weight, value_weight, output_weight
    )
    attn_grad = (residual_mult * hidden_grad).astype(jnp.bfloat16)
    out_term = dot_first(attn_grad, attended)
    mixed_grad = jnp.dot(attn_grad, attn_back[4], preferred_element_type=jnp.float32).astype(
        jnp.bfloat16
    )
    mixed_grad_heads = mixed_grad.reshape(local_rows, kv_local, per_group, HEAD).transpose(
        1, 0, 2, 3
    )

    def head_backward(pieces):
        query_head, key_head, value_head, grad_head, log_head = pieces
        scores = head_scores(query_head, key_head)
        probabilities = jnp.exp(scores - log_head[..., None])
        prob_low = probabilities.astype(jnp.bfloat16)
        prob_grad = jnp.einsum(
            "tgd,sd->gts", grad_head, value_head, preferred_element_type=jnp.float32
        )
        row_dot = jnp.sum(probabilities * prob_grad, axis=-1, keepdims=True)
        score_grad = (attention_mult * probabilities * (prob_grad - row_dot)).astype(jnp.bfloat16)
        query_grad = jnp.einsum(
            "gts,sd->tgd", score_grad, key_head, preferred_element_type=jnp.float32
        )
        key_grad = jnp.einsum(
            "gts,tgd->sd", score_grad, query_head, preferred_element_type=jnp.float32
        )
        value_grad = jnp.einsum(
            "gts,tgd->sd", prob_low, grad_head, preferred_element_type=jnp.float32
        )
        return (query_grad, key_grad, value_grad)

    query_grads, key_grads, value_grads = lax.map(
        head_backward, (query_heads, key_heads, value_heads, mixed_grad_heads, log_totals)
    )
    key_grads = key_grads.transpose(1, 0, 2).reshape(group_rows, kv_local * HEAD)
    value_grads = value_grads.transpose(1, 0, 2).reshape(group_rows, kv_local * HEAD)
    local_key_grad, local_value_grad = (
        lax.psum_scatter(
            key_grads.astype(jnp.bfloat16), CONTEXT, scatter_dimension=0, tiled=True
        ).astype(jnp.float32),
        lax.psum_scatter(
            value_grads.astype(jnp.bfloat16), CONTEXT, scatter_dimension=0, tiled=True
        ).astype(jnp.float32),
    )
    query_grad_rot = query_grads.transpose(1, 0, 2, 3).reshape(local_rows, heads_local, HEAD)
    query_grad_low = (
        rotate_back(query_grad_rot, cos_table, sine_table)
        .reshape(local_rows, heads_local * HEAD)
        .astype(jnp.bfloat16)
    )
    key_grad_low = (
        rotate_back(local_key_grad.reshape(local_rows, kv_local, HEAD), cos_table, sine_table)
        .reshape(local_rows, kv_local * HEAD)
        .astype(jnp.bfloat16)
    )
    value_grad_low = local_value_grad.astype(jnp.bfloat16)
    query_term = dot_first(normed_one, query_grad_low)
    key_term = dot_first(normed_one, key_grad_low)
    value_term = dot_first(normed_one, value_grad_low)
    normed_part_one = dot_last(query_grad_low, attn_back[1])
    normed_part_one = normed_part_one + dot_last(key_grad_low, attn_back[2])
    normed_part_one = normed_part_one + dot_last(value_grad_low, attn_back[3])
    normed_grad_one = lax.psum(normed_part_one.astype(jnp.bfloat16), TENSOR).astype(jnp.float32)
    attn_gain_term = jnp.sum(normed_grad_one * unit_one, axis=0)
    input_grad = hidden_grad + norm_back(normed_grad_one, unit_one, gain_one, inverse_one)
    attn_sums = (
        lax.psum_scatter(attn_gain_term, (FSDP, CONTEXT), scatter_dimension=0, tiled=True),
        lax.psum_scatter(query_term, (FSDP, CONTEXT), scatter_dimension=0, tiled=True),
        lax.psum_scatter(key_term, (FSDP, CONTEXT), scatter_dimension=0, tiled=True),
        lax.psum_scatter(value_term, (FSDP, CONTEXT), scatter_dimension=0, tiled=True),
        lax.psum_scatter(out_term, (FSDP, CONTEXT), scatter_dimension=0, tiled=True),
    )
    return (
        output.astype(jnp.bfloat16)[None],
        input_grad.astype(jnp.bfloat16)[None],
        attn_sums[0],
        attn_sums[1],
        attn_sums[2],
        attn_sums[3],
        attn_sums[4],
        feed_sums[0],
        feed_sums[1],
        feed_sums[2],
        feed_sums[3],
    )


def flip(i, k):
    if k == 0:
        return i
    if k == 1:
        return i + 1 - 2 * lax.rem(i, 2)
    if k == 2:
        return lax.rem(i + 2, 4)
    return 3 - i


class Copies:
    def __init__(self, send, receive):
        self.send, self.receive = send, receive
        self.count, self.started = 0, []

    def index(self):
        self.count += 1
        return self.count - 1

    def make(self, i, source, target, device):
        return pltpu.make_async_remote_copy(
            src_ref=source,
            dst_ref=target,
            send_sem=self.send.at[i],
            recv_sem=self.receive.at[i],
            device_id=device,
            device_id_type=pl.DeviceIdType.MESH,
        )

    def start(self, source, target, device, i=None):
        i = self.index() if i is None else i
        copy = self.make(i, source, target, device)
        copy.start()
        self.started.append(copy)
        return copy


def greet(partners):
    barrier = pltpu.get_barrier_semaphore()
    for device in partners:
        pl.semaphore_signal(barrier, inc=1, device_id=device, device_id_type=pl.DeviceIdType.MESH)
    pl.semaphore_wait(barrier, len(partners))


def dot_tile(left, right, left_axis, right_axis):
    return lax.dot_general(left, right, (((left_axis,), (right_axis,)), ((), ())), preferred_element_type=jnp.float32)


TILE = 256


def turn_lanes(x, low):
    return jnp.where(low, pltpu.roll(x, x.shape[1] - HEAD // 2, 1), pltpu.roll(x, HEAD // 2, 1))


def low_lanes(shape, width):
    return lax.rem(lax.broadcasted_iota(jnp.int32, shape, 1), 2 * width) < width


def split_pair(x):
    low = low_lanes(x.shape, HEAD)
    a, b = jnp.where(low, x, 0.0), jnp.where(low, 0.0, x)
    return a, pltpu.roll(a, HEAD, 1), pltpu.roll(b, HEAD, 1), b


def attention_kernel(
    wa, wf, xt, gain, fgx, cos, sin, seg_col, seg_row,
    wa_out, wf_all, normed_out, q, kv, logs, attended, hidden_out, normed_two, fg_all, gains,
    wa_all, x_all, gain_all, normed, pairs, sums, mine, cross, crossed, totals, landed, send, receive, local,
):
    f32, bf16 = jnp.float32, jnp.bfloat16
    z, c, t = (lax.axis_index(a) for a in (FSDP, CONTEXT, TENSOR))
    peers = [(flip(z, i), flip(c, j), t) for i in range(4) for j in range(4) if i or j]
    core = (z, c, 1 - t)
    greet(peers + [core])
    net = Copies(send, receive)
    middle = (z == 1) | (z == 2)
    nt, part, width = xt.shape
    rows = nt * part
    q_cols = q.shape[1]
    hidden = wf_all.shape[4]

    def columns(owner):
        return pl.ds(pl.multiple_of(owner * hidden, hidden), hidden)

    qkv_cols = q_cols + 2 * HEAD
    ends = []
    own = []
    for i, (source, target) in enumerate(
        (
            (wa.at[c], wa_all.at[z, c]),
            (xt, x_all.at[c]),
            (wf.at[:, :, columns(z)], wf_all.at[:, z, c]),
            (gain, gain_all.at[z, c]),
            (fgx, fg_all.at[0, 0]),
        )
    ):
        own.append(pltpu.make_async_copy(source, target, local.at[i]))
        own[-1].start()

    def spread(source, slot, forward):
        one = net.start(source, slot(1), (flip(z, 1), c, t))
        two = net.start(source, slot(2), (flip(z, 2), c, t))
        three = net.index()
        direct = net.make(three, source, slot(3), (3 - z, c, t))
        pl.when(middle)(direct.start)
        passed = pltpu.make_async_remote_copy(
            src_ref=forward[0],
            dst_ref=forward[1],
            send_sem=send.at[net.index()],
            recv_sem=receive.at[three],
            device_id=(flip(z, 1), c, t),
            device_id_type=pl.DeviceIdType.MESH,
        )
        return one, two, direct, passed

    class Chain:
        def __init__(self, source, block):
            self.one = net.start(source, block(0, 1), (flip(z, 1), c, t))
            two, three = net.index(), net.index()
            self.direct = net.make(three, source, block(0, 3), (3 - z, c, t))
            self.near = net.make(two, block(1, 1), block(1, 2), (3 - z, c, t))
            self.over = self.hop(two, block(3, 3), block(3, 2))
            self.far = self.hop(three, block(2, 2), block(2, 3))
            pl.when(middle)(self.direct.start)

        def hop(self, receives, source, target):
            return pltpu.make_async_remote_copy(
                src_ref=source,
                dst_ref=target,
                send_sem=send.at[net.index()],
                recv_sem=receive.at[receives],
                device_id=(flip(z, 1), c, t),
                device_id_type=pl.DeviceIdType.MESH,
            )

        def pass_near(self):
            self.one.wait_recv()
            pl.when(middle)(self.near.start)

        def pass_far(self):
            self.direct.wait_recv()
            pl.when(middle)(self.over.start)
            self.near.wait_recv()
            pl.when(middle)(self.far.start)

        def end(self):
            for copy in (self.direct, self.near, self.over, self.far):
                pl.when(middle)(copy.wait_send)

    attn_in = [net.start(wa.at[flip(c, k)], wa_all.at[z, c], (z, flip(c, k), t)) for k in (1, 2, 3)]
    tokens_in = [net.start(xt.at[t], x_all.at[c, t], (z, flip(c, k), t)) for k in (1, 2, 3)]
    parts = {k: (0, 1, 2) if k == 2 else (slice(None),) for k in range(4)}

    def weights_to(k):
        there = columns(flip(z, k))
        return [net.start(wf.at[m, :, there], wf_all.at[m, z, c], (flip(z, k), c, t)) for m in parts[k]]

    ff_in = {1: weights_to(1)}
    for device in peers:
        ends.append(net.start(gain, gain_all.at[z, c], device))
    own[2].wait()
    ff_out = {}

    def pass_on(k, m):
        piece = wf_all.at[m, flip(z, k), c]
        ff_out.setdefault(k, []).append([net.start(piece, piece, (z, flip(c, j), t)) for j in (1, 2)])

    pass_on(0, slice(None))
    weights = []
    for j in range(4):
        if j:
            attn_in[j - 1].wait_recv()
        else:
            own[0].wait()
        piece = wa_all.at[z, flip(c, j)]
        passed_piece = wa_all.at[flip(z, 2), flip(c, j)]
        weights.append(spread(piece, lambda k, piece=piece: piece, (passed_piece, passed_piece)))
    for k in (3, 2):
        ff_in[k] = weights_to(k)
    feed = Chain(fgx, lambda _, j: fg_all.at[j, 0])
    swaps = [net.start(fgx, fg_all.at[0, 1], core)]
    token_swaps = []
    for k, copy in zip((1, 2, 3), tokens_in):
        copy.wait_recv()
        piece = x_all.at[flip(c, k), t]
        token_swaps.append(net.start(piece, piece, core))
    halves = []

    def corner(k):
        zs = flip(z, k)
        for m, (one, two) in zip(parts[k], ff_out[k]):
            two.wait_recv()
            piece = wf_all.at[m, zs, flip(c, 2), pl.ds(0, 64)]
            halves.append(net.start(piece, piece, (z, flip(c, 1), t)))
            one.wait_recv()
            piece = wf_all.at[m, zs, flip(c, 1), pl.ds(64, 64)]
            halves.append(net.start(piece, piece, (z, flip(c, 2), t)))

    def onward(k):
        for m, copy in zip(parts[k], ff_in[k]):
            copy.wait_recv()
            pass_on(k, m)

    own[1].wait()
    own[3].wait()
    for copy in token_swaps + ends:
        copy.wait_recv()
    for i in range(2):
        gains[i : i + 1, :] = jnp.concatenate(
            [gain_all[a, b, i : i + 1, :].astype(f32) for a in range(4) for b in range(4)], axis=1
        )

    def norm_rows(i, carry):
        x = x_all[i].reshape(rows, width).astype(f32)
        inverse = lax.rsqrt(jnp.mean(x * x, axis=-1, keepdims=True) + norm_eps)
        normed[i] = (x * inverse * gains[0:1, :]).astype(bf16)
        return carry

    lax.fori_loop(0, 4, norm_rows, 0)
    save = [pltpu.make_async_copy(normed, normed_out, local.at[5])]
    save[0].start()
    onward(1)
    corner(0)
    for one, two, direct, passed in weights:
        two.wait_recv()
        pl.when(middle)(passed.start)
    for one, two, direct, passed in weights:
        one.wait_recv()
        direct.wait_recv()
    save.append(pltpu.make_async_copy(wa_all, wa_out, local.at[6]))
    save[1].start()

    def project(i, carry):
        here = pl.ds(pl.multiple_of(i * rows, rows), rows)
        w = wa_all[...].reshape(width, wa_all.shape[3])
        qkv = dot_tile(normed[i], w[:, :qkv_cols], 1, 0)
        cos_b, sin_b = cos[here, :], sin[here, :]
        quarter = low_lanes(cos_b.shape, HEAD // 2)
        half = low_lanes(cos_b.shape, HEAD)
        for p in range(q_cols // 128):
            block = qkv[:, p * 128 : (p + 1) * 128]
            q[here, p * 128 : (p + 1) * 128] = (block * cos_b + turn_lanes(block, quarter) * sin_b).astype(bf16)
        block = qkv[:, q_cols:]
        block = jnp.where(half, block * cos_b + turn_lanes(block, quarter) * sin_b, block)
        kv[here, :] = block.astype(bf16)
        for j, piece in enumerate(split_pair(block)):
            pairs[j, here, :] = piece.astype(bf16)
        return carry

    lax.fori_loop(0, 4, project, 0)
    corner(1)
    feed.pass_near()

    def attend(i):
        count = (i + 1) * rows
        here = pl.ds(i * rows, rows)
        keep = (seg_col[here, :] == seg_row[:, :count]) & (
            lax.broadcasted_iota(jnp.int32, (rows, count), 0) + i * rows
            >= lax.broadcasted_iota(jnp.int32, (rows, count), 1)
        )
        lane = lax.broadcasted_iota(jnp.int32, (rows, 128), 1)

        def pair(p, log_sums):
            block = pl.ds(pl.multiple_of(p * 128, 128), 128)
            out = jnp.zeros((rows, 128), f32)
            for e in range(2):
                scores = dot_tile(q[here, block], pairs[e, :count, :], 1, 1)
                scores = jnp.where(keep, scores * attention_mult, -1e30)
                highest = jnp.max(scores, axis=-1, keepdims=True)
                weight = jnp.exp(scores - highest)
                total = jnp.sum(weight, axis=-1, keepdims=True)
                out = out + dot_tile((weight / total).astype(bf16), pairs[2 + e, :count, :], 1, 0)
                log_sums = jnp.where(lane == 2 * p + e, highest + jnp.log(total), log_sums)
            attended[here, block] = out.astype(bf16)
            return log_sums

        logs[here, :] = lax.fori_loop(0, q_cols // 128, pair, jnp.zeros((rows, 128), f32))

    attend(0)
    attend(1)
    onward(3)
    attend(2)
    last = pl.ds(3 * rows, rows)
    both = (pairs[2, last, :] + pairs[3, last, :]).astype(bf16)
    for p in range(q_cols // 128):
        attended[last, p * 128 : (p + 1) * 128] = both
    corner(3)

    crosses, outs = {}, {}
    for k in (3, 1, 2, 0):
        mine_rows = pl.ds(pl.multiple_of(flip(c, k) * rows, rows), rows)

        def out_tile(n, carry, mine_rows=mine_rows):
            here = pl.ds(pl.multiple_of(n * 128, 128), 128)
            w = wa_all[lax.div(n, 4), lax.rem(n, 4), :, qkv_cols:]
            sums[:, here] = dot_tile(attended[mine_rows, :], w, 1, 1)
            return carry

        lax.fori_loop(0, width // 128, out_tile, 0)
        mine[k] = sums[pl.ds(pl.multiple_of(t * part, part), part), :]
        cross[k] = sums[pl.ds(pl.multiple_of((1 - t) * part, part), part), :].astype(bf16)
        crosses[k] = net.start(cross.at[k], crossed.at[k], core)
    for k in (3, 1, 2):
        crosses[k].wait_recv()
        totals[k - 1] = (mine[k] + crossed[k].astype(f32)).astype(bf16)
        outs[k] = net.start(totals.at[k - 1], landed.at[k - 1], (z, flip(c, k), t))
    onward(2)
    swaps.append(net.start(fg_all.at[1, 0], fg_all.at[1, 1], core))
    crosses[0].wait_recv()
    total = mine[0] + crossed[0].astype(f32)
    for k in (1, 2, 3):
        outs[k].wait_recv()
        total = total + landed[k - 1].astype(f32)
    hidden = xt[t].astype(f32) + residual_mult * total
    hidden_out[...] = hidden
    inverse = lax.rsqrt(jnp.mean(hidden * hidden, axis=-1, keepdims=True) + norm_eps)
    normed_two[...] = (hidden * inverse * gains[1:2, :]).astype(bf16)
    feed.pass_far()
    for k in (2, 3):
        swaps.append(net.start(fg_all.at[k, 0], fg_all.at[k, 1], core))
    corner(2)
    for copy in halves + swaps:
        copy.wait_recv()
    feed.end()
    for _, _, direct, passed in weights:
        pl.when(middle)(direct.wait_send)
        pl.when(middle)(passed.wait_send)
    for copy in net.started:
        copy.wait_send()
    own[4].wait()
    for copy in save:
        copy.wait()


def attention_forward(wa, wf, xt, gain, fgx, cos, sin, seg_col, seg_row):
    bf16, f32 = jnp.bfloat16, jnp.float32
    nt, part, width = xt.shape
    rows = nt * part
    total = 4 * rows
    wa_cols = wa.shape[2]
    q_cols = (wa_cols - 2 * HEAD) // 2
    filled = seg_col.shape[0]
    copies = 112
    vmem, anywhere = pl.BlockSpec(memory_space=pltpu.VMEM), pl.BlockSpec(memory_space=pl.ANY)
    outs = (
        ((4, 4) + wa.shape[1:], bf16, anywhere),
        ((3, 4, 4, wf.shape[1], wf.shape[2] // 4), bf16, anywhere),
        ((4, rows, width), bf16, anywhere),
        ((total, q_cols), bf16, vmem),
        ((total, 2 * HEAD), bf16, vmem),
        ((filled, 128), f32, vmem),
        ((total, q_cols), bf16, vmem),
        ((part, width), f32, vmem),
        ((part, width), bf16, vmem),
        ((4, nt, part, width), bf16, anywhere),
        ((2, width), f32, vmem),
    )
    return pl.pallas_call(
        attention_kernel,
        out_shape=[jax.ShapeDtypeStruct(shape, dtype) for shape, dtype, _ in outs],
        in_specs=[vmem] * 9,
        out_specs=[spec for _, _, spec in outs],
        scratch_shapes=[
            pltpu.VMEM((4, 4) + wa.shape[1:], bf16),
            pltpu.VMEM((4, nt, part, width), bf16),
            pltpu.VMEM((4, 4) + gain.shape, bf16),
            pltpu.VMEM((4, rows, width), bf16),
            pltpu.VMEM((4, total, 2 * HEAD), bf16),
            pltpu.VMEM((rows, width), f32),
            pltpu.VMEM((4, part, width), f32),
            pltpu.VMEM((4, part, width), bf16),
            pltpu.VMEM((4, part, width), bf16),
            pltpu.VMEM((3, part, width), bf16),
            pltpu.VMEM((3, part, width), bf16),
            pltpu.SemaphoreType.DMA((copies,)),
            pltpu.SemaphoreType.DMA((copies,)),
            pltpu.SemaphoreType.DMA((7,)),
        ],
        compiler_params=pltpu.CompilerParams(collective_id=1, has_side_effects=True, vmem_limit_bytes=60 * 2**20),
    )(wa, wf, xt, gain, fgx, cos, sin, seg_col, seg_row)


def feed_kernel(
    x, fg, w, back, feed_own, feed_send, terms,
    xs, wv, gate_g, up_g, inner, mine, cross, crossed, totals, landed, send, receive, local,
):
    f32, bf16 = jnp.float32, jnp.bfloat16
    z, c, t = (lax.axis_index(a) for a in (FSDP, CONTEXT, TENSOR))
    core = (z, c, 1 - t)
    greet([(flip(z, k), c, t) for k in (1, 2, 3)] + [core])
    net = Copies(send, receive)
    part, width = x.shape
    hidden = wv.shape[2]
    load = pltpu.make_async_copy(w, wv, local.at[0])
    load.start()
    middle = (z == 1) | (z == 2)
    swaps = {0: net.start(x, xs.at[0, 1], core)}
    arrive = {2: net.start(x, xs.at[2, 0], (flip(z, 2), c, t))}
    three = net.index()
    direct = net.make(three, x, xs.at[3, 0], (3 - z, c, t))
    pl.when(middle)(direct.start)
    arrive[3] = direct
    arrive[1] = net.start(x, xs.at[1, 0], (flip(z, 1), c, t))
    passed = pltpu.make_async_remote_copy(
        src_ref=xs.at[2, 0],
        dst_ref=xs.at[3, 0],
        send_sem=send.at[net.index()],
        recv_sem=receive.at[three],
        device_id=(flip(z, 1), c, t),
        device_id_type=pl.DeviceIdType.MESH,
    )
    xs[0, 0] = x[...]
    load.wait()

    def first(k):
        swaps[k].wait_recv()
        rows = xs[k].reshape(2 * part, width)
        grads = fg[k]

        def step(n, carry):
            at = pl.multiple_of(n * TILE, TILE)
            g = dot_tile(rows, wv[0, :, pl.ds(at, TILE)], 1, 0)
            u = dot_tile(rows, wv[1, :, pl.ds(at, TILE)], 1, 0)
            d = dot_tile(grads, wv[2, :, pl.ds(at, TILE)], 1, 0)
            sig = jax.nn.sigmoid(g)
            here = pl.ds(at, TILE)
            inner[k, :, here] = (g * sig * u).astype(bf16)
            gate_g[k, :, here] = (d * u * sig * (1.0 + g * (1.0 - sig))).astype(bf16)
            up_g[k, :, here] = (d * g * sig).astype(bf16)
            return carry

        lax.fori_loop(0, hidden // TILE, step, 0)

    crosses = {}

    def second(k):
        def step(n, carry):
            here = pl.ds(pl.multiple_of(n * TILE, TILE), TILE)
            b = dot_tile(gate_g[k], wv[0, here, :], 1, 1) + dot_tile(up_g[k], wv[1, here, :], 1, 1)
            f = dot_tile(inner[k], wv[2, here, :], 1, 1)
            mine[k, 0, :, here] = b[:part]
            mine[k, 1, :, here] = f[:part]
            cross[k, 0, :, here] = b[part:].astype(bf16)
            cross[k, 1, :, here] = f[part:].astype(bf16)
            return carry

        lax.fori_loop(0, width // TILE, step, 0)
        crosses[k] = net.start(cross.at[k], crossed.at[k], core)

    sums = {}

    def finish(k):
        crosses[k].wait_recv()
        if k:
            totals[k - 1] = (mine[k, 0] + crossed[k, 0].astype(f32)).astype(bf16)
            sums[k] = net.start(totals.at[k - 1], landed.at[k - 1], (flip(z, k), c, t))
            feed_send[k - 1] = (mine[k, 1] + crossed[k, 1].astype(f32)).astype(bf16)
        else:
            back[...] = mine[0, 0] + crossed[0, 0].astype(f32)
            feed_own[...] = mine[0, 1] + crossed[0, 1].astype(f32)

    def fetch(k):
        arrive[k].wait_recv()
        if k == 2:
            pl.when(middle)(passed.start)
        swaps[k] = net.start(xs.at[k, 0], xs.at[k, 1], core)

    order = (0, 2, 3, 1)
    for i, k in enumerate(order):
        first(k)
        if i:
            finish(order[i - 1])
        if i < 3:
            fetch(order[i + 1])
        second(k)

    rows = xs.shape[0] * 2 * part

    def term(source, grads, i):
        def step(m, carry):
            here = pl.ds(pl.multiple_of(m * TILE, TILE), TILE)
            left = source[:, :, here].reshape(rows, TILE)
            value = dot_tile(left, grads[...].reshape(rows, hidden), 0, 0)
            wv[i, here, :] = value.astype(bf16)
            return carry

        lax.fori_loop(0, width // TILE, step, 0)

    flat = xs.reshape(xs.shape[0], 2 * part, width)
    term(flat, gate_g, 0)
    finish(order[3])
    term(flat, up_g, 1)
    term(fg, inner, 2)
    store = pltpu.make_async_copy(wv, terms, local.at[1])
    store.start()
    for k in (1, 2, 3):
        sums[k].wait_recv()
    back[...] = back[...] + landed[0].astype(f32) + landed[1].astype(f32) + landed[2].astype(f32)
    pl.when(middle)(direct.wait_send)
    pl.when(middle)(passed.wait_send)
    for copy in net.started:
        copy.wait_send()
    store.wait()


def feed_forward(x, fg, w):
    bf16, f32 = jnp.bfloat16, jnp.float32
    part, width = x.shape
    hidden = w.shape[2]
    blocks = fg.shape[0]
    copies = 20
    vmem, anywhere = pl.BlockSpec(memory_space=pltpu.VMEM), pl.BlockSpec(memory_space=pl.ANY)
    return pl.pallas_call(
        feed_kernel,
        out_shape=[
            jax.ShapeDtypeStruct((part, width), f32),
            jax.ShapeDtypeStruct((part, width), f32),
            jax.ShapeDtypeStruct((blocks - 1, part, width), bf16),
            jax.ShapeDtypeStruct(w.shape, bf16),
        ],
        in_specs=[vmem, vmem, anywhere],
        out_specs=[vmem, vmem, vmem, anywhere],
        scratch_shapes=[
            pltpu.VMEM((blocks, 2, part, width), bf16),
            pltpu.VMEM(w.shape, bf16),
            pltpu.VMEM((blocks, 2 * part, hidden), bf16),
            pltpu.VMEM((blocks, 2 * part, hidden), bf16),
            pltpu.VMEM((blocks, 2 * part, hidden), bf16),
            pltpu.VMEM((blocks, 2, part, width), f32),
            pltpu.VMEM((blocks, 2, part, width), bf16),
            pltpu.VMEM((blocks, 2, part, width), bf16),
            pltpu.VMEM((blocks - 1, part, width), bf16),
            pltpu.VMEM((blocks - 1, part, width), bf16),
            pltpu.SemaphoreType.DMA((copies,)),
            pltpu.SemaphoreType.DMA((copies,)),
            pltpu.SemaphoreType.DMA((2,)),
        ],
        compiler_params=pltpu.CompilerParams(collective_id=3, has_side_effects=True, vmem_limit_bytes=62 * 2**20),
    )(x, fg, w)


def swap(x, axis, k):
    return lax.ppermute(x, axis, [(i, i ^ k) for i in range(lax.axis_size(axis))])


def cut(x, index, size, axis):
    return lax.dynamic_slice_in_dim(x, index * size, size, axis)


def backward_kernel(
    ff, fs, al, wa_in, normed_in, q, kv, logs, attended, cos, sin, seg_col, seg_row,
    feed_in, back_own, back_in, ff_out, query_out, kv_out, output_out,
    terms, corner_x, corner_y, side_x, side_y, at_terms, at_in, at_total, wa, normed, ag, pairs, mixed, acc, dqkv,
    sums, mine, cross, crossed, totals, held_feed, held_terms, send, receive, local,
):
    f32, bf16 = jnp.float32, jnp.bfloat16
    z, c, t = (lax.axis_index(a) for a in (FSDP, CONTEXT, TENSOR))
    core = (z, c, 1 - t)
    greet([(flip(z, k), c, t) for k in (1, 2, 3)] + [(z, flip(c, k), t) for k in (1, 2, 3)] + [core])
    net = Copies(send, receive)
    wrows, hidden = ff.shape[3:]
    half = wrows // 2
    part, width = al.shape
    rows = 2 * part
    q_cols = q.shape[1]
    qkv_cols = q_cols + 2 * HEAD
    blocks = normed.shape[0]
    order = (3, 2, 1, 0)
    loads = {}
    for k in order:
        zs = flip(z, k)
        loads[k] = pltpu.make_async_copy(ff.at[:, zs], terms.at[:, zs], local.at[k])
        loads[k].start()
    wa_load = pltpu.make_async_copy(wa_in, wa, local.at[4])
    wa_load.start()
    normed_load = pltpu.make_async_copy(normed_in.at[pl.ds(0, blocks)], normed, local.at[5])
    normed_load.start()
    first = {}

    def corners(k):
        zs = flip(z, k)
        loads[k].wait()
        first[k] = (
            net.start(terms.at[:, zs, flip(c, 3), pl.ds(0, half)], corner_x.at[k], (z, flip(c, 1), t)),
            net.start(terms.at[:, zs, flip(c, 3), pl.ds(half, half)], corner_y.at[k], (z, flip(c, 2), t)),
        )

    corners(3)
    ag_in = [net.start(al, ag.at[c, t], (z, flip(c, k), t)) for k in (3, 1, 2)]
    swaps = [net.start(al, ag.at[c, t], core)]
    middle = (z == 1) | (z == 2)
    chains = []

    class Sums:
        def __init__(self, mine, held, landed):
            self.mine, self.held, self.landed = mine, held, landed
            neighbour = (flip(z, 1), c, t)
            self.ends = [net.make(net.index(), mine(k), held(k), neighbour) for k in (3, 2)]
            for copy in self.ends:
                pl.when(jnp.logical_not(middle))(copy.start)
            self.one = net.start(mine(1), landed(0), neighbour)
            two, spare = net.index(), net.index()
            self.out = [net.make(two, held(2), landed(1), (3 - z, c, t))]
            self.out.append(
                pltpu.make_async_remote_copy(
                    src_ref=held(3),
                    dst_ref=landed(1),
                    send_sem=send.at[spare],
                    recv_sem=receive.at[two],
                    device_id=(flip(z, 2), c, t),
                    device_id_type=pl.DeviceIdType.MESH,
                )
            )
            chains.append(self)

        def add(self, k, own):
            held, mine = self.held(k), self.mine(own)
            for i in range(held.shape[0]) if len(held.shape) == 3 else (slice(None),):
                held[i] = (held[i].astype(f32) + mine[i].astype(f32)).astype(bf16)

        def hand_on(self):
            @pl.when(middle)
            def _():
                for copy in self.ends:
                    copy.wait_recv()
                self.add(3, 2)
                self.out[1].start()
                self.add(2, 3)
                self.out[0].start()

        def wait_in(self):
            self.one.wait_recv()
            self.out[0].wait_recv()

        def wait_out(self):
            for copy in self.ends:
                pl.when(jnp.logical_not(middle))(copy.wait_send)
            for copy in self.out:
                pl.when(middle)(copy.wait_send)

    feed = Sums(lambda k: fs.at[k - 1], lambda k: held_feed.at[k - 2], lambda i: feed_in.at[i])
    corners(2)
    ag[c, t] = al[...]
    for j, piece in enumerate(split_pair(kv[...].astype(f32))):
        pairs[j] = piece.astype(bf16)
    acc[...] = jnp.zeros_like(acc)
    dqkv[pl.ds(blocks * rows, rows), :] = jnp.zeros((rows, qkv_cols), bf16)
    for k, copy in zip((3, 1, 2), ag_in):
        copy.wait_recv()
        piece = ag.at[flip(c, k), t]
        swaps.append(net.start(piece, piece, core))
    second, third = {}, {}

    def sides(k):
        zs = flip(z, k)
        for copy in first[k]:
            copy.wait_recv()
        low, high = pl.ds(0, half), pl.ds(half, half)
        xb, yb = flip(c, 1), flip(c, 2)
        for m in range(3):
            terms[m, zs, yb, low] = (terms[m, zs, yb, low].astype(f32) + corner_x[k, m].astype(f32)).astype(bf16)
            terms[m, zs, xb, high] = (terms[m, zs, xb, high].astype(f32) + corner_y[k, m].astype(f32)).astype(bf16)
        second[k] = (
            net.start(terms.at[:, zs, yb], side_y.at[k], (z, yb, t)),
            net.start(terms.at[:, zs, xb], side_x.at[k], (z, xb, t)),
        )

    def owners(k):
        zs = flip(z, k)
        for copy in second[k]:
            copy.wait_recv()
        for m in range(3):
            total = terms[m, zs, c].astype(f32) + side_x[k, m].astype(f32) + side_y[k, m].astype(f32)
            terms[m, zs, c] = total.astype(bf16)
        columns = ff_out.at[:, :, pl.ds(pl.multiple_of(z * hidden, hidden), hidden)]
        if k:
            third[k] = net.start(terms.at[:, zs, c], columns, (zs, c, t))
        else:
            third[0] = pltpu.make_async_copy(terms.at[:, z, c], columns, local.at[6])
            third[0].start()

    for copy in swaps:
        copy.wait_recv()
    wa_load.wait()
    normed_load.wait()

    def mix(i, carry):
        w = wa[...].reshape(width, wa.shape[3])[:, qkv_cols:]
        here = pl.ds(pl.multiple_of(i * rows, rows), rows)
        mixed[here, :] = dot_tile(ag[i].reshape(rows, width), w, 1, 0).astype(bf16)
        return carry

    lax.fori_loop(0, blocks, mix, 0)
    sides(3)
    corners(1)

    def out_term(m, carry):
        here = pl.ds(pl.multiple_of(m * wrows, wrows), wrows)
        left = ag[0:blocks, :, :, here].reshape(blocks * rows, wrows)
        value = dot_tile(left, attended[0 : blocks * rows, :], 0, 0)
        at_terms[lax.div(m, 4), lax.rem(m, 4), :, qkv_cols:] = value.astype(bf16)
        return carry

    lax.fori_loop(0, width // wrows, out_term, 0)

    def terms_to(columns):
        return Sums(
            lambda k: at_terms.at[flip(z, k), :, :, columns],
            lambda k: held_terms.at[k - 2, :, :, columns],
            lambda i: at_in.at[i, :, :, columns],
        )

    output_sums = terms_to(pl.ds(qkv_cols, q_cols))
    feed.hand_on()
    sides(2)
    corners(0)

    def attend(i):
        count = (i + 1) * rows
        here = pl.ds(i * rows, rows)
        keep = (seg_col[here, :] == seg_row[:, :count]) & (
            lax.broadcasted_iota(jnp.int32, (rows, count), 0) + i * rows
            >= lax.broadcasted_iota(jnp.int32, (rows, count), 1)
        )
        log_sums = logs[here, :]
        lane = lax.broadcasted_iota(jnp.int32, (rows, 128), 1)
        cos_b, sin_b = cos[here, :], sin[here, :]
        quarter = low_lanes(cos_b.shape, HEAD // 2)

        def pair(p, carry):
            block = pl.ds(pl.multiple_of(p * 128, 128), 128)
            grad = jnp.zeros((rows, 128), f32)
            for e in range(2):
                scores = dot_tile(q[here, block], pairs[e, :count, :], 1, 1)
                scores = jnp.where(keep, scores * attention_mult, -1e30)
                log = jnp.sum(jnp.where(lane == 2 * p + e, log_sums, 0.0), axis=-1, keepdims=True)
                prob = jnp.exp(scores - log)
                prob_grad = dot_tile(mixed[here, block], pairs[2 + e, :count, :], 1, 1)
                row_dot = jnp.sum(prob * prob_grad, axis=-1, keepdims=True)
                score_grad = (attention_mult * prob * (prob_grad - row_dot)).astype(bf16)
                grad = grad + dot_tile(score_grad, pairs[e, :count, :], 1, 0)
                acc[e, :count, :] += dot_tile(score_grad, q[here, block], 0, 0)
                acc[2 + e, :count, :] += dot_tile(prob.astype(bf16), mixed[here, block], 0, 0)
            dqkv[here, block] = (grad * cos_b + turn_lanes(grad * sin_b, quarter)).astype(bf16)
            return carry

        lax.fori_loop(0, q_cols // 128, pair, 0)

    attend(0)
    output_sums.hand_on()
    attend(1)
    owners(3)
    sides(1)
    attend(2)
    sides(0)
    owners(2)
    filled = blocks * rows
    low = low_lanes((filled, 128), HEAD)
    key_grad = jnp.where(low, acc[0], 0.0) + pltpu.roll(jnp.where(low, 0.0, acc[1]), HEAD, 1)
    value_grad = jnp.where(low, 0.0, acc[3]) + pltpu.roll(jnp.where(low, acc[2], 0.0), HEAD, 1)
    turned = turn_lanes(key_grad * sin[0:filled, :], low_lanes((filled, 128), HEAD // 2))
    key_grad = key_grad * cos[0:filled, :] + turned
    dqkv[0:filled, q_cols:] = jnp.where(low, key_grad, value_grad).astype(bf16)

    crosses, outs = {}, {}
    for k in (3, 1, 2, 0):
        mine_rows = pl.ds(pl.multiple_of(flip(c, k) * rows, rows), rows)

        def back_tile(n, carry, mine_rows=mine_rows):
            here = pl.ds(pl.multiple_of(n * 128, 128), 128)
            w = wa[lax.div(n, 4), lax.rem(n, 4), :, :qkv_cols]
            sums[:, here] = dot_tile(dqkv[mine_rows, :], w, 1, 1)
            return carry

        lax.fori_loop(0, width // 128, back_tile, 0)
        mine[k] = sums[pl.ds(pl.multiple_of(t * part, part), part), :]
        cross[k] = sums[pl.ds(pl.multiple_of((1 - t) * part, part), part), :].astype(bf16)
        crosses[k] = net.start(cross.at[k], crossed.at[k], core)
    for k in (3, 1, 2):
        crosses[k].wait_recv()
        totals[k - 1] = (mine[k] + crossed[k].astype(f32)).astype(bf16)
        outs[k] = net.start(totals.at[k - 1], back_in.at[k - 1], (z, flip(c, k), t))
    crosses[0].wait_recv()
    back_own[...] = mine[0] + crossed[0].astype(f32)

    def qkv_term(m, carry):
        here = pl.ds(pl.multiple_of(m * wrows, wrows), wrows)
        left = normed[:, :, here].reshape(filled, wrows)
        value = dot_tile(left, dqkv[0:filled, :], 0, 0)
        at_terms[lax.div(m, 4), lax.rem(m, 4), :, :qkv_cols] = value.astype(bf16)
        return carry

    lax.fori_loop(0, width // wrows, qkv_term, 0)
    qkv_sums = terms_to(pl.ds(0, qkv_cols))
    owners(1)
    owners(0)
    qkv_sums.hand_on()
    output_sums.wait_in()
    qkv_sums.wait_in()
    for j in range(4):
        total = at_terms[z, j].astype(f32)
        for i in range(2):
            total = total + at_in[i, j].astype(f32)
        at_total[j] = total.astype(bf16)
    here = pl.ds(pl.multiple_of(c * q_cols, q_cols), q_cols)
    attn_out, keep_own = [], []
    for i, (columns, target) in enumerate(
        (
            (pl.ds(0, q_cols), query_out.at[:, here]),
            (pl.ds(q_cols, 2 * HEAD), kv_out.at[c]),
            (pl.ds(qkv_cols, q_cols), output_out.at[:, here]),
        )
    ):
        attn_out += [net.start(at_total.at[flip(c, k), :, columns], target, (z, flip(c, k), t)) for k in (1, 2, 3)]
        keep_own.append(pltpu.make_async_copy(at_total.at[c, :, columns], target, local.at[7 + i]))
        keep_own[-1].start()
    feed.wait_in()
    for chain in chains:
        chain.wait_out()
    for copy in attn_out + [outs[k] for k in (1, 2, 3)] + [third[k] for k in (1, 2, 3)]:
        copy.wait_recv()
    for copy in net.started:
        copy.wait_send()
    third[0].wait()
    for copy in keep_own:
        copy.wait()


def backward(ff, fs, al, wa, normed, q, kv, logs, attended, cos, sin, seg_col, seg_row):
    bf16, f32 = jnp.bfloat16, jnp.float32
    wrows, hidden = ff.shape[3:]
    attn_cols = wa.shape[3]
    part, width = al.shape
    total = q.shape[0]
    filled = seg_col.shape[0]
    rows = 2 * part
    blocks = filled // rows
    copies = 64
    vmem, anywhere = pl.BlockSpec(memory_space=pltpu.VMEM), pl.BlockSpec(memory_space=pl.ANY)
    return pl.pallas_call(
        backward_kernel,
        out_shape=[
            jax.ShapeDtypeStruct((2,) + al.shape, bf16),
            jax.ShapeDtypeStruct(al.shape, f32),
            jax.ShapeDtypeStruct(fs.shape, bf16),
            jax.ShapeDtypeStruct((3, wrows, 4 * hidden), bf16),
            jax.ShapeDtypeStruct((wrows, 4 * q.shape[1]), bf16),
            jax.ShapeDtypeStruct((4, wrows, 2 * HEAD), bf16),
            jax.ShapeDtypeStruct((wrows, 4 * q.shape[1]), bf16),
        ],
        in_specs=[anywhere, vmem, vmem, anywhere, anywhere] + [vmem] * 8,
        out_specs=[anywhere, vmem] + [anywhere] * 5,
        scratch_shapes=[
            pltpu.VMEM(ff.shape, bf16),
            pltpu.VMEM((4, 3, wrows // 2, hidden), bf16),
            pltpu.VMEM((4, 3, wrows // 2, hidden), bf16),
            pltpu.VMEM((4, 3, wrows, hidden), bf16),
            pltpu.VMEM((4, 3, wrows, hidden), bf16),
            pltpu.VMEM((4, 4, wrows, attn_cols), bf16),
            pltpu.VMEM((2, 4, wrows, attn_cols), bf16),
            pltpu.VMEM((4, wrows, attn_cols), bf16),
            pltpu.VMEM(wa.shape, bf16),
            pltpu.VMEM((blocks, rows, width), bf16),
            pltpu.VMEM((4, 2, part, width), bf16),
            pltpu.VMEM((4, total, 2 * HEAD), bf16),
            pltpu.VMEM((filled, q.shape[1]), bf16),
            pltpu.VMEM((4, filled, 2 * HEAD), f32),
            pltpu.VMEM((total, q.shape[1] + 2 * HEAD), bf16),
            pltpu.VMEM((rows, width), f32),
            pltpu.VMEM((4, part, width), f32),
            pltpu.VMEM((4, part, width), bf16),
            pltpu.VMEM((4, part, width), bf16),
            pltpu.VMEM((3, part, width), bf16),
            pltpu.VMEM((2, part, width), bf16),
            pltpu.VMEM((2, 4, wrows, attn_cols), bf16),
            pltpu.SemaphoreType.DMA((copies,)),
            pltpu.SemaphoreType.DMA((copies,)),
            pltpu.SemaphoreType.DMA((10,)),
        ],
        compiler_params=pltpu.CompilerParams(collective_id=2, has_side_effects=True, vmem_limit_bytes=63 * 2**20),
    )(ff, fs, al, wa, normed, q, kv, logs, attended, cos, sin, seg_col, seg_row)


def on_device_split(
    tokens,
    out_grad,
    lengths,
    attention_gain,
    query_weight,
    key_weight,
    value_weight,
    output_weight,
    feed_gain,
    gate_weight,
    up_weight,
    down_weight,
):
    f32, bf16 = jnp.float32, jnp.bfloat16
    nz, nc, nt = (lax.axis_size(a) for a in (FSDP, CONTEXT, TENSOR))
    z, c, t = (lax.axis_index(a) for a in (FSDP, CONTEXT, TENSOR))
    local_rows, width = tokens.shape[1:]
    group_rows = local_rows * nc
    filled = group_rows * 3 // 4
    part = local_rows // nt
    wrows = query_weight.shape[0]
    kv_cols = key_weight.shape[1] // nc
    q_cols = query_weight.shape[1] // nc
    qkv_cols = q_cols + 2 * kv_cols
    ff_cols = gate_weight.shape[1] // nz
    per_group = q_cols // kv_cols
    segment, position, valid_rows = slot_layout(lengths[0], group_rows)
    cos_table, sine_table = rope_tables(position, HEAD)

    wa = jnp.concatenate(
        [
            w.astype(bf16).reshape(wrows, nc, -1).transpose(1, 0, 2)
            for w in (query_weight, key_weight, value_weight, output_weight)
        ],
        axis=2,
    )
    wf = jnp.stack([w.astype(bf16) for w in (gate_weight, up_weight, down_weight)])
    gain = jnp.pad(jnp.stack([attention_gain, feed_gain]).astype(bf16), ((0, 14), (0, 0)))
    my_valid = lax.dynamic_slice_in_dim(valid_rows, c * local_rows + t * part, part)
    cotangent = cut(out_grad[0], t, part, 0).astype(f32) * my_valid[:, None].astype(f32)
    feed_grad = (residual_mult * cotangent).astype(bf16)
    sign = jnp.where(jnp.arange(HEAD) < HEAD // 2, -1.0, 1.0).astype(f32)
    wide_cos = jnp.concatenate([cos_table, cos_table], axis=1)
    wide_sin = jnp.concatenate([sine_table * sign, sine_table * sign], axis=1)
    wa, wf, normed_one, queries, pair, logs, attended, hidden, normed_two, feed_grads, gains = attention_forward(
        wa, wf, tokens[0].reshape(nt, part, width), gain, feed_grad, wide_cos, wide_sin,
        segment[:filled, None], segment[None, :filled],
    )
    gain_one, gain_two = gains[0], gains[1]
    w_feed = wf.reshape(3, width, ff_cols)
    my_inputs = cut(tokens[0], t, part, 0).astype(f32)
    inverse_two = lax.rsqrt(jnp.mean(hidden * hidden, axis=-1, keepdims=True) + norm_eps)
    unit_two = hidden * inverse_two

    normed_grad_two, feed_own, feed_send, ff_terms = feed_forward(
        normed_two, feed_grads.reshape(nz, local_rows, width), w_feed
    )
    ff_terms = ff_terms.reshape(3, nz, nc, wrows, ff_cols)

    def both_cores(x):
        other = swap(x, TENSOR, 1)
        first, last = jnp.where(t == 0, x, other), jnp.where(t == 0, other, x)
        return jnp.concatenate([first, last], axis=0)[None]

    feed_gain_term = jnp.sum(normed_grad_two * unit_two, axis=0)
    hidden_grad = cotangent + norm_back(normed_grad_two, unit_two, gain_two, inverse_two)

    attn_low = (residual_mult * hidden_grad).astype(bf16)
    feed_in, back_own, back_in, ff_grads, grad_query, kv_grads, grad_output = backward(
        ff_terms, feed_send, attn_low, wa, normed_one, queries, pair, logs, attended, wide_cos, wide_sin,
        segment[:filled, None], segment[None, :filled],
    )
    output = both_cores((hidden + residual_mult * (feed_own + jnp.sum(feed_in.astype(f32), axis=0))).astype(bf16))
    normed_grad_one = back_own + jnp.sum(back_in.astype(f32), axis=0)
    inverse_one = lax.rsqrt(jnp.mean(my_inputs * my_inputs, axis=-1, keepdims=True) + norm_eps)
    unit_one = my_inputs * inverse_one
    attn_gain_term = jnp.sum(normed_grad_one * unit_one, axis=0)
    input_grad = both_cores((hidden_grad + norm_back(normed_grad_one, unit_one, gain_one, inverse_one)).astype(bf16))

    gain_terms = jnp.stack([attn_gain_term, feed_gain_term])
    for axis in (TENSOR, CONTEXT, FSDP):
        gain_terms = gain_terms + sum(swap(gain_terms, axis, k) for k in range(1, lax.axis_size(axis)))
    gain_terms = cut(gain_terms, z * nc + c, wrows, 1)

    grad_gate, grad_up, grad_down = (ff_grads[i].astype(f32) for i in range(3))
    grad_key, grad_value = (
        kv_grads[:, :, i : i + HEAD].transpose(1, 0, 2).reshape(wrows, -1).astype(f32) for i in (0, HEAD)
    )
    attn_terms = (grad_query.astype(f32), grad_key, grad_value, grad_output.astype(f32))
    return (output, input_grad, gain_terms[0], *attn_terms, gain_terms[1], grad_gate, grad_up, grad_down)


def solution(mesh):
    split = tuple(mesh.shape[a] for a in (FSDP, CONTEXT, TENSOR)) == (4, 4, 2)
    return jax.shard_map(
        on_device_split if split else on_device,
        mesh=mesh,
        in_specs=(
            P(FSDP, CONTEXT, None),
            P(FSDP, CONTEXT, None),
            P(FSDP, None),
            P((FSDP, CONTEXT)),
            P((FSDP, CONTEXT), TENSOR),
            P((FSDP, CONTEXT), TENSOR),
            P((FSDP, CONTEXT), TENSOR),
            P((FSDP, CONTEXT), TENSOR),
            P((FSDP, CONTEXT)),
            P((FSDP, CONTEXT), TENSOR),
            P((FSDP, CONTEXT), TENSOR),
            P((FSDP, CONTEXT), TENSOR),
        ),
        out_specs=(
            P(FSDP, CONTEXT, None),
            P(FSDP, CONTEXT, None),
            P((FSDP, CONTEXT)),
            P((FSDP, CONTEXT), TENSOR),
            P((FSDP, CONTEXT), TENSOR),
            P((FSDP, CONTEXT), TENSOR),
            P((FSDP, CONTEXT), TENSOR),
            P((FSDP, CONTEXT)),
            P((FSDP, CONTEXT), TENSOR),
            P((FSDP, CONTEXT), TENSOR),
            P((FSDP, CONTEXT), TENSOR),
        ),
        check_vma=False,
    )
```

```python
import jax
import jax.numpy as jnp
from jax import lax
from jax.experimental import pallas as pl
from jax.experimental.pallas import tpu as pltpu
from jax.sharding import PartitionSpec as P

HEAD = 64
FSDP, CONTEXT, TENSOR = "fsdp", "context", "tensor"


norm_eps = 1e-05
attention_mult = 0.015625
residual_mult = 0.22
rope_base = 10000000.0


def slot_layout(seq_lengths, total_rows):
    seq_ends = jnp.cumsum(seq_lengths)
    starts = seq_ends - seq_lengths
    slot_ids = jnp.arange(total_rows, dtype=jnp.int32)
    before = (slot_ids[:, None] >= seq_ends[None, :]).astype(jnp.int32)
    segment = jnp.sum(before, axis=1)
    seq_count = seq_lengths.shape[0]
    valid_rows = segment < seq_count
    inside = (slot_ids[:, None] >= starts[None, :]) & (slot_ids[:, None] < seq_ends[None, :])
    position = jnp.sum(jnp.where(inside, slot_ids[:, None] - starts[None, :], 0), axis=1)
    segment = jnp.where(valid_rows, segment, seq_count + slot_ids)
    return (segment, position, valid_rows)


def rope_tables(position, width):
    half_width = width // 2
    frequency = rope_base ** (-jnp.arange(half_width, dtype=jnp.float32) * 2.0 / width)
    angles = position.astype(jnp.float32)[:, None] * frequency[None, :]
    angles = jnp.concatenate([angles, angles], axis=1)
    return (jnp.cos(angles), jnp.sin(angles))


def turn_half(vectors):
    half_width = vectors.shape[-1] // 2
    return jnp.concatenate([-vectors[..., half_width:], vectors[..., :half_width]], axis=-1)


def rotate(vectors, cos_table, sine_table):
    return vectors * cos_table[:, None, :] + turn_half(vectors) * sine_table[:, None, :]


def rotate_back(grads, cos_table, sine_table):
    return grads * cos_table[:, None, :] - turn_half(grads * sine_table[:, None, :])


def norm_back(normed_grad, unit, gain, inverse):
    scaled = normed_grad * gain
    return inverse * (scaled - unit * jnp.mean(scaled * unit, axis=-1, keepdims=True))


def dot_first(left, right):
    return lax.dot_general(left, right, (((0,), (0,)), ((), ())), preferred_element_type=jnp.float32)


def dot_last(left, right):
    return lax.dot_general(left, right, (((1,), (1,)), ((), ())), preferred_element_type=jnp.float32)


def attention_shards(attention_gain, query_weight, key_weight, value_weight, output_weight):
    return (
        lax.all_gather(
            attention_gain.astype(jnp.bfloat16), (FSDP, CONTEXT), axis=0, tiled=True
        ),
        lax.all_gather(query_weight.astype(jnp.bfloat16), (FSDP, CONTEXT), axis=0, tiled=True),
        lax.all_gather(key_weight.astype(jnp.bfloat16), (FSDP, CONTEXT), axis=0, tiled=True),
        lax.all_gather(value_weight.astype(jnp.bfloat16), (FSDP, CONTEXT), axis=0, tiled=True),
        lax.all_gather(output_weight.astype(jnp.bfloat16), (FSDP, CONTEXT), axis=0, tiled=True),
    )


def feed_shards(feed_gain, gate_weight, up_weight, down_weight):
    return (
        lax.all_gather(feed_gain.astype(jnp.bfloat16), (FSDP, CONTEXT), axis=0, tiled=True),
        lax.all_gather(gate_weight.astype(jnp.bfloat16), (FSDP, CONTEXT), axis=0, tiled=True),
        lax.all_gather(up_weight.astype(jnp.bfloat16), (FSDP, CONTEXT), axis=0, tiled=True),
        lax.all_gather(down_weight.astype(jnp.bfloat16), (FSDP, CONTEXT), axis=0, tiled=True),
    )


def on_device(
    tokens,
    out_grad,
    lengths,
    attention_gain,
    query_weight,
    key_weight,
    value_weight,
    output_weight,
    feed_gain,
    gate_weight,
    up_weight,
    down_weight,
):
    local_rows = tokens.shape[1]
    group_rows = local_rows * lax.axis_size(CONTEXT)
    first_row = lax.axis_index(CONTEXT) * local_rows
    segment, position, valid_rows = slot_layout(lengths[0], group_rows)
    local_segment = lax.dynamic_slice_in_dim(segment, first_row, local_rows)
    local_position = lax.dynamic_slice_in_dim(position, first_row, local_rows)
    local_valid = lax.dynamic_slice_in_dim(valid_rows, first_row, local_rows)
    slot_ids = jnp.arange(group_rows, dtype=jnp.int32)
    local_slots = first_row + jnp.arange(local_rows, dtype=jnp.int32)
    allowed = (local_segment[:, None] == segment[None, :]) & (
        local_slots[:, None] >= slot_ids[None, :]
    )
    inputs = tokens[0].astype(jnp.float32)
    attn_set = attention_shards(
        attention_gain, query_weight, key_weight, value_weight, output_weight
    )
    gain_one = attn_set[0].astype(jnp.float32)
    inverse_one = lax.rsqrt(jnp.mean(inputs * inputs, axis=-1, keepdims=True) + norm_eps)
    unit_one = inputs * inverse_one
    normed_one = (unit_one * gain_one).astype(jnp.bfloat16)
    queries = jnp.dot(normed_one, attn_set[1], preferred_element_type=jnp.float32)
    keys_lin = jnp.dot(normed_one, attn_set[2], preferred_element_type=jnp.float32)
    values_low = jnp.dot(normed_one, attn_set[3], preferred_element_type=jnp.float32).astype(
        jnp.bfloat16
    )
    heads_local = queries.shape[1] // HEAD
    kv_local = keys_lin.shape[1] // HEAD
    per_group = heads_local // kv_local
    cos_table, sine_table = rope_tables(local_position, HEAD)
    queries_rot = rotate(
        queries.reshape(local_rows, heads_local, HEAD), cos_table, sine_table
    ).astype(jnp.bfloat16)
    keys_rot = rotate(keys_lin.reshape(local_rows, kv_local, HEAD), cos_table, sine_table).astype(
        jnp.bfloat16
    )
    keys_all, values_all = (
        lax.all_gather(
            keys_rot.reshape(local_rows, kv_local * HEAD), CONTEXT, axis=0, tiled=True
        ),
        lax.all_gather(values_low, CONTEXT, axis=0, tiled=True),
    )
    query_heads = queries_rot.reshape(local_rows, kv_local, per_group, HEAD).transpose(1, 0, 2, 3)
    key_heads = keys_all.reshape(group_rows, kv_local, HEAD).transpose(1, 0, 2)
    value_heads = values_all.reshape(group_rows, kv_local, HEAD).transpose(1, 0, 2)

    def head_scores(query_head, key_head):
        raw_scores = jnp.einsum(
            "tgd,sd->gts", query_head, key_head, preferred_element_type=jnp.float32
        )
        return jnp.where(allowed[None], raw_scores * attention_mult, -1e30)

    def head_forward(pieces):
        query_head, key_head, value_head = pieces
        scores = head_scores(query_head, key_head)
        highest = jnp.max(scores, axis=-1, keepdims=True)
        weight = jnp.exp(scores - highest)
        row_totals = jnp.sum(weight, axis=-1, keepdims=True)
        probabilities = (weight / row_totals).astype(jnp.bfloat16)
        mixed = jnp.einsum(
            "gts,sd->tgd", probabilities, value_head, preferred_element_type=jnp.float32
        )
        return (mixed, (highest + jnp.log(row_totals))[..., 0])

    mixed_heads, log_totals = lax.map(head_forward, (query_heads, key_heads, value_heads))
    attended = (
        mixed_heads.transpose(1, 0, 2, 3)
        .reshape(local_rows, heads_local * HEAD)
        .astype(jnp.bfloat16)
    )
    attn_part = dot_last(attended, attn_set[4])
    attn_out = lax.psum(attn_part.astype(jnp.bfloat16), TENSOR).astype(jnp.float32)
    hidden_state = inputs + residual_mult * attn_out
    feed_set = feed_shards(feed_gain, gate_weight, up_weight, down_weight)
    gain_two = feed_set[0].astype(jnp.float32)
    inverse_two = lax.rsqrt(
        jnp.mean(hidden_state * hidden_state, axis=-1, keepdims=True) + norm_eps
    )
    unit_two = hidden_state * inverse_two
    normed_two = (unit_two * gain_two).astype(jnp.bfloat16)
    gate_out = jnp.dot(normed_two, feed_set[1], preferred_element_type=jnp.float32)
    up_out = jnp.dot(normed_two, feed_set[2], preferred_element_type=jnp.float32)
    inner_act = (jax.nn.silu(gate_out) * up_out).astype(jnp.bfloat16)
    feed_part = dot_last(inner_act, feed_set[3])
    feed_out = lax.psum(feed_part.astype(jnp.bfloat16), TENSOR).astype(jnp.float32)
    output = hidden_state + residual_mult * feed_out
    cotangent = out_grad[0].astype(jnp.float32) * local_valid[:, None].astype(jnp.float32)
    feed_back = feed_shards(feed_gain, gate_weight, up_weight, down_weight)
    feed_grad = (residual_mult * cotangent).astype(jnp.bfloat16)
    down_term = dot_first(feed_grad, inner_act)
    inner_grad = jnp.dot(feed_grad, feed_back[3], preferred_element_type=jnp.float32)
    sigmoid_gate = jax.nn.sigmoid(gate_out)
    gate_grad = (
        inner_grad * up_out * sigmoid_gate * (1.0 + gate_out * (1.0 - sigmoid_gate))
    ).astype(jnp.bfloat16)
    up_grad = (inner_grad * jax.nn.silu(gate_out)).astype(jnp.bfloat16)
    gate_term = dot_first(normed_two, gate_grad)
    up_term = dot_first(normed_two, up_grad)
    normed_part_two = dot_last(gate_grad, feed_back[1])
    normed_part_two = normed_part_two + dot_last(up_grad, feed_back[2])
    normed_grad_two = lax.psum(normed_part_two.astype(jnp.bfloat16), TENSOR).astype(jnp.float32)
    feed_gain_term = jnp.sum(normed_grad_two * unit_two, axis=0)
    hidden_grad = cotangent + norm_back(normed_grad_two, unit_two, gain_two, inverse_two)
    feed_sums = (
        lax.psum_scatter(feed_gain_term, (FSDP, CONTEXT), scatter_dimension=0, tiled=True),
        lax.psum_scatter(gate_term, (FSDP, CONTEXT), scatter_dimension=0, tiled=True),
        lax.psum_scatter(up_term, (FSDP, CONTEXT), scatter_dimension=0, tiled=True),
        lax.psum_scatter(down_term, (FSDP, CONTEXT), scatter_dimension=0, tiled=True),
    )
    attn_back = attention_shards(
        attention_gain, query_weight, key_weight, value_weight, output_weight
    )
    attn_grad = (residual_mult * hidden_grad).astype(jnp.bfloat16)
    out_term = dot_first(attn_grad, attended)
    mixed_grad = jnp.dot(attn_grad, attn_back[4], preferred_element_type=jnp.float32).astype(
        jnp.bfloat16
    )
    mixed_grad_heads = mixed_grad.reshape(local_rows, kv_local, per_group, HEAD).transpose(
        1, 0, 2, 3
    )

    def head_backward(pieces):
        query_head, key_head, value_head, grad_head, log_head = pieces
        scores = head_scores(query_head, key_head)
        probabilities = jnp.exp(scores - log_head[..., None])
        prob_low = probabilities.astype(jnp.bfloat16)
        prob_grad = jnp.einsum(
            "tgd,sd->gts", grad_head, value_head, preferred_element_type=jnp.float32
        )
        row_dot = jnp.sum(probabilities * prob_grad, axis=-1, keepdims=True)
        score_grad = (attention_mult * probabilities * (prob_grad - row_dot)).astype(jnp.bfloat16)
        query_grad = jnp.einsum(
            "gts,sd->tgd", score_grad, key_head, preferred_element_type=jnp.float32
        )
        key_grad = jnp.einsum(
            "gts,tgd->sd", score_grad, query_head, preferred_element_type=jnp.float32
        )
        value_grad = jnp.einsum(
            "gts,tgd->sd", prob_low, grad_head, preferred_element_type=jnp.float32
        )
        return (query_grad, key_grad, value_grad)

    query_grads, key_grads, value_grads = lax.map(
        head_backward, (query_heads, key_heads, value_heads, mixed_grad_heads, log_totals)
    )
    key_grads = key_grads.transpose(1, 0, 2).reshape(group_rows, kv_local * HEAD)
    value_grads = value_grads.transpose(1, 0, 2).reshape(group_rows, kv_local * HEAD)
    local_key_grad, local_value_grad = (
        lax.psum_scatter(
            key_grads.astype(jnp.bfloat16), CONTEXT, scatter_dimension=0, tiled=True
        ).astype(jnp.float32),
        lax.psum_scatter(
            value_grads.astype(jnp.bfloat16), CONTEXT, scatter_dimension=0, tiled=True
        ).astype(jnp.float32),
    )
    query_grad_rot = query_grads.transpose(1, 0, 2, 3).reshape(local_rows, heads_local, HEAD)
    query_grad_low = (
        rotate_back(query_grad_rot, cos_table, sine_table)
        .reshape(local_rows, heads_local * HEAD)
        .astype(jnp.bfloat16)
    )
    key_grad_low = (
        rotate_back(local_key_grad.reshape(local_rows, kv_local, HEAD), cos_table, sine_table)
        .reshape(local_rows, kv_local * HEAD)
        .astype(jnp.bfloat16)
    )
    value_grad_low = local_value_grad.astype(jnp.bfloat16)
    query_term = dot_first(normed_one, query_grad_low)
    key_term = dot_first(normed_one, key_grad_low)
    value_term = dot_first(normed_one, value_grad_low)
    normed_part_one = dot_last(query_grad_low, attn_back[1])
    normed_part_one = normed_part_one + dot_last(key_grad_low, attn_back[2])
    normed_part_one = normed_part_one + dot_last(value_grad_low, attn_back[3])
    normed_grad_one = lax.psum(normed_part_one.astype(jnp.bfloat16), TENSOR).astype(jnp.float32)
    attn_gain_term = jnp.sum(normed_grad_one * unit_one, axis=0)
    input_grad = hidden_grad + norm_back(normed_grad_one, unit_one, gain_one, inverse_one)
    attn_sums = (
        lax.psum_scatter(attn_gain_term, (FSDP, CONTEXT), scatter_dimension=0, tiled=True),
        lax.psum_scatter(query_term, (FSDP, CONTEXT), scatter_dimension=0, tiled=True),
        lax.psum_scatter(key_term, (FSDP, CONTEXT), scatter_dimension=0, tiled=True),
        lax.psum_scatter(value_term, (FSDP, CONTEXT), scatter_dimension=0, tiled=True),
        lax.psum_scatter(out_term, (FSDP, CONTEXT), scatter_dimension=0, tiled=True),
    )
    return (
        output.astype(jnp.bfloat16)[None],
        input_grad.astype(jnp.bfloat16)[None],
        attn_sums[0],
        attn_sums[1],
        attn_sums[2],
        attn_sums[3],
        attn_sums[4],
        feed_sums[0],
        feed_sums[1],
        feed_sums[2],
        feed_sums[3],
    )


def flip(i, k):
    if k == 0:
        return i
    if k == 1:
        return i + 1 - 2 * lax.rem(i, 2)
    if k == 2:
        return lax.rem(i + 2, 4)
    return 3 - i


class Copies:
    def __init__(self, send, receive):
        self.send, self.receive = send, receive
        self.count, self.started = 0, []

    def index(self):
        self.count += 1
        return self.count - 1

    def make(self, i, source, target, device):
        return pltpu.make_async_remote_copy(
            src_ref=source,
            dst_ref=target,
            send_sem=self.send.at[i],
            recv_sem=self.receive.at[i],
            device_id=device,
            device_id_type=pl.DeviceIdType.MESH,
        )

    def start(self, source, target, device, i=None):
        i = self.index() if i is None else i
        copy = self.make(i, source, target, device)
        copy.start()
        self.started.append(copy)
        return copy


def greet(partners):
    barrier = pltpu.get_barrier_semaphore()
    for device in partners:
        pl.semaphore_signal(barrier, inc=1, device_id=device, device_id_type=pl.DeviceIdType.MESH)
    pl.semaphore_wait(barrier, len(partners))


def dot_tile(left, right, left_axis, right_axis):
    return lax.dot_general(left, right, (((left_axis,), (right_axis,)), ((), ())), preferred_element_type=jnp.float32)


TILE = 256


def turn_lanes(x, low):
    return jnp.where(low, pltpu.roll(x, x.shape[1] - HEAD // 2, 1), pltpu.roll(x, HEAD // 2, 1))


def low_lanes(shape, width):
    return lax.rem(lax.broadcasted_iota(jnp.int32, shape, 1), 2 * width) < width


def split_pair(x):
    low = low_lanes(x.shape, HEAD)
    a, b = jnp.where(low, x, 0.0), jnp.where(low, 0.0, x)
    return a, pltpu.roll(a, HEAD, 1), pltpu.roll(b, HEAD, 1), b


def attention_kernel(
    wa, wf, xt, gain, fgx, cos, sin, seg_col, seg_row,
    wa_out, wf_all, normed_out, q, kv, logs, attended, hidden_out, normed_two, fg_all, gains,
    wa_all, x_all, gain_all, normed, pairs, sums, mine, cross, crossed, totals, landed, send, receive, local,
):
    f32, bf16 = jnp.float32, jnp.bfloat16
    z, c, t = (lax.axis_index(a) for a in (FSDP, CONTEXT, TENSOR))
    peers = [(flip(z, i), flip(c, j), t) for i in range(4) for j in range(4) if i or j]
    core = (z, c, 1 - t)
    greet(peers + [core])
    net = Copies(send, receive)
    middle = (z == 1) | (z == 2)
    nt, part, width = xt.shape
    rows = nt * part
    q_cols = q.shape[1]
    hidden = wf_all.shape[4]

    def columns(owner):
        return pl.ds(pl.multiple_of(owner * hidden, hidden), hidden)

    qkv_cols = q_cols + 2 * HEAD
    ends = []
    own = []
    for i, (source, target) in enumerate(
        (
            (wa.at[c], wa_all.at[z, c]),
            (xt, x_all.at[c]),
            (wf.at[:, :, columns(z)], wf_all.at[:, z, c]),
            (gain, gain_all.at[z, c]),
            (fgx, fg_all.at[0, 0]),
        )
    ):
        own.append(pltpu.make_async_copy(source, target, local.at[i]))
        own[-1].start()

    def spread(source, slot, forward):
        one = net.start(source, slot(1), (flip(z, 1), c, t))
        two = net.start(source, slot(2), (flip(z, 2), c, t))
        three = net.index()
        direct = net.make(three, source, slot(3), (3 - z, c, t))
        pl.when(middle)(direct.start)
        passed = pltpu.make_async_remote_copy(
            src_ref=forward[0],
            dst_ref=forward[1],
            send_sem=send.at[net.index()],
            recv_sem=receive.at[three],
            device_id=(flip(z, 1), c, t),
            device_id_type=pl.DeviceIdType.MESH,
        )
        return one, two, direct, passed

    class Chain:
        def __init__(self, source, block):
            self.one = net.start(source, block(0, 1), (flip(z, 1), c, t))
            two, three = net.index(), net.index()
            self.direct = net.make(three, source, block(0, 3), (3 - z, c, t))
            self.near = net.make(two, block(1, 1), block(1, 2), (3 - z, c, t))
            self.over = self.hop(two, block(3, 3), block(3, 2))
            self.far = self.hop(three, block(2, 2), block(2, 3))
            pl.when(middle)(self.direct.start)

        def hop(self, receives, source, target):
            return pltpu.make_async_remote_copy(
                src_ref=source,
                dst_ref=target,
                send_sem=send.at[net.index()],
                recv_sem=receive.at[receives],
                device_id=(flip(z, 1), c, t),
                device_id_type=pl.DeviceIdType.MESH,
            )

        def pass_near(self):
            self.one.wait_recv()
            pl.when(middle)(self.near.start)

        def pass_far(self):
            self.direct.wait_recv()
            pl.when(middle)(self.over.start)
            self.near.wait_recv()
            pl.when(middle)(self.far.start)

        def end(self):
            for copy in (self.direct, self.near, self.over, self.far):
                pl.when(middle)(copy.wait_send)

    attn_in = [net.start(wa.at[flip(c, k)], wa_all.at[z, c], (z, flip(c, k), t)) for k in (1, 2, 3)]
    tokens_in = [net.start(xt.at[t], x_all.at[c, t], (z, flip(c, k), t)) for k in (1, 2, 3)]
    parts = {k: (0, 1, 2) if k == 2 else (slice(None),) for k in range(4)}

    def weights_to(k):
        there = columns(flip(z, k))
        return [net.start(wf.at[m, :, there], wf_all.at[m, z, c], (flip(z, k), c, t)) for m in parts[k]]

    ff_in = {1: weights_to(1)}
    for device in peers:
        ends.append(net.start(gain, gain_all.at[z, c], device))
    own[2].wait()
    ff_out = {}

    def pass_on(k, m):
        piece = wf_all.at[m, flip(z, k), c]
        ff_out.setdefault(k, []).append([net.start(piece, piece, (z, flip(c, j), t)) for j in (1, 2)])

    pass_on(0, slice(None))
    weights = []
    for j in range(4):
        if j:
            attn_in[j - 1].wait_recv()
        else:
            own[0].wait()
        piece = wa_all.at[z, flip(c, j)]
        passed_piece = wa_all.at[flip(z, 2), flip(c, j)]
        weights.append(spread(piece, lambda k, piece=piece: piece, (passed_piece, passed_piece)))
    for k in (3, 2):
        ff_in[k] = weights_to(k)
    feed = Chain(fgx, lambda _, j: fg_all.at[j, 0])
    swaps = [net.start(fgx, fg_all.at[0, 1], core)]
    token_swaps = []
    for k, copy in zip((1, 2, 3), tokens_in):
        copy.wait_recv()
        piece = x_all.at[flip(c, k), t]
        token_swaps.append(net.start(piece, piece, core))
    halves = []

    def corner(k):
        zs = flip(z, k)
        for m, (one, two) in zip(parts[k], ff_out[k]):
            two.wait_recv()
            piece = wf_all.at[m, zs, flip(c, 2), pl.ds(0, 64)]
            halves.append(net.start(piece, piece, (z, flip(c, 1), t)))
            one.wait_recv()
            piece = wf_all.at[m, zs, flip(c, 1), pl.ds(64, 64)]
            halves.append(net.start(piece, piece, (z, flip(c, 2), t)))

    def onward(k):
        for m, copy in zip(parts[k], ff_in[k]):
            copy.wait_recv()
            pass_on(k, m)

    own[1].wait()
    own[3].wait()
    for copy in token_swaps + ends:
        copy.wait_recv()
    for i in range(2):
        gains[i : i + 1, :] = jnp.concatenate(
            [gain_all[a, b, i : i + 1, :].astype(f32) for a in range(4) for b in range(4)], axis=1
        )

    def norm_rows(i, carry):
        x = x_all[i].reshape(rows, width).astype(f32)
        inverse = lax.rsqrt(jnp.mean(x * x, axis=-1, keepdims=True) + norm_eps)
        normed[i] = (x * inverse * gains[0:1, :]).astype(bf16)
        return carry

    lax.fori_loop(0, 4, norm_rows, 0)
    save = [pltpu.make_async_copy(normed, normed_out, local.at[5])]
    save[0].start()
    onward(1)
    corner(0)
    for one, two, direct, passed in weights:
        two.wait_recv()
        pl.when(middle)(passed.start)
    for one, two, direct, passed in weights:
        one.wait_recv()
        direct.wait_recv()
    save.append(pltpu.make_async_copy(wa_all, wa_out, local.at[6]))
    save[1].start()

    def project(i, carry):
        here = pl.ds(pl.multiple_of(i * rows, rows), rows)
        w = wa_all[...].reshape(width, wa_all.shape[3])
        qkv = dot_tile(normed[i], w[:, :qkv_cols], 1, 0)
        cos_b, sin_b = cos[here, :], sin[here, :]
        quarter = low_lanes(cos_b.shape, HEAD // 2)
        half = low_lanes(cos_b.shape, HEAD)
        for p in range(q_cols // 128):
            block = qkv[:, p * 128 : (p + 1) * 128]
            q[here, p * 128 : (p + 1) * 128] = (block * cos_b + turn_lanes(block, quarter) * sin_b).astype(bf16)
        block = qkv[:, q_cols:]
        block = jnp.where(half, block * cos_b + turn_lanes(block, quarter) * sin_b, block)
        kv[here, :] = block.astype(bf16)
        for j, piece in enumerate(split_pair(block)):
            pairs[j, here, :] = piece.astype(bf16)
        return carry

    lax.fori_loop(0, 4, project, 0)
    corner(1)
    feed.pass_near()

    def attend(i):
        count = (i + 1) * rows
        here = pl.ds(i * rows, rows)
        keep = (seg_col[here, :] == seg_row[:, :count]) & (
            lax.broadcasted_iota(jnp.int32, (rows, count), 0) + i * rows
            >= lax.broadcasted_iota(jnp.int32, (rows, count), 1)
        )
        lane = lax.broadcasted_iota(jnp.int32, (rows, 128), 1)

        def pair(p, log_sums):
            block = pl.ds(pl.multiple_of(p * 128, 128), 128)
            out = jnp.zeros((rows, 128), f32)
            for e in range(2):
                scores = dot_tile(q[here, block], pairs[e, :count, :], 1, 1)
                scores = jnp.where(keep, scores * attention_mult, -1e30)
                highest = jnp.max(scores, axis=-1, keepdims=True)
                weight = jnp.exp(scores - highest)
                total = jnp.sum(weight, axis=-1, keepdims=True)
                out = out + dot_tile((weight / total).astype(bf16), pairs[2 + e, :count, :], 1, 0)
                log_sums = jnp.where(lane == 2 * p + e, highest + jnp.log(total), log_sums)
            attended[here, block] = out.astype(bf16)
            return log_sums

        logs[here, :] = lax.fori_loop(0, q_cols // 128, pair, jnp.zeros((rows, 128), f32))

    attend(0)
    attend(1)
    onward(3)
    attend(2)
    last = pl.ds(3 * rows, rows)
    both = (pairs[2, last, :] + pairs[3, last, :]).astype(bf16)
    for p in range(q_cols // 128):
        attended[last, p * 128 : (p + 1) * 128] = both
    corner(3)

    crosses, outs = {}, {}
    for k in (3, 1, 2, 0):
        mine_rows = pl.ds(pl.multiple_of(flip(c, k) * rows, rows), rows)

        def out_tile(n, carry, mine_rows=mine_rows):
            here = pl.ds(pl.multiple_of(n * 128, 128), 128)
            w = wa_all[lax.div(n, 4), lax.rem(n, 4), :, qkv_cols:]
            sums[:, here] = dot_tile(attended[mine_rows, :], w, 1, 1)
            return carry

        lax.fori_loop(0, width // 128, out_tile, 0)
        mine[k] = sums[pl.ds(pl.multiple_of(t * part, part), part), :]
        cross[k] = sums[pl.ds(pl.multiple_of((1 - t) * part, part), part), :].astype(bf16)
        crosses[k] = net.start(cross.at[k], crossed.at[k], core)
    for k in (3, 1, 2):
        crosses[k].wait_recv()
        totals[k - 1] = (mine[k] + crossed[k].astype(f32)).astype(bf16)
        outs[k] = net.start(totals.at[k - 1], landed.at[k - 1], (z, flip(c, k), t))
    onward(2)
    swaps.append(net.start(fg_all.at[1, 0], fg_all.at[1, 1], core))
    crosses[0].wait_recv()
    total = mine[0] + crossed[0].astype(f32)
    for k in (1, 2, 3):
        outs[k].wait_recv()
        total = total + landed[k - 1].astype(f32)
    hidden = xt[t].astype(f32) + residual_mult * total
    hidden_out[...] = hidden
    inverse = lax.rsqrt(jnp.mean(hidden * hidden, axis=-1, keepdims=True) + norm_eps)
    normed_two[...] = (hidden * inverse * gains[1:2, :]).astype(bf16)
    feed.pass_far()
    for k in (2, 3):
        swaps.append(net.start(fg_all.at[k, 0], fg_all.at[k, 1], core))
    corner(2)
    for copy in halves + swaps:
        copy.wait_recv()
    feed.end()
    for _, _, direct, passed in weights:
        pl.when(middle)(direct.wait_send)
        pl.when(middle)(passed.wait_send)
    for copy in net.started:
        copy.wait_send()
    own[4].wait()
    for copy in save:
        copy.wait()


def attention_forward(wa, wf, xt, gain, fgx, cos, sin, seg_col, seg_row):
    bf16, f32 = jnp.bfloat16, jnp.float32
    nt, part, width = xt.shape
    rows = nt * part
    total = 4 * rows
    wa_cols = wa.shape[2]
    q_cols = (wa_cols - 2 * HEAD) // 2
    filled = seg_col.shape[0]
    copies = 112
    vmem, anywhere = pl.BlockSpec(memory_space=pltpu.VMEM), pl.BlockSpec(memory_space=pl.ANY)
    outs = (
        ((4, 4) + wa.shape[1:], bf16, anywhere),
        ((3, 4, 4, wf.shape[1], wf.shape[2] // 4), bf16, anywhere),
        ((4, rows, width), bf16, anywhere),
        ((total, q_cols), bf16, vmem),
        ((total, 2 * HEAD), bf16, vmem),
        ((filled, 128), f32, vmem),
        ((total, q_cols), bf16, vmem),
        ((part, width), f32, vmem),
        ((part, width), bf16, vmem),
        ((4, nt, part, width), bf16, anywhere),
        ((2, width), f32, vmem),
    )
    return pl.pallas_call(
        attention_kernel,
        out_shape=[jax.ShapeDtypeStruct(shape, dtype) for shape, dtype, _ in outs],
        in_specs=[vmem] * 9,
        out_specs=[spec for _, _, spec in outs],
        scratch_shapes=[
            pltpu.VMEM((4, 4) + wa.shape[1:], bf16),
            pltpu.VMEM((4, nt, part, width), bf16),
            pltpu.VMEM((4, 4) + gain.shape, bf16),
            pltpu.VMEM((4, rows, width), bf16),
            pltpu.VMEM((4, total, 2 * HEAD), bf16),
            pltpu.VMEM((rows, width), f32),
            pltpu.VMEM((4, part, width), f32),
            pltpu.VMEM((4, part, width), bf16),
            pltpu.VMEM((4, part, width), bf16),
            pltpu.VMEM((3, part, width), bf16),
            pltpu.VMEM((3, part, width), bf16),
            pltpu.SemaphoreType.DMA((copies,)),
            pltpu.SemaphoreType.DMA((copies,)),
            pltpu.SemaphoreType.DMA((7,)),
        ],
        compiler_params=pltpu.CompilerParams(collective_id=1, has_side_effects=True, vmem_limit_bytes=60 * 2**20),
    )(wa, wf, xt, gain, fgx, cos, sin, seg_col, seg_row)


def feed_kernel(
    x, fg, w, back, feed_own, feed_send, terms,
    xs, wv, gate_g, up_g, inner, mine, cross, crossed, totals, landed, send, receive, local,
):
    f32, bf16 = jnp.float32, jnp.bfloat16
    z, c, t = (lax.axis_index(a) for a in (FSDP, CONTEXT, TENSOR))
    core = (z, c, 1 - t)
    greet([(flip(z, k), c, t) for k in (1, 2, 3)] + [core])
    net = Copies(send, receive)
    part, width = x.shape
    hidden = wv.shape[2]
    load = pltpu.make_async_copy(w, wv, local.at[0])
    load.start()
    middle = (z == 1) | (z == 2)
    swaps = {0: net.start(x, xs.at[0, 1], core)}
    arrive = {2: net.start(x, xs.at[2, 0], (flip(z, 2), c, t))}
    three = net.index()
    direct = net.make(three, x, xs.at[3, 0], (3 - z, c, t))
    pl.when(middle)(direct.start)
    arrive[3] = direct
    arrive[1] = net.start(x, xs.at[1, 0], (flip(z, 1), c, t))
    passed = pltpu.make_async_remote_copy(
        src_ref=xs.at[2, 0],
        dst_ref=xs.at[3, 0],
        send_sem=send.at[net.index()],
        recv_sem=receive.at[three],
        device_id=(flip(z, 1), c, t),
        device_id_type=pl.DeviceIdType.MESH,
    )
    xs[0, 0] = x[...]
    load.wait()

    def first(k):
        swaps[k].wait_recv()
        rows = xs[k].reshape(2 * part, width)
        grads = fg[k]

        def step(n, carry):
            at = pl.multiple_of(n * TILE, TILE)
            g = dot_tile(rows, wv[0, :, pl.ds(at, TILE)], 1, 0)
            u = dot_tile(rows, wv[1, :, pl.ds(at, TILE)], 1, 0)
            d = dot_tile(grads, wv[2, :, pl.ds(at, TILE)], 1, 0)
            sig = jax.nn.sigmoid(g)
            here = pl.ds(at, TILE)
            inner[k, :, here] = (g * sig * u).astype(bf16)
            gate_g[k, :, here] = (d * u * sig * (1.0 + g * (1.0 - sig))).astype(bf16)
            up_g[k, :, here] = (d * g * sig).astype(bf16)
            return carry

        lax.fori_loop(0, hidden // TILE, step, 0)

    crosses = {}

    def second(k):
        def step(n, carry):
            here = pl.ds(pl.multiple_of(n * TILE, TILE), TILE)
            b = dot_tile(gate_g[k], wv[0, here, :], 1, 1) + dot_tile(up_g[k], wv[1, here, :], 1, 1)
            f = dot_tile(inner[k], wv[2, here, :], 1, 1)
            mine[k, 0, :, here] = b[:part]
            mine[k, 1, :, here] = f[:part]
            cross[k, 0, :, here] = b[part:].astype(bf16)
            cross[k, 1, :, here] = f[part:].astype(bf16)
            return carry

        lax.fori_loop(0, width // TILE, step, 0)
        crosses[k] = net.start(cross.at[k], crossed.at[k], core)

    sums = {}

    def finish(k):
        crosses[k].wait_recv()
        if k:
            totals[k - 1] = (mine[k, 0] + crossed[k, 0].astype(f32)).astype(bf16)
            sums[k] = net.start(totals.at[k - 1], landed.at[k - 1], (flip(z, k), c, t))
            feed_send[k - 1] = (mine[k, 1] + crossed[k, 1].astype(f32)).astype(bf16)
        else:
            back[...] = mine[0, 0] + crossed[0, 0].astype(f32)
            feed_own[...] = mine[0, 1] + crossed[0, 1].astype(f32)

    def fetch(k):
        arrive[k].wait_recv()
        if k == 2:
            pl.when(middle)(passed.start)
        swaps[k] = net.start(xs.at[k, 0], xs.at[k, 1], core)

    order = (0, 2, 3, 1)
    for i, k in enumerate(order):
        first(k)
        if i:
            finish(order[i - 1])
        if i < 3:
            fetch(order[i + 1])
        second(k)

    rows = xs.shape[0] * 2 * part

    def term(source, grads, i):
        def step(m, carry):
            here = pl.ds(pl.multiple_of(m * TILE, TILE), TILE)
            left = source[:, :, here].reshape(rows, TILE)
            value = dot_tile(left, grads[...].reshape(rows, hidden), 0, 0)
            wv[i, here, :] = value.astype(bf16)
            return carry

        lax.fori_loop(0, width // TILE, step, 0)

    flat = xs.reshape(xs.shape[0], 2 * part, width)
    term(flat, gate_g, 0)
    finish(order[3])
    term(flat, up_g, 1)
    term(fg, inner, 2)
    store = pltpu.make_async_copy(wv, terms, local.at[1])
    store.start()
    for k in (1, 2, 3):
        sums[k].wait_recv()
    back[...] = back[...] + landed[0].astype(f32) + landed[1].astype(f32) + landed[2].astype(f32)
    pl.when(middle)(direct.wait_send)
    pl.when(middle)(passed.wait_send)
    for copy in net.started:
        copy.wait_send()
    store.wait()


def feed_forward(x, fg, w):
    bf16, f32 = jnp.bfloat16, jnp.float32
    part, width = x.shape
    hidden = w.shape[2]
    blocks = fg.shape[0]
    copies = 20
    vmem, anywhere = pl.BlockSpec(memory_space=pltpu.VMEM), pl.BlockSpec(memory_space=pl.ANY)
    return pl.pallas_call(
        feed_kernel,
        out_shape=[
            jax.ShapeDtypeStruct((part, width), f32),
            jax.ShapeDtypeStruct((part, width), f32),
            jax.ShapeDtypeStruct((blocks - 1, part, width), bf16),
            jax.ShapeDtypeStruct(w.shape, bf16),
        ],
        in_specs=[vmem, vmem, anywhere],
        out_specs=[vmem, vmem, vmem, anywhere],
        scratch_shapes=[
            pltpu.VMEM((blocks, 2, part, width), bf16),
            pltpu.VMEM(w.shape, bf16),
            pltpu.VMEM((blocks, 2 * part, hidden), bf16),
            pltpu.VMEM((blocks, 2 * part, hidden), bf16),
            pltpu.VMEM((blocks, 2 * part, hidden), bf16),
            pltpu.VMEM((blocks, 2, part, width), f32),
            pltpu.VMEM((blocks, 2, part, width), bf16),
            pltpu.VMEM((blocks, 2, part, width), bf16),
            pltpu.VMEM((blocks - 1, part, width), bf16),
            pltpu.VMEM((blocks - 1, part, width), bf16),
            pltpu.SemaphoreType.DMA((copies,)),
            pltpu.SemaphoreType.DMA((copies,)),
            pltpu.SemaphoreType.DMA((2,)),
        ],
        compiler_params=pltpu.CompilerParams(collective_id=3, has_side_effects=True, vmem_limit_bytes=62 * 2**20),
    )(x, fg, w)


def swap(x, axis, k):
    return lax.ppermute(x, axis, [(i, i ^ k) for i in range(lax.axis_size(axis))])


def cut(x, index, size, axis):
    return lax.dynamic_slice_in_dim(x, index * size, size, axis)


def backward_kernel(
    ff, fs, al, wa_in, normed_in, q, kv, logs, attended, cos, sin, seg_col, seg_row,
    feed_in, back_own, back_in, ff_out, query_out, kv_out, output_out,
    terms, corner_x, corner_y, side_x, side_y, at_terms, at_in, at_total, wa, normed, ag, pairs, mixed, acc, dqkv,
    sums, mine, cross, crossed, totals, held_feed, held_terms, send, receive, local,
):
    f32, bf16 = jnp.float32, jnp.bfloat16
    z, c, t = (lax.axis_index(a) for a in (FSDP, CONTEXT, TENSOR))
    core = (z, c, 1 - t)
    greet([(flip(z, k), c, t) for k in (1, 2, 3)] + [(z, flip(c, k), t) for k in (1, 2, 3)] + [core])
    net = Copies(send, receive)
    wrows, hidden = ff.shape[3:]
    half = wrows // 2
    part, width = al.shape
    rows = 2 * part
    q_cols = q.shape[1]
    qkv_cols = q_cols + 2 * HEAD
    blocks = normed.shape[0]
    order = (3, 2, 1, 0)
    loads = {}
    for k in order:
        zs = flip(z, k)
        loads[k] = pltpu.make_async_copy(ff.at[:, zs], terms.at[:, zs], local.at[k])
        loads[k].start()
    wa_load = pltpu.make_async_copy(wa_in, wa, local.at[4])
    wa_load.start()
    normed_load = pltpu.make_async_copy(normed_in.at[pl.ds(0, blocks)], normed, local.at[5])
    normed_load.start()
    first = {}

    def corners(k):
        zs = flip(z, k)
        loads[k].wait()
        first[k] = (
            net.start(terms.at[:, zs, flip(c, 3), pl.ds(0, half)], corner_x.at[k], (z, flip(c, 1), t)),
            net.start(terms.at[:, zs, flip(c, 3), pl.ds(half, half)], corner_y.at[k], (z, flip(c, 2), t)),
        )

    corners(3)
    ag_in = [net.start(al, ag.at[c, t], (z, flip(c, k), t)) for k in (3, 1, 2)]
    swaps = [net.start(al, ag.at[c, t], core)]
    middle = (z == 1) | (z == 2)
    chains = []

    class Sums:
        def __init__(self, mine, held, landed):
            self.mine, self.held, self.landed = mine, held, landed
            neighbour = (flip(z, 1), c, t)
            self.ends = [net.make(net.index(), mine(k), held(k), neighbour) for k in (3, 2)]
            for copy in self.ends:
                pl.when(jnp.logical_not(middle))(copy.start)
            self.one = net.start(mine(1), landed(0), neighbour)
            two, spare = net.index(), net.index()
            self.out = [net.make(two, held(2), landed(1), (3 - z, c, t))]
            self.out.append(
                pltpu.make_async_remote_copy(
                    src_ref=held(3),
                    dst_ref=landed(1),
                    send_sem=send.at[spare],
                    recv_sem=receive.at[two],
                    device_id=(flip(z, 2), c, t),
                    device_id_type=pl.DeviceIdType.MESH,
                )
            )
            chains.append(self)

        def add(self, k, own):
            held, mine = self.held(k), self.mine(own)
            for i in range(held.shape[0]) if len(held.shape) == 3 else (slice(None),):
                held[i] = (held[i].astype(f32) + mine[i].astype(f32)).astype(bf16)

        def hand_on(self):
            @pl.when(middle)
            def _():
                for copy in self.ends:
                    copy.wait_recv()
                self.add(3, 2)
                self.out[1].start()
                self.add(2, 3)
                self.out[0].start()

        def wait_in(self):
            self.one.wait_recv()
            self.out[0].wait_recv()

        def wait_out(self):
            for copy in self.ends:
                pl.when(jnp.logical_not(middle))(copy.wait_send)
            for copy in self.out:
                pl.when(middle)(copy.wait_send)

    feed = Sums(lambda k: fs.at[k - 1], lambda k: held_feed.at[k - 2], lambda i: feed_in.at[i])
    corners(2)
    ag[c, t] = al[...]
    for j, piece in enumerate(split_pair(kv[...].astype(f32))):
        pairs[j] = piece.astype(bf16)
    acc[...] = jnp.zeros_like(acc)
    dqkv[pl.ds(blocks * rows, rows), :] = jnp.zeros((rows, qkv_cols), bf16)
    for k, copy in zip((3, 1, 2), ag_in):
        copy.wait_recv()
        piece = ag.at[flip(c, k), t]
        swaps.append(net.start(piece, piece, core))
    second, third = {}, {}

    def sides(k):
        zs = flip(z, k)
        for copy in first[k]:
            copy.wait_recv()
        low, high = pl.ds(0, half), pl.ds(half, half)
        xb, yb = flip(c, 1), flip(c, 2)
        for m in range(3):
            terms[m, zs, yb, low] = (terms[m, zs, yb, low].astype(f32) + corner_x[k, m].astype(f32)).astype(bf16)
            terms[m, zs, xb, high] = (terms[m, zs, xb, high].astype(f32) + corner_y[k, m].astype(f32)).astype(bf16)
        second[k] = (
            net.start(terms.at[:, zs, yb], side_y.at[k], (z, yb, t)),
            net.start(terms.at[:, zs, xb], side_x.at[k], (z, xb, t)),
        )

    def owners(k):
        zs = flip(z, k)
        for copy in second[k]:
            copy.wait_recv()
        for m in range(3):
            total = terms[m, zs, c].astype(f32) + side_x[k, m].astype(f32) + side_y[k, m].astype(f32)
            terms[m, zs, c] = total.astype(bf16)
        columns = ff_out.at[:, :, pl.ds(pl.multiple_of(z * hidden, hidden), hidden)]
        if k:
            third[k] = net.start(terms.at[:, zs, c], columns, (zs, c, t))
        else:
            third[0] = pltpu.make_async_copy(terms.at[:, z, c], columns, local.at[6])
            third[0].start()

    for copy in swaps:
        copy.wait_recv()
    wa_load.wait()
    normed_load.wait()

    def mix(i, carry):
        w = wa[...].reshape(width, wa.shape[3])[:, qkv_cols:]
        here = pl.ds(pl.multiple_of(i * rows, rows), rows)
        mixed[here, :] = dot_tile(ag[i].reshape(rows, width), w, 1, 0).astype(bf16)
        return carry

    lax.fori_loop(0, blocks, mix, 0)
    sides(3)
    corners(1)

    def out_term(m, carry):
        here = pl.ds(pl.multiple_of(m * wrows, wrows), wrows)
        left = ag[0:blocks, :, :, here].reshape(blocks * rows, wrows)
        value = dot_tile(left, attended[0 : blocks * rows, :], 0, 0)
        at_terms[lax.div(m, 4), lax.rem(m, 4), :, qkv_cols:] = value.astype(bf16)
        return carry

    lax.fori_loop(0, width // wrows, out_term, 0)

    def terms_to(columns):
        return Sums(
            lambda k: at_terms.at[flip(z, k), :, :, columns],
            lambda k: held_terms.at[k - 2, :, :, columns],
            lambda i: at_in.at[i, :, :, columns],
        )

    output_sums = terms_to(pl.ds(qkv_cols, q_cols))
    feed.hand_on()
    sides(2)
    corners(0)

    def attend(i):
        count = (i + 1) * rows
        here = pl.ds(i * rows, rows)
        keep = (seg_col[here, :] == seg_row[:, :count]) & (
            lax.broadcasted_iota(jnp.int32, (rows, count), 0) + i * rows
            >= lax.broadcasted_iota(jnp.int32, (rows, count), 1)
        )
        log_sums = logs[here, :]
        lane = lax.broadcasted_iota(jnp.int32, (rows, 128), 1)
        cos_b, sin_b = cos[here, :], sin[here, :]
        quarter = low_lanes(cos_b.shape, HEAD // 2)

        def pair(p, carry):
            block = pl.ds(pl.multiple_of(p * 128, 128), 128)
            grad = jnp.zeros((rows, 128), f32)
            for e in range(2):
                scores = dot_tile(q[here, block], pairs[e, :count, :], 1, 1)
                scores = jnp.where(keep, scores * attention_mult, -1e30)
                log = jnp.sum(jnp.where(lane == 2 * p + e, log_sums, 0.0), axis=-1, keepdims=True)
                prob = jnp.exp(scores - log)
                prob_grad = dot_tile(mixed[here, block], pairs[2 + e, :count, :], 1, 1)
                row_dot = jnp.sum(prob * prob_grad, axis=-1, keepdims=True)
                score_grad = (attention_mult * prob * (prob_grad - row_dot)).astype(bf16)
                grad = grad + dot_tile(score_grad, pairs[e, :count, :], 1, 0)
                acc[e, :count, :] += dot_tile(score_grad, q[here, block], 0, 0)
                acc[2 + e, :count, :] += dot_tile(prob.astype(bf16), mixed[here, block], 0, 0)
            dqkv[here, block] = (grad * cos_b + turn_lanes(grad * sin_b, quarter)).astype(bf16)
            return carry

        lax.fori_loop(0, q_cols // 128, pair, 0)

    attend(0)
    output_sums.hand_on()
    attend(1)
    owners(3)
    sides(1)
    sides(0)
    attend(2)
    owners(2)
    filled = blocks * rows
    low = low_lanes((filled, 128), HEAD)
    key_grad = jnp.where(low, acc[0], 0.0) + pltpu.roll(jnp.where(low, 0.0, acc[1]), HEAD, 1)
    value_grad = jnp.where(low, 0.0, acc[3]) + pltpu.roll(jnp.where(low, acc[2], 0.0), HEAD, 1)
    turned = turn_lanes(key_grad * sin[0:filled, :], low_lanes((filled, 128), HEAD // 2))
    key_grad = key_grad * cos[0:filled, :] + turned
    dqkv[0:filled, q_cols:] = jnp.where(low, key_grad, value_grad).astype(bf16)

    def qkv_term(m, carry):
        here = pl.ds(pl.multiple_of(m * wrows, wrows), wrows)
        left = normed[:, :, here].reshape(filled, wrows)
        value = dot_tile(left, dqkv[0:filled, :], 0, 0)
        at_terms[lax.div(m, 4), lax.rem(m, 4), :, :qkv_cols] = value.astype(bf16)
        return carry

    lax.fori_loop(0, width // wrows, qkv_term, 0)
    qkv_sums = terms_to(pl.ds(0, qkv_cols))
    crosses, outs = {}, {}
    for k in (3, 1, 2, 0):
        mine_rows = pl.ds(pl.multiple_of(flip(c, k) * rows, rows), rows)

        def back_tile(n, carry, mine_rows=mine_rows):
            here = pl.ds(pl.multiple_of(n * 128, 128), 128)
            w = wa[lax.div(n, 4), lax.rem(n, 4), :, :qkv_cols]
            sums[:, here] = dot_tile(dqkv[mine_rows, :], w, 1, 1)
            return carry

        lax.fori_loop(0, width // 128, back_tile, 0)
        mine[k] = sums[pl.ds(pl.multiple_of(t * part, part), part), :]
        cross[k] = sums[pl.ds(pl.multiple_of((1 - t) * part, part), part), :].astype(bf16)
        crosses[k] = net.start(cross.at[k], crossed.at[k], core)
    for k in (3, 1, 2):
        crosses[k].wait_recv()
        totals[k - 1] = (mine[k] + crossed[k].astype(f32)).astype(bf16)
        outs[k] = net.start(totals.at[k - 1], back_in.at[k - 1], (z, flip(c, k), t))
    crosses[0].wait_recv()
    back_own[...] = mine[0] + crossed[0].astype(f32)

    owners(1)
    owners(0)
    qkv_sums.hand_on()
    output_sums.wait_in()
    qkv_sums.wait_in()
    for j in range(4):
        total = at_terms[z, j].astype(f32)
        for i in range(2):
            total = total + at_in[i, j].astype(f32)
        at_total[j] = total.astype(bf16)
    here = pl.ds(pl.multiple_of(c * q_cols, q_cols), q_cols)
    attn_out, keep_own = [], []
    for i, (columns, target) in enumerate(
        (
            (pl.ds(0, q_cols), query_out.at[:, here]),
            (pl.ds(q_cols, 2 * HEAD), kv_out.at[c]),
            (pl.ds(qkv_cols, q_cols), output_out.at[:, here]),
        )
    ):
        attn_out += [net.start(at_total.at[flip(c, k), :, columns], target, (z, flip(c, k), t)) for k in (1, 2, 3)]
        keep_own.append(pltpu.make_async_copy(at_total.at[c, :, columns], target, local.at[7 + i]))
        keep_own[-1].start()
    feed.wait_in()
    for chain in chains:
        chain.wait_out()
    for copy in attn_out + [outs[k] for k in (1, 2, 3)] + [third[k] for k in (1, 2, 3)]:
        copy.wait_recv()
    for copy in net.started:
        copy.wait_send()
    third[0].wait()
    for copy in keep_own:
        copy.wait()


def backward(ff, fs, al, wa, normed, q, kv, logs, attended, cos, sin, seg_col, seg_row):
    bf16, f32 = jnp.bfloat16, jnp.float32
    wrows, hidden = ff.shape[3:]
    attn_cols = wa.shape[3]
    part, width = al.shape
    total = q.shape[0]
    filled = seg_col.shape[0]
    rows = 2 * part
    blocks = filled // rows
    copies = 64
    vmem, anywhere = pl.BlockSpec(memory_space=pltpu.VMEM), pl.BlockSpec(memory_space=pl.ANY)
    return pl.pallas_call(
        backward_kernel,
        out_shape=[
            jax.ShapeDtypeStruct((2,) + al.shape, bf16),
            jax.ShapeDtypeStruct(al.shape, f32),
            jax.ShapeDtypeStruct(fs.shape, bf16),
            jax.ShapeDtypeStruct((3, wrows, 4 * hidden), bf16),
            jax.ShapeDtypeStruct((wrows, 4 * q.shape[1]), bf16),
            jax.ShapeDtypeStruct((4, wrows, 2 * HEAD), bf16),
            jax.ShapeDtypeStruct((wrows, 4 * q.shape[1]), bf16),
        ],
        in_specs=[anywhere, vmem, vmem, anywhere, anywhere] + [vmem] * 8,
        out_specs=[anywhere, vmem] + [anywhere] * 5,
        scratch_shapes=[
            pltpu.VMEM(ff.shape, bf16),
            pltpu.VMEM((4, 3, wrows // 2, hidden), bf16),
            pltpu.VMEM((4, 3, wrows // 2, hidden), bf16),
            pltpu.VMEM((4, 3, wrows, hidden), bf16),
            pltpu.VMEM((4, 3, wrows, hidden), bf16),
            pltpu.VMEM((4, 4, wrows, attn_cols), bf16),
            pltpu.VMEM((2, 4, wrows, attn_cols), bf16),
            pltpu.VMEM((4, wrows, attn_cols), bf16),
            pltpu.VMEM(wa.shape, bf16),
            pltpu.VMEM((blocks, rows, width), bf16),
            pltpu.VMEM((4, 2, part, width), bf16),
            pltpu.VMEM((4, total, 2 * HEAD), bf16),
            pltpu.VMEM((filled, q.shape[1]), bf16),
            pltpu.VMEM((4, filled, 2 * HEAD), f32),
            pltpu.VMEM((total, q.shape[1] + 2 * HEAD), bf16),
            pltpu.VMEM((rows, width), f32),
            pltpu.VMEM((4, part, width), f32),
            pltpu.VMEM((4, part, width), bf16),
            pltpu.VMEM((4, part, width), bf16),
            pltpu.VMEM((3, part, width), bf16),
            pltpu.VMEM((2, part, width), bf16),
            pltpu.VMEM((2, 4, wrows, attn_cols), bf16),
            pltpu.SemaphoreType.DMA((copies,)),
            pltpu.SemaphoreType.DMA((copies,)),
            pltpu.SemaphoreType.DMA((10,)),
        ],
        compiler_params=pltpu.CompilerParams(collective_id=2, has_side_effects=True, vmem_limit_bytes=63 * 2**20),
    )(ff, fs, al, wa, normed, q, kv, logs, attended, cos, sin, seg_col, seg_row)


def on_device_split(
    tokens,
    out_grad,
    lengths,
    attention_gain,
    query_weight,
    key_weight,
    value_weight,
    output_weight,
    feed_gain,
    gate_weight,
    up_weight,
    down_weight,
):
    f32, bf16 = jnp.float32, jnp.bfloat16
    nz, nc, nt = (lax.axis_size(a) for a in (FSDP, CONTEXT, TENSOR))
    z, c, t = (lax.axis_index(a) for a in (FSDP, CONTEXT, TENSOR))
    local_rows, width = tokens.shape[1:]
    group_rows = local_rows * nc
    filled = group_rows * 3 // 4
    part = local_rows // nt
    wrows = query_weight.shape[0]
    kv_cols = key_weight.shape[1] // nc
    q_cols = query_weight.shape[1] // nc
    qkv_cols = q_cols + 2 * kv_cols
    ff_cols = gate_weight.shape[1] // nz
    per_group = q_cols // kv_cols
    segment, position, valid_rows = slot_layout(lengths[0], group_rows)
    cos_table, sine_table = rope_tables(position, HEAD)

    wa = jnp.concatenate(
        [
            w.astype(bf16).reshape(wrows, nc, -1).transpose(1, 0, 2)
            for w in (query_weight, key_weight, value_weight, output_weight)
        ],
        axis=2,
    )
    wf = jnp.stack([w.astype(bf16) for w in (gate_weight, up_weight, down_weight)])
    gain = jnp.pad(jnp.stack([attention_gain, feed_gain]).astype(bf16), ((0, 14), (0, 0)))
    my_valid = lax.dynamic_slice_in_dim(valid_rows, c * local_rows + t * part, part)
    cotangent = cut(out_grad[0], t, part, 0).astype(f32) * my_valid[:, None].astype(f32)
    feed_grad = (residual_mult * cotangent).astype(bf16)
    sign = jnp.where(jnp.arange(HEAD) < HEAD // 2, -1.0, 1.0).astype(f32)
    wide_cos = jnp.concatenate([cos_table, cos_table], axis=1)
    wide_sin = jnp.concatenate([sine_table * sign, sine_table * sign], axis=1)
    wa, wf, normed_one, queries, pair, logs, attended, hidden, normed_two, feed_grads, gains = attention_forward(
        wa, wf, tokens[0].reshape(nt, part, width), gain, feed_grad, wide_cos, wide_sin,
        segment[:filled, None], segment[None, :filled],
    )
    gain_one, gain_two = gains[0], gains[1]
    w_feed = wf.reshape(3, width, ff_cols)
    my_inputs = cut(tokens[0], t, part, 0).astype(f32)
    inverse_two = lax.rsqrt(jnp.mean(hidden * hidden, axis=-1, keepdims=True) + norm_eps)
    unit_two = hidden * inverse_two

    normed_grad_two, feed_own, feed_send, ff_terms = feed_forward(
        normed_two, feed_grads.reshape(nz, local_rows, width), w_feed
    )
    ff_terms = ff_terms.reshape(3, nz, nc, wrows, ff_cols)

    def both_cores(x):
        other = swap(x, TENSOR, 1)
        first, last = jnp.where(t == 0, x, other), jnp.where(t == 0, other, x)
        return jnp.concatenate([first, last], axis=0)[None]

    feed_gain_term = jnp.sum(normed_grad_two * unit_two, axis=0)
    hidden_grad = cotangent + norm_back(normed_grad_two, unit_two, gain_two, inverse_two)

    attn_low = (residual_mult * hidden_grad).astype(bf16)
    feed_in, back_own, back_in, ff_grads, grad_query, kv_grads, grad_output = backward(
        ff_terms, feed_send, attn_low, wa, normed_one, queries, pair, logs, attended, wide_cos, wide_sin,
        segment[:filled, None], segment[None, :filled],
    )
    output = both_cores((hidden + residual_mult * (feed_own + jnp.sum(feed_in.astype(f32), axis=0))).astype(bf16))
    normed_grad_one = back_own + jnp.sum(back_in.astype(f32), axis=0)
    inverse_one = lax.rsqrt(jnp.mean(my_inputs * my_inputs, axis=-1, keepdims=True) + norm_eps)
    unit_one = my_inputs * inverse_one
    attn_gain_term = jnp.sum(normed_grad_one * unit_one, axis=0)
    input_grad = both_cores((hidden_grad + norm_back(normed_grad_one, unit_one, gain_one, inverse_one)).astype(bf16))

    gain_terms = jnp.stack([attn_gain_term, feed_gain_term])
    for axis in (TENSOR, CONTEXT, FSDP):
        gain_terms = gain_terms + sum(swap(gain_terms, axis, k) for k in range(1, lax.axis_size(axis)))
    gain_terms = cut(gain_terms, z * nc + c, wrows, 1)

    grad_gate, grad_up, grad_down = (ff_grads[i].astype(f32) for i in range(3))
    grad_key, grad_value = (
        kv_grads[:, :, i : i + HEAD].transpose(1, 0, 2).reshape(wrows, -1).astype(f32) for i in (0, HEAD)
    )
    attn_terms = (grad_query.astype(f32), grad_key, grad_value, grad_output.astype(f32))
    return (output, input_grad, gain_terms[0], *attn_terms, gain_terms[1], grad_gate, grad_up, grad_down)


def solution(mesh):
    split = tuple(mesh.shape[a] for a in (FSDP, CONTEXT, TENSOR)) == (4, 4, 2)
    return jax.shard_map(
        on_device_split if split else on_device,
        mesh=mesh,
        in_specs=(
            P(FSDP, CONTEXT, None),
            P(FSDP, CONTEXT, None),
            P(FSDP, None),
            P((FSDP, CONTEXT)),
            P((FSDP, CONTEXT), TENSOR),
            P((FSDP, CONTEXT), TENSOR),
            P((FSDP, CONTEXT), TENSOR),
            P((FSDP, CONTEXT), TENSOR),
            P((FSDP, CONTEXT)),
            P((FSDP, CONTEXT), TENSOR),
            P((FSDP, CONTEXT), TENSOR),
            P((FSDP, CONTEXT), TENSOR),
        ),
        out_specs=(
            P(FSDP, CONTEXT, None),
            P(FSDP, CONTEXT, None),
            P((FSDP, CONTEXT)),
            P((FSDP, CONTEXT), TENSOR),
            P((FSDP, CONTEXT), TENSOR),
            P((FSDP, CONTEXT), TENSOR),
            P((FSDP, CONTEXT), TENSOR),
            P((FSDP, CONTEXT)),
            P((FSDP, CONTEXT), TENSOR),
            P((FSDP, CONTEXT), TENSOR),
            P((FSDP, CONTEXT), TENSOR),
        ),
        check_vma=False,
    )
```
